32 devices in a mesh: wide: 8 (over y, x, core), narrow: 4 (over z).
Axes of the slice: x: 2, y: 2, z: 4, core: 2. Of those that a mesh axis runs over, the one named last changes fastest.
Arguments:
- tokens: bfloat16 [8, 2048, 768], P('narrow', 'wide'), may hold values from -6 to 6
- cotangent: bfloat16 [8, 2048, 768], P('narrow', 'wide'), may hold values from -6 to 6
- selected: int32 [8, 2048], P('narrow'), may hold values from 0 to 1, as said below
- segments: int32 [8, 2048], P('narrow'), may hold values from 0 to 3, never falling along the last dimension, each value on 1 to 1024 neighbouring positions
- router_vector: bfloat16 [768], replicated, may hold values from -0.21875 to 0.21875
- project_routed: bfloat16 [768, 2304], replicated, may hold values from -0.21875 to 0.21875
- output_routed: bfloat16 [768, 768], replicated, may hold values from -0.875 to 0.875
- prenorm_routed: bfloat16 [768], replicated, may hold values from 0.5 to 1.5
- midnorm_routed: bfloat16 [768], replicated, may hold values from 0.5 to 1.5
- expand_routed: bfloat16 [768, 3072], P(None, 'narrow'), may hold values from -0.21875 to 0.21875
- reduce_routed: bfloat16 [3072, 768], P('narrow'), may hold values from -0.109375 to 0.109375
- project_dense: bfloat16 [768, 2304], replicated, may hold values from -0.21875 to 0.21875
- output_dense: bfloat16 [768, 768], replicated, may hold values from -1.25 to 1.25
- prenorm_dense: bfloat16 [768], replicated, may hold values from 0.5 to 1.5
- midnorm_dense: bfloat16 [768], replicated, may hold values from 0.5 to 1.5
- expand_dense: bfloat16 [768, 3072], P(None, 'narrow'), may hold values from -0.21875 to 0.21875
- reduce_dense: bfloat16 [3072, 768], P('narrow'), may hold values from -0.109375 to 0.109375
Outputs:
- activations: bfloat16 [8, 2048, 768], P('narrow', 'wide')
- tokens_gradient: float32 [8, 2048, 768], P('narrow', 'wide')
- router_gradient: float32 [768], P('wide')
- project_routed_gradient: float32 [768, 2304], P('wide')
- output_routed_gradient: float32 [768, 768], P('wide')
- prenorm_routed_gradient: float32 [768], P('wide')
- midnorm_routed_gradient: float32 [768], P('wide')
- expand_routed_gradient: float32 [768, 3072], P('wide', 'narrow')
- reduce_routed_gradient: float32 [3072, 768], P('narrow', 'wide')
- project_dense_gradient: float32 [768, 2304], P('wide')
- output_dense_gradient: float32 [768, 768], P('wide')
- prenorm_dense_gradient: float32 [768], P('wide')
- midnorm_dense_gradient: float32 [768], P('wide')
- expand_dense_gradient: float32 [768, 3072], P('wide', 'narrow')
- reduce_dense_gradient: float32 [3072, 768], P('narrow', 'wide')
The draws below stay inside these ranges and needn't reach their ends.
Inputs may be any that keep to these rules, and one draw needn't show every extreme that they name: `selected`: every row holds exactly 256 ones. Of the 256 positions that one index of wide holds in a row, at most 64 are 1, and in every row some index of wide holds exactly 64.
All inputs are finite; a program needn't handle non-finite values.
Results may differ from the reference program's by a relative error of at most 0.024.
Values may be sent and summed in bfloat16 or wider, within the bound.
No kernel may reach another device: no remote copies, remote signals or barrier semaphores. Data moves between devices by JAX's collectives and lax.ppermute only.
A program may use at most 320 MiB of HBM per device.

```python
import math
import jax
import jax.numpy as jnp
import numpy as np
from jax import lax

D = 768
H = 12
HD = 64
FF = 3072
L = 2048
SEQS = 8
POS_DEV = 256
SELECT = 256


def draw_selected(key, part):
    group_count = L // POS_DEV
    pair_count = group_count // 2
    base_count = POS_DEV // 8
    key_shift, key_forced, key_flip, key_rank = jax.random.split(key, 4)
    shift_amount = jax.random.randint(key_shift, (SEQS, pair_count), 0, base_count + 1)
    forced = jax.random.randint(key_forced, (SEQS, 1), 0, pair_count)
    shift_amount = jnp.where(jnp.arange(pair_count)[None, :] == forced, base_count, shift_amount)
    flip_sign = 1 - 2 * jax.random.randint(key_flip, (SEQS, pair_count), 0, 2)
    counts = jnp.stack([base_count + flip_sign * shift_amount, base_count - flip_sign * shift_amount], axis=-1).reshape(SEQS * group_count)
    rank_keys = jax.random.split(key_rank, SEQS * group_count)
    orders = jax.vmap(lambda one_key: jax.random.permutation(one_key, POS_DEV))(rank_keys)
    rank_table = jnp.argsort(orders, axis=-1, stable=True)
    chosen = rank_table < counts[:, None]
    return chosen.reshape(SEQS, L).astype(jnp.int32)


def levels(key, shape, cuts, smallest, top_value):
    loudness, own = 1.0, jax.random.fold_in(key, 6)
    for axis_at, shards_of in cuts:
        heights = jnp.exp(jax.random.uniform(jax.random.fold_in(own, axis_at), (shards_of,), jnp.float32, smallest / len(cuts), top_value / len(cuts)))
        loudness = loudness * jnp.repeat(heights, shape[axis_at] // shards_of).reshape([-1 if axis == axis_at else 1 for axis in range(len(shape))])
    return loudness


def profile(number_of, total, limit, slope):
    portions = [(1 << 20) // math.isqrt(rank ** slope) + 1 for rank in range(2, number_of + 1)]
    rest, given = total - limit - (number_of - 1), [1] * (number_of - 1)
    while rest > 0:
        free = [i for i in range(number_of - 1) if given[i] < limit]
        pool, remaining = sum([portions[i] for i in free]), rest
        for i in free:
            more = min(limit - given[i], max(1, remaining * portions[i] // pool), rest)
            given[i] = given[i] + more
            rest = rest - more
    return np.array([limit] + given)


def uneven(key, number_of, total, most, slope):
    if number_of == 2:
        one = jax.random.randint(key, (), max(1, total - most), min(most, total - 1) + 1)
        return jnp.stack([one, total - one])
    sizes = jnp.asarray(profile(number_of, total, most, slope), jnp.int32)
    couples = (number_of - 1) // 2
    donor, sink = sizes[1:1 + 2 * couples:2], sizes[2:2 + 2 * couples:2]
    margin = jnp.minimum(donor - 1, most - sink)
    passed = jax.random.randint(jax.random.fold_in(key, 1), (couples,), 0, 1 << 20) % (margin + 1)
    sizes = sizes.at[1:1 + 2 * couples:2].set(donor - passed).at[2:2 + 2 * couples:2].set(sink + passed)
    return sizes[jax.random.permutation(jax.random.fold_in(key, 2), number_of)]


def bell_draw(rng, extent, spread, limit, cuts=(), kind=jnp.bfloat16):
    entries = spread * jax.random.normal(rng, extent, jnp.float32)
    if cuts:
        entries = entries * levels(rng, extent, cuts, -0.22, 0.18)
    return jnp.clip(entries, -limit, limit).astype(kind)


def setup_inputs(seed: int = 0) -> dict:
    seeds = jax.random.split(jax.random.key(seed), 18)
    tokens = bell_draw(seeds[0], (SEQS, L, D), 1.0, 6.0, ((0, 4), (1, 8)))
    cotangent = bell_draw(seeds[1], (SEQS, L, D), 1.0, 6.0, ((0, 4), (1, 8)))
    selected = draw_selected(jax.random.fold_in(seeds[17], 71), 0)
    segments = jax.vmap(lambda own: jnp.searchsorted(jnp.cumsum(uneven(own, 4, L, L // 2, 0)), jnp.arange(L), side="right"))(jax.random.split(seeds[3], SEQS)).reshape((SEQS, L)).astype(jnp.int32)
    router_vector = bell_draw(seeds[4], (D,), D ** -0.5, 0.21875)
    project_routed = bell_draw(seeds[5], (D, 3 * D), D ** -0.5, 0.21875)
    output_routed = bell_draw(seeds[6], (D, D), (D // 16) ** -0.5, 0.875)
    prenorm_routed = jnp.clip(1.0 + 0.1 * jax.random.normal(seeds[7], (D,), jnp.float32), 0.5, 1.5).astype(jnp.bfloat16)
    midnorm_routed = jnp.clip(1.0 + 0.1 * jax.random.normal(seeds[8], (D,), jnp.float32), 0.5, 1.5).astype(jnp.bfloat16)
    expand_routed = bell_draw(seeds[9], (D, FF), D ** -0.5, 0.21875, ((1, 4),))
    reduce_routed = bell_draw(seeds[10], (FF, D), FF ** -0.5, 0.109375, ((0, 4),))
    project_dense = bell_draw(seeds[11], (D, 3 * D), D ** -0.5, 0.21875)
    output_dense = bell_draw(seeds[12], (D, D), (D // 32) ** -0.5, 1.25)
    prenorm_dense = jnp.clip(1.0 + 0.1 * jax.random.normal(seeds[13], (D,), jnp.float32), 0.5, 1.5).astype(jnp.bfloat16)
    midnorm_dense = jnp.clip(1.0 + 0.1 * jax.random.normal(seeds[14], (D,), jnp.float32), 0.5, 1.5).astype(jnp.bfloat16)
    expand_dense = bell_draw(seeds[15], (D, FF), D ** -0.5, 0.21875, ((1, 4),))
    reduce_dense = bell_draw(seeds[16], (FF, D), FF ** -0.5, 0.109375, ((0, 4),))
    return {"tokens": tokens, "cotangent": cotangent, "selected": selected, "segments": segments, "router_vector": router_vector, "project_routed": project_routed, "output_routed": output_routed, "prenorm_routed": prenorm_routed, "midnorm_routed": midnorm_routed, "expand_routed": expand_routed, "reduce_routed": reduce_routed, "project_dense": project_dense, "output_dense": output_dense, "prenorm_dense": prenorm_dense, "midnorm_dense": midnorm_dense, "expand_dense": expand_dense, "reduce_dense": reduce_dense}


EPSILON = 1e-06
NEGATIVE = -1e+30
SCORE_SCALE = 0.125
PRECISE = lax.Precision.HIGHEST

@jax.custom_vjp
def low(v):
    return lax.optimization_barrier(v.astype(jnp.bfloat16)).astype(jnp.float32)

@jax.custom_vjp
def low_back(v):
    return v

def low_keep(v):
    return (low(v), None)

def low_pass(kept, grad):
    return (grad,)

def back_keep(v):
    return (v, None)

def back_low(kept, grad):
    return (low(grad),)
low.defvjp(low_keep, low_pass)
low_back.defvjp(back_keep, back_low)

def rms_gain(vector_in, gain_vector):
    return vector_in * lax.rsqrt(lax.optimization_barrier(jnp.mean(vector_in * vector_in, axis=-1, keepdims=True)) + EPSILON) * gain_vector

def attend_rows(query_rows, query_pos, query_seg, key_rows, value_rows, key_pos, key_seg):
    row_count = query_rows.shape[0]
    key_count = key_rows.shape[0]
    query_heads = query_rows.reshape(row_count, H, HD)
    key_heads = key_rows.reshape(key_count, H, HD)
    value_heads = value_rows.reshape(key_count, H, HD)
    scores = jnp.einsum('qhd,khd->hqk', query_heads, key_heads, precision=PRECISE) * SCORE_SCALE
    scores = low_back(scores)
    allowed = (key_pos[None, :] <= query_pos[:, None]) & (key_seg[None, :] == query_seg[:, None])
    scores = jnp.where(allowed[None], scores, NEGATIVE)
    weights_soft = low(jax.nn.softmax(scores, axis=-1))
    attended = jnp.einsum('hqk,khd->qhd', weights_soft, value_heads, precision=PRECISE)
    return attended.reshape(row_count, H * HD)

def block(rows_in, positions, seg_rows, project, output, prenorm, midnorm, expand, reduce_weights):
    row_count = rows_in.shape[0]
    model_width = rows_in.shape[1]
    normed = low(rms_gain(rows_in, prenorm))
    projected = low(low_back(jnp.dot(normed, project, precision=PRECISE)))
    queries = projected[:, :model_width]
    key_rows = projected[:, model_width:2 * model_width]
    value_rows = projected[:, 2 * model_width:]
    block_rows = min(row_count, 512)
    block_count = row_count // block_rows
    kept_attend = jax.checkpoint(attend_rows)
    attended = lax.map(lambda inputs_block: kept_attend(inputs_block[0], inputs_block[1], inputs_block[2], key_rows, value_rows, positions, seg_rows), (queries.reshape(block_count, block_rows, model_width), positions.reshape(block_count, block_rows), seg_rows.reshape(block_count, block_rows)))
    attended = low(low_back(attended.reshape(row_count, model_width)))
    branch = low_back(jnp.dot(attended, output, precision=PRECISE))
    middle = rows_in + branch
    normed_mid = low(rms_gain(middle, midnorm))
    hidden_pre = low_back(jnp.dot(normed_mid, expand, precision=PRECISE))
    hidden = low(jax.nn.gelu(hidden_pre, approximate=True))
    reduced = low_back(jnp.dot(hidden, reduce_weights, precision=PRECISE))
    return branch + reduced

def forward(row_tokens, picked_order, row_segments, router_vector, project_routed, output_routed, prenorm_routed, midnorm_routed, expand_routed, reduce_routed, project_dense, output_dense, prenorm_dense, midnorm_dense, expand_dense, reduce_dense):
    logits = jnp.dot(row_tokens, router_vector, precision=PRECISE)
    picked = jnp.take(row_tokens, picked_order, axis=0)
    routed_delta = block(picked, picked_order, jnp.take(row_segments, picked_order), project_routed, output_routed, prenorm_routed, midnorm_routed, expand_routed, reduce_routed)
    mixed = row_tokens.at[picked_order].add(jnp.take(logits, picked_order)[:, None] * routed_delta)
    positions = jnp.arange(row_tokens.shape[0], dtype=jnp.int32)
    dense_delta = block(mixed, positions, row_segments, project_dense, output_dense, prenorm_dense, midnorm_dense, expand_dense, reduce_dense)
    return mixed + dense_delta

def reference(tokens, cotangent, selected, segments, router_vector, project_routed, output_routed, prenorm_routed, midnorm_routed, expand_routed, reduce_routed, project_dense, output_dense, prenorm_dense, midnorm_dense, expand_dense, reduce_dense):
    weights = tuple((weight.astype(jnp.float32) for weight in (router_vector, project_routed, output_routed, prenorm_routed, midnorm_routed, expand_routed, reduce_routed, project_dense, output_dense, prenorm_dense, midnorm_dense, expand_dense, reduce_dense)))

    def scan_step(totals, inputs_row):
        row_tokens, row_cotangent, row_selected, row_segments = inputs_row
        picked_order = jnp.argsort(1 - row_selected, stable=True)[:SELECT].astype(jnp.int32)

        def run_forward(tokens_float, *weight_list):
            return forward(tokens_float, picked_order, row_segments, *weight_list)
        result, pullback = jax.vjp(run_forward, row_tokens.astype(jnp.float32), *weights)
        gradients = pullback(row_cotangent.astype(jnp.float32))
        totals = tuple((total_now + grad_now for total_now, grad_now in zip(totals, gradients[1:])))
        return (totals, (result.astype(jnp.bfloat16), gradients[0]))
    start_totals = tuple((jnp.zeros_like(weight) for weight in weights))
    totals, (activations, tokens_gradient) = lax.scan(scan_step, start_totals, (tokens, cotangent, selected, segments))
    return (activations, tokens_gradient, totals[0], totals[1], totals[2], totals[3], totals[4], totals[5], totals[6], totals[7], totals[8], totals[9], totals[10], totals[11], totals[12])
```

```python
from functools import partial

import jax
import jax.numpy as jnp
from jax import lax
from jax.experimental import pallas as pl
from jax.experimental.pallas import tpu as pltpu
from jax.sharding import PartitionSpec as P

H = 12
HD = 64
GROUPS = 4
HG = H // GROUPS
GW = HG * HD

EPSILON = 1e-06
NEGATIVE = -1e30
SCORE_SCALE = 0.125
LOG2E = 1.4426950408889634
PRECISE = lax.Precision.HIGHEST
BF = jnp.bfloat16
F32 = jnp.float32
VMEM = 48 << 20


def rms_gain(vector_in, gain_vector):
    return (
        vector_in
        * lax.rsqrt(jnp.mean(vector_in * vector_in, axis=-1, keepdims=True) + EPSILON)
        * gain_vector
    )


def smooth_gelu(hidden_pre):
    return jax.nn.gelu(hidden_pre, approximate=True)


def nt_dot(left, right):
    return lax.dot_general(left, right, (((1,), (1,)), ((), ())), preferred_element_type=F32)


def tn_dot(left, right):
    return lax.dot_general(left, right, (((0,), (0,)), ((), ())), preferred_element_type=F32)


def dot(left, right):
    return jnp.dot(left, right, preferred_element_type=F32)


def head_parts(rows):
    lane = lax.broadcasted_iota(jnp.int32, rows.shape, 1)
    zero = jnp.zeros_like(rows)
    return [
        jnp.where((lane >= h * HD) & (lane < (h + 1) * HD), rows, zero) for h in range(HG)
    ]


def pair_mask(row_ref, col_ref, q_at, k_at, bk, bq):
    k_iota = lax.broadcasted_iota(jnp.int32, (bk, bq), 0) + k_at
    q_iota = lax.broadcasted_iota(jnp.int32, (bk, bq), 1) + q_at
    info = row_ref[0:1, pl.ds(q_at, bq)]
    if col_ref is None:
        return (k_iota >= info) & (k_iota <= q_iota)
    return (col_ref[pl.ds(k_at, bk), :] == info) & (k_iota <= q_iota)


def attend_kernel(bq, bk, by_column, first_ref, x_ref, row_ref, *rest):
    if by_column:
        col_ref, o_ref, lse_ref, k_s, vt_s = rest
    else:
        col_ref = None
        o_ref, lse_ref, k_s, vt_s = rest
    i = pl.program_id(0)

    @pl.when(i == 0)
    def _():
        k_s[...] = x_ref[:, GW : 2 * GW]
        vt_s[...] = x_ref[:, 2 * GW : 3 * GW].T

    q_at = pl.multiple_of(i * bq, bq)
    q_heads = head_parts(x_ref[pl.ds(q_at, bq), 0:GW])

    def step(j, carry):
        k_at = pl.multiple_of(j * bk, bk)
        keys = k_s[pl.ds(k_at, bk), :]
        mask = pair_mask(row_ref, col_ref, q_at, k_at, bk, bq)
        out = []
        for h in range(HG):
            top, total, acc = carry[h]
            scores = nt_dot(keys, q_heads[h]) * (SCORE_SCALE * LOG2E)
            scores = jnp.where(mask, scores, NEGATIVE)
            top_new = jnp.maximum(top, jnp.max(scores, axis=0, keepdims=True))
            weight = jnp.exp2(scores - top_new)
            fade = jnp.exp2(top - top_new)
            total = total * fade + jnp.sum(weight, axis=0, keepdims=True)
            values_t = vt_s[h * HD : (h + 1) * HD, pl.ds(k_at, bk)]
            acc = acc * fade + dot(values_t, weight.astype(BF))
            out.append((top_new, total, acc))
        return tuple(out)

    start = tuple(
        (
            jnp.full((1, bq), NEGATIVE, F32),
            jnp.zeros((1, bq), F32),
            jnp.zeros((HD, bq), F32),
        )
        for _ in range(HG)
    )
    done = lax.fori_loop(first_ref[i], (q_at + bq + bk - 1) // bk, step, start)
    outs = jnp.concatenate([acc / total for _, total, acc in done], axis=0)
    o_ref[...] = outs.T.astype(BF)
    for h in range(HG):
        top, total, _ = done[h]
        lse_ref[h : h + 1, :] = top + jnp.log2(total)


def attend_back_kernel(bq, bk, by_column, first_ref, x_ref, row_ref, *rest):
    if by_column:
        col_ref, o_ref, g_ref, lse_ref, dx_ref, k_s, v_s, dk_s, dv_s = rest
    else:
        col_ref = None
        o_ref, g_ref, lse_ref, dx_ref, k_s, v_s, dk_s, dv_s = rest
    i = pl.program_id(0)

    @pl.when(i == 0)
    def _():
        k_s[...] = x_ref[:, GW : 2 * GW]
        v_s[...] = x_ref[:, 2 * GW : 3 * GW]
        dk_s[...] = jnp.zeros_like(dk_s)
        dv_s[...] = jnp.zeros_like(dv_s)

    q_at = pl.multiple_of(i * bq, bq)
    grad = g_ref[...]
    q_heads = head_parts(x_ref[pl.ds(q_at, bq), 0:GW])
    g_heads = head_parts(grad)
    dots = (grad.astype(F32) * o_ref[...].astype(F32)).T
    row_dot = [
        jnp.sum(dots[h * HD : (h + 1) * HD, :], axis=0, keepdims=True) for h in range(HG)
    ]

    def step(j, dq):
        k_at = pl.multiple_of(j * bk, bk)
        here = pl.ds(k_at, bk)
        keys = k_s[here, :]
        values = v_s[here, :]
        key_heads = head_parts(keys)
        mask = pair_mask(row_ref, col_ref, q_at, k_at, bk, bq)
        dk = dk_s[here, :]
        dv = dv_s[here, :]
        for h in range(HG):
            scores = nt_dot(keys, q_heads[h]) * (SCORE_SCALE * LOG2E)
            scores = jnp.where(mask, scores - lse_ref[h : h + 1, :], NEGATIVE)
            soft = jnp.exp2(scores)
            g_soft = nt_dot(values, g_heads[h])
            g_scores = (soft * (g_soft - row_dot[h])).astype(BF)
            dv = dv + dot(soft.astype(BF), g_heads[h])
            dk = dk + dot(g_scores, q_heads[h])
            dq = dq + tn_dot(g_scores, key_heads[h])
        dk_s[here, :] = dk
        dv_s[here, :] = dv
        return dq

    dq = lax.fori_loop(
        first_ref[i], (q_at + bq + bk - 1) // bk, step, jnp.zeros((bq, GW), F32)
    )
    dx_ref[pl.ds(q_at, bq), 0:GW] = (dq * SCORE_SCALE).astype(BF)

    @pl.when(i == pl.num_programs(0) - 1)
    def _():
        dx_ref[:, GW : 2 * GW] = (dk_s[...] * SCORE_SCALE).astype(BF)
        dx_ref[:, 2 * GW : 3 * GW] = dv_s[...].astype(BF)


def whole(shape):
    return pl.BlockSpec(shape, lambda i, *_: (0, 0))


def attend(x, first, row_info, col_info, bq):
    length = x.shape[0]
    by_column = col_info is not None
    in_specs = [whole(x.shape), whole(row_info.shape)]
    operands = [x, row_info]
    if by_column:
        in_specs.append(whole(col_info.shape))
        operands.append(col_info)
    return pl.pallas_call(
        partial(attend_kernel, bq, bq, by_column),
        out_shape=(
            jax.ShapeDtypeStruct((length, GW), BF),
            jax.ShapeDtypeStruct((8, length), F32),
        ),
        grid_spec=pltpu.PrefetchScalarGridSpec(
            num_scalar_prefetch=1,
            grid=(length // bq,),
            in_specs=in_specs,
            out_specs=(
                pl.BlockSpec((bq, GW), lambda i, *_: (i, 0)),
                pl.BlockSpec((8, bq), lambda i, *_: (0, i)),
            ),
            scratch_shapes=[pltpu.VMEM((length, GW), BF), pltpu.VMEM((GW, length), BF)],
        ),
        compiler_params=pltpu.CompilerParams(vmem_limit_bytes=VMEM),
        cost_estimate=pl.CostEstimate(
            flops=length * length * GW, bytes_accessed=length * GW * 8, transcendentals=0
        ),
        name="attend",
    )(first, *operands)


def attend_back(x, first, row_info, col_info, attended, grad, lse, bq):
    length = x.shape[0]
    by_column = col_info is not None
    in_specs = [whole(x.shape), whole(row_info.shape)]
    operands = [x, row_info]
    if by_column:
        in_specs.append(whole(col_info.shape))
        operands.append(col_info)
    in_specs += [
        pl.BlockSpec((bq, GW), lambda i, *_: (i, 0)),
        pl.BlockSpec((bq, GW), lambda i, *_: (i, 0)),
        pl.BlockSpec((8, bq), lambda i, *_: (0, i)),
    ]
    operands += [attended, grad, lse]
    return pl.pallas_call(
        partial(attend_back_kernel, bq, bq, by_column),
        out_shape=jax.ShapeDtypeStruct(x.shape, BF),
        grid_spec=pltpu.PrefetchScalarGridSpec(
            num_scalar_prefetch=1,
            grid=(length // bq,),
            in_specs=in_specs,
            out_specs=whole(x.shape),
            scratch_shapes=[
                pltpu.VMEM((length, GW), BF),
                pltpu.VMEM((length, GW), BF),
                pltpu.VMEM((length, GW), F32),
                pltpu.VMEM((length, GW), F32),
            ],
        ),
        compiler_params=pltpu.CompilerParams(vmem_limit_bytes=VMEM),
        cost_estimate=pl.CostEstimate(
            flops=3 * length * length * GW, bytes_accessed=length * GW * 16, transcendentals=0
        ),
        name="attend_back",
    )(first, *operands)


def exchange(parts):
    return lax.all_to_all(parts, "wide", 0, 0)


def to_heads(parts):
    groups, rows, width = parts.shape
    wide_count = lax.axis_size("wide")
    parts = parts.reshape(groups * 2, rows // 2, width)
    parts = jnp.tile(parts, (wide_count // (groups * 2), 1, 1))
    return exchange(parts).reshape(-1, width)


def to_rows(rows):
    wide_count = lax.axis_size("wide")
    width = rows.shape[1]
    parts = exchange(rows.reshape(wide_count, -1, width))
    return parts[: GROUPS * 2].reshape(GROUPS, -1, width)


def mlp_forward(rows_in, expand_part, reduce_part):
    gathered = lax.all_gather(rows_in, "narrow", axis=0, tiled=True)
    hidden_pre = jnp.dot(gathered, expand_part, preferred_element_type=jnp.float32)
    hidden = smooth_gelu(hidden_pre).astype(jnp.bfloat16)
    partial_sum = jnp.dot(hidden, reduce_part, preferred_element_type=jnp.float32)
    reduced = lax.psum_scatter(
        partial_sum.astype(jnp.bfloat16), "narrow", scatter_dimension=0, tiled=True
    ).astype(jnp.float32)
    kept = (gathered, hidden_pre, hidden, expand_part, reduce_part)
    return (reduced, kept)


def mlp_backward(grad_rows, kept):
    rows_used, hidden_pre, hidden, expand_use, reduce_use = kept
    grad_low = grad_rows.astype(jnp.bfloat16)
    grad_low = lax.all_gather(grad_low, "narrow", axis=0, tiled=True)
    grad_hidden = jnp.dot(grad_low, reduce_use.T, preferred_element_type=jnp.float32)
    grad_pre = jax.vjp(smooth_gelu, hidden_pre)[1](grad_hidden)[0].astype(jnp.bfloat16)
    reduce_grad = jnp.dot(hidden.T, grad_low, preferred_element_type=jnp.float32)
    expand_grad = jnp.dot(rows_used.T, grad_pre, preferred_element_type=jnp.float32)
    grad_in = jnp.dot(grad_pre, expand_use.T, preferred_element_type=jnp.float32)
    grad_in = lax.psum_scatter(
        grad_in.astype(jnp.bfloat16), "narrow", scatter_dimension=0, tiled=True
    ).astype(jnp.float32)
    return (grad_in, expand_grad, reduce_grad)


def block_forward(rows_in, weights, meta, bq):
    project, output, prenorm, midnorm, expand_part, reduce_part = weights
    first, row_info, col_info = meta
    normed = rms_gain(rows_in, prenorm.astype(F32)).astype(BF)
    projected = jnp.einsum("rd,cdn->crn", normed, project, preferred_element_type=F32).astype(BF)
    x = to_heads(projected)
    attended_h, lse = attend(x, first, row_info, col_info, bq)
    attended = to_rows(attended_h)
    branch = jnp.einsum("crn,cnd->rd", attended, output, preferred_element_type=F32)
    middle = rows_in + branch
    normed_mid = rms_gain(middle, midnorm.astype(F32)).astype(BF)
    reduced, mlp_kept = mlp_forward(normed_mid, expand_part, reduce_part)
    delta = branch + reduced
    return (delta, (rows_in, normed, x, attended_h, lse, attended, middle, mlp_kept))


def block_backward(grad_delta, kept, weights, meta, bq):
    project, output, prenorm, midnorm, expand_part, reduce_part = weights
    first, row_info, col_info = meta
    rows_in, normed, x, attended_h, lse, attended, middle, mlp_kept = kept
    grad_normed_mid, expand_grad, reduce_grad = mlp_backward(grad_delta, mlp_kept)
    mid_pull = jax.vjp(rms_gain, middle, midnorm.astype(F32))[1]
    grad_middle, midnorm_grad = mid_pull(grad_normed_mid)
    grad_branch = (grad_delta + grad_middle).astype(BF)
    output_grad = jnp.einsum("crn,rd->cnd", attended, grad_branch, preferred_element_type=F32)
    grad_attended = jnp.einsum(
        "rd,cnd->crn", grad_branch, output, preferred_element_type=F32
    ).astype(BF)
    dx = attend_back(
        x, first, row_info, col_info, attended_h, to_heads(grad_attended), lse, bq
    )
    grad_projected = to_rows(dx)
    project_grad = jnp.einsum("rd,crn->cdn", normed, grad_projected, preferred_element_type=F32)
    grad_normed = jnp.einsum("crn,cdn->rd", grad_projected, project, preferred_element_type=F32)
    first_pull = jax.vjp(rms_gain, rows_in, prenorm.astype(F32))[1]
    grad_first, prenorm_grad = first_pull(grad_normed)
    model_width = rows_in.shape[1]
    project_grad = (
        project_grad.astype(BF)
        .reshape(GROUPS, model_width, 3, GW)
        .transpose(1, 2, 0, 3)
        .reshape(model_width, 3 * model_width)
    )
    output_grad = output_grad.astype(BF).reshape(model_width, model_width)
    return (
        grad_middle + grad_first,
        (project_grad, output_grad, prenorm_grad, midnorm_grad, expand_grad, reduce_grad),
    )


def on_device(
    tokens,
    cotangent,
    selected,
    segments,
    router_vector,
    project_routed,
    output_routed,
    prenorm_routed,
    midnorm_routed,
    expand_routed,
    reduce_routed,
    project_dense,
    output_dense,
    prenorm_dense,
    midnorm_dense,
    expand_dense,
    reduce_dense,
):
    seq_count, span_rows, model_width = tokens.shape
    row_length = selected.shape[1]
    wide_count = lax.axis_size("wide")
    here = lax.axis_index("wide")
    slot_count = span_rows // 4
    bq_dense = min(256, row_length)
    bq_routed = min(256, slot_count * wide_count)

    def grouped_weights(project, output):
        project = (
            project.reshape(model_width, 3, GROUPS, GW)
            .transpose(2, 0, 1, 3)
            .reshape(GROUPS, model_width, 3 * GW)
        )
        return project, output.reshape(GROUPS, GW, model_width)

    upper = (
        lax.broadcasted_iota(jnp.int32, (span_rows, span_rows), 0)
        <= lax.broadcasted_iota(jnp.int32, (span_rows, span_rows), 1)
    ).astype(BF)
    slots = jnp.arange(slot_count, dtype=jnp.int32)
    own_selected = lax.dynamic_slice_in_dim(selected, here * span_rows, span_rows, 1)
    own_rank = jnp.dot(own_selected.astype(BF), upper, preferred_element_type=F32)
    own_rank = jnp.where(own_selected > 0, own_rank.astype(jnp.int32) - 1, -1)
    one_hot = own_rank[:, None, :] == slots[None, :, None]
    placed = one_hot.astype(F32)

    mine = here % seq_count
    seq_segments = lax.dynamic_slice_in_dim(segments, mine, 1, 0)[0]
    seq_selected = lax.dynamic_slice_in_dim(selected, mine, 1, 0)[0].reshape(wide_count, span_rows)
    seq_rank = jnp.dot(seq_selected.astype(BF), upper, preferred_element_type=F32)
    seq_rank = jnp.where(seq_selected > 0, seq_rank.astype(jnp.int32) - 1, -1)
    slot_segments = (
        jnp.sum(
            jnp.where(
                seq_rank[:, None, :] == slots[None, :, None],
                seq_segments.reshape(wide_count, 1, span_rows) + 1,
                0,
            ),
            axis=-1,
        )
        - 1
    ).reshape(-1)
    meta_routed = (
        jnp.zeros((slot_segments.shape[0] // bq_routed,), jnp.int32),
        jnp.broadcast_to(slot_segments[None], (8, slot_segments.shape[0])),
        slot_segments[:, None],
    )
    starts = sum(
        jnp.where(seq_segments == value, jnp.sum((seq_segments < value).astype(jnp.int32)), 0)
        for value in range(1, 4)
    )
    meta_dense = (
        starts[::bq_dense] // bq_dense,
        jnp.broadcast_to(starts[None], (8, row_length)),
        None,
    )

    picked = jnp.einsum(
        "scp,spd->scd", one_hot.astype(BF), tokens, preferred_element_type=F32
    )
    logits = jnp.dot(
        tokens.reshape(-1, model_width), router_vector, preferred_element_type=F32
    ).reshape(seq_count, span_rows)
    gate = jnp.einsum("scp,sp->sc", placed, logits, precision=PRECISE)
    weights_routed = grouped_weights(project_routed, output_routed) + (
        prenorm_routed,
        midnorm_routed,
        expand_routed,
        reduce_routed,
    )
    weights_dense = grouped_weights(project_dense, output_dense) + (
        prenorm_dense,
        midnorm_dense,
        expand_dense,
        reduce_dense,
    )
    routed_shape = (seq_count, slot_count, model_width)
    routed_delta, kept_routed = block_forward(
        picked.reshape(-1, model_width), weights_routed, meta_routed, bq_routed
    )
    routed_delta = routed_delta.reshape(routed_shape)
    lifted = jnp.einsum("scp,scd->spd", placed, gate[..., None] * routed_delta, precision=PRECISE)
    mixed = tokens.astype(F32) + lifted
    dense_delta, kept_dense = block_forward(
        mixed.reshape(-1, model_width), weights_dense, meta_dense, bq_dense
    )
    activations = (mixed + dense_delta.reshape(mixed.shape)).astype(BF)
    grad_output = cotangent.astype(F32)
    grad_dense_in, grads_dense = block_backward(
        grad_output.reshape(-1, model_width), kept_dense, weights_dense, meta_dense, bq_dense
    )
    grad_mixed = grad_output + grad_dense_in.reshape(grad_output.shape)
    grad_lifted = jnp.einsum("scp,spd->scd", placed, grad_mixed, precision=PRECISE)
    grad_routed_delta = gate[..., None] * grad_lifted
    grad_gate = jnp.sum(grad_lifted * routed_delta, axis=-1)
    grad_picked, grads_routed = block_backward(
        grad_routed_delta.reshape(-1, model_width),
        kept_routed,
        weights_routed,
        meta_routed,
        bq_routed,
    )
    grad_logits = jnp.einsum("scp,sc->sp", placed, grad_gate, precision=PRECISE)
    tokens_gradient = (
        grad_mixed
        + jnp.einsum("scp,scd->spd", placed, grad_picked.reshape(routed_shape), precision=PRECISE)
        + grad_logits[..., None] * router_vector.astype(F32)
    )
    router_grad = jnp.dot(
        grad_logits.reshape(1, -1),
        tokens.reshape(-1, model_width).astype(F32),
        precision=PRECISE,
    )[0]

    def scatter(grad, dimension=0):
        return lax.psum_scatter(
            grad.astype(BF), "wide", scatter_dimension=dimension, tiled=True
        )

    vectors = jnp.stack(
        [grads_routed[2], grads_routed[3], grads_dense[2], grads_dense[3], router_grad], axis=1
    )
    shares = [
        scatter(grads_routed[0]),
        scatter(grads_routed[1]),
        scatter(grads_dense[0]),
        scatter(grads_dense[1]),
        scatter(vectors),
    ]
    summed = [lax.psum(share, "narrow").astype(F32) for share in shares]
    ffn = [
        scatter(grads_routed[4]).astype(F32),
        scatter(grads_dense[4]).astype(F32),
        scatter(grads_routed[5], 1).astype(F32),
        scatter(grads_dense[5], 1).astype(F32),
    ]
    vector_sums = summed[4]
    return (
        activations,
        tokens_gradient,
        vector_sums[:, 4],
        summed[0],
        summed[1],
        vector_sums[:, 0],
        vector_sums[:, 1],
        ffn[0],
        ffn[2],
        summed[2],
        summed[3],
        vector_sums[:, 2],
        vector_sums[:, 3],
        ffn[1],
        ffn[3],
    )


def solution(mesh):
    return jax.shard_map(
        on_device,
        mesh=mesh,
        in_specs=(
            P("narrow", "wide", None),
            P("narrow", "wide", None),
            P("narrow", None),
            P("narrow", None),
            P(),
            P(),
            P(),
            P(),
            P(),
            P(None, "narrow"),
            P("narrow", None),
            P(),
            P(),
            P(),
            P(),
            P(None, "narrow"),
            P("narrow", None),
        ),
        out_specs=(
            P("narrow", "wide", None),
            P("narrow", "wide", None),
            P("wide"),
            P("wide", None),
            P("wide", None),
            P("wide"),
            P("wide"),
            P("wide", "narrow"),
            P("narrow", "wide"),
            P("wide", None),
            P("wide", None),
            P("wide"),
            P("wide"),
            P("wide", "narrow"),
            P("narrow", "wide"),
        ),
        check_vma=False,
    )
```

```python
from functools import partial

import jax
import jax.numpy as jnp
from jax import lax
from jax.experimental import pallas as pl
from jax.experimental.pallas import tpu as pltpu
from jax.sharding import PartitionSpec as P

H = 12
HD = 64
GROUPS = 4
HG = H // GROUPS
GW = HG * HD

EPSILON = 1e-06
NEGATIVE = -1e30
SCORE_SCALE = 0.125
LOG2E = 1.4426950408889634
GELU_A = 0.7978845608028654
GELU_B = 0.044715
BF = jnp.bfloat16
F32 = jnp.float32
VMEM = 56 << 20


def nt_dot(left, right):
    return lax.dot_general(left, right, (((1,), (1,)), ((), ())), preferred_element_type=F32)


def tn_dot(left, right):
    return lax.dot_general(left, right, (((0,), (0,)), ((), ())), preferred_element_type=F32)


def dot(left, right):
    return jnp.dot(left, right, preferred_element_type=F32)


def sds(shape, dtype):
    return jax.ShapeDtypeStruct(shape, dtype)


def norm_scale(rows):
    return lax.rsqrt(jnp.mean(rows * rows, axis=-1, keepdims=True) + EPSILON)


def norm_back(grad, rows, gain):
    scale = norm_scale(rows)
    inner = grad * gain
    mean = jnp.mean(inner * rows, axis=-1, keepdims=True)
    grad_rows = scale * inner - rows * (scale * scale * scale * mean)
    return grad_rows, jnp.sum(grad * rows * scale, axis=0, keepdims=True)


def gelu(a):
    return 0.5 * a * (1.0 + jnp.tanh(GELU_A * (a + GELU_B * (a * a * a))))


def gelu_both(a):
    square = a * a
    bend = jnp.tanh(GELU_A * (a + GELU_B * (square * a)))
    half = 0.5 * (1.0 + bend)
    slope = half + 0.5 * a * (1.0 - bend * bend) * (GELU_A * (1.0 + 3.0 * GELU_B * square))
    return a * half, slope


def three_parts(x):
    first = x.astype(BF)
    rest = x - first.astype(F32)
    second = rest.astype(BF)
    third = (rest - second.astype(F32)).astype(BF)
    return [first, second, third]


def place(one_hot, x):
    return tn_dot(
        jnp.concatenate([one_hot] * 3, axis=0), jnp.concatenate(three_parts(x), axis=0)
    )


def pick(one_hot, x):
    return dot(jnp.concatenate([one_hot] * 3, axis=1), jnp.concatenate(three_parts(x), axis=0))


def combo(index):
    return lax.rem(lax.div(index, 2), GROUPS), lax.rem(index, 2)


def save_pieces(me, full, parts, pieces):
    rows = full.shape[0] // 2
    thirds = full.shape[1] // (GROUPS * GW)
    for c in range(GROUPS):
        for t in range(thirds):
            at = t * GROUPS * GW + c * GW
            parts[c, :, t * GW : (t + 1) * GW] = full[:, at : at + GW]
    for s, piece in enumerate(pieces):
        c, r = combo(me ^ s)
        piece[...] = parts[c, pl.ds(pl.multiple_of(r * rows, rows), rows), :]


def load_pieces(me, pieces, parts, thirds):
    rows = pieces[0].shape[0]
    for s, piece in enumerate(pieces):
        c, r = combo(me ^ s)
        parts[c, pl.ds(pl.multiple_of(r * rows, rows), rows), :] = piece[...]
    return jnp.concatenate(
        [parts[c, :, t * GW : (t + 1) * GW] for t in range(thirds) for c in range(GROUPS)],
        axis=1,
    )


def stage(body, name, ids, operands, outs, scratch=(), flops=0, grid=None, specs=None):
    kwargs = {}
    if grid is not None:
        kwargs["grid"] = grid
    in_specs = [pl.BlockSpec(memory_space=pltpu.SMEM)]
    for k, operand in enumerate(operands):
        spec = None if specs is None else specs.get(k)
        if spec is None:
            zeros = (0,) * operand.ndim
            spec = pl.BlockSpec(operand.shape, lambda *_, z=zeros: z)
        in_specs.append(spec)
    out_specs = tuple(
        pl.BlockSpec(out.shape, lambda *_, z=(0,) * len(out.shape): z) for out in outs
    )
    moved = sum(a.size * a.dtype.itemsize for a in operands)
    moved += sum(math_prod(a.shape) * a.dtype.itemsize for a in outs)
    return pl.pallas_call(
        body,
        out_shape=tuple(outs),
        in_specs=in_specs,
        out_specs=out_specs,
        scratch_shapes=list(scratch),
        compiler_params=pltpu.CompilerParams(vmem_limit_bytes=VMEM),
        cost_estimate=pl.CostEstimate(flops=flops, bytes_accessed=moved, transcendentals=0),
        name=name,
        **kwargs,
    )(ids, *operands)


def math_prod(shape):
    total = 1
    for size in shape:
        total *= size
    return total


def head_parts(rows):
    lane = lax.broadcasted_iota(jnp.int32, rows.shape, 1)
    zero = jnp.zeros_like(rows)
    return [
        jnp.where((lane >= h * HD) & (lane < (h + 1) * HD), rows, zero) for h in range(HG)
    ]


def pair_mask(row_ref, col_ref, q_at, k_at, bk, bq):
    k_iota = lax.broadcasted_iota(jnp.int32, (bk, bq), 0) + k_at
    q_iota = lax.broadcasted_iota(jnp.int32, (bk, bq), 1) + q_at
    info = row_ref[0:1, pl.ds(q_at, bq)]
    if col_ref is None:
        return (k_iota >= info) & (k_iota <= q_iota)
    return (col_ref[pl.ds(k_at, bk), :] == info) & (k_iota <= q_iota)


def attend_kernel(bq, count, sends, by_column, ids, first_ref, row_ref, *rest):
    rest = list(rest)
    col_ref = rest.pop(0) if by_column else None
    pieces, rest = rest[:count], rest[count:]
    out_pieces, rest = rest[:sends], rest[sends:]
    o_ref, lse_ref, q_s, k_s, v_s, vt_s = rest
    i = pl.program_id(0)
    me = ids[0]
    rows = pieces[0].shape[0]
    bk = bq

    @pl.when(i == 0)
    def _():
        for s in range(count):
            at = pl.ds(pl.multiple_of((me ^ s) * rows, rows), rows)
            q_s[at, :] = pieces[s][:, 0:GW]
            k_s[at, :] = pieces[s][:, GW : 2 * GW]
            v_s[at, :] = pieces[s][:, 2 * GW : 3 * GW]
        vt_s[...] = v_s[...].T

    q_at = pl.multiple_of(i * bq, bq)
    q_heads = head_parts(q_s[pl.ds(q_at, bq), :])

    def step(j, carry):
        k_at = pl.multiple_of(j * bk, bk)
        keys = k_s[pl.ds(k_at, bk), :]
        mask = pair_mask(row_ref, col_ref, q_at, k_at, bk, bq)
        out = []
        for h in range(HG):
            top, total, acc = carry[h]
            scores = nt_dot(keys, q_heads[h]) * (SCORE_SCALE * LOG2E)
            scores = jnp.where(mask, scores, NEGATIVE)
            top_new = jnp.maximum(top, jnp.max(scores, axis=0, keepdims=True))
            weight = jnp.exp2(scores - top_new)
            fade = jnp.exp2(top - top_new)
            total = total * fade + jnp.sum(weight, axis=0, keepdims=True)
            values_t = vt_s[h * HD : (h + 1) * HD, pl.ds(k_at, bk)]
            acc = acc * fade + dot(values_t, weight.astype(BF))
            out.append((top_new, total, acc))
        return tuple(out)

    start = tuple(
        (
            jnp.full((1, bq), NEGATIVE, F32),
            jnp.zeros((1, bq), F32),
            jnp.zeros((HD, bq), F32),
        )
        for _ in range(HG)
    )
    done = lax.fori_loop(first_ref[i], i + 1, step, start)
    outs = jnp.concatenate([acc / total for _, total, acc in done], axis=0)
    o_ref[pl.ds(q_at, bq), :] = outs.T.astype(BF)
    for h in range(HG):
        top, total, _ = done[h]
        lse_ref[h : h + 1, pl.ds(q_at, bq)] = top + jnp.log2(total)

    @pl.when(i == pl.num_programs(0) - 1)
    def _():
        for s in range(sends):
            at = pl.ds(pl.multiple_of((me ^ s) * rows, rows), rows)
            out_pieces[s][...] = o_ref[at, :]


def attend_back_kernel(bq, count, sends, by_column, ids, first_ref, row_ref, *rest):
    rest = list(rest)
    col_ref = rest.pop(0) if by_column else None
    pieces, rest = rest[:count], rest[count:]
    grads, rest = rest[:count], rest[count:]
    o_ref, lse_ref = rest[:2]
    out_pieces, rest = rest[2 : 2 + sends], rest[2 + sends :]
    q_s, k_s, v_s, g_s, dq_s, dk_s, dv_s = rest
    i = pl.program_id(0)
    me = ids[0]
    rows = pieces[0].shape[0]
    bk = bq

    @pl.when(i == 0)
    def _():
        for s in range(count):
            at = pl.ds(pl.multiple_of((me ^ s) * rows, rows), rows)
            q_s[at, :] = pieces[s][:, 0:GW]
            k_s[at, :] = pieces[s][:, GW : 2 * GW]
            v_s[at, :] = pieces[s][:, 2 * GW : 3 * GW]
            g_s[at, :] = grads[s][...]
        dk_s[...] = jnp.zeros_like(dk_s)
        dv_s[...] = jnp.zeros_like(dv_s)

    q_at = pl.multiple_of(i * bq, bq)
    grad = g_s[pl.ds(q_at, bq), :]
    q_heads = head_parts(q_s[pl.ds(q_at, bq), :])
    g_heads = head_parts(grad)
    dots = (grad.astype(F32) * o_ref[pl.ds(q_at, bq), :].astype(F32)).T
    row_dot = [
        jnp.sum(dots[h * HD : (h + 1) * HD, :], axis=0, keepdims=True) for h in range(HG)
    ]
    lse = [lse_ref[h : h + 1, pl.ds(q_at, bq)] for h in range(HG)]

    def step(j, dq):
        k_at = pl.multiple_of(j * bk, bk)
        here = pl.ds(k_at, bk)
        keys = k_s[here, :]
        values = v_s[here, :]
        key_heads = head_parts(keys)
        mask = pair_mask(row_ref, col_ref, q_at, k_at, bk, bq)
        dk = dk_s[here, :]
        dv = dv_s[here, :]
        for h in range(HG):
            scores = nt_dot(keys, q_heads[h]) * (SCORE_SCALE * LOG2E)
            scores = jnp.where(mask, scores - lse[h], NEGATIVE)
            soft = jnp.exp2(scores)
            g_soft = nt_dot(values, g_heads[h])
            g_scores = (soft * (g_soft - row_dot[h])).astype(BF)
            dv = dv + dot(soft.astype(BF), g_heads[h])
            dk = dk + dot(g_scores, q_heads[h])
            dq = dq + tn_dot(g_scores, key_heads[h])
        dk_s[here, :] = dk
        dv_s[here, :] = dv
        return dq

    dq = lax.fori_loop(first_ref[i], i + 1, step, jnp.zeros((bq, GW), F32))
    dq_s[pl.ds(q_at, bq), :] = (dq * SCORE_SCALE).astype(BF)

    @pl.when(i == pl.num_programs(0) - 1)
    def _():
        for s in range(sends):
            at = pl.ds(pl.multiple_of((me ^ s) * rows, rows), rows)
            out_pieces[s][:, 0:GW] = dq_s[at, :]
            out_pieces[s][:, GW : 2 * GW] = (dk_s[at, :] * SCORE_SCALE).astype(BF)
            out_pieces[s][:, 2 * GW : 3 * GW] = dv_s[at, :].astype(BF)


def attend(ids, meta, pieces, bq):
    first, row_info, col_info = meta
    rows = pieces[0].shape[0]
    count, sends = len(pieces), min(len(pieces), 2 * GROUPS)
    length = rows * count
    operands = [first, row_info] + ([] if col_info is None else [col_info]) + list(pieces)
    outs = [sds((rows, GW), BF)] * sends + [sds((length, GW), BF), sds((8, length), F32)]
    got = stage(
        partial(attend_kernel, bq, count, sends, col_info is not None),
        "attend",
        ids,
        operands,
        outs,
        [pltpu.VMEM((length, GW), BF)] * 3 + [pltpu.VMEM((GW, length), BF)],
        flops=length * length * GW * 2,
        grid=(length // bq,),
        specs={0: pl.BlockSpec(memory_space=pltpu.SMEM)},
    )
    return got[:sends], got[sends], got[sends + 1]


def attend_back(ids, meta, pieces, grads, attended, lse, bq):
    first, row_info, col_info = meta
    rows = pieces[0].shape[0]
    count, sends = len(pieces), min(len(pieces), 2 * GROUPS)
    length = rows * count
    operands = [first, row_info] + ([] if col_info is None else [col_info])
    operands += list(pieces) + list(grads) + [attended, lse]
    return stage(
        partial(attend_back_kernel, bq, count, sends, col_info is not None),
        "attend_back",
        ids,
        operands,
        [sds((rows, 3 * GW), BF)] * sends,
        [pltpu.VMEM((length, GW), BF)] * 5 + [pltpu.VMEM((length, GW), F32)] * 2,
        flops=length * length * GW * 5,
        grid=(length // bq,),
        specs={0: pl.BlockSpec(memory_space=pltpu.SMEM)},
    )


def routed_pre_kernel(steps, ids, tok, sel, router, gain, project, *rest):
    pieces = rest[:steps]
    one_hot_ref, picked_ref, normed_ref, parts = rest[steps:]
    seqs, span = sel.shape
    slots = span // 4
    upper = (
        lax.broadcasted_iota(jnp.int32, (span, span), 0)
        <= lax.broadcasted_iota(jnp.int32, (span, span), 1)
    ).astype(F32).astype(BF)
    slot = lax.broadcasted_iota(jnp.int32, (slots, span), 0).astype(F32)
    for q in range(seqs):
        chosen = jnp.broadcast_to(sel[q : q + 1, :].astype(F32), (8, span))
        rank = dot(chosen.astype(BF), upper)[0:1, :] * chosen[0:1, :] - 1.0
        one_hot = (slot == rank).astype(F32).astype(BF)
        one_hot_ref[q * slots : (q + 1) * slots, :] = one_hot
        picked_ref[q * slots : (q + 1) * slots, :] = dot(
            one_hot, tok[q * span : (q + 1) * span, :]
        ).astype(BF)
    picked = picked_ref[...].astype(F32)
    normed = (picked * norm_scale(picked) * gain[...].astype(F32)).astype(BF)
    normed_ref[...] = normed
    save_pieces(ids[0], dot(normed, project[...]).astype(BF), parts, pieces)


def routed_pre(ids, steps, tok, sel, router, gain, project):
    rows, width = sel.shape[0] * sel.shape[1] // 4, tok.shape[1]
    outs = [sds((rows // 2, 3 * GW), BF)] * steps
    outs += [sds((rows, sel.shape[1]), BF), sds((rows, width), BF), sds((rows, width), BF)]
    got = stage(
        partial(routed_pre_kernel, steps),
        "routed_pre",
        ids,
        [tok, sel, router, gain, project],
        outs,
        [pltpu.VMEM((GROUPS, rows, 3 * GW), BF)],
        flops=2 * rows * width * 3 * width,
    )
    return got[:steps], got[steps], got[steps + 1], got[steps + 2]


def routed_mid_kernel(count, ids, *rest):
    pieces = rest[:count]
    output, picked, gain, branch_ref, low_ref, att_ref, parts = rest[count:]
    attended = load_pieces(ids[0], pieces, parts, 1)
    att_ref[...] = attended
    branch = dot(attended, output[...])
    branch_ref[...] = branch
    middle = picked[...].astype(F32) + branch
    low_ref[...] = (middle * norm_scale(middle) * gain[...].astype(F32)).astype(BF)


def routed_mid(ids, pieces, output, picked, gain):
    shape = picked.shape
    return stage(
        partial(routed_mid_kernel, len(pieces)),
        "routed_mid",
        ids,
        list(pieces) + [output, picked, gain],
        [sds(shape, F32), sds(shape, BF), sds(shape, BF)],
        [pltpu.VMEM((GROUPS, shape[0], GW), BF)],
        flops=2 * shape[0] * shape[1] * shape[1],
    )


def hidden_forward_kernel(count, ids, *rest):
    pieces = rest[:count]
    expand, reduce_ref = rest[count : count + 2]
    outs = rest[count + 2 :]
    rows = pieces[0].shape[0]
    low = jnp.concatenate([piece[...] for piece in pieces], axis=0)
    hidden = gelu(dot(low, expand[...])).astype(BF)
    total = dot(hidden, reduce_ref[...]).astype(BF)
    for s, out in enumerate(outs):
        out[...] = total[s * rows : (s + 1) * rows, :]


def hidden_forward(ids, pieces, expand, reduce_part):
    return stage(
        partial(hidden_forward_kernel, len(pieces)),
        "hidden_forward",
        ids,
        list(pieces) + [expand, reduce_part],
        [sds(pieces[0].shape, BF)] * len(pieces),
        flops=4 * len(pieces) * pieces[0].size * expand.shape[1],
    )


def hidden_back_kernel(count, ids, *rest):
    pieces, grads = rest[:count], rest[count : 2 * count]
    expand, reduce_ref = rest[2 * count : 2 * count + 2]
    outs = rest[2 * count + 2 :]
    rows = pieces[0].shape[0]
    low = jnp.concatenate([piece[...] for piece in pieces], axis=0)
    grad = jnp.concatenate([piece[...] for piece in grads], axis=0)
    _, slope = gelu_both(dot(low, expand[...]))
    grad_pre = (nt_dot(grad, reduce_ref[...]) * slope).astype(BF)
    total = nt_dot(grad_pre, expand[...]).astype(BF)
    for s, out in enumerate(outs):
        out[...] = total[s * rows : (s + 1) * rows, :]


def hidden_back(ids, pieces, grads, expand, reduce_part):
    return stage(
        partial(hidden_back_kernel, len(pieces)),
        "hidden_back",
        ids,
        list(pieces) + list(grads) + [expand, reduce_part],
        [sds(pieces[0].shape, BF)] * len(pieces),
        flops=6 * len(pieces) * pieces[0].size * expand.shape[1],
    )


def dense_pre_kernel(steps, shares, ids, tok, one_hot, picked, router, branch, *rest):
    partials = rest[:shares]
    gain, project = rest[shares : shares + 2]
    rest = rest[shares + 2 :]
    pieces = rest[:steps]
    mixed_ref, delta_ref, normed_ref, parts = rest[steps:]
    slots, span = one_hot.shape[0] // 2, one_hot.shape[1]
    delta = branch[...]
    for share in partials:
        delta = delta + share[...].astype(F32)
    delta_ref[...] = delta
    gate = jnp.sum(
        picked[...].astype(F32) * router[...].astype(F32), axis=-1, keepdims=True
    )
    lifted = gate * delta
    for q in range(2):
        at, spots = slice(q * span, (q + 1) * span), slice(q * slots, (q + 1) * slots)
        mixed = tok[at, :].astype(F32) + place(one_hot[spots, :], lifted[spots, :])
        mixed_ref[at, :] = mixed
        normed_ref[at, :] = (mixed * norm_scale(mixed) * gain[...].astype(F32)).astype(BF)
    save_pieces(ids[0], dot(normed_ref[...], project[...]).astype(BF), parts, pieces)


def dense_pre(ids, steps, tok, one_hot, picked, router, branch, partials, gain, project):
    rows, width = tok.shape
    outs = [sds((rows // 2, 3 * GW), BF)] * steps
    outs += [sds(tok.shape, F32), sds(picked.shape, F32), sds(tok.shape, BF)]
    got = stage(
        partial(dense_pre_kernel, steps, len(partials)),
        "dense_pre",
        ids,
        [tok, one_hot, picked, router, branch] + list(partials) + [gain, project],
        outs,
        [pltpu.VMEM((GROUPS, rows, 3 * GW), BF)],
        flops=6 * rows * width * width,
    )
    return got[:steps], got[steps], got[steps + 1], got[steps + 2]


def dense_ffn_kernel(count, steps, split, ids, *rest):
    pieces, rest = rest[:count], rest[count:]
    output, mixed, cot, gain = rest[:4]
    rest = rest[4:]
    weights, rest = rest[:split], rest[split:]
    act_ref, low_ref, back_ref, sum_ref, att_ref, gain_ref = rest[:6]
    g_pieces, rest = rest[6 : 6 + steps], rest[6 + steps :]
    parts, branch_s, delta_s, grad_s = rest[:4]
    n = pl.program_id(0)
    me = ids[0]

    @pl.when(n == 0)
    def _():
        attended = load_pieces(me, pieces, parts, 1)
        att_ref[...] = attended
        branch = dot(attended, output[...])
        branch_s[...] = branch
        middle = mixed[...] + branch
        low_ref[...] = (middle * norm_scale(middle) * gain[...].astype(F32)).astype(BF)
        delta_s[...] = jnp.zeros_like(delta_s)
        grad_s[...] = jnp.zeros_like(grad_s)

    if split == 2:
        expand, reduce_w = weights[0][0], weights[1][0]
    else:
        e_s, r_s = rest[4:]
        rows = weights[0].shape[2]
        for s, weight in enumerate(weights):
            at = pl.ds(pl.multiple_of((me ^ s) * rows, rows), rows)
            e_s[at, :] = weight[0, 0]
            r_s[at, :] = weight[0, 1]
        expand, reduce_w = e_s[...], r_s[...]
    value, slope = gelu_both(dot(low_ref[...], expand))
    delta_s[...] += dot(value.astype(BF), reduce_w)
    grad_pre = (nt_dot(cot[...], reduce_w) * slope).astype(BF)
    grad_s[...] += nt_dot(grad_pre, expand)

    @pl.when(n == pl.num_programs(0) - 1)
    def _():
        middle = mixed[...] + branch_s[...]
        act_ref[...] = (middle + delta_s[...]).astype(BF)
        grad_middle, gain_grad = norm_back(grad_s[...], middle, gain[...].astype(F32))
        gain_ref[...] = jnp.broadcast_to(gain_grad, gain_ref.shape)
        total = cot[...].astype(F32) + grad_middle
        sum_ref[...] = total
        back = total.astype(BF)
        back_ref[...] = back
        save_pieces(me, nt_dot(back, output[...]).astype(BF), parts, g_pieces)


def dense_ffn(ids, steps, pieces, output, mixed, cot, gain, weights):
    rows, width = mixed.shape
    split = len(weights)
    parts_n = weights[0].shape[0]
    hidden = weights[0].shape[-1]
    base = len(pieces) + 4
    specs = {
        base + k: pl.BlockSpec(
            (1,) + w.shape[1:], lambda n, z=(0,) * (w.ndim - 1): (n,) + z
        )
        for k, w in enumerate(weights)
    }
    scratch = [pltpu.VMEM((GROUPS, rows, GW), BF)] + [pltpu.VMEM((rows, width), F32)] * 3
    if split != 2:
        scratch += [pltpu.VMEM((width, hidden), BF)] * 2
    outs = [
        sds((rows, width), BF),
        sds((rows, width), BF),
        sds((rows, width), BF),
        sds((rows, width), F32),
        sds((rows, width), BF),
        sds((8, width), F32),
    ] + [sds((rows // 2, GW), BF)] * steps
    got = stage(
        partial(dense_ffn_kernel, len(pieces), steps, split),
        "dense_ffn",
        ids,
        list(pieces) + [output, mixed, cot, gain] + list(weights),
        outs,
        scratch,
        flops=8 * rows * width * hidden * parts_n + 4 * rows * width * width,
        grid=(parts_n,),
        specs=specs,
    )
    return got[:6], got[6:]


def dense_post_kernel(count, ids, *rest):
    pieces = rest[:count]
    project, gain, mixed, total, one_hot, picked, router, delta = rest[count : count + 8]
    g_mixed_ref, g_proj_ref, g_delta_ref, g_low_ref, g_gate_ref, gain_ref, parts = rest[
        count + 8 :
    ]
    g_proj = load_pieces(ids[0], pieces, parts, 3)
    g_proj_ref[...] = g_proj
    grad_rows, gain_grad = norm_back(
        nt_dot(g_proj, project[...]), mixed[...], gain[...].astype(F32)
    )
    gain_ref[...] = jnp.broadcast_to(gain_grad, gain_ref.shape)
    g_mixed_ref[...] = total[...] + grad_rows
    slots, span = one_hot.shape[0] // 2, one_hot.shape[1]
    gate = jnp.sum(
        picked[...].astype(F32) * router[...].astype(F32), axis=-1, keepdims=True
    )
    for q in range(2):
        at, spots = slice(q * span, (q + 1) * span), slice(q * slots, (q + 1) * slots)
        lifted = pick(one_hot[spots, :], g_mixed_ref[at, :])
        g_delta = gate[spots, :] * lifted
        g_delta_ref[spots, :] = g_delta
        g_low_ref[spots, :] = g_delta.astype(BF)
        g_gate = jnp.sum(lifted * delta[spots, :], axis=-1, keepdims=True)
        g_gate_ref[spots, :] = jnp.broadcast_to(g_gate, (slots, g_gate_ref.shape[1]))


def dense_post(ids, pieces, project, gain, mixed, total, one_hot, picked, router, delta):
    rows, width = mixed.shape
    return stage(
        partial(dense_post_kernel, len(pieces)),
        "dense_post",
        ids,
        list(pieces) + [project, gain, mixed, total, one_hot, picked, router, delta],
        [
            sds((rows, width), F32),
            sds((rows, 3 * width), BF),
            sds(picked.shape, F32),
            sds(picked.shape, BF),
            sds((picked.shape[0], 128), F32),
            sds((8, width), F32),
        ],
        [pltpu.VMEM((GROUPS, rows, 3 * GW), BF)],
        flops=6 * rows * width * width,
    )


def routed_back_kernel(shares, steps, ids, *rest):
    partials = rest[:shares]
    branch, picked, gain, g_delta, output = rest[shares : shares + 5]
    rest = rest[shares + 5 :]
    g_mid_ref, back_ref, gain_ref = rest[:3]
    pieces, parts = rest[3 : 3 + steps], rest[3 + steps]
    grad = partials[0][...].astype(F32)
    for share in partials[1:]:
        grad = grad + share[...].astype(F32)
    middle = picked[...].astype(F32) + branch[...]
    g_middle, gain_grad = norm_back(grad, middle, gain[...].astype(F32))
    gain_ref[...] = jnp.broadcast_to(gain_grad, gain_ref.shape)
    g_mid_ref[...] = g_middle
    back = (g_delta[...] + g_middle).astype(BF)
    back_ref[...] = back
    save_pieces(ids[0], nt_dot(back, output[...]).astype(BF), parts, pieces)


def routed_back(ids, steps, partials, branch, picked, gain, g_delta, output):
    rows, width = branch.shape
    got = stage(
        partial(routed_back_kernel, len(partials), steps),
        "routed_back",
        ids,
        list(partials) + [branch, picked, gain, g_delta, output],
        [sds((rows, width), F32), sds((rows, width), BF), sds((8, width), F32)]
        + [sds((rows // 2, GW), BF)] * steps,
        [pltpu.VMEM((GROUPS, rows, GW), BF)],
        flops=2 * rows * width * width,
    )
    return got[0], got[1], got[2], got[3:]


def routed_post_kernel(count, ids, *rest):
    pieces = rest[:count]
    project, gain, picked, g_mid, g_mixed, one_hot, g_gate, router = rest[count : count + 8]
    out_ref, g_proj_ref, gain_ref, router_ref, parts = rest[count + 8 :]
    g_proj = load_pieces(ids[0], pieces, parts, 3)
    g_proj_ref[...] = g_proj
    rows = picked[...].astype(F32)
    grad_rows, gain_grad = norm_back(
        nt_dot(g_proj, project[...]), rows, gain[...].astype(F32)
    )
    gain_ref[...] = jnp.broadcast_to(gain_grad, gain_ref.shape)
    gate_grad = g_gate[:, 0:1]
    router_ref[...] = jnp.broadcast_to(
        jnp.sum(rows * gate_grad, axis=0, keepdims=True), router_ref.shape
    )
    spread = g_mid[...] + grad_rows + gate_grad * router[...].astype(F32)
    slots, span = one_hot.shape[0] // 2, one_hot.shape[1]
    for q in range(2):
        at, spots = slice(q * span, (q + 1) * span), slice(q * slots, (q + 1) * slots)
        out_ref[at, :] = g_mixed[at, :] + place(one_hot[spots, :], spread[spots, :])


def routed_post(ids, pieces, project, gain, picked, g_mid, g_mixed, one_hot, g_gate, router):
    rows, width = picked.shape
    return stage(
        partial(routed_post_kernel, len(pieces)),
        "routed_post",
        ids,
        list(pieces) + [project, gain, picked, g_mid, g_mixed, one_hot, g_gate, router],
        [
            sds(g_mixed.shape, F32),
            sds((rows, 3 * width), BF),
            sds((8, width), F32),
            sds((8, width), F32),
        ],
        [pltpu.VMEM((GROUPS, rows, 3 * GW), BF)],
        flops=6 * rows * width * width,
    )


def split_rows(me, total, keep, send):
    chips, rows = keep.shape[0], keep.shape[1]
    core = lax.rem(me, 2)
    for c in range(chips):
        mine = pl.multiple_of((2 * c + core) * rows, rows)
        other = pl.multiple_of((2 * c + 1 - core) * rows, rows)
        keep[c] = total[pl.ds(mine, rows), :].astype(BF)
        send[c] = total[pl.ds(other, rows), :].astype(BF)


def hidden_grads_kernel(ids, low, grad, expand, reduce_ref, keep, send, total):
    i = pl.program_id(0)
    hidden = expand.shape[1]

    @pl.when(i == 0)
    def _():
        total[...] = jnp.zeros_like(total)

    value, slope = gelu_both(dot(low[...], expand[...]))
    grad_pre = (nt_dot(grad[...], reduce_ref[...]) * slope).astype(BF)
    total[:, 0:hidden] += tn_dot(low[...], grad_pre)
    total[:, hidden : 2 * hidden] += tn_dot(grad[...], value.astype(BF))

    @pl.when(i == pl.num_programs(0) - 1)
    def _():
        split_rows(ids[0], total, keep, send)


def hidden_grads(ids, wide_count, low, grad, expand, reduce_part):
    width, hidden = expand.shape
    block = min(512, low.shape[0])
    shape = (wide_count // 2, width // wide_count, 2 * hidden)
    row_spec = pl.BlockSpec((block, width), lambda i: (i, 0))
    return stage(
        hidden_grads_kernel,
        "hidden_grads",
        ids,
        [low, grad, expand, reduce_part],
        [sds(shape, BF), sds(shape, BF)],
        [pltpu.VMEM((width, 2 * hidden), F32)],
        flops=8 * low.size * hidden,
        grid=(low.shape[0] // block,),
        specs={0: row_spec, 1: row_spec},
    )


def attend_grads_kernel(vectors, ids, normed, g_proj, att, back, *rest):
    rest = list(rest)
    vecs, rest = rest[:vectors], rest[vectors:]
    keep, send, total = rest
    width = normed.shape[1]
    total[:, 0 : 3 * width] = tn_dot(normed[...], g_proj[...])
    total[:, 3 * width : 4 * width] = tn_dot(att[...], back[...])
    if vectors:
        rows = [vec[0:1, :] for vec in vecs]
        rows.append(jnp.zeros((128 - vectors, width), F32))
        total[:, 4 * width : 4 * width + 128] = jnp.concatenate(rows, axis=0).T
    split_rows(ids[0], total, keep, send)


def attend_grads(ids, wide_count, normed, g_proj, att, back, vecs):
    rows, width = normed.shape
    columns = 4 * width + (128 if vecs else 0)
    shape = (wide_count // 2, width // wide_count, columns)
    return stage(
        partial(attend_grads_kernel, len(vecs)),
        "attend_grads",
        ids,
        [normed, g_proj, att, back] + list(vecs),
        [sds(shape, BF), sds(shape, BF)],
        [pltpu.VMEM((width, columns), F32)],
        flops=8 * rows * width * width,
    )


def join_kernel(chips, ids, keep, came, *outs):
    chip = lax.div(ids[0], 2)
    for s, out in enumerate(outs):
        at = chip ^ s
        out[...] = (keep[at].astype(F32) + came[at].astype(F32)).astype(BF)


def reduce_wide(ids, wide_count, keep, send):
    came = lax.ppermute(send, "wide", [(j, j ^ 1) for j in range(wide_count)])
    chips = keep.shape[0]
    parts = stage(
        partial(join_kernel, chips), "join", ids, [keep, came], [sds(keep.shape[1:], BF)] * chips
    )
    return [parts[0]] + [
        lax.ppermute(parts[s], "wide", [(j, j ^ (2 * s)) for j in range(wide_count)])
        for s in range(1, chips)
    ]


def sum_terms(terms):
    total = terms[0].astype(F32)
    for term in terms[1:]:
        total = total + term.astype(F32)
    return total


def sum_split_kernel(count, ids, *rest):
    terms, outs, total = rest[:count], rest[count:-1], rest[-1]
    got = terms[0][...].astype(F32)
    for term in terms[1:]:
        got = got + term[...].astype(F32)
    total[...] = got
    rows = outs[0].shape[0]
    for s, out in enumerate(outs):
        at = pl.multiple_of((ids[1] ^ s) * rows, rows)
        out[...] = total[pl.ds(at, rows), :].astype(BF)


def sum_kernel(ids, *rest):
    got = rest[0][...].astype(F32)
    for term in rest[1:-1]:
        got = got + term[...].astype(F32)
    rest[-1][...] = got.astype(BF)


def gather_out_kernel(count, ids, *rest):
    pieces, outs = rest[:count], rest[count:]
    rows = pieces[0].shape[0]
    for s, piece in enumerate(pieces):
        at = pl.ds(pl.multiple_of((ids[1] ^ s) * rows, rows), rows)
        low = 0
        for out in outs:
            columns = out.shape[1]
            out[at, :] = piece[:, low : low + columns].astype(F32)
            low += columns


def reduce_narrow(ids, terms, widths):
    narrow_count = lax.axis_size("narrow")
    rows, columns = terms[0].shape
    if rows % (8 * narrow_count):
        total = lax.psum(sum_terms(terms).astype(BF), "narrow").astype(F32)
        outs, low = [], 0
        for size in widths:
            outs.append(total[:, low : low + size])
            low += size
        return outs
    share = rows // narrow_count
    parts = stage(
        partial(sum_split_kernel, len(terms)),
        "sum_split",
        ids,
        terms,
        [sds((share, columns), BF)] * narrow_count,
        [pltpu.VMEM((rows, columns), F32)],
    )
    came = [parts[0]] + [narrow_step(parts[s], s) for s in range(1, narrow_count)]
    (total,) = stage(sum_kernel, "sum_terms", ids, came, [sds((share, columns), BF)])
    pieces = [total] + [narrow_step(total, s) for s in range(1, narrow_count)]
    return stage(
        partial(gather_out_kernel, narrow_count),
        "gather_out",
        ids,
        pieces,
        [sds((rows, size), F32) for size in widths],
    )


def narrow_step(x, s):
    return lax.ppermute(x, "narrow", [(j, j ^ s) for j in range(lax.axis_size("narrow"))])


def narrow_gather(x):
    return [x] + [narrow_step(x, s) for s in range(1, lax.axis_size("narrow"))]


def narrow_return(parts):
    return [parts[0]] + [narrow_step(parts[s], s) for s in range(1, len(parts))]


def exchange(pieces):
    wide_count = lax.axis_size("wide")
    return [pieces[0]] + [
        lax.ppermute(pieces[s], "wide", [(j, j ^ s) for j in range(wide_count)])
        for s in range(1, len(pieces))
    ]


def gather_hidden_weights(expand, reduce_part):
    wide_count = lax.axis_size("wide")
    here = lax.axis_index("wide")
    width, hidden = expand.shape
    rows = width // wide_count
    if width != hidden or rows % 16:
        return [
            lax.all_gather(expand, "narrow", axis=0),
            lax.all_gather(reduce_part, "narrow", axis=0),
        ]
    share = jnp.stack(
        [
            lax.dynamic_slice_in_dim(expand, here * rows, rows, 0),
            lax.dynamic_slice_in_dim(reduce_part, here * rows, rows, 0),
        ]
    )
    mine = lax.all_gather(share, "narrow", axis=0)
    pieces = [None] * wide_count
    pieces[0] = mine
    for s in range(2, wide_count, 2):
        pieces[s] = lax.ppermute(mine, "wide", [(j, j ^ s) for j in range(wide_count)])
    for s in range(1, wide_count, 2):
        pieces[s] = lax.ppermute(
            pieces[s - 1], "wide", [(j, j ^ 1) for j in range(wide_count)]
        )
    return pieces


def on_device(
    tokens,
    cotangent,
    selected,
    segments,
    router_vector,
    project_routed,
    output_routed,
    prenorm_routed,
    midnorm_routed,
    expand_routed,
    reduce_routed,
    project_dense,
    output_dense,
    prenorm_dense,
    midnorm_dense,
    expand_dense,
    reduce_dense,
):
    seq_count, span_rows, width = tokens.shape
    row_length = selected.shape[1]
    hidden = expand_dense.shape[1]
    wide_count = lax.axis_size("wide")
    here = lax.axis_index("wide")
    slot_count = span_rows // 4
    bq_dense = min(256, row_length)
    bq_routed = min(256, slot_count * wide_count)
    ids = jnp.stack([here, lax.axis_index("narrow")]).astype(jnp.int32)
    router = router_vector[None]
    gains = [
        gain[None] for gain in (prenorm_routed, midnorm_routed, prenorm_dense, midnorm_dense)
    ]
    tok = tokens.reshape(-1, width)
    cot = cotangent.reshape(-1, width)

    ffn_weights = gather_hidden_weights(expand_dense, reduce_dense)
    cot_all = lax.all_gather(cot, "narrow", axis=0, tiled=True)

    mine = here % seq_count
    seq_segments = lax.dynamic_slice_in_dim(segments, mine, 1, 0)[0]
    seq_selected = lax.dynamic_slice_in_dim(selected, mine, 1, 0)[0].reshape(wide_count, span_rows)
    upper = (
        lax.broadcasted_iota(jnp.int32, (span_rows, span_rows), 0)
        <= lax.broadcasted_iota(jnp.int32, (span_rows, span_rows), 1)
    ).astype(BF)
    slots = jnp.arange(slot_count, dtype=jnp.int32)
    seq_rank = jnp.dot(seq_selected.astype(BF), upper, preferred_element_type=F32)
    seq_rank = jnp.where(seq_selected > 0, seq_rank.astype(jnp.int32) - 1, -1)
    slot_segments = (
        jnp.sum(
            jnp.where(
                seq_rank[:, None, :] == slots[None, :, None],
                seq_segments.reshape(wide_count, 1, span_rows) + 1,
                0,
            ),
            axis=-1,
        )
        - 1
    ).reshape(-1)
    meta_routed = (
        jnp.zeros((slot_segments.shape[0] // bq_routed,), jnp.int32),
        jnp.broadcast_to(slot_segments[None], (8, slot_segments.shape[0])),
        slot_segments[:, None],
    )
    starts = sum(
        jnp.where(seq_segments == value, jnp.sum((seq_segments < value).astype(jnp.int32)), 0)
        for value in range(1, 4)
    )
    meta_dense = (
        starts[::bq_dense] // bq_dense,
        jnp.broadcast_to(starts[None], (8, row_length)),
        None,
    )

    own_selected = lax.dynamic_slice_in_dim(selected, here * span_rows, span_rows, 1)
    pieces, one_hot, picked, normed_r = routed_pre(
        ids, wide_count, tok, own_selected, router, gains[0], project_routed
    )
    x_r = exchange(pieces)
    pieces, att_seq_r, lse_r = attend(ids, meta_routed, x_r, bq_routed)
    branch_r, low_r, att_r = routed_mid(ids, exchange(pieces), output_routed, picked, gains[1])
    low_pieces = narrow_gather(low_r)
    partials = narrow_return(hidden_forward(ids, low_pieces, expand_routed, reduce_routed))

    pieces, mixed, delta_r, normed_d = dense_pre(
        ids,
        wide_count,
        tok,
        one_hot,
        picked,
        router,
        branch_r,
        partials,
        gains[2],
        project_dense,
    )
    x_d = exchange(pieces)
    pieces, att_seq_d, lse_d = attend(ids, meta_dense, x_d, bq_dense)
    (activations, low_d, back_d, sum_d, att_d, mid_gain_d), pieces = dense_ffn(
        ids, wide_count, exchange(pieces), output_dense, mixed, cot, gains[3], ffn_weights
    )
    low_all = lax.all_gather(low_d, "narrow", axis=0, tiled=True)
    pieces = attend_back(ids, meta_dense, x_d, exchange(pieces), att_seq_d, lse_d, bq_dense)
    g_mixed, g_proj_d, g_delta, g_low, g_gate, pre_gain_d = dense_post(
        ids,
        exchange(pieces),
        project_dense,
        gains[2],
        mixed,
        sum_d,
        one_hot,
        picked,
        router,
        delta_r,
    )
    keep, send = hidden_grads(ids, wide_count, low_all, cot_all, expand_dense, reduce_dense)
    ffn_d = reduce_wide(ids, wide_count, keep, send)

    g_pieces = narrow_gather(g_low)
    partials = narrow_return(
        hidden_back(ids, low_pieces, g_pieces, expand_routed, reduce_routed)
    )
    g_mid_r, back_r, mid_gain_r, pieces = routed_back(
        ids, wide_count, partials, branch_r, picked, gains[1], g_delta, output_routed
    )
    keep, send = attend_grads(ids, wide_count, normed_d, g_proj_d, att_d, back_d, [])
    att_terms_d = reduce_wide(ids, wide_count, keep, send)
    keep, send = hidden_grads(
        ids,
        wide_count,
        jnp.concatenate(low_pieces, axis=0),
        jnp.concatenate(g_pieces, axis=0),
        expand_routed,
        reduce_routed,
    )
    ffn_r = reduce_wide(ids, wide_count, keep, send)
    pieces = attend_back(ids, meta_routed, x_r, exchange(pieces), att_seq_r, lse_r, bq_routed)
    tokens_gradient, g_proj_r, pre_gain_r, router_grad = routed_post(
        ids,
        exchange(pieces),
        project_routed,
        gains[0],
        picked,
        g_mid_r,
        g_mixed,
        one_hot,
        g_gate,
        router,
    )
    keep, send = attend_grads(
        ids,
        wide_count,
        normed_r,
        g_proj_r,
        att_r,
        back_r,
        [pre_gain_r, mid_gain_r, pre_gain_d, mid_gain_d, router_grad],
    )
    att_terms_r = reduce_wide(ids, wide_count, keep, send)

    project_d_grad, output_d_grad = reduce_narrow(ids, att_terms_d, [3 * width, width])
    project_r_grad, output_r_grad, vectors = reduce_narrow(
        ids, att_terms_r, [3 * width, width, 128]
    )
    ffn_r_sum, ffn_d_sum = sum_terms(ffn_r), sum_terms(ffn_d)
    return (
        activations.reshape(tokens.shape),
        tokens_gradient.reshape(tokens.shape),
        vectors[:, 4],
        project_r_grad,
        output_r_grad,
        vectors[:, 0],
        vectors[:, 1],
        ffn_r_sum[:, :hidden],
        ffn_r_sum[:, hidden:].T,
        project_d_grad,
        output_d_grad,
        vectors[:, 2],
        vectors[:, 3],
        ffn_d_sum[:, :hidden],
        ffn_d_sum[:, hidden:].T,
    )


def solution(mesh):
    return jax.shard_map(
        on_device,
        mesh=mesh,
        in_specs=(
            P("narrow", "wide", None),
            P("narrow", "wide", None),
            P("narrow", None),
            P("narrow", None),
            P(),
            P(),
            P(),
            P(),
            P(),
            P(None, "narrow"),
            P("narrow", None),
            P(),
            P(),
            P(),
            P(),
            P(None, "narrow"),
            P("narrow", None),
        ),
        out_specs=(
            P("narrow", "wide", None),
            P("narrow", "wide", None),
            P("wide"),
            P("wide", None),
            P("wide", None),
            P("wide"),
            P("wide"),
            P("wide", "narrow"),
            P("narrow", "wide"),
            P("wide", None),
            P("wide", None),
            P("wide"),
            P("wide"),
            P("wide", "narrow"),
            P("narrow", "wide"),
        ),
        check_vma=False,
    )
```

```python
from functools import partial

import jax
import jax.numpy as jnp
from jax import lax
from jax.experimental import pallas as pl
from jax.experimental.pallas import tpu as pltpu
from jax.sharding import PartitionSpec as P

H = 12
HD = 64
GROUPS = 4
HG = H // GROUPS
GW = HG * HD

EPSILON = 1e-06
NEGATIVE = -1e30
SCORE_SCALE = 0.125
LOG2E = 1.4426950408889634
GELU_A = 0.7978845608028654
GELU_B = 0.044715
BF = jnp.bfloat16
F32 = jnp.float32
VMEM = 56 << 20


def nt_dot(left, right):
    return lax.dot_general(left, right, (((1,), (1,)), ((), ())), preferred_element_type=F32)


def tn_dot(left, right):
    return lax.dot_general(left, right, (((0,), (0,)), ((), ())), preferred_element_type=F32)


def dot(left, right):
    return jnp.dot(left, right, preferred_element_type=F32)


def sds(shape, dtype):
    return jax.ShapeDtypeStruct(shape, dtype)


def norm_scale(rows):
    return lax.rsqrt(jnp.mean(rows * rows, axis=-1, keepdims=True) + EPSILON)


def norm_back(grad, rows, gain):
    scale = norm_scale(rows)
    inner = grad * gain
    mean = jnp.mean(inner * rows, axis=-1, keepdims=True)
    grad_rows = scale * inner - rows * (scale * scale * scale * mean)
    return grad_rows, jnp.sum(grad * rows * scale, axis=0, keepdims=True)


def gelu(a):
    return 0.5 * a * (1.0 + jnp.tanh(GELU_A * (a + GELU_B * (a * a * a))))


def gelu_both(a):
    square = a * a
    bend = jnp.tanh(GELU_A * (a + GELU_B * (square * a)))
    half = 0.5 * (1.0 + bend)
    slope = half + 0.5 * a * (1.0 - bend * bend) * (GELU_A * (1.0 + 3.0 * GELU_B * square))
    return a * half, slope


def three_parts(x):
    first = x.astype(BF)
    rest = x - first.astype(F32)
    second = rest.astype(BF)
    third = (rest - second.astype(F32)).astype(BF)
    return [first, second, third]


def place(one_hot, x):
    return tn_dot(
        jnp.concatenate([one_hot] * 3, axis=0), jnp.concatenate(three_parts(x), axis=0)
    )


def pick(one_hot, x):
    return dot(jnp.concatenate([one_hot] * 3, axis=1), jnp.concatenate(three_parts(x), axis=0))


def combo(index):
    return lax.rem(lax.div(index, 2), GROUPS), lax.rem(index, 2)


def save_pieces(me, full, parts, pieces):
    rows = full.shape[0] // 2
    thirds = full.shape[1] // (GROUPS * GW)
    for c in range(GROUPS):
        for t in range(thirds):
            at = t * GROUPS * GW + c * GW
            parts[c, :, t * GW : (t + 1) * GW] = full[:, at : at + GW]
    for s, piece in enumerate(pieces):
        c, r = combo(me ^ s)
        piece[...] = parts[c, pl.ds(pl.multiple_of(r * rows, rows), rows), :]


def load_pieces(me, pieces, parts, thirds):
    rows = pieces[0].shape[0]
    for s, piece in enumerate(pieces):
        c, r = combo(me ^ s)
        parts[c, pl.ds(pl.multiple_of(r * rows, rows), rows), :] = piece[...]
    return jnp.concatenate(
        [parts[c, :, t * GW : (t + 1) * GW] for t in range(thirds) for c in range(GROUPS)],
        axis=1,
    )


def load_stack(me, stack, parts, thirds):
    rows = stack.shape[1]
    first = lax.div(me, 2 * GROUPS) * (2 * GROUPS)
    for w in range(2 * GROUPS):
        c, r = w // 2, w % 2
        parts[c, r * rows : (r + 1) * rows, :] = stack[first + w]
    return jnp.concatenate(
        [parts[c, :, t * GW : (t + 1) * GW] for t in range(thirds) for c in range(GROUPS)],
        axis=1,
    )


def stage(body, name, ids, operands, outs, scratch=(), flops=0, grid=None, specs=None):
    kwargs = {}
    if grid is not None:
        kwargs["grid"] = grid
    in_specs = [pl.BlockSpec(memory_space=pltpu.SMEM)]
    for k, operand in enumerate(operands):
        spec = None if specs is None else specs.get(k)
        if spec is None:
            zeros = (0,) * operand.ndim
            spec = pl.BlockSpec(operand.shape, lambda *_, z=zeros: z)
        in_specs.append(spec)
    out_specs = tuple(
        pl.BlockSpec(out.shape, lambda *_, z=(0,) * len(out.shape): z) for out in outs
    )
    moved = sum(a.size * a.dtype.itemsize for a in operands)
    moved += sum(math_prod(a.shape) * a.dtype.itemsize for a in outs)
    return pl.pallas_call(
        body,
        out_shape=tuple(outs),
        in_specs=in_specs,
        out_specs=out_specs,
        scratch_shapes=list(scratch),
        compiler_params=pltpu.CompilerParams(vmem_limit_bytes=VMEM),
        cost_estimate=pl.CostEstimate(flops=flops, bytes_accessed=moved, transcendentals=0),
        name=name,
        **kwargs,
    )(ids, *operands)


def math_prod(shape):
    total = 1
    for size in shape:
        total *= size
    return total


def head_parts(rows):
    lane = lax.broadcasted_iota(jnp.int32, rows.shape, 1)
    zero = jnp.zeros_like(rows)
    return [
        jnp.where((lane >= h * HD) & (lane < (h + 1) * HD), rows, zero) for h in range(HG)
    ]


def pair_mask(row_ref, col_ref, q_at, k_at, bk, bq):
    k_iota = lax.broadcasted_iota(jnp.int32, (bk, bq), 0) + k_at
    q_iota = lax.broadcasted_iota(jnp.int32, (bk, bq), 1) + q_at
    info = row_ref[0:1, pl.ds(q_at, bq)]
    if col_ref is None:
        return (k_iota >= info) & (k_iota <= q_iota)
    return (col_ref[pl.ds(k_at, bk), :] == info) & (k_iota <= q_iota)


def attend_kernel(bq, count, sends, by_column, ids, first_ref, row_ref, *rest):
    rest = list(rest)
    col_ref = rest.pop(0) if by_column else None
    pieces, rest = rest[:count], rest[count:]
    columns = rest.pop(0)
    out_pieces, rest = rest[:sends], rest[sends:]
    o_ref, lse_ref, x_ref, k_s, v_s, vt_s = rest
    i = pl.program_id(0)
    me = ids[0]
    rows = pieces[0].shape[0]
    bk = bq

    @pl.when(i == 0)
    def _():
        for s in range(count):
            at = pl.ds(pl.multiple_of((me ^ s) * rows, rows), rows)
            x = dot(pieces[s][...], columns[...]).astype(BF)
            x_ref[at, :] = x
            k_s[at, :] = x[:, GW : 2 * GW]
            v_s[at, :] = x[:, 2 * GW : 3 * GW]
        vt_s[...] = v_s[...].T

    q_at = pl.multiple_of(i * bq, bq)
    q_heads = head_parts(x_ref[pl.ds(q_at, bq), 0:GW])

    def step(j, carry):
        k_at = pl.multiple_of(j * bk, bk)
        keys = k_s[pl.ds(k_at, bk), :]
        mask = pair_mask(row_ref, col_ref, q_at, k_at, bk, bq)
        out = []
        for h in range(HG):
            top, total, acc = carry[h]
            scores = nt_dot(keys, q_heads[h]) * (SCORE_SCALE * LOG2E)
            scores = jnp.where(mask, scores, NEGATIVE)
            top_new = jnp.maximum(top, jnp.max(scores, axis=0, keepdims=True))
            weight = jnp.exp2(scores - top_new)
            fade = jnp.exp2(top - top_new)
            total = total * fade + jnp.sum(weight, axis=0, keepdims=True)
            values_t = vt_s[h * HD : (h + 1) * HD, pl.ds(k_at, bk)]
            acc = acc * fade + dot(values_t, weight.astype(BF))
            out.append((top_new, total, acc))
        return tuple(out)

    start = tuple(
        (
            jnp.full((1, bq), NEGATIVE, F32),
            jnp.zeros((1, bq), F32),
            jnp.zeros((HD, bq), F32),
        )
        for _ in range(HG)
    )
    done = lax.fori_loop(first_ref[i], i + 1, step, start)
    outs = jnp.concatenate([acc / total for _, total, acc in done], axis=0)
    o_ref[pl.ds(q_at, bq), :] = outs.T.astype(BF)
    for h in range(HG):
        top, total, _ = done[h]
        lse_ref[h : h + 1, pl.ds(q_at, bq)] = top + jnp.log2(total)

    @pl.when(i == pl.num_programs(0) - 1)
    def _():
        for s in range(sends):
            at = pl.ds(pl.multiple_of((me ^ s) * rows, rows), rows)
            out_pieces[s][...] = o_ref[at, :]


def attend_back_kernel(bq, count, sends, by_column, ids, first_ref, row_ref, *rest):
    rest = list(rest)
    col_ref = rest.pop(0) if by_column else None
    x_ref = rest.pop(0)
    grads, rest = rest[:count], rest[count:]
    o_ref, lse_ref = rest[:2]
    out_pieces, rest = rest[2 : 2 + sends], rest[2 + sends :]
    dx_ref, k_s, v_s, g_s, dk_s, dv_s = rest
    i = pl.program_id(0)
    me = ids[0]
    rows = grads[0].shape[0]
    bk = bq

    @pl.when(i == 0)
    def _():
        k_s[...] = x_ref[:, GW : 2 * GW]
        v_s[...] = x_ref[:, 2 * GW : 3 * GW]
        for s in range(count):
            at = pl.ds(pl.multiple_of((me ^ s) * rows, rows), rows)
            g_s[at, :] = grads[s][...]
        dk_s[...] = jnp.zeros_like(dk_s)
        dv_s[...] = jnp.zeros_like(dv_s)

    q_at = pl.multiple_of(i * bq, bq)
    grad = g_s[pl.ds(q_at, bq), :]
    q_heads = head_parts(x_ref[pl.ds(q_at, bq), 0:GW])
    g_heads = head_parts(grad)
    dots = (grad.astype(F32) * o_ref[pl.ds(q_at, bq), :].astype(F32)).T
    row_dot = [
        jnp.sum(dots[h * HD : (h + 1) * HD, :], axis=0, keepdims=True) for h in range(HG)
    ]
    lse = [lse_ref[h : h + 1, pl.ds(q_at, bq)] for h in range(HG)]

    def step(j, dq):
        k_at = pl.multiple_of(j * bk, bk)
        here = pl.ds(k_at, bk)
        keys = k_s[here, :]
        values = v_s[here, :]
        key_heads = head_parts(keys)
        mask = pair_mask(row_ref, col_ref, q_at, k_at, bk, bq)
        dk = dk_s[here, :]
        dv = dv_s[here, :]
        for h in range(HG):
            scores = nt_dot(keys, q_heads[h]) * (SCORE_SCALE * LOG2E)
            scores = jnp.where(mask, scores - lse[h], NEGATIVE)
            soft = jnp.exp2(scores)
            g_soft = nt_dot(values, g_heads[h])
            g_scores = (soft * (g_soft - row_dot[h])).astype(BF)
            dv = dv + dot(soft.astype(BF), g_heads[h])
            dk = dk + dot(g_scores, q_heads[h])
            dq = dq + tn_dot(g_scores, key_heads[h])
        dk_s[here, :] = dk
        dv_s[here, :] = dv
        return dq

    dq = lax.fori_loop(first_ref[i], i + 1, step, jnp.zeros((bq, GW), F32))
    dx_ref[pl.ds(q_at, bq), 0:GW] = (dq * SCORE_SCALE).astype(BF)

    @pl.when(i == pl.num_programs(0) - 1)
    def _():
        dx_ref[:, GW : 2 * GW] = (dk_s[...] * SCORE_SCALE).astype(BF)
        dx_ref[:, 2 * GW : 3 * GW] = dv_s[...].astype(BF)
        for s in range(sends):
            at = pl.ds(pl.multiple_of((me ^ s) * rows, rows), rows)
            out_pieces[s][...] = dx_ref[at, :]


def attend(ids, meta, pieces, columns, bq):
    first, row_info, col_info = meta
    rows, width = pieces[0].shape
    count, sends = len(pieces), min(len(pieces), 2 * GROUPS)
    length = rows * count
    operands = [first, row_info] + ([] if col_info is None else [col_info])
    operands += list(pieces) + [columns]
    outs = [sds((rows, GW), BF)] * sends + [
        sds((length, GW), BF),
        sds((8, length), F32),
        sds((length, 3 * GW), BF),
    ]
    got = stage(
        partial(attend_kernel, bq, count, sends, col_info is not None),
        "attend",
        ids,
        operands,
        outs,
        [pltpu.VMEM((length, GW), BF)] * 2 + [pltpu.VMEM((GW, length), BF)],
        flops=length * length * GW * 2 + 6 * length * width * GW,
        grid=(length // bq,),
        specs={0: pl.BlockSpec(memory_space=pltpu.SMEM)},
    )
    return got[:sends], got[sends:]


def attend_back(ids, meta, kept, grads, bq, send=True):
    first, row_info, col_info = meta
    attended, lse, x = kept
    rows = grads[0].shape[0]
    count, sends = len(grads), min(len(grads), 2 * GROUPS) if send else 0
    length = rows * count
    operands = [first, row_info] + ([] if col_info is None else [col_info])
    operands += [x] + list(grads) + [attended, lse]
    got = stage(
        partial(attend_back_kernel, bq, count, sends, col_info is not None),
        "attend_back",
        ids,
        operands,
        [sds((rows, 3 * GW), BF)] * sends + [sds(x.shape, BF)],
        [pltpu.VMEM((length, GW), BF)] * 3 + [pltpu.VMEM((length, GW), F32)] * 2,
        flops=length * length * GW * 5,
        grid=(length // bq,),
        specs={0: pl.BlockSpec(memory_space=pltpu.SMEM)},
    )
    return got[:sends], got[sends]


def project_grads_kernel(count, ids, dx_ref, *rest):
    pieces, (keep, send, total) = rest[:count], rest[count:]
    rows = pieces[0].shape[0]
    for s, piece in enumerate(pieces):
        at = pl.ds(pl.multiple_of((ids[0] ^ s) * rows, rows), rows)
        term = tn_dot(piece[...], dx_ref[at, :])
        total[...] = term if s == 0 else total[...] + term
    split_rows(ids[0], total, keep, send)


def project_grads(ids, wide_count, pieces, dx):
    rows, width = pieces[0].shape
    shape = (wide_count // 2, width // wide_count, 3 * GW)
    return stage(
        partial(project_grads_kernel, len(pieces)),
        "project_grads",
        ids,
        [dx] + list(pieces),
        [sds(shape, BF)] * 2,
        [pltpu.VMEM((width, 3 * GW), F32)],
        flops=6 * dx.size * width // 3,
    )


def group_columns_kernel(ids, project, out):
    group, _ = combo(ids[0])
    width = GROUPS * GW
    for c in range(GROUPS):

        @pl.when(group == c)
        def _():
            for t in range(3):
                at = t * width + c * GW
                out[:, t * GW : (t + 1) * GW] = project[:, at : at + GW]


def group_columns(ids, project):
    (out,) = stage(
        group_columns_kernel,
        "group_columns",
        ids,
        [project],
        [sds((project.shape[0], 3 * GW), BF)],
    )
    return out


def save_halves(me, normed, mine_ref, other_ref):
    rows = mine_ref.shape[0]
    core = lax.rem(me, 2)
    mine_ref[...] = normed[pl.ds(pl.multiple_of(core * rows, rows), rows), :]
    other_ref[...] = normed[pl.ds(pl.multiple_of((1 - core) * rows, rows), rows), :]


def routed_pre_kernel(count, ids, tok, sel, *rest):
    vectors, rest = rest[:count], rest[count:]
    mine_ref, other_ref, one_hot_ref, picked_ref, vecs, normed = rest
    rows = [vector[...].astype(F32).reshape(1, -1) for vector in vectors]
    rows.append(jnp.zeros((8 - count, tok.shape[1]), F32))
    vecs[...] = jnp.concatenate(rows, axis=0)
    span = one_hot_ref.shape[1]
    seqs = sel.shape[0]
    if sel.shape[1] != span:
        sel = sel[:, pl.ds(pl.multiple_of(ids[0] * span, span), span)]
    slots = span // 4
    upper = (
        lax.broadcasted_iota(jnp.int32, (span, span), 0)
        <= lax.broadcasted_iota(jnp.int32, (span, span), 1)
    ).astype(F32).astype(BF)
    slot = lax.broadcasted_iota(jnp.int32, (slots, span), 0).astype(F32)
    for q in range(seqs):
        chosen = jnp.broadcast_to(sel[q : q + 1, :].astype(F32), (8, span))
        rank = dot(chosen.astype(BF), upper)[0:1, :] * chosen[0:1, :] - 1.0
        one_hot = (slot == rank).astype(F32).astype(BF)
        one_hot_ref[q * slots : (q + 1) * slots, :] = one_hot
        picked_ref[q * slots : (q + 1) * slots, :] = dot(
            one_hot, tok[q * span : (q + 1) * span, :]
        ).astype(BF)
    picked = picked_ref[...].astype(F32)
    normed[...] = (picked * norm_scale(picked) * gain_of(vecs, 1)).astype(BF)
    save_halves(ids[0], normed, mine_ref, other_ref)


def gain_of(vecs, k):
    return vecs[k : k + 1, :]


def routed_pre(ids, tok, sel, span, vectors):
    rows, width = tok.shape[0] // 4, tok.shape[1]
    return stage(
        partial(routed_pre_kernel, len(vectors)),
        "routed_pre",
        ids,
        [tok, sel] + vectors,
        [
            sds((rows // 2, width), BF),
            sds((rows // 2, width), BF),
            sds((rows, span), BF),
            sds((rows, width), BF),
            sds((8, width), F32),
        ],
        [pltpu.VMEM((rows, width), BF)],
        flops=4 * rows * width * span,
    )


def routed_mid_kernel(count, ids, *rest):
    pieces = rest[:count]
    output, picked, vecs, branch_ref, low_ref, att_ref, parts = rest[count:]
    attended = load_pieces(ids[0], pieces, parts, 1)
    att_ref[...] = attended
    branch = dot(attended, output[...])
    branch_ref[...] = branch
    middle = picked[...].astype(F32) + branch
    low_ref[...] = (middle * norm_scale(middle) * gain_of(vecs, 2)).astype(BF)


def routed_mid(ids, pieces, output, picked, vecs):
    shape = picked.shape
    return stage(
        partial(routed_mid_kernel, len(pieces)),
        "routed_mid",
        ids,
        list(pieces) + [output, picked, vecs],
        [sds(shape, F32), sds(shape, BF), sds(shape, BF)],
        [pltpu.VMEM((GROUPS, shape[0], GW), BF)],
        flops=2 * shape[0] * shape[1] * shape[1],
    )


def hidden_forward_kernel(count, ids, *rest):
    pieces = rest[:count]
    expand, reduce_ref = rest[count : count + 2]
    outs = rest[count + 2 :]
    rows = pieces[0].shape[0]
    low = jnp.concatenate([piece[...] for piece in pieces], axis=0)
    hidden = gelu(dot(low, expand[...])).astype(BF)
    total = dot(hidden, reduce_ref[...]).astype(BF)
    for s, out in enumerate(outs):
        out[...] = total[s * rows : (s + 1) * rows, :]


def hidden_forward(ids, pieces, expand, reduce_part):
    return stage(
        partial(hidden_forward_kernel, len(pieces)),
        "hidden_forward",
        ids,
        list(pieces) + [expand, reduce_part],
        [sds(pieces[0].shape, BF)] * len(pieces),
        flops=4 * len(pieces) * pieces[0].size * expand.shape[1],
    )


def hidden_back_kernel(count, ids, *rest):
    pieces, grads = rest[:count], rest[count : 2 * count]
    expand, reduce_ref = rest[2 * count : 2 * count + 2]
    outs = rest[2 * count + 2 :]
    rows = pieces[0].shape[0]
    low = jnp.concatenate([piece[...] for piece in pieces], axis=0)
    grad = jnp.concatenate([piece[...] for piece in grads], axis=0)
    _, slope = gelu_both(dot(low, expand[...]))
    grad_pre = (nt_dot(grad, reduce_ref[...]) * slope).astype(BF)
    total = nt_dot(grad_pre, expand[...]).astype(BF)
    for s, out in enumerate(outs):
        out[...] = total[s * rows : (s + 1) * rows, :]


def hidden_back(ids, pieces, grads, expand, reduce_part):
    return stage(
        partial(hidden_back_kernel, len(pieces)),
        "hidden_back",
        ids,
        list(pieces) + list(grads) + [expand, reduce_part],
        [sds(pieces[0].shape, BF)] * len(pieces),
        flops=6 * len(pieces) * pieces[0].size * expand.shape[1],
    )


def dense_pre_kernel(shares, ids, tok, one_hot, picked, vecs, branch, *rest):
    partials = rest[:shares]
    mine_ref, other_ref, mixed_ref, delta_ref, normed = rest[shares:]
    slots, span = one_hot.shape[0] // 2, one_hot.shape[1]
    delta = branch[...]
    for share in partials:
        delta = delta + share[...].astype(F32)
    delta_ref[...] = delta
    gate = jnp.sum(picked[...].astype(F32) * gain_of(vecs, 0), axis=-1, keepdims=True)
    lifted = gate * delta
    for q in range(2):
        at, spots = slice(q * span, (q + 1) * span), slice(q * slots, (q + 1) * slots)
        mixed = tok[at, :].astype(F32) + place(one_hot[spots, :], lifted[spots, :])
        mixed_ref[at, :] = mixed
        normed[at, :] = (mixed * norm_scale(mixed) * gain_of(vecs, 3)).astype(BF)
    save_halves(ids[0], normed, mine_ref, other_ref)


def dense_pre(ids, tok, one_hot, picked, vecs, branch, partials):
    rows, width = tok.shape
    return stage(
        partial(dense_pre_kernel, len(partials)),
        "dense_pre",
        ids,
        [tok, one_hot, picked, vecs, branch] + list(partials),
        [
            sds((rows // 2, width), BF),
            sds((rows // 2, width), BF),
            sds(tok.shape, F32),
            sds(picked.shape, F32),
        ],
        [pltpu.VMEM((rows, width), BF)],
        flops=6 * rows * width * one_hot.shape[0],
    )


def this_part(me, weights, scratch):
    if not scratch:
        return weights[0][0], weights[1][0]
    e_s, r_s = scratch
    chips, rows = weights[0].shape[0], weights[0].shape[3]
    core = lax.rem(me, 2)
    for c in range(chips):
        for weight, at in ((weights[0], 2 * c + core), (weights[1], 2 * c + 1 - core)):
            at = pl.ds(pl.multiple_of(at * rows, rows), rows)
            e_s[at, :] = weight[c, 0, 0]
            r_s[at, :] = weight[c, 0, 1]
    return e_s[...], r_s[...]


def part_specs(base, weights):
    if weights[0].ndim == 3:
        return {
            base + k: pl.BlockSpec((1,) + w.shape[1:], lambda n: (n, 0, 0))
            for k, w in enumerate(weights)
        }
    return {
        base + k: pl.BlockSpec(
            (w.shape[0], 1) + w.shape[2:], lambda n: (0, n, 0, 0, 0)
        )
        for k, w in enumerate(weights)
    }


def part_scratch(width, weights):
    if weights[0].ndim == 3:
        return []
    return [pltpu.VMEM((width, weights[0].shape[-1]), BF)] * 2


def dense_ffn_kernel(count, steps, split, ids, *rest):
    pieces, rest = rest[:count], rest[count:]
    output, mixed, cot, vecs = rest[:4]
    gain = gain_of(vecs, 4)
    rest = rest[4:]
    weights, rest = rest[:split], rest[split:]
    act_ref, low_ref, back_ref, sum_ref, att_ref, gain_ref = rest[:6]
    g_pieces, rest = rest[6 : 6 + steps], rest[6 + steps :]
    parts, branch_s, delta_s, grad_s = rest[:4]
    n = pl.program_id(0)
    me = ids[0]

    @pl.when(n == 0)
    def _():
        attended = load_pieces(me, pieces, parts, 1)
        att_ref[...] = attended
        branch = dot(attended, output[...])
        branch_s[...] = branch
        middle = mixed[...] + branch
        low_ref[...] = (middle * norm_scale(middle) * gain).astype(BF)
        delta_s[...] = jnp.zeros_like(delta_s)
        grad_s[...] = jnp.zeros_like(grad_s)

    expand, reduce_w = this_part(me, weights, rest[4:])
    value, slope = gelu_both(dot(low_ref[...], expand))
    delta_s[...] += dot(value.astype(BF), reduce_w)
    grad_pre = (nt_dot(cot[...], reduce_w) * slope).astype(BF)
    grad_s[...] += nt_dot(grad_pre, expand)

    @pl.when(n == pl.num_programs(0) - 1)
    def _():
        middle = mixed[...] + branch_s[...]
        act_ref[...] = (middle + delta_s[...]).astype(BF)
        grad_middle, gain_grad = norm_back(grad_s[...], middle, gain)
        gain_ref[...] = jnp.broadcast_to(gain_grad, gain_ref.shape)
        total = cot[...].astype(F32) + grad_middle
        sum_ref[...] = total
        back = total.astype(BF)
        back_ref[...] = back
        save_pieces(me, nt_dot(back, output[...]).astype(BF), parts, g_pieces)


def dense_ffn(ids, steps, pieces, output, mixed, cot, vecs, weights):
    rows, width = mixed.shape
    split = len(weights)
    parts_n = weights[0].shape[0 if weights[0].ndim == 3 else 1]
    hidden = weights[0].shape[-1]
    base = len(pieces) + 4
    specs = part_specs(base, weights)
    scratch = [pltpu.VMEM((GROUPS, rows, GW), BF)] + [pltpu.VMEM((rows, width), F32)] * 3
    scratch += part_scratch(width, weights)
    outs = [
        sds((rows, width), BF),
        sds((rows, width), BF),
        sds((rows, width), BF),
        sds((rows, width), F32),
        sds((rows, width), BF),
        sds((8, width), F32),
    ] + [sds((rows // 2, GW), BF)] * steps
    got = stage(
        partial(dense_ffn_kernel, len(pieces), steps, split),
        "dense_ffn",
        ids,
        list(pieces) + [output, mixed, cot, vecs] + list(weights),
        outs,
        scratch,
        flops=8 * rows * width * hidden * parts_n + 4 * rows * width * width,
        grid=(parts_n,),
        specs=specs,
    )
    return got[:6], got[6:]


def dense_post_kernel(ids, stack, *rest):
    project, vecs, mixed, total, one_hot, picked, delta = rest[:7]
    g_mixed_ref, g_delta_ref, g_low_ref, g_gate_ref, router_ref, parts = rest[7:]
    g_proj = load_stack(ids[0], stack, parts, 3)
    grad_rows, _ = norm_back(nt_dot(g_proj, project[...]), mixed[...], gain_of(vecs, 3))
    g_mixed_ref[...] = total[...] + grad_rows
    slots, span = one_hot.shape[0] // 2, one_hot.shape[1]
    rows = picked[...].astype(F32)
    gate = jnp.sum(rows * gain_of(vecs, 0), axis=-1, keepdims=True)
    router = jnp.zeros((1, rows.shape[1]), F32)
    for q in range(2):
        at, spots = slice(q * span, (q + 1) * span), slice(q * slots, (q + 1) * slots)
        lifted = pick(one_hot[spots, :], g_mixed_ref[at, :])
        g_delta = gate[spots, :] * lifted
        g_delta_ref[spots, :] = g_delta
        g_low_ref[spots, :] = g_delta.astype(BF)
        g_gate = jnp.sum(lifted * delta[spots, :], axis=-1, keepdims=True)
        g_gate_ref[spots, :] = jnp.broadcast_to(g_gate, (slots, g_gate_ref.shape[1]))
        router = router + jnp.sum(rows[spots, :] * g_gate, axis=0, keepdims=True)
    router_ref[...] = jnp.broadcast_to(router, router_ref.shape)


def dense_post(ids, stack, project, vecs, mixed, total, one_hot, picked, delta):
    rows, width = mixed.shape
    return stage(
        dense_post_kernel,
        "dense_post",
        ids,
        [stack, project, vecs, mixed, total, one_hot, picked, delta],
        [
            sds((rows, width), F32),
            sds(picked.shape, F32),
            sds(picked.shape, BF),
            sds((picked.shape[0], 128), F32),
            sds((8, width), F32),
        ],
        [pltpu.VMEM((GROUPS, rows, 3 * GW), BF)],
        flops=6 * rows * width * width,
    )


def routed_back_kernel(shares, steps, ids, *rest):
    partials = rest[:shares]
    branch, picked, vecs, g_delta, output = rest[shares : shares + 5]
    rest = rest[shares + 5 :]
    g_mid_ref, back_ref, gain_ref = rest[:3]
    pieces, parts = rest[3 : 3 + steps], rest[3 + steps]
    grad = partials[0][...].astype(F32)
    for share in partials[1:]:
        grad = grad + share[...].astype(F32)
    middle = picked[...].astype(F32) + branch[...]
    g_middle, gain_grad = norm_back(grad, middle, gain_of(vecs, 2))
    gain_ref[...] = jnp.broadcast_to(gain_grad, gain_ref.shape)
    g_mid_ref[...] = g_middle
    back = (g_delta[...] + g_middle).astype(BF)
    back_ref[...] = back
    save_pieces(ids[0], nt_dot(back, output[...]).astype(BF), parts, pieces)


def routed_back(ids, steps, partials, branch, picked, vecs, g_delta, output):
    rows, width = branch.shape
    got = stage(
        partial(routed_back_kernel, len(partials), steps),
        "routed_back",
        ids,
        list(partials) + [branch, picked, vecs, g_delta, output],
        [sds((rows, width), F32), sds((rows, width), BF), sds((8, width), F32)]
        + [sds((rows // 2, GW), BF)] * steps,
        [pltpu.VMEM((GROUPS, rows, GW), BF)],
        flops=2 * rows * width * width,
    )
    return got[0], got[1], got[2], got[3:]


def routed_post_kernel(count, ids, *rest):
    pieces = rest[:count]
    project, vecs, picked, g_mid, g_mixed, one_hot, g_gate = rest[count : count + 7]
    out_ref, parts = rest[count + 7 :]
    g_proj = load_pieces(ids[0], pieces, parts, 3)
    rows = picked[...].astype(F32)
    grad_rows, _ = norm_back(nt_dot(g_proj, project[...]), rows, gain_of(vecs, 1))
    spread = g_mid[...] + grad_rows + g_gate[:, 0:1] * gain_of(vecs, 0)
    slots, span = one_hot.shape[0] // 2, one_hot.shape[1]
    for q in range(2):
        at, spots = slice(q * span, (q + 1) * span), slice(q * slots, (q + 1) * slots)
        out_ref[at, :] = g_mixed[at, :] + place(one_hot[spots, :], spread[spots, :])


def routed_post(ids, pieces, project, vecs, picked, g_mid, g_mixed, one_hot, g_gate):
    rows, width = picked.shape
    (out,) = stage(
        partial(routed_post_kernel, len(pieces)),
        "routed_post",
        ids,
        list(pieces) + [project, vecs, picked, g_mid, g_mixed, one_hot, g_gate],
        [sds(g_mixed.shape, F32)],
        [pltpu.VMEM((GROUPS, rows, 3 * GW), BF)],
        flops=6 * rows * width * width,
    )
    return out


def split_rows(me, total, keep, send):
    chips, rows = keep.shape[0], keep.shape[1]
    core = lax.rem(me, 2)
    for c in range(chips):
        mine = pl.multiple_of((2 * c + core) * rows, rows)
        other = pl.multiple_of((2 * c + 1 - core) * rows, rows)
        keep[c] = total[pl.ds(mine, rows), :].astype(BF)
        send[c] = total[pl.ds(other, rows), :].astype(BF)


def hidden_grads_kernel(ids, low, grad, expand, reduce_ref, out, total):
    i = pl.program_id(0)
    hidden = expand.shape[1]

    @pl.when(i == 0)
    def _():
        total[...] = jnp.zeros_like(total)

    value, slope = gelu_both(dot(low[...], expand[...]))
    grad_pre = (nt_dot(grad[...], reduce_ref[...]) * slope).astype(BF)
    total[:, 0:hidden] += tn_dot(low[...], grad_pre)
    total[:, hidden : 2 * hidden] += tn_dot(grad[...], value.astype(BF))

    @pl.when(i == pl.num_programs(0) - 1)
    def _():
        out[...] = total[...].astype(BF)


def hidden_grads(ids, low, grad, expand, reduce_part):
    width, hidden = expand.shape
    block = min(512, low.shape[0])
    row_spec = pl.BlockSpec((block, width), lambda i: (i, 0))
    (out,) = stage(
        hidden_grads_kernel,
        "hidden_grads",
        ids,
        [low, grad, expand, reduce_part],
        [sds((width, 2 * hidden), BF)],
        [pltpu.VMEM((width, 2 * hidden), F32)],
        flops=8 * low.size * hidden,
        grid=(low.shape[0] // block,),
        specs={0: row_spec, 1: row_spec},
    )
    return out


def output_grads_kernel(vectors, ids, att_d, back_d, att_r, back_r, *rest):
    rest = list(rest)
    vecs, rest = rest[:vectors], rest[vectors:]
    keep, send, total = rest
    width = att_d.shape[1]
    total[:, 0:width] = tn_dot(att_d[...], back_d[...])
    total[:, width : 2 * width] = tn_dot(att_r[...], back_r[...])
    rows = [vec[0:1, :] for vec in vecs]
    rows.append(jnp.zeros((128 - vectors, width), F32))
    total[:, 2 * width : 2 * width + 128] = jnp.concatenate(rows, axis=0).T
    split_rows(ids[0], total, keep, send)


def output_grads(ids, wide_count, att_d, back_d, att_r, back_r, vecs):
    rows, width = att_d.shape
    columns = 2 * width + 128
    shape = (wide_count // 2, width // wide_count, columns)
    return stage(
        partial(output_grads_kernel, len(vecs)),
        "output_grads",
        ids,
        [att_d, back_d, att_r, back_r] + list(vecs),
        [sds(shape, BF), sds(shape, BF)],
        [pltpu.VMEM((width, columns), F32)],
        flops=3 * rows * width * width,
    )


def join_kernel(chips, ids, keep, came, *outs):
    chip = lax.div(ids[0], 2)
    for s, out in enumerate(outs):
        at = chip ^ s
        out[...] = (keep[at].astype(F32) + came[at].astype(F32)).astype(BF)


def join_chips(ids, keep, came):
    chips = keep.shape[0]
    return stage(
        partial(join_kernel, chips), "join", ids, [keep, came], [sds(keep.shape[1:], BF)] * chips
    )


def chips_return(parts):
    return [parts[0]] + [chip_step(parts[s], s) for s in range(1, len(parts))]


def sum_terms(terms):
    total = terms[0].astype(F32)
    for term in terms[1:]:
        total = total + term.astype(F32)
    return total


def sum_split_kernel(count, ids, *rest):
    terms, outs, total = rest[:count], rest[count:-1], rest[-1]
    got = terms[0][...].astype(F32)
    for term in terms[1:]:
        got = got + term[...].astype(F32)
    total[...] = got
    rows = outs[0].shape[0]
    for s, out in enumerate(outs):
        at = pl.multiple_of((ids[1] ^ s) * rows, rows)
        out[...] = total[pl.ds(at, rows), :].astype(BF)


def sum_kernel(ids, *rest):
    got = rest[0][...].astype(F32)
    for term in rest[1:-1]:
        got = got + term[...].astype(F32)
    rest[-1][...] = got.astype(BF)


def gather_out_kernel(count, ids, *rest):
    pieces, outs, wide_s = rest[:count], rest[count:-1], rest[-1]
    rows = pieces[0].shape[0]
    for s, piece in enumerate(pieces):
        at = pl.ds(pl.multiple_of((ids[1] ^ s) * rows, rows), rows)
        low = 0
        for out in outs[:-1]:
            columns = out.shape[1]
            out[at, :] = piece[:, low : low + columns].astype(F32)
            low += columns
        wide_s[at, :] = piece[:, low:].astype(F32)
    outs[-1][...] = wide_s[...].T[: outs[-1].shape[0], :]


def reduce_narrow(ids, terms, widths):
    narrow_count = lax.axis_size("narrow")
    rows, columns = terms[0].shape
    if rows % (8 * narrow_count):
        total = lax.psum(sum_terms(terms).astype(BF), "narrow").astype(F32)
        outs, low = [], 0
        for size in widths:
            outs.append(total[:, low : low + size])
            low += size
        outs[-1] = outs[-1].T[:8]
        return outs
    share = rows // narrow_count
    parts = stage(
        partial(sum_split_kernel, len(terms)),
        "sum_split",
        ids,
        terms,
        [sds((share, columns), BF)] * narrow_count,
        [pltpu.VMEM((rows, columns), F32)],
    )
    came = [parts[0]] + [narrow_step(parts[s], s) for s in range(1, narrow_count)]
    (total,) = stage(sum_kernel, "sum_terms", ids, came, [sds((share, columns), BF)])
    pieces = [total] + [narrow_step(total, s) for s in range(1, narrow_count)]
    return stage(
        partial(gather_out_kernel, narrow_count),
        "gather_out",
        ids,
        pieces,
        [sds((rows, size), F32) for size in widths[:-1]] + [sds((8, rows), F32)],
        [pltpu.VMEM((rows, widths[-1]), F32)],
    )


def join_narrow_kernel(count, ids, keep, came, *outs):
    each = outs[0].shape[0]
    for t, out in enumerate(outs):
        for j in range(each):
            at = (ids[1] ^ t) * each + j
            out[j] = (keep[at].astype(F32) + came[at].astype(F32)).astype(BF)


def route_kernel(count, ids, *rest):
    pieces, outs, blocks = rest[:count], rest[count:-1], rest[-1]
    each = pieces[0].shape[0]
    for t, piece in enumerate(pieces):
        for j in range(each):
            blocks[(ids[1] ^ t) * each + j] = piece[j]
    chip = lax.div(ids[0], 2)
    for s, out in enumerate(outs):
        out[...] = blocks[chip ^ s]


def unpack_kernel(ids, *rest):
    pieces, own, own_gain, out, gain_ref, parts = (rest[:GROUPS],) + rest[GROUPS:]
    for s, piece in enumerate(pieces):
        group = lax.rem(lax.div(ids[0], 2) ^ s, GROUPS)
        parts[group] = piece[...].astype(F32)
    rows = out.shape[0]
    total = jnp.zeros((rows, GW), F32)
    for t in range(3):
        for c in range(GROUPS):
            at = (t * GROUPS + c) * GW
            part = parts[c, :, t * GW : (t + 1) * GW]
            out[:, at : at + GW] = part
            total = total + part * own[:, at : at + GW].astype(F32)
    sums = jnp.broadcast_to(jnp.sum(total, axis=1, keepdims=True), (rows, 128)).T
    gain_ref[...] = sums[0:8, :] / own_gain[...]


def unpack(ids, pieces, own, own_gain):
    rows, columns = pieces[0].shape
    return stage(
        unpack_kernel,
        "unpack",
        ids,
        list(pieces) + [own, own_gain],
        [sds((rows, GROUPS * columns), F32), sds((8, rows), F32)],
        [pltpu.VMEM((GROUPS, rows, columns), F32)],
    )


def split_narrow(ids, keep, came):
    narrow_count = lax.axis_size("narrow")
    chips, rows, columns = keep.shape
    shape = (chips // narrow_count, rows, columns)
    return stage(
        partial(join_narrow_kernel, narrow_count),
        "join_narrow",
        ids,
        [keep, came],
        [sds(shape, BF)] * narrow_count,
    )


def sum_project(ids, parts):
    (total,) = stage(
        sum_kernel, "sum_terms", ids, narrow_return(parts), [sds(parts[0].shape, BF)]
    )
    return total


def route_project(ids, gathered, chips):
    rows, columns = gathered[0].shape[1:]
    return stage(
        partial(route_kernel, len(gathered)),
        "route",
        ids,
        gathered,
        [sds((rows, columns), BF)] * GROUPS,
        [pltpu.VMEM((chips, rows, columns), BF)],
    )


def finish_hidden_kernel(ids, dense, routed, e_d, r_d, e_r, r_r):
    hidden = e_d.shape[1]
    for total, e_ref, r_ref in ((dense, e_d, r_d), (routed, e_r, r_r)):
        e_ref[...] = total[:, 0:hidden].astype(F32)
        r_ref[...] = total[:, hidden : 2 * hidden].astype(F32)


def finish_hidden(ids, dense, routed):
    rows, columns = dense.shape
    return stage(
        finish_hidden_kernel,
        "finish_hidden",
        ids,
        [dense, routed],
        [sds((rows, columns // 2), F32)] * 4,
    )


def tie(x, *first):
    return lax.optimization_barrier((x, first))[0]


def narrow_step(x, s):
    return lax.ppermute(x, "narrow", [(j, j ^ s) for j in range(lax.axis_size("narrow"))])


def narrow_gather(x):
    return [x] + [narrow_step(x, s) for s in range(1, lax.axis_size("narrow"))]


def narrow_return(parts):
    return [parts[0]] + [narrow_step(parts[s], s) for s in range(1, len(parts))]


def exchange(pieces):
    wide_count = lax.axis_size("wide")
    return [pieces[0]] + [
        lax.ppermute(pieces[s], "wide", [(j, j ^ s) for j in range(wide_count)])
        for s in range(1, len(pieces))
    ]


def exchange_rows(mine, other):
    wide_count = lax.axis_size("wide")
    if wide_count != 8:
        return exchange([mine, other] * (wide_count // 2))
    beside = core_step(other)
    from_x = [chip_step(mine, 1), chip_step(beside, 1)]
    from_y = [chip_step(mine, 2), chip_step(beside, 2)]
    corner = [chip_step(from_y[0], 1), chip_step(from_x[1], 2)]
    return [mine, beside] + from_x + from_y + corner


def hidden_share(expand, reduce_part):
    wide_count = lax.axis_size("wide")
    here = lax.axis_index("wide")
    width, hidden = expand.shape
    rows = width // wide_count
    if width != hidden or rows % 16:
        return None
    return jnp.stack(
        [
            lax.dynamic_slice_in_dim(expand, here * rows, rows, 0),
            lax.dynamic_slice_in_dim(reduce_part, here * rows, rows, 0),
        ]
    )


def chip_step(x, s):
    return lax.ppermute(
        x, "wide", [(j, j ^ (2 * s)) for j in range(lax.axis_size("wide"))]
    )


def core_step(x):
    return lax.ppermute(x, "wide", [(j, j ^ 1) for j in range(lax.axis_size("wide"))])


def on_device(
    tokens,
    cotangent,
    selected,
    segments,
    router_vector,
    project_routed,
    output_routed,
    prenorm_routed,
    midnorm_routed,
    expand_routed,
    reduce_routed,
    project_dense,
    output_dense,
    prenorm_dense,
    midnorm_dense,
    expand_dense,
    reduce_dense,
):
    seq_count, span_rows, width = tokens.shape
    row_length = selected.shape[1]
    hidden = expand_dense.shape[1]
    wide_count = lax.axis_size("wide")
    here = lax.axis_index("wide")
    slot_count = span_rows // 4
    bq_dense = min(256, row_length)
    bq_routed = min(256, slot_count * wide_count)
    ids = jnp.stack([here, lax.axis_index("narrow")]).astype(jnp.int32)
    tok = tokens.reshape(-1, width)
    cot = cotangent.reshape(-1, width)

    share_d = hidden_share(expand_dense, reduce_dense)
    staged = share_d is not None
    if staged:
        own_d = lax.all_gather(share_d, "narrow", axis=0)

    mine = here % seq_count
    seq_segments = lax.dynamic_slice_in_dim(segments, mine, 1, 0)[0]
    seq_selected = lax.dynamic_slice_in_dim(selected, mine, 1, 0)[0].reshape(wide_count, span_rows)
    upper = (
        lax.broadcasted_iota(jnp.int32, (span_rows, span_rows), 0)
        <= lax.broadcasted_iota(jnp.int32, (span_rows, span_rows), 1)
    ).astype(BF)
    slots = jnp.arange(slot_count, dtype=jnp.int32)
    seq_rank = jnp.dot(seq_selected.astype(BF), upper, preferred_element_type=F32)
    seq_rank = jnp.where(seq_selected > 0, seq_rank.astype(jnp.int32) - 1, -1)
    slot_segments = (
        jnp.sum(
            jnp.where(
                seq_rank[:, None, :] == slots[None, :, None],
                seq_segments.reshape(wide_count, 1, span_rows) + 1,
                0,
            ),
            axis=-1,
        )
        - 1
    ).reshape(-1)
    meta_routed = (
        jnp.zeros((slot_segments.shape[0] // bq_routed,), jnp.int32),
        jnp.broadcast_to(slot_segments[None], (8, slot_segments.shape[0])),
        slot_segments[:, None],
    )
    own_selected = selected
    if span_rows % 128:
        own_selected = lax.dynamic_slice_in_dim(selected, here * span_rows, span_rows, 1)
    mine_r, other_r, one_hot, picked, vecs = routed_pre(
        ids,
        tok,
        own_selected,
        span_rows,
        [router_vector, prenorm_routed, midnorm_routed, prenorm_dense, midnorm_dense],
    )
    columns_r = group_columns(ids, tie(project_routed, mine_r))
    rows_r = exchange([mine_r, other_r] * (wide_count // 2))
    rows_r, meta_routed = lax.optimization_barrier((rows_r, meta_routed))
    pieces, kept_r = attend(ids, meta_routed, rows_r, columns_r, bq_routed)
    pieces = exchange(pieces)
    if staged:
        pieces, own_d = lax.optimization_barrier((pieces, own_d))
        chips_d = lax.all_gather(
            own_d,
            "wide",
            axis=0,
            axis_index_groups=[list(range(r, wide_count, 2)) for r in range(2)],
        )
    branch_r, low_r, att_r = routed_mid(ids, pieces, output_routed, picked, vecs)
    dense_segments = tie(seq_segments, low_r)
    starts = sum(
        jnp.where(dense_segments == value, jnp.sum((dense_segments < value).astype(jnp.int32)), 0)
        for value in range(1, 4)
    )
    meta_dense = (
        starts[::bq_dense] // bq_dense,
        jnp.broadcast_to(starts[None], (8, row_length)),
        None,
    )

    own_at = here * (width // wide_count)

    def own_slice(x):
        return lax.dynamic_slice_in_dim(tie(x, low_r), own_at, width // wide_count, 0)

    own_rows = (
        own_slice(project_routed),
        own_slice(project_dense),
        own_slice(prenorm_routed).astype(F32)[None],
        own_slice(prenorm_dense).astype(F32)[None],
    )
    columns_d = group_columns(ids, tie(project_dense, low_r))
    low_pieces, columns_d, meta_dense, own_rows = lax.optimization_barrier(
        (narrow_gather(low_r), columns_d, meta_dense, own_rows)
    )
    partials = narrow_return(hidden_forward(ids, low_pieces, expand_routed, reduce_routed))

    mine_d, other_d, mixed, delta_r = dense_pre(
        ids, tok, one_hot, picked, vecs, branch_r, partials
    )
    if staged:
        mine_d, other_d, chips_d = lax.optimization_barrier((mine_d, other_d, chips_d))
    cot_all = lax.all_gather(tie(cot, mine_d), "narrow", axis=0, tiled=True)
    rows_d = exchange_rows(mine_d, other_d)
    if staged:
        weights_d = [chips_d, core_step(chips_d)]
    else:
        weights_d = [
            lax.all_gather(expand_dense, "narrow", axis=0),
            lax.all_gather(reduce_dense, "narrow", axis=0),
        ]
    pieces, kept_d = attend(ids, meta_dense, rows_d, columns_d, bq_dense)
    pieces, weights_d = lax.optimization_barrier((pieces, weights_d))
    pieces, cot_all = lax.optimization_barrier((exchange(pieces), cot_all))
    (activations, low_d, back_d, sum_d, att_d, mid_gain_d), pieces = dense_ffn(
        ids, wide_count, pieces, output_dense, mixed, cot, vecs, weights_d
    )
    low_all = lax.all_gather(low_d, "narrow", axis=0, tiled=True)
    _, dx_d = attend_back(ids, meta_dense, kept_d, exchange(pieces), bq_dense, send=False)
    stack = lax.all_to_all(dx_d.reshape(wide_count, span_rows, 3 * GW), "wide", 0, 0)
    keep, send = project_grads(ids, wide_count, rows_d, dx_d)
    project_d = sum_project(ids, split_narrow(ids, keep, core_step(send)))
    stack, project_d = lax.optimization_barrier((stack, project_d))
    project_d_parts = route_project(ids, narrow_gather(project_d), keep.shape[0])
    g_mixed, g_delta, g_low, g_gate, router_grad = dense_post(
        ids, stack, project_dense, vecs, mixed, sum_d, one_hot, picked, delta_r
    )

    g_pieces = narrow_gather(g_low)
    hidden_d = hidden_grads(ids, tie(low_all, g_low), cot_all, expand_dense, reduce_dense)
    g_pieces, hidden_d, project_d_parts = lax.optimization_barrier(
        (g_pieces, hidden_d, project_d_parts)
    )
    project_d_grad, pre_gain_d = unpack(
        ids, chips_return(project_d_parts), own_rows[1], own_rows[3]
    )
    ffn_d = lax.psum_scatter(hidden_d, "wide", scatter_dimension=0, tiled=True)
    partials = hidden_back(ids, low_pieces, g_pieces, expand_routed, reduce_routed)
    hidden_r = hidden_grads(
        ids,
        jnp.concatenate(low_pieces, axis=0),
        jnp.concatenate(g_pieces, axis=0),
        expand_routed,
        reduce_routed,
    )
    partials, hidden_r, project_d_grad = lax.optimization_barrier(
        (narrow_return(partials), hidden_r, project_d_grad)
    )
    ffn_r = lax.psum_scatter(hidden_r, "wide", scatter_dimension=0, tiled=True)
    g_mid_r, back_r, mid_gain_r, pieces = routed_back(
        ids, wide_count, partials, branch_r, picked, vecs, g_delta, output_routed
    )
    keep_o, send_o = output_grads(
        ids,
        wide_count,
        att_d,
        back_d,
        att_r,
        back_r,
        [mid_gain_r, mid_gain_d, router_grad],
    )
    pieces, keep_o, send_o = lax.optimization_barrier((exchange(pieces), keep_o, send_o))
    pieces, dx_r = attend_back(ids, meta_routed, kept_r, pieces, bq_routed)
    keep, send = project_grads(ids, wide_count, rows_r, dx_r)
    output_parts = join_chips(ids, tie(keep_o, send), core_step(send_o))
    project_parts = split_narrow(ids, keep, core_step(tie(send, output_parts)))
    output_terms, pieces, project_parts = lax.optimization_barrier(
        (chips_return(output_parts), pieces, project_parts)
    )
    project_r = sum_project(ids, project_parts)
    project_r_terms = chips_return(
        route_project(ids, narrow_gather(project_r), keep.shape[0])
    )
    output_d_grad, output_r_grad, vectors = reduce_narrow(
        ids, output_terms, [width, width, 128]
    )
    project_r_grad, pre_gain_r = unpack(ids, project_r_terms, own_rows[0], own_rows[2])
    tokens_gradient = routed_post(
        ids, exchange(pieces), project_routed, vecs, picked, g_mid_r, g_mixed, one_hot, g_gate
    )
    expand_d_grad, reduce_d_grad, expand_r_grad, reduce_r_grad = finish_hidden(
        ids, ffn_d, ffn_r
    )
    return (
        activations.reshape(tokens.shape),
        tokens_gradient.reshape(tokens.shape),
        vectors[2],
        project_r_grad,
        output_r_grad,
        pre_gain_r[0],
        vectors[0],
        expand_r_grad,
        reduce_r_grad.T,
        project_d_grad,
        output_d_grad,
        pre_gain_d[0],
        vectors[1],
        expand_d_grad,
        reduce_d_grad.T,
    )


def solution(mesh):
    return jax.shard_map(
        on_device,
        mesh=mesh,
        in_specs=(
            P("narrow", "wide", None),
            P("narrow", "wide", None),
            P("narrow", None),
            P("narrow", None),
            P(),
            P(),
            P(),
            P(),
            P(),
            P(None, "narrow"),
            P("narrow", None),
            P(),
            P(),
            P(),
            P(),
            P(None, "narrow"),
            P("narrow", None),
        ),
        out_specs=(
            P("narrow", "wide", None),
            P("narrow", "wide", None),
            P("wide"),
            P("wide", None),
            P("wide", None),
            P("wide"),
            P("wide"),
            P("wide", "narrow"),
            P("narrow", "wide"),
            P("wide", None),
            P("wide", None),
            P("wide"),
            P("wide"),
            P("wide", "narrow"),
            P("narrow", "wide"),
        ),
        check_vma=False,
    )
```

```python
from functools import partial

import jax
import jax.numpy as jnp
from jax import lax
from jax.experimental import pallas as pl
from jax.experimental.pallas import tpu as pltpu
from jax.sharding import PartitionSpec as P

H = 12
HD = 64
GROUPS = 4
HG = H // GROUPS
GW = HG * HD

EPSILON = 1e-06
NEGATIVE = -1e30
SCORE_SCALE = 0.125
LOG2E = 1.4426950408889634
GELU_A = 0.7978845608028654
GELU_B = 0.044715
BF = jnp.bfloat16
F32 = jnp.float32
VMEM = 56 << 20


def nt_dot(left, right):
    return lax.dot_general(left, right, (((1,), (1,)), ((), ())), preferred_element_type=F32)


def tn_dot(left, right):
    return lax.dot_general(left, right, (((0,), (0,)), ((), ())), preferred_element_type=F32)


def dot(left, right):
    return jnp.dot(left, right, preferred_element_type=F32)


def sds(shape, dtype):
    return jax.ShapeDtypeStruct(shape, dtype)


def norm_scale(rows):
    return lax.rsqrt(jnp.mean(rows * rows, axis=-1, keepdims=True) + EPSILON)


def norm_back(grad, rows, gain):
    scale = norm_scale(rows)
    inner = grad * gain
    mean = jnp.mean(inner * rows, axis=-1, keepdims=True)
    grad_rows = scale * inner - rows * (scale * scale * scale * mean)
    return grad_rows, jnp.sum(grad * rows * scale, axis=0, keepdims=True)


def gelu(a):
    return 0.5 * a * (1.0 + jnp.tanh(GELU_A * (a + GELU_B * (a * a * a))))


def gelu_both(a):
    square = a * a
    bend = jnp.tanh(GELU_A * (a + GELU_B * (square * a)))
    half = 0.5 * (1.0 + bend)
    slope = half + 0.5 * a * (1.0 - bend * bend) * (GELU_A * (1.0 + 3.0 * GELU_B * square))
    return a * half, slope


def three_parts(x):
    first = x.astype(BF)
    rest = x - first.astype(F32)
    second = rest.astype(BF)
    third = (rest - second.astype(F32)).astype(BF)
    return [first, second, third]


def place(one_hot, x):
    return tn_dot(
        jnp.concatenate([one_hot] * 3, axis=0), jnp.concatenate(three_parts(x), axis=0)
    )


def pick(one_hot, x):
    return dot(jnp.concatenate([one_hot] * 3, axis=1), jnp.concatenate(three_parts(x), axis=0))


def combo(index):
    return lax.rem(lax.div(index, 2), GROUPS), lax.rem(index, 2)


def save_pieces(me, full, parts, pieces):
    rows = full.shape[0] // 2
    thirds = full.shape[1] // (GROUPS * GW)
    for c in range(GROUPS):
        for t in range(thirds):
            at = t * GROUPS * GW + c * GW
            parts[c, :, t * GW : (t + 1) * GW] = full[:, at : at + GW]
    for s, piece in enumerate(pieces):
        c, r = combo(me ^ s)
        piece[...] = parts[c, pl.ds(pl.multiple_of(r * rows, rows), rows), :]


def load_pieces(me, pieces, parts, thirds):
    rows = pieces[0].shape[0]
    for s, piece in enumerate(pieces):
        c, r = combo(me ^ s)
        parts[c, pl.ds(pl.multiple_of(r * rows, rows), rows), :] = piece[...]
    return jnp.concatenate(
        [parts[c, :, t * GW : (t + 1) * GW] for t in range(thirds) for c in range(GROUPS)],
        axis=1,
    )


def save_stack(full, parts, stack):
    rows = full.shape[0] // 2
    thirds = full.shape[1] // (GROUPS * GW)
    half, columns = rows // 2, thirds * GW
    for c in range(GROUPS):
        for t in range(thirds):
            at = t * GROUPS * GW + c * GW
            parts[c, :, t * GW : (t + 1) * GW] = full[:, at : at + GW]
    for b in range(stack.shape[0]):
        c, at = (b // 2) % GROUPS, (b % 2) * rows
        stack[b, :, 0:columns] = parts[c, at : at + half, :]
        stack[b, :, columns : 2 * columns] = parts[c, at + half : at + rows, :]


def load_stack(me, stack, parts, thirds):
    half, columns = stack.shape[1], stack.shape[2] // 2
    first = lax.div(me, 2 * GROUPS) * (2 * GROUPS)
    for w in range(2 * GROUPS):
        c, at = w // 2, (w % 2) * 2 * half
        parts[c, at : at + half, :] = stack[first + w, :, 0:columns]
        parts[c, at + half : at + 2 * half, :] = stack[first + w, :, columns : 2 * columns]
    return jnp.concatenate(
        [parts[c, :, t * GW : (t + 1) * GW] for t in range(thirds) for c in range(GROUPS)],
        axis=1,
    )


def stage(body, name, ids, operands, outs, scratch=(), flops=0, grid=None, specs=None):
    kwargs = {}
    if grid is not None:
        kwargs["grid"] = grid
    in_specs = [pl.BlockSpec(memory_space=pltpu.SMEM)]
    for k, operand in enumerate(operands):
        spec = None if specs is None else specs.get(k)
        if spec is None:
            zeros = (0,) * operand.ndim
            spec = pl.BlockSpec(operand.shape, lambda *_, z=zeros: z)
        in_specs.append(spec)
    out_specs = tuple(
        pl.BlockSpec(out.shape, lambda *_, z=(0,) * len(out.shape): z) for out in outs
    )
    moved = sum(a.size * a.dtype.itemsize for a in operands)
    moved += sum(math_prod(a.shape) * a.dtype.itemsize for a in outs)
    return pl.pallas_call(
        body,
        out_shape=tuple(outs),
        in_specs=in_specs,
        out_specs=out_specs,
        scratch_shapes=list(scratch),
        compiler_params=pltpu.CompilerParams(vmem_limit_bytes=VMEM),
        cost_estimate=pl.CostEstimate(flops=flops, bytes_accessed=moved, transcendentals=0),
        name=name,
        **kwargs,
    )(ids, *operands)


def math_prod(shape):
    total = 1
    for size in shape:
        total *= size
    return total


def head_parts(rows):
    lane = lax.broadcasted_iota(jnp.int32, rows.shape, 1)
    zero = jnp.zeros_like(rows)
    return [
        jnp.where((lane >= h * HD) & (lane < (h + 1) * HD), rows, zero) for h in range(HG)
    ]


def pair_mask(row_ref, col_ref, q_at, k_at, bk, bq):
    k_iota = lax.broadcasted_iota(jnp.int32, (bk, bq), 0) + k_at
    q_iota = lax.broadcasted_iota(jnp.int32, (bk, bq), 1) + q_at
    info = row_ref[0:1, pl.ds(q_at, bq)]
    if col_ref is None:
        return (k_iota >= info) & (k_iota <= q_iota)
    return (col_ref[pl.ds(k_at, bk), :] == info) & (k_iota <= q_iota)


def attend_kernel(bq, count, sends, stacked, by_column, ids, first_ref, row_ref, *rest):
    rest = list(rest)
    col_ref = rest.pop(0) if by_column else None
    pieces, rest = rest[:count], rest[count:]
    columns = rest.pop(0)
    out_pieces, rest = rest[:sends], rest[sends:]
    stack_ref = rest.pop(0) if stacked else None
    o_ref, lse_ref, x_ref, k_s, v_s, vt_s = rest
    i = pl.program_id(0)
    me = ids[0]
    rows = pieces[0].shape[0]
    bk = bq

    @pl.when(i == 0)
    def _():
        for s in range(count):
            at = pl.ds(pl.multiple_of((me ^ s) * rows, rows), rows)
            x = dot(pieces[s][...], columns[...]).astype(BF)
            x_ref[at, :] = x
            k_s[at, :] = x[:, GW : 2 * GW]
            v_s[at, :] = x[:, 2 * GW : 3 * GW]
        vt_s[...] = v_s[...].T

    q_at = pl.multiple_of(i * bq, bq)
    q_heads = head_parts(x_ref[pl.ds(q_at, bq), 0:GW])

    def step(j, carry):
        k_at = pl.multiple_of(j * bk, bk)
        keys = k_s[pl.ds(k_at, bk), :]
        mask = pair_mask(row_ref, col_ref, q_at, k_at, bk, bq)
        out = []
        for h in range(HG):
            top, total, acc = carry[h]
            scores = nt_dot(keys, q_heads[h]) * (SCORE_SCALE * LOG2E)
            scores = jnp.where(mask, scores, NEGATIVE)
            top_new = jnp.maximum(top, jnp.max(scores, axis=0, keepdims=True))
            weight = jnp.exp2(scores - top_new)
            fade = jnp.exp2(top - top_new)
            total = total * fade + jnp.sum(weight, axis=0, keepdims=True)
            values_t = vt_s[h * HD : (h + 1) * HD, pl.ds(k_at, bk)]
            acc = acc * fade + dot(values_t, weight.astype(BF))
            out.append((top_new, total, acc))
        return tuple(out)

    start = tuple(
        (
            jnp.full((1, bq), NEGATIVE, F32),
            jnp.zeros((1, bq), F32),
            jnp.zeros((HD, bq), F32),
        )
        for _ in range(HG)
    )
    done = lax.fori_loop(first_ref[i], i + 1, step, start)
    outs = jnp.concatenate([acc / total for _, total, acc in done], axis=0)
    o_ref[pl.ds(q_at, bq), :] = outs.T.astype(BF)
    for h in range(HG):
        top, total, _ = done[h]
        lse_ref[h : h + 1, pl.ds(q_at, bq)] = top + jnp.log2(total)

    @pl.when(i == pl.num_programs(0) - 1)
    def _():
        for s in range(sends):
            at = pl.ds(pl.multiple_of((me ^ s) * rows, rows), rows)
            out_pieces[s][...] = o_ref[at, :]
        if stacked:
            half = rows // 2
            for b in range(count):
                at = b * rows
                stack_ref[b, :, 0:GW] = o_ref[at : at + half, :]
                stack_ref[b, :, GW : 2 * GW] = o_ref[at + half : at + rows, :]


def attend_back_kernel(bq, count, sends, stacked, by_column, ids, first_ref, row_ref, *rest):
    rest = list(rest)
    col_ref = rest.pop(0) if by_column else None
    x_ref = rest.pop(0)
    given = 1 if stacked else count
    grads, rest = rest[:given], rest[given:]
    o_ref, lse_ref = rest[:2]
    out_pieces, rest = rest[2 : 2 + sends], rest[2 + sends :]
    stack_ref = rest.pop(0) if stacked else None
    dx_ref, k_s, v_s, g_s, dk_s, dv_s = rest
    i = pl.program_id(0)
    me = ids[0]
    rows = g_s.shape[0] // count
    bk = bq

    @pl.when(i == 0)
    def _():
        k_s[...] = x_ref[:, GW : 2 * GW]
        v_s[...] = x_ref[:, 2 * GW : 3 * GW]
        for s in range(count):
            if stacked:
                half = rows // 2
                g_s[s * rows : s * rows + half, :] = grads[0][s, :, 0:GW]
                g_s[s * rows + half : (s + 1) * rows, :] = grads[0][s, :, GW : 2 * GW]
            else:
                at = pl.ds(pl.multiple_of((me ^ s) * rows, rows), rows)
                g_s[at, :] = grads[s][...]
        dk_s[...] = jnp.zeros_like(dk_s)
        dv_s[...] = jnp.zeros_like(dv_s)

    q_at = pl.multiple_of(i * bq, bq)
    grad = g_s[pl.ds(q_at, bq), :]
    q_heads = head_parts(x_ref[pl.ds(q_at, bq), 0:GW])
    g_heads = head_parts(grad)
    dots = (grad.astype(F32) * o_ref[pl.ds(q_at, bq), :].astype(F32)).T
    row_dot = [
        jnp.sum(dots[h * HD : (h + 1) * HD, :], axis=0, keepdims=True) for h in range(HG)
    ]
    lse = [lse_ref[h : h + 1, pl.ds(q_at, bq)] for h in range(HG)]

    def step(j, dq):
        k_at = pl.multiple_of(j * bk, bk)
        here = pl.ds(k_at, bk)
        keys = k_s[here, :]
        values = v_s[here, :]
        key_heads = head_parts(keys)
        mask = pair_mask(row_ref, col_ref, q_at, k_at, bk, bq)
        dk = dk_s[here, :]
        dv = dv_s[here, :]
        for h in range(HG):
            scores = nt_dot(keys, q_heads[h]) * (SCORE_SCALE * LOG2E)
            scores = jnp.where(mask, scores - lse[h], NEGATIVE)
            soft = jnp.exp2(scores)
            g_soft = nt_dot(values, g_heads[h])
            g_scores = (soft * (g_soft - row_dot[h])).astype(BF)
            dv = dv + dot(soft.astype(BF), g_heads[h])
            dk = dk + dot(g_scores, q_heads[h])
            dq = dq + tn_dot(g_scores, key_heads[h])
        dk_s[here, :] = dk
        dv_s[here, :] = dv
        return dq

    dq = lax.fori_loop(first_ref[i], i + 1, step, jnp.zeros((bq, GW), F32))
    dx_ref[pl.ds(q_at, bq), 0:GW] = (dq * SCORE_SCALE).astype(BF)

    @pl.when(i == pl.num_programs(0) - 1)
    def _():
        dx_ref[:, GW : 2 * GW] = (dk_s[...] * SCORE_SCALE).astype(BF)
        dx_ref[:, 2 * GW : 3 * GW] = dv_s[...].astype(BF)
        for s in range(sends):
            at = pl.ds(pl.multiple_of((me ^ s) * rows, rows), rows)
            out_pieces[s][...] = dx_ref[at, :]
        if stacked:
            half = rows // 2
            for b in range(count):
                at = b * rows
                stack_ref[b, :, 0 : 3 * GW] = dx_ref[at : at + half, :]
                stack_ref[b, :, 3 * GW : 6 * GW] = dx_ref[at + half : at + rows, :]


def attend(ids, meta, pieces, columns, bq, stacked=False):
    first, row_info, col_info = meta
    rows, width = pieces[0].shape
    count = len(pieces)
    sends = 0 if stacked else min(count, 2 * GROUPS)
    length = rows * count
    operands = [first, row_info] + ([] if col_info is None else [col_info])
    operands += list(pieces) + [columns]
    outs = [sds((rows, GW), BF)] * sends
    outs += [sds((count, rows // 2, 2 * GW), BF)] if stacked else []
    outs += [
        sds((length, GW), BF),
        sds((8, length), F32),
        sds((length, 3 * GW), BF),
    ]
    got = stage(
        partial(attend_kernel, bq, count, sends, stacked, col_info is not None),
        "attend",
        ids,
        operands,
        outs,
        [pltpu.VMEM((length, GW), BF)] * 2 + [pltpu.VMEM((GW, length), BF)],
        flops=length * length * GW * 2 + 6 * length * width * GW,
        grid=(length // bq,),
        specs={0: pl.BlockSpec(memory_space=pltpu.SMEM)},
    )
    return got[:-3], got[-3:]


def attend_back(ids, meta, kept, grads, bq, stacked=False):
    first, row_info, col_info = meta
    attended, lse, x = kept
    count = grads[0].shape[0] if stacked else len(grads)
    rows = attended.shape[0] // count
    sends = 0 if stacked else min(count, 2 * GROUPS)
    length = rows * count
    operands = [first, row_info] + ([] if col_info is None else [col_info])
    operands += [x] + list(grads) + [attended, lse]
    got = stage(
        partial(attend_back_kernel, bq, count, sends, stacked, col_info is not None),
        "attend_back",
        ids,
        operands,
        [sds((rows, 3 * GW), BF)] * sends
        + ([sds((count, rows // 2, 6 * GW), BF)] if stacked else [])
        + [sds(x.shape, BF)],
        [pltpu.VMEM((length, GW), BF)] * 3 + [pltpu.VMEM((length, GW), F32)] * 2,
        flops=length * length * GW * 5,
        grid=(length // bq,),
        specs={0: pl.BlockSpec(memory_space=pltpu.SMEM)},
    )
    return got[:-1], got[-1]


def project_grads_kernel(count, ids, dx_ref, *rest):
    pieces, (keep, send, total) = rest[:count], rest[count:]
    rows = pieces[0].shape[0]
    for s, piece in enumerate(pieces):
        at = pl.ds(pl.multiple_of((ids[0] ^ s) * rows, rows), rows)
        term = tn_dot(piece[...], dx_ref[at, :])
        total[...] = term if s == 0 else total[...] + term
    split_rows(ids[0], total, keep, send)


def project_grads(ids, wide_count, pieces, dx):
    rows, width = pieces[0].shape
    shape = (wide_count // 2, width // wide_count, 3 * GW)
    return stage(
        partial(project_grads_kernel, len(pieces)),
        "project_grads",
        ids,
        [dx] + list(pieces),
        [sds(shape, BF)] * 2,
        [pltpu.VMEM((width, 3 * GW), F32)],
        flops=6 * dx.size * width // 3,
    )


def group_columns_kernel(ids, project, out):
    group, _ = combo(ids[0])
    width = GROUPS * GW
    for c in range(GROUPS):

        @pl.when(group == c)
        def _():
            for t in range(3):
                at = t * width + c * GW
                out[:, t * GW : (t + 1) * GW] = project[:, at : at + GW]


def group_columns(ids, project):
    (out,) = stage(
        group_columns_kernel,
        "group_columns",
        ids,
        [project],
        [sds((project.shape[0], 3 * GW), BF)],
    )
    return out


def save_halves(me, normed, mine_ref, other_ref):
    rows = mine_ref.shape[0]
    core = lax.rem(me, 2)
    mine_ref[...] = normed[pl.ds(pl.multiple_of(core * rows, rows), rows), :]
    other_ref[...] = normed[pl.ds(pl.multiple_of((1 - core) * rows, rows), rows), :]


def routed_pre_kernel(count, ids, tok, sel, *rest):
    vectors, rest = rest[:count], rest[count:]
    mine_ref, other_ref, one_hot_ref, picked_ref, vecs, normed = rest
    rows = [vector[...].astype(F32).reshape(1, -1) for vector in vectors]
    rows.append(jnp.zeros((8 - count, tok.shape[1]), F32))
    vecs[...] = jnp.concatenate(rows, axis=0)
    span = one_hot_ref.shape[1]
    seqs = sel.shape[0]
    if sel.shape[1] != span:
        sel = sel[:, pl.ds(pl.multiple_of(ids[0] * span, span), span)]
    slots = span // 4
    upper = (
        lax.broadcasted_iota(jnp.int32, (span, span), 0)
        <= lax.broadcasted_iota(jnp.int32, (span, span), 1)
    ).astype(F32).astype(BF)
    slot = lax.broadcasted_iota(jnp.int32, (slots, span), 0).astype(F32)
    for q in range(seqs):
        chosen = jnp.broadcast_to(sel[q : q + 1, :].astype(F32), (8, span))
        rank = dot(chosen.astype(BF), upper)[0:1, :] * chosen[0:1, :] - 1.0
        one_hot = (slot == rank).astype(F32).astype(BF)
        one_hot_ref[q * slots : (q + 1) * slots, :] = one_hot
        picked_ref[q * slots : (q + 1) * slots, :] = dot(
            one_hot, tok[q * span : (q + 1) * span, :]
        ).astype(BF)
    picked = picked_ref[...].astype(F32)
    normed[...] = (picked * norm_scale(picked) * gain_of(vecs, 1)).astype(BF)
    save_halves(ids[0], normed, mine_ref, other_ref)


def gain_of(vecs, k):
    return vecs[k : k + 1, :]


def routed_pre(ids, tok, sel, span, vectors):
    rows, width = tok.shape[0] // 4, tok.shape[1]
    return stage(
        partial(routed_pre_kernel, len(vectors)),
        "routed_pre",
        ids,
        [tok, sel] + vectors,
        [
            sds((rows // 2, width), BF),
            sds((rows // 2, width), BF),
            sds((rows, span), BF),
            sds((rows, width), BF),
            sds((8, width), F32),
        ],
        [pltpu.VMEM((rows, width), BF)],
        flops=4 * rows * width * span,
    )


def routed_mid_kernel(count, ids, *rest):
    pieces = rest[:count]
    output, picked, vecs, branch_ref, low_ref, att_ref, parts = rest[count:]
    attended = load_pieces(ids[0], pieces, parts, 1)
    att_ref[...] = attended
    branch = dot(attended, output[...])
    branch_ref[...] = branch
    middle = picked[...].astype(F32) + branch
    low_ref[...] = (middle * norm_scale(middle) * gain_of(vecs, 2)).astype(BF)


def routed_mid(ids, pieces, output, picked, vecs):
    shape = picked.shape
    return stage(
        partial(routed_mid_kernel, len(pieces)),
        "routed_mid",
        ids,
        list(pieces) + [output, picked, vecs],
        [sds(shape, F32), sds(shape, BF), sds(shape, BF)],
        [pltpu.VMEM((GROUPS, shape[0], GW), BF)],
        flops=2 * shape[0] * shape[1] * shape[1],
    )


def hidden_forward_kernel(count, ids, *rest):
    pieces = rest[:count]
    expand, reduce_ref = rest[count : count + 2]
    outs = rest[count + 2 :]
    rows = pieces[0].shape[0]
    low = jnp.concatenate([piece[...] for piece in pieces], axis=0)
    hidden = gelu(dot(low, expand[...])).astype(BF)
    total = dot(hidden, reduce_ref[...]).astype(BF)
    for s, out in enumerate(outs):
        out[...] = total[s * rows : (s + 1) * rows, :]


def hidden_forward(ids, pieces, expand, reduce_part):
    return stage(
        partial(hidden_forward_kernel, len(pieces)),
        "hidden_forward",
        ids,
        list(pieces) + [expand, reduce_part],
        [sds(pieces[0].shape, BF)] * len(pieces),
        flops=4 * len(pieces) * pieces[0].size * expand.shape[1],
    )


def dense_pre_kernel(shares, ids, tok, one_hot, picked, vecs, branch, *rest):
    partials = rest[:shares]
    mine_ref, other_ref, mixed_ref, delta_ref, normed = rest[shares:]
    slots, span = one_hot.shape[0] // 2, one_hot.shape[1]
    delta = branch[...]
    for share in partials:
        delta = delta + share[...].astype(F32)
    delta_ref[...] = delta
    gate = jnp.sum(picked[...].astype(F32) * gain_of(vecs, 0), axis=-1, keepdims=True)
    lifted = gate * delta
    for q in range(2):
        at, spots = slice(q * span, (q + 1) * span), slice(q * slots, (q + 1) * slots)
        mixed = tok[at, :].astype(F32) + place(one_hot[spots, :], lifted[spots, :])
        mixed_ref[at, :] = mixed
        normed[at, :] = (mixed * norm_scale(mixed) * gain_of(vecs, 3)).astype(BF)
    save_halves(ids[0], normed, mine_ref, other_ref)


def dense_pre(ids, tok, one_hot, picked, vecs, branch, partials):
    rows, width = tok.shape
    return stage(
        partial(dense_pre_kernel, len(partials)),
        "dense_pre",
        ids,
        [tok, one_hot, picked, vecs, branch] + list(partials),
        [
            sds((rows // 2, width), BF),
            sds((rows // 2, width), BF),
            sds(tok.shape, F32),
            sds(picked.shape, F32),
        ],
        [pltpu.VMEM((rows, width), BF)],
        flops=6 * rows * width * one_hot.shape[0],
    )


def this_part(me, weights, scratch):
    if not scratch:
        return weights[0][0], weights[1][0]
    e_s, r_s = scratch
    chips, rows = weights[0].shape[0], weights[0].shape[3]
    core = lax.rem(me, 2)
    for c in range(chips):
        for weight, at in ((weights[0], 2 * c + core), (weights[1], 2 * c + 1 - core)):
            at = pl.ds(pl.multiple_of(at * rows, rows), rows)
            e_s[at, :] = weight[c, 0, 0]
            r_s[at, :] = weight[c, 0, 1]
    return e_s[...], r_s[...]


def part_specs(base, weights):
    if weights[0].ndim == 3:
        return {
            base + k: pl.BlockSpec((1,) + w.shape[1:], lambda n: (n, 0, 0))
            for k, w in enumerate(weights)
        }
    return {
        base + k: pl.BlockSpec(
            (w.shape[0], 1) + w.shape[2:], lambda n: (0, n, 0, 0, 0)
        )
        for k, w in enumerate(weights)
    }


def part_scratch(width, weights):
    if weights[0].ndim == 3:
        return []
    return [pltpu.VMEM((width, weights[0].shape[-1]), BF)] * 2


def dense_ffn_kernel(split, ids, stack, *rest):
    output, mixed, cot, vecs = rest[:4]
    gain = gain_of(vecs, 4)
    rest = rest[4:]
    weights, rest = rest[:split], rest[split:]
    act_ref, low_ref, back_ref, sum_ref, att_ref, gain_ref = rest[:6]
    g_stack, rest = rest[6], rest[7:]
    parts, branch_s, delta_s, grad_s = rest[:4]
    n = pl.program_id(0)
    me = ids[0]

    @pl.when(n == 0)
    def _():
        attended = load_stack(me, stack, parts, 1)
        att_ref[...] = attended
        branch = dot(attended, output[...])
        branch_s[...] = branch
        middle = mixed[...] + branch
        low_ref[...] = (middle * norm_scale(middle) * gain).astype(BF)
        delta_s[...] = jnp.zeros_like(delta_s)
        grad_s[...] = jnp.zeros_like(grad_s)

    expand, reduce_w = this_part(me, weights, rest[4:])
    value, slope = gelu_both(dot(low_ref[...], expand))
    delta_s[...] += dot(value.astype(BF), reduce_w)
    grad_pre = (nt_dot(cot[...], reduce_w) * slope).astype(BF)
    grad_s[...] += nt_dot(grad_pre, expand)

    @pl.when(n == pl.num_programs(0) - 1)
    def _():
        middle = mixed[...] + branch_s[...]
        act_ref[...] = (middle + delta_s[...]).astype(BF)
        grad_middle, gain_grad = norm_back(grad_s[...], middle, gain)
        gain_ref[...] = jnp.broadcast_to(gain_grad, gain_ref.shape)
        total = cot[...].astype(F32) + grad_middle
        sum_ref[...] = total
        back = total.astype(BF)
        back_ref[...] = back
        save_stack(nt_dot(back, output[...]).astype(BF), parts, g_stack)


def dense_ffn(ids, stack, output, mixed, cot, vecs, weights):
    rows, width = mixed.shape
    split = len(weights)
    parts_n = weights[0].shape[0 if weights[0].ndim == 3 else 1]
    hidden = weights[0].shape[-1]
    base = 5
    specs = part_specs(base, weights)
    scratch = [pltpu.VMEM((GROUPS, rows, GW), BF)] + [pltpu.VMEM((rows, width), F32)] * 3
    scratch += part_scratch(width, weights)
    outs = [
        sds((rows, width), BF),
        sds((rows, width), BF),
        sds((rows, width), BF),
        sds((rows, width), F32),
        sds((rows, width), BF),
        sds((8, width), F32),
        sds(stack.shape, BF),
    ]
    got = stage(
        partial(dense_ffn_kernel, split),
        "dense_ffn",
        ids,
        [stack, output, mixed, cot, vecs] + list(weights),
        outs,
        scratch,
        flops=8 * rows * width * hidden * parts_n + 4 * rows * width * width,
        grid=(parts_n,),
        specs=specs,
    )
    return got[:6], got[6]


def dense_post_kernel(ids, stack, *rest):
    project, vecs, mixed, total, one_hot, picked, delta = rest[:7]
    g_mixed_ref, g_delta_ref, g_low_ref, g_gate_ref, router_ref, parts = rest[7:]
    g_proj = load_stack(ids[0], stack, parts, 3)
    grad_rows, _ = norm_back(nt_dot(g_proj, project[...]), mixed[...], gain_of(vecs, 3))
    g_mixed_ref[...] = total[...] + grad_rows
    slots, span = one_hot.shape[0] // 2, one_hot.shape[1]
    rows = picked[...].astype(F32)
    gate = jnp.sum(rows * gain_of(vecs, 0), axis=-1, keepdims=True)
    router = jnp.zeros((1, rows.shape[1]), F32)
    for q in range(2):
        at, spots = slice(q * span, (q + 1) * span), slice(q * slots, (q + 1) * slots)
        lifted = pick(one_hot[spots, :], g_mixed_ref[at, :])
        g_delta = gate[spots, :] * lifted
        g_delta_ref[spots, :] = g_delta
        g_low_ref[spots, :] = g_delta.astype(BF)
        g_gate = jnp.sum(lifted * delta[spots, :], axis=-1, keepdims=True)
        g_gate_ref[spots, :] = jnp.broadcast_to(g_gate, (slots, g_gate_ref.shape[1]))
        router = router + jnp.sum(rows[spots, :] * g_gate, axis=0, keepdims=True)
    router_ref[...] = jnp.broadcast_to(router, router_ref.shape)


def dense_post(ids, stack, project, vecs, mixed, total, one_hot, picked, delta):
    rows, width = mixed.shape
    return stage(
        dense_post_kernel,
        "dense_post",
        ids,
        [stack, project, vecs, mixed, total, one_hot, picked, delta],
        [
            sds((rows, width), F32),
            sds(picked.shape, F32),
            sds(picked.shape, BF),
            sds((picked.shape[0], 128), F32),
            sds((8, width), F32),
        ],
        [pltpu.VMEM((GROUPS, rows, 3 * GW), BF)],
        flops=6 * rows * width * width,
    )


def routed_back_kernel(split, ids, low, g_low, branch, picked, vecs, g_delta, output, *rest):
    weights, rest = rest[:split], rest[split:]
    g_mid_ref, back_ref, gain_ref, stack, parts, grad_s = rest[:6]
    n = pl.program_id(0)

    @pl.when(n == 0)
    def _():
        grad_s[...] = jnp.zeros_like(grad_s)

    expand, reduce_w = this_part(ids[0], weights, rest[6:])
    _, slope = gelu_both(dot(low[...], expand))
    grad_pre = (nt_dot(g_low[...], reduce_w) * slope).astype(BF)
    grad_s[...] += nt_dot(grad_pre, expand)

    @pl.when(n == pl.num_programs(0) - 1)
    def _():
        middle = picked[...].astype(F32) + branch[...]
        g_middle, gain_grad = norm_back(grad_s[...], middle, gain_of(vecs, 2))
        gain_ref[...] = jnp.broadcast_to(gain_grad, gain_ref.shape)
        g_mid_ref[...] = g_middle
        back = (g_delta[...] + g_middle).astype(BF)
        back_ref[...] = back
        save_stack(nt_dot(back, output[...]).astype(BF), parts, stack)


def routed_back(ids, wide_count, low, g_low, branch, picked, vecs, g_delta, output, weights):
    rows, width = branch.shape
    parts_n = weights[0].shape[0 if weights[0].ndim == 3 else 1]
    return stage(
        partial(routed_back_kernel, len(weights)),
        "routed_back",
        ids,
        [low, g_low, branch, picked, vecs, g_delta, output] + list(weights),
        [
            sds((rows, width), F32),
            sds((rows, width), BF),
            sds((8, width), F32),
            sds((wide_count, rows // 4, 2 * GW), BF),
        ],
        [pltpu.VMEM((GROUPS, rows, GW), BF), pltpu.VMEM((rows, width), F32)]
        + part_scratch(width, weights),
        flops=6 * rows * width * parts_n * weights[0].shape[-1],
        grid=(parts_n,),
        specs=part_specs(7, weights),
    )


def routed_post_kernel(ids, stack, *rest):
    project, vecs, picked, g_mid, g_mixed, one_hot, g_gate = rest[:7]
    out_ref, parts = rest[7:]
    g_proj = load_stack(ids[0], stack, parts, 3)
    rows = picked[...].astype(F32)
    grad_rows, _ = norm_back(nt_dot(g_proj, project[...]), rows, gain_of(vecs, 1))
    spread = g_mid[...] + grad_rows + g_gate[:, 0:1] * gain_of(vecs, 0)
    slots, span = one_hot.shape[0] // 2, one_hot.shape[1]
    for q in range(2):
        at, spots = slice(q * span, (q + 1) * span), slice(q * slots, (q + 1) * slots)
        out_ref[at, :] = g_mixed[at, :] + place(one_hot[spots, :], spread[spots, :])


def routed_post(ids, stack, project, vecs, picked, g_mid, g_mixed, one_hot, g_gate):
    rows, width = picked.shape
    (out,) = stage(
        routed_post_kernel,
        "routed_post",
        ids,
        [stack, project, vecs, picked, g_mid, g_mixed, one_hot, g_gate],
        [sds(g_mixed.shape, F32)],
        [pltpu.VMEM((GROUPS, rows, 3 * GW), BF)],
        flops=6 * rows * width * width,
    )
    return out


def split_rows(me, total, keep, send):
    chips, rows = keep.shape[0], keep.shape[1]
    core = lax.rem(me, 2)
    for c in range(chips):
        mine = pl.multiple_of((2 * c + core) * rows, rows)
        other = pl.multiple_of((2 * c + 1 - core) * rows, rows)
        keep[c] = total[pl.ds(mine, rows), :].astype(BF)
        send[c] = total[pl.ds(other, rows), :].astype(BF)


def hidden_grads_kernel(spans, ids, *rest):
    count = len(spans)
    grads, rest = rest[:count], rest[count:]
    lows, (expand, reduce_ref, out, total) = rest[:-4], rest[-4:]
    hidden = expand.shape[1]
    for k, (step, low_at, rows, whole) in enumerate(spans):
        grad = grads[k][...]
        if len(lows) == count:
            low = lows[k][...]
        else:
            at = pl.multiple_of((ids[1] ^ step) * whole + low_at, rows)
            low = lows[0][pl.ds(at, rows), :]
        value, slope = gelu_both(dot(low, expand[...]))
        grad_pre = (nt_dot(grad, reduce_ref[...]) * slope).astype(BF)
        e_term = tn_dot(low, grad_pre)
        r_term = tn_dot(grad, value.astype(BF))
        if k:
            e_term, r_term = total[:, 0:hidden] + e_term, total[:, hidden:] + r_term
        if k < count - 1:
            total[:, 0:hidden] = e_term
            total[:, hidden:] = r_term
        else:
            out[:, 0:hidden] = e_term.astype(BF)
            out[:, hidden:] = r_term.astype(BF)


def hidden_grads(ids, lows, grads, expand, reduce_part, halved=None):
    width, hidden = expand.shape
    whole_rows = grads[0].shape[0]
    spans, flat = [], []
    for step, grad in enumerate(grads):
        low_at = 0
        for part in grad if step == halved else [grad]:
            spans.append((step, low_at, part.shape[0], whole_rows))
            flat.append(part)
            low_at += part.shape[0]
    (out,) = stage(
        partial(hidden_grads_kernel, spans),
        "hidden_grads",
        ids,
        flat + list(lows) + [expand, reduce_part],
        [sds((width, 2 * hidden), BF)],
        [pltpu.VMEM((width, 2 * hidden), F32)],
        flops=8 * len(grads) * grads[0].size * hidden,
    )
    return out


def output_grads_kernel(vectors, ids, att, back, *rest):
    rest = list(rest)
    vecs, rest = rest[:vectors], rest[vectors:]
    keep, send, total = rest
    width = att.shape[1]
    total[:, 0:width] = tn_dot(att[...], back[...])
    if vectors:
        rows = [vec[0:1, :] for vec in vecs]
        rows.append(jnp.zeros((128 - vectors, width), F32))
        total[:, width : width + 128] = jnp.concatenate(rows, axis=0).T
    split_rows(ids[0], total, keep, send)


def output_grads(ids, wide_count, att, back, vecs):
    rows, width = att.shape
    columns = width + (128 if vecs else 0)
    shape = (wide_count // 2, width // wide_count, columns)
    return stage(
        partial(output_grads_kernel, len(vecs)),
        "output_grads",
        ids,
        [att, back] + list(vecs),
        [sds(shape, BF), sds(shape, BF)],
        [pltpu.VMEM((width, columns), F32)],
        flops=3 * rows * width * width,
    )


def join_kernel(pairs, ids, *rest):
    keeps, cames, outs = rest[:pairs], rest[pairs : 2 * pairs], rest[2 * pairs :]
    chip = lax.div(ids[0], 2)
    for s, out in enumerate(outs):
        low = 0
        for keep, came in zip(keeps, cames):
            columns = keep.shape[2]
            total = keep[chip ^ s].astype(F32) + came[chip ^ s].astype(F32)
            out[:, low : low + columns] = total.astype(BF)
            low += columns


def join_chips(ids, keeps, cames):
    chips, rows = keeps[0].shape[:2]
    columns = sum(keep.shape[2] for keep in keeps)
    return stage(
        partial(join_kernel, len(keeps)),
        "join",
        ids,
        list(keeps) + list(cames),
        [sds((rows, columns), BF)] * chips,
    )


def chips_return(parts):
    return [parts[0]] + [chip_step(parts[s], s) for s in range(1, len(parts))]


def sum_terms(terms):
    total = terms[0].astype(F32)
    for term in terms[1:]:
        total = total + term.astype(F32)
    return total


def sum_split_kernel(count, ids, *rest):
    terms, outs, total = rest[:count], rest[count:-1], rest[-1]
    got = terms[0][...].astype(F32)
    for term in terms[1:]:
        got = got + term[...].astype(F32)
    total[...] = got
    rows = outs[0].shape[0]
    for s, out in enumerate(outs):
        at = pl.multiple_of((ids[1] ^ s) * rows, rows)
        out[...] = total[pl.ds(at, rows), :].astype(BF)


def sum_kernel(ids, *rest):
    got = rest[0][...].astype(F32)
    for term in rest[1:-1]:
        got = got + term[...].astype(F32)
    rest[-1][...] = got.astype(BF)


def gather_out_kernel(count, vectors, ids, *rest):
    pieces, outs = rest[:count], rest[count : -1 - vectors]
    vecs, wide_s = rest[-1 - vectors : -1], rest[-1]
    rows = pieces[0].shape[0]
    for s, piece in enumerate(pieces):
        at = pl.ds(pl.multiple_of((ids[1] ^ s) * rows, rows), rows)
        low = 0
        for out in outs:
            columns = out.shape[1]
            out[at, :] = piece[:, low : low + columns].astype(F32)
            low += columns
        wide_s[at, :] = piece[:, low:].astype(F32)
    turned = wide_s[...].T
    for k, vec in enumerate(vecs):
        vec[...] = turned[k : k + 1, :].reshape(vec.shape[0])


def narrow_terms(ids, terms):
    narrow_count = lax.axis_size("narrow")
    rows, columns = terms[0].shape
    if rows % (8 * narrow_count):
        return [sum_terms(terms).astype(BF)]
    return stage(
        partial(sum_split_kernel, len(terms)),
        "sum_split",
        ids,
        terms,
        [sds((rows // narrow_count, columns), BF)] * narrow_count,
        [pltpu.VMEM((rows, columns), F32)],
    )


def sum_narrow(ids, parts, first):
    if len(parts) == 1:
        return lax.psum(parts[0], "narrow")
    return sum_parts(ids, tie(narrow_return(parts), first))


def spread_narrow(ids, total, rows, widths, vectors):
    narrow_count = lax.axis_size("narrow")
    if total.shape[0] == rows:
        total = total.astype(F32)
        outs, low = [], 0
        for size in widths:
            outs.append(total[:, low : low + size])
            low += size
        return outs[:-1] + [outs[-1][:, k] for k in range(vectors)]
    return stage(
        partial(gather_out_kernel, narrow_count, vectors),
        "gather_out",
        ids,
        narrow_gather(total),
        [sds((rows, size), F32) for size in widths[:-1]] + [sds((rows,), F32)] * vectors,
        [pltpu.VMEM((rows, widths[-1]), F32)],
    )


def join_narrow_kernel(turned, ids, keep, came, *outs):
    each = outs[0].shape[0]
    turn = lax.div(ids[0], 2) if turned else 0
    for t, out in enumerate(outs):
        for j in range(each):
            at = ((ids[1] ^ t) * each + j) ^ turn
            out[j] = (keep[at].astype(F32) + came[at].astype(F32)).astype(BF)


def route_kernel(count, ids, *rest):
    pieces, outs, blocks = rest[:count], rest[count:-1], rest[-1]
    each = pieces[0].shape[0]
    for t, piece in enumerate(pieces):
        for j in range(each):
            blocks[(ids[1] ^ t) * each + j] = piece[j]
    chip = lax.div(ids[0], 2)
    for s, out in enumerate(outs):
        out[...] = blocks[chip ^ s]


def unpack_kernel(turned, ids, *rest):
    pieces, (own, gain, out, gain_out, parts) = rest[:GROUPS], rest[GROUPS:]
    at = lax.div(ids[0], 2)
    if turned:
        at = at ^ ids[1]
    rows = out.shape[0]
    for s, piece in enumerate(pieces):
        parts[lax.rem(at ^ s, GROUPS)] = piece[...].astype(F32)
    total = jnp.zeros((rows, GW), F32)
    for t in range(3):
        for c in range(GROUPS):
            low = (t * GROUPS + c) * GW
            part = parts[c, :, t * GW : (t + 1) * GW]
            out[:, low : low + GW] = part
            total = total + part * own[:, low : low + GW].astype(F32)
    sums = jnp.broadcast_to(jnp.sum(total, axis=1, keepdims=True), (rows, 128)).T
    gain_out[...] = (sums[0:1, :] / gain[...]).reshape(rows)


def unpack(ids, pieces, own, gain):
    rows, columns = pieces[0].shape
    return stage(
        partial(unpack_kernel, direct_delivery()),
        "unpack",
        ids,
        list(pieces) + [own, gain],
        [sds((rows, GROUPS * columns), F32), sds((rows,), F32)],
        [pltpu.VMEM((GROUPS, rows, columns), F32)],
    )


def split_narrow(ids, keep, came):
    narrow_count = lax.axis_size("narrow")
    chips, rows, columns = keep.shape
    shape = (chips // narrow_count, rows, columns)
    return stage(
        partial(join_narrow_kernel, direct_delivery()),
        "join_narrow",
        ids,
        [keep, came],
        [sds(shape, BF)] * narrow_count,
    )


def sum_parts(ids, terms):
    (total,) = stage(sum_kernel, "sum_terms", ids, terms, [sds(terms[0].shape, BF)])
    return total


def route_project(ids, gathered, chips):
    rows, columns = gathered[0].shape[1:]
    return stage(
        partial(route_kernel, len(gathered)),
        "route",
        ids,
        gathered,
        [sds((rows, columns), BF)] * GROUPS,
        [pltpu.VMEM((chips, rows, columns), BF)],
    )


def direct_delivery():
    return lax.axis_size("narrow") == GROUPS and lax.axis_size("wide") == 2 * GROUPS


def deliver(ids, total, chips):
    narrow_count = lax.axis_size("narrow")
    if not direct_delivery():
        return chips_return(route_project(ids, narrow_gather(total), chips))
    total = total[0]

    def moves(k):
        pairs = []
        for chip in range(chips):
            for core in range(2):
                for n in range(narrow_count):
                    to = (2 * (chip ^ n) + core) * narrow_count + (n ^ k)
                    pairs.append(((2 * chip + core) * narrow_count + n, to))
        return pairs

    return [lax.ppermute(total, ("wide", "narrow"), moves(k)) for k in range(narrow_count)]


def finish_hidden_kernel(ids, dense, routed, e_d, r_d, e_r, r_r):
    hidden = e_d.shape[1]
    for total, e_ref, r_ref in ((dense, e_d, r_d), (routed, e_r, r_r)):
        e_ref[...] = total[:, 0:hidden].astype(F32)
        r_ref[...] = total[:, hidden : 2 * hidden].astype(F32)


def finish_hidden(ids, dense, routed):
    rows, columns = dense.shape
    return stage(
        finish_hidden_kernel,
        "finish_hidden",
        ids,
        [dense, routed],
        [sds((rows, columns // 2), F32)] * 4,
    )


def tie(x, *first):
    return lax.optimization_barrier((x, first))[0]


def narrow_step(x, s):
    return lax.ppermute(x, "narrow", [(j, j ^ s) for j in range(lax.axis_size("narrow"))])


def narrow_gather(x):
    return [x] + [narrow_step(x, s) for s in range(1, lax.axis_size("narrow"))]


def narrow_return(parts):
    return [parts[0]] + [narrow_step(parts[s], s) for s in range(1, len(parts))]


def exchange(pieces):
    wide_count = lax.axis_size("wide")
    return [pieces[0]] + [
        lax.ppermute(pieces[s], "wide", [(j, j ^ s) for j in range(wide_count)])
        for s in range(1, len(pieces))
    ]


def exchange_rows(mine, other):
    wide_count = lax.axis_size("wide")
    if wide_count != 8:
        return exchange([mine, other] * (wide_count // 2))
    beside = core_step(other)
    from_x = [chip_step(mine, 1), chip_step(beside, 1)]
    from_y = [chip_step(mine, 2), chip_step(beside, 2)]
    corner = [chip_step(from_y[0], 1), chip_step(from_x[1], 2)]
    return [mine, beside] + from_x + from_y + corner


def hidden_share(expand, reduce_part):
    wide_count = lax.axis_size("wide")
    here = lax.axis_index("wide")
    width, hidden = expand.shape
    rows = width // wide_count
    if width != hidden or rows % 16:
        return None
    return jnp.stack(
        [
            lax.dynamic_slice_in_dim(expand, here * rows, rows, 0),
            lax.dynamic_slice_in_dim(reduce_part, here * rows, rows, 0),
        ]
    )


def all_chips(x):
    groups = [list(range(core, lax.axis_size("wide"), 2)) for core in range(2)]
    return lax.all_gather(x, "wide", axis=0, axis_index_groups=groups)


def chip_step(x, s):
    return lax.ppermute(
        x, "wide", [(j, j ^ (2 * s)) for j in range(lax.axis_size("wide"))]
    )


def core_step(x):
    return lax.ppermute(x, "wide", [(j, j ^ 1) for j in range(lax.axis_size("wide"))])


def on_device(
    tokens,
    cotangent,
    selected,
    segments,
    router_vector,
    project_routed,
    output_routed,
    prenorm_routed,
    midnorm_routed,
    expand_routed,
    reduce_routed,
    project_dense,
    output_dense,
    prenorm_dense,
    midnorm_dense,
    expand_dense,
    reduce_dense,
):
    seq_count, span_rows, width = tokens.shape
    row_length = selected.shape[1]
    hidden = expand_dense.shape[1]
    wide_count = lax.axis_size("wide")
    narrow_count = lax.axis_size("narrow")
    here = lax.axis_index("wide")
    slot_count = span_rows // 4
    bq_dense = min(256, row_length)
    bq_routed = min(256, slot_count * wide_count)
    ids = jnp.stack([here, lax.axis_index("narrow")]).astype(jnp.int32)
    tok = tokens.reshape(-1, width)
    cot = cotangent.reshape(-1, width)

    share_d = hidden_share(expand_dense, reduce_dense)
    staged = share_d is not None
    if staged:
        own_d = lax.all_gather(share_d, "narrow", axis=0)

    mine = here % seq_count
    seq_segments = lax.dynamic_slice_in_dim(segments, mine, 1, 0)[0]
    seq_selected = lax.dynamic_slice_in_dim(selected, mine, 1, 0)[0].reshape(wide_count, span_rows)
    upper = (
        lax.broadcasted_iota(jnp.int32, (span_rows, span_rows), 0)
        <= lax.broadcasted_iota(jnp.int32, (span_rows, span_rows), 1)
    ).astype(BF)
    slots = jnp.arange(slot_count, dtype=jnp.int32)
    seq_rank = jnp.dot(seq_selected.astype(BF), upper, preferred_element_type=F32)
    seq_rank = jnp.where(seq_selected > 0, seq_rank.astype(jnp.int32) - 1, -1)
    slot_segments = (
        jnp.sum(
            jnp.where(
                seq_rank[:, None, :] == slots[None, :, None],
                seq_segments.reshape(wide_count, 1, span_rows) + 1,
                0,
            ),
            axis=-1,
        )
        - 1
    ).reshape(-1)
    meta_routed = (
        jnp.zeros((slot_segments.shape[0] // bq_routed,), jnp.int32),
        jnp.broadcast_to(slot_segments[None], (8, slot_segments.shape[0])),
        slot_segments[:, None],
    )
    own_selected = selected
    if span_rows % 128:
        own_selected = lax.dynamic_slice_in_dim(selected, here * span_rows, span_rows, 1)
    mine_r, other_r, one_hot, picked, vecs = routed_pre(
        ids,
        tok,
        own_selected,
        span_rows,
        [router_vector, prenorm_routed, midnorm_routed, prenorm_dense, midnorm_dense],
    )
    columns_r = group_columns(ids, tie(project_routed, mine_r))
    rows_r = exchange([mine_r, other_r] * (wide_count // 2))
    rows_r, meta_routed = lax.optimization_barrier((rows_r, meta_routed))
    pieces, kept_r = attend(ids, meta_routed, rows_r, columns_r, bq_routed)
    pieces = exchange(pieces)
    if staged:
        pieces, own_d = lax.optimization_barrier((pieces, own_d))
        chips_d = all_chips(own_d)
    branch_r, low_r, att_r = routed_mid(ids, pieces, output_routed, picked, vecs)
    dense_segments = tie(seq_segments, low_r)
    starts = sum(
        jnp.where(dense_segments == value, jnp.sum((dense_segments < value).astype(jnp.int32)), 0)
        for value in range(1, 4)
    )
    meta_dense = (
        starts[::bq_dense] // bq_dense,
        jnp.broadcast_to(starts[None], (8, row_length)),
        None,
    )

    own_at = here * (width // wide_count)

    def own_slice(x):
        return lax.dynamic_slice_in_dim(tie(x, low_r), own_at, width // wide_count, 0)

    own_rows = (
        own_slice(project_routed),
        own_slice(project_dense),
        own_slice(prenorm_routed).astype(F32)[None],
        own_slice(prenorm_dense).astype(F32)[None],
    )
    columns_d = group_columns(ids, tie(project_dense, low_r))
    low_pieces, columns_d, meta_dense, own_rows = lax.optimization_barrier(
        (narrow_gather(low_r), columns_d, meta_dense, own_rows)
    )
    partials = narrow_return(hidden_forward(ids, low_pieces, expand_routed, reduce_routed))

    mine_d, other_d, mixed, delta_r = dense_pre(
        ids, tok, one_hot, picked, vecs, branch_r, partials
    )
    if staged:
        mine_d, other_d, chips_d = lax.optimization_barrier((mine_d, other_d, chips_d))
        share_r = hidden_share(tie(expand_routed, mine_d), reduce_routed)
        own_r = lax.all_gather(share_r, "narrow", axis=0)
        rows_d, own_r = lax.optimization_barrier((exchange_rows(mine_d, other_d), own_r))
        chips_r = all_chips(own_r)
        weights_d = [chips_d, core_step(chips_d)]
    else:
        rows_d = exchange_rows(mine_d, other_d)
        weights_d = [
            lax.all_gather(expand_dense, "narrow", axis=0),
            lax.all_gather(reduce_dense, "narrow", axis=0),
        ]
        weights_r = [
            lax.all_gather(expand_routed, "narrow", axis=0),
            lax.all_gather(reduce_routed, "narrow", axis=0),
        ]
    cot_halves = cot.reshape(2, -1, width)
    cot_first = tie(cot, rows_d)
    cot_pieces = [cot] + [narrow_step(cot_first, s) for s in range(1, narrow_count)]
    cot_pieces[2] = [narrow_step(tie(cot_halves[0], rows_d), 2), None]
    (stack,), kept_d = attend(ids, meta_dense, rows_d, columns_d, bq_dense, stacked=True)
    stack, weights_d, cot_pieces[1] = lax.optimization_barrier(
        (stack, weights_d, cot_pieces[1])
    )
    stack, cot_pieces[2][0], cot_pieces[3:] = lax.optimization_barrier(
        (lax.all_to_all(stack, "wide", 0, 0), cot_pieces[2][0], cot_pieces[3:])
    )
    cot_pieces[2][1] = narrow_step(tie(cot_halves[1], stack), 2)
    (activations, low_d, back_d, sum_d, att_d, mid_gain_d), stack = dense_ffn(
        ids, stack, output_dense, mixed, cot, vecs, weights_d
    )
    stack, low_d, cot_pieces = lax.optimization_barrier((stack, low_d, cot_pieces))
    if staged:
        stack, chips_r, low_d = lax.optimization_barrier((stack, chips_r, low_d))
    low_all = lax.all_gather(low_d, "narrow", axis=0, tiled=True)
    keep_d, send_d = output_grads(ids, wide_count, att_d, back_d, [])
    stack, keep_d, send_d = lax.optimization_barrier(
        (lax.all_to_all(stack, "wide", 0, 0), keep_d, send_d)
    )
    came_d = core_step(send_d)
    if staged:
        weights_r = [chips_r, core_step(chips_r)]
    (stack,), dx_d = attend_back(ids, meta_dense, kept_d, [stack], bq_dense, stacked=True)
    stack, dx_d, weights_r, came_d = lax.optimization_barrier(
        (stack, dx_d, weights_r, came_d)
    )
    stack = lax.all_to_all(stack, "wide", 0, 0)
    keep, send = project_grads(ids, wide_count, rows_d, dx_d)
    project_d_parts = split_narrow(ids, keep, core_step(send))
    hidden_d = hidden_grads(
        ids, [tie(low_all, project_d_parts)], cot_pieces, expand_dense, reduce_dense, 2
    )
    project_d = sum_parts(ids, tie(narrow_return(project_d_parts), hidden_d))
    stack, project_d, hidden_d = lax.optimization_barrier((stack, project_d, hidden_d))
    ffn_d = lax.psum_scatter(hidden_d, "wide", scatter_dimension=0, tiled=True)
    delivered_d = deliver(ids, project_d, keep.shape[0])
    g_mixed, g_delta, g_low, g_gate, router_grad = dense_post(
        ids, stack, project_dense, vecs, mixed, sum_d, one_hot, picked, delta_r
    )

    g_mid_r, back_r, mid_gain_r, stack = routed_back(
        ids,
        wide_count,
        low_r,
        g_low,
        branch_r,
        picked,
        vecs,
        g_delta,
        output_routed,
        weights_r,
    )
    stack, delivered_d, back_r = lax.optimization_barrier((stack, delivered_d, back_r))
    keep_r, send_r = output_grads(
        ids, wide_count, att_r, back_r, [mid_gain_r, mid_gain_d, router_grad]
    )
    came_r = core_step(send_r)
    g_pieces = narrow_gather(tie(g_low, keep_r))
    stack, keep_r, send_r = lax.optimization_barrier(
        (lax.all_to_all(stack, "wide", 0, 0), keep_r, send_r)
    )
    (stack,), dx_r = attend_back(ids, meta_routed, kept_r, [stack], bq_routed, stacked=True)
    stack, dx_r, g_pieces, came_r = lax.optimization_barrier((stack, dx_r, g_pieces, came_r))
    keep, send = project_grads(ids, wide_count, rows_r, dx_r)
    came = core_step(send)
    output_parts = join_chips(ids, tie([keep_d, keep_r], send), [came_d, came_r])
    hidden_r = hidden_grads(
        ids, tie(low_pieces, output_parts), g_pieces, expand_routed, reduce_routed
    )
    ffn_r = lax.psum_scatter(hidden_r, "wide", scatter_dimension=0, tiled=True)
    output_parts = narrow_terms(ids, tie(chips_return(output_parts), hidden_r))
    project_parts = split_narrow(ids, tie(keep, output_parts), came)
    stack, project_parts, output_parts = lax.optimization_barrier(
        (stack, project_parts, output_parts)
    )
    stack = lax.all_to_all(stack, "wide", 0, 0)
    returned, stack = lax.optimization_barrier((narrow_return(project_parts), stack))
    project_r = sum_parts(ids, returned)
    output_total = sum_narrow(ids, tie(output_parts, project_parts), project_r)
    stack, output_total = lax.optimization_barrier((stack, output_total))
    tokens_gradient = routed_post(
        ids, stack, project_routed, vecs, picked, g_mid_r, g_mixed, one_hot, g_gate
    )
    delivered_r = deliver(ids, project_r, keep.shape[0])
    project_d_grad, pre_gain_d = unpack(
        ids, tie(delivered_d, project_r), own_rows[1], own_rows[3]
    )
    output_d_grad, output_r_grad, mid_r_grad, mid_d_grad, router_grad = spread_narrow(
        ids, output_total, width // wide_count, [width, width, 128], 3
    )
    project_r_grad, pre_gain_r = unpack(
        ids, tie(delivered_r, tokens_gradient), own_rows[0], own_rows[2]
    )
    expand_d_grad, reduce_d_grad, expand_r_grad, reduce_r_grad = finish_hidden(
        ids, ffn_d, ffn_r
    )
    return (
        activations.reshape(tokens.shape),
        tokens_gradient.reshape(tokens.shape),
        router_grad,
        project_r_grad,
        output_r_grad,
        pre_gain_r,
        mid_r_grad,
        expand_r_grad,
        reduce_r_grad.T,
        project_d_grad,
        output_d_grad,
        pre_gain_d,
        mid_d_grad,
        expand_d_grad,
        reduce_d_grad.T,
    )


def solution(mesh):
    return jax.shard_map(
        on_device,
        mesh=mesh,
        in_specs=(
            P("narrow", "wide", None),
            P("narrow", "wide", None),
            P("narrow", None),
            P("narrow", None),
            P(),
            P(),
            P(),
            P(),
            P(),
            P(None, "narrow"),
            P("narrow", None),
            P(),
            P(),
            P(),
            P(),
            P(None, "narrow"),
            P("narrow", None),
        ),
        out_specs=(
            P("narrow", "wide", None),
            P("narrow", "wide", None),
            P("wide"),
            P("wide", None),
            P("wide", None),
            P("wide"),
            P("wide"),
            P("wide", "narrow"),
            P("narrow", "wide"),
            P("wide", None),
            P("wide", None),
            P("wide"),
            P("wide"),
            P("wide", "narrow"),
            P("narrow", "wide"),
        ),
        check_vma=False,
    )
```

```python
from functools import partial

import jax
import jax.numpy as jnp
from jax import lax
from jax.experimental import pallas as pl
from jax.experimental.pallas import tpu as pltpu
from jax.sharding import PartitionSpec as P

H = 12
HD = 64
GROUPS = 4
HG = H // GROUPS
GW = HG * HD

EPSILON = 1e-06
NEGATIVE = -1e30
SCORE_SCALE = 0.125
LOG2E = 1.4426950408889634
GELU_A = 0.7978845608028654
GELU_B = 0.044715
BF = jnp.bfloat16
F32 = jnp.float32
VMEM = 56 << 20


def nt_dot(left, right):
    return lax.dot_general(left, right, (((1,), (1,)), ((), ())), preferred_element_type=F32)


def tn_dot(left, right):
    return lax.dot_general(left, right, (((0,), (0,)), ((), ())), preferred_element_type=F32)


def dot(left, right):
    return jnp.dot(left, right, preferred_element_type=F32)


def sds(shape, dtype):
    return jax.ShapeDtypeStruct(shape, dtype)


def norm_scale(rows):
    return lax.rsqrt(jnp.mean(rows * rows, axis=-1, keepdims=True) + EPSILON)


def norm_back(grad, rows, gain):
    scale = norm_scale(rows)
    inner = grad * gain
    mean = jnp.mean(inner * rows, axis=-1, keepdims=True)
    grad_rows = scale * inner - rows * (scale * scale * scale * mean)
    return grad_rows, jnp.sum(grad * rows * scale, axis=0, keepdims=True)


def gelu(a):
    return 0.5 * a * (1.0 + jnp.tanh(GELU_A * (a + GELU_B * (a * a * a))))


def gelu_both(a):
    square = a * a
    bend = jnp.tanh(GELU_A * (a + GELU_B * (square * a)))
    half = 0.5 * (1.0 + bend)
    slope = half + 0.5 * a * (1.0 - bend * bend) * (GELU_A * (1.0 + 3.0 * GELU_B * square))
    return a * half, slope


def three_parts(x):
    first = x.astype(BF)
    rest = x - first.astype(F32)
    second = rest.astype(BF)
    third = (rest - second.astype(F32)).astype(BF)
    return [first, second, third]


def place(one_hot, x):
    return tn_dot(
        jnp.concatenate([one_hot] * 3, axis=0), jnp.concatenate(three_parts(x), axis=0)
    )


def pick(one_hot, x):
    return dot(jnp.concatenate([one_hot] * 3, axis=1), jnp.concatenate(three_parts(x), axis=0))


def combo(index):
    return lax.rem(lax.div(index, 2), GROUPS), lax.rem(index, 2)


def save_pieces(me, full, parts, pieces):
    rows = full.shape[0] // 2
    thirds = full.shape[1] // (GROUPS * GW)
    for c in range(GROUPS):
        for t in range(thirds):
            at = t * GROUPS * GW + c * GW
            parts[c, :, t * GW : (t + 1) * GW] = full[:, at : at + GW]
    for s, piece in enumerate(pieces):
        c, r = combo(me ^ s)
        piece[...] = parts[c, pl.ds(pl.multiple_of(r * rows, rows), rows), :]


def load_pieces(me, pieces, parts, thirds):
    rows = pieces[0].shape[0]
    for s, piece in enumerate(pieces):
        c, r = combo(me ^ s)
        parts[c, pl.ds(pl.multiple_of(r * rows, rows), rows), :] = piece[...]
    return jnp.concatenate(
        [parts[c, :, t * GW : (t + 1) * GW] for t in range(thirds) for c in range(GROUPS)],
        axis=1,
    )


def save_stack(full, parts, stack):
    rows = full.shape[0] // 2
    thirds = full.shape[1] // (GROUPS * GW)
    half, columns = rows // 2, thirds * GW
    for c in range(GROUPS):
        for t in range(thirds):
            at = t * GROUPS * GW + c * GW
            parts[c, :, t * GW : (t + 1) * GW] = full[:, at : at + GW]
    for b in range(stack.shape[0]):
        c, at = (b // 2) % GROUPS, (b % 2) * rows
        stack[b, :, 0:columns] = parts[c, at : at + half, :]
        stack[b, :, columns : 2 * columns] = parts[c, at + half : at + rows, :]


def load_stack(me, stack, parts, thirds):
    half, columns = stack.shape[1], stack.shape[2] // 2
    first = lax.div(me, 2 * GROUPS) * (2 * GROUPS)
    for w in range(2 * GROUPS):
        c, at = w // 2, (w % 2) * 2 * half
        parts[c, at : at + half, :] = stack[first + w, :, 0:columns]
        parts[c, at + half : at + 2 * half, :] = stack[first + w, :, columns : 2 * columns]
    return jnp.concatenate(
        [parts[c, :, t * GW : (t + 1) * GW] for t in range(thirds) for c in range(GROUPS)],
        axis=1,
    )


def stage(body, name, ids, operands, outs, scratch=(), flops=0, grid=None, specs=None):
    kwargs = {}
    if grid is not None:
        kwargs["grid"] = grid
    in_specs = [pl.BlockSpec(memory_space=pltpu.SMEM)]
    for k, operand in enumerate(operands):
        spec = None if specs is None else specs.get(k)
        if spec is None:
            zeros = (0,) * operand.ndim
            spec = pl.BlockSpec(operand.shape, lambda *_, z=zeros: z)
        in_specs.append(spec)
    out_specs = tuple(
        pl.BlockSpec(out.shape, lambda *_, z=(0,) * len(out.shape): z) for out in outs
    )
    moved = sum(a.size * a.dtype.itemsize for a in operands)
    moved += sum(math_prod(a.shape) * a.dtype.itemsize for a in outs)
    return pl.pallas_call(
        body,
        out_shape=tuple(outs),
        in_specs=in_specs,
        out_specs=out_specs,
        scratch_shapes=list(scratch),
        compiler_params=pltpu.CompilerParams(vmem_limit_bytes=VMEM),
        cost_estimate=pl.CostEstimate(flops=flops, bytes_accessed=moved, transcendentals=0),
        name=name,
        **kwargs,
    )(ids, *operands)


def math_prod(shape):
    total = 1
    for size in shape:
        total *= size
    return total


def head_parts(rows):
    lane = lax.broadcasted_iota(jnp.int32, rows.shape, 1)
    zero = jnp.zeros_like(rows)
    return [
        jnp.where((lane >= h * HD) & (lane < (h + 1) * HD), rows, zero) for h in range(HG)
    ]


def pair_mask(row_ref, col_ref, q_at, k_at, bk, bq):
    k_iota = lax.broadcasted_iota(jnp.int32, (bk, bq), 0) + k_at
    q_iota = lax.broadcasted_iota(jnp.int32, (bk, bq), 1) + q_at
    info = row_ref[0:1, pl.ds(q_at, bq)]
    if col_ref is None:
        return (k_iota >= info) & (k_iota <= q_iota)
    return (col_ref[pl.ds(k_at, bk), :] == info) & (k_iota <= q_iota)


def attend_kernel(bq, count, sends, stacked, by_column, ids, first_ref, row_ref, *rest):
    rest = list(rest)
    col_ref = rest.pop(0) if by_column else None
    pieces, rest = rest[:count], rest[count:]
    columns = rest.pop(0)
    out_pieces, rest = rest[:sends], rest[sends:]
    stack_ref = rest.pop(0) if stacked else None
    o_ref, lse_ref, x_ref, k_s, v_s, vt_s = rest
    i = pl.program_id(0)
    me = ids[0]
    rows = pieces[0].shape[0]
    bk = bq

    @pl.when(i == 0)
    def _():
        for s in range(count):
            at = pl.ds(pl.multiple_of((me ^ s) * rows, rows), rows)
            x = dot(pieces[s][...], columns[...]).astype(BF)
            x_ref[at, :] = x
            k_s[at, :] = x[:, GW : 2 * GW]
            v_s[at, :] = x[:, 2 * GW : 3 * GW]
        vt_s[...] = v_s[...].T

    q_at = pl.multiple_of(i * bq, bq)
    q_heads = head_parts(x_ref[pl.ds(q_at, bq), 0:GW])

    def step(j, carry):
        k_at = pl.multiple_of(j * bk, bk)
        keys = k_s[pl.ds(k_at, bk), :]
        mask = pair_mask(row_ref, col_ref, q_at, k_at, bk, bq)
        out = []
        for h in range(HG):
            top, total, acc = carry[h]
            scores = nt_dot(keys, q_heads[h]) * (SCORE_SCALE * LOG2E)
            scores = jnp.where(mask, scores, NEGATIVE)
            top_new = jnp.maximum(top, jnp.max(scores, axis=0, keepdims=True))
            weight = jnp.exp2(scores - top_new)
            fade = jnp.exp2(top - top_new)
            total = total * fade + jnp.sum(weight, axis=0, keepdims=True)
            values_t = vt_s[h * HD : (h + 1) * HD, pl.ds(k_at, bk)]
            acc = acc * fade + dot(values_t, weight.astype(BF))
            out.append((top_new, total, acc))
        return tuple(out)

    start = tuple(
        (
            jnp.full((1, bq), NEGATIVE, F32),
            jnp.zeros((1, bq), F32),
            jnp.zeros((HD, bq), F32),
        )
        for _ in range(HG)
    )
    done = lax.fori_loop(first_ref[i], i + 1, step, start)
    outs = jnp.concatenate([acc / total for _, total, acc in done], axis=0)
    o_ref[pl.ds(q_at, bq), :] = outs.T.astype(BF)
    for h in range(HG):
        top, total, _ = done[h]
        lse_ref[h : h + 1, pl.ds(q_at, bq)] = top + jnp.log2(total)

    @pl.when(i == pl.num_programs(0) - 1)
    def _():
        for s in range(sends):
            at = pl.ds(pl.multiple_of((me ^ s) * rows, rows), rows)
            out_pieces[s][...] = o_ref[at, :]
        if stacked:
            half = rows // 2
            for b in range(count):
                at = b * rows
                stack_ref[b, :, 0:GW] = o_ref[at : at + half, :]
                stack_ref[b, :, GW : 2 * GW] = o_ref[at + half : at + rows, :]


def attend_back_kernel(bq, count, sends, stacked, by_column, ids, first_ref, row_ref, *rest):
    rest = list(rest)
    col_ref = rest.pop(0) if by_column else None
    x_ref = rest.pop(0)
    given = 1 if stacked else count
    grads, rest = rest[:given], rest[given:]
    o_ref, lse_ref = rest[:2]
    out_pieces, rest = rest[2 : 2 + sends], rest[2 + sends :]
    stack_ref = rest.pop(0) if stacked else None
    dx_ref, k_s, v_s, g_s, dk_s, dv_s = rest
    i = pl.program_id(0)
    me = ids[0]
    rows = g_s.shape[0] // count
    bk = bq

    @pl.when(i == 0)
    def _():
        k_s[...] = x_ref[:, GW : 2 * GW]
        v_s[...] = x_ref[:, 2 * GW : 3 * GW]
        for s in range(count):
            if stacked:
                half = rows // 2
                g_s[s * rows : s * rows + half, :] = grads[0][s, :, 0:GW]
                g_s[s * rows + half : (s + 1) * rows, :] = grads[0][s, :, GW : 2 * GW]
            else:
                at = pl.ds(pl.multiple_of((me ^ s) * rows, rows), rows)
                g_s[at, :] = grads[s][...]
        dk_s[...] = jnp.zeros_like(dk_s)
        dv_s[...] = jnp.zeros_like(dv_s)

    q_at = pl.multiple_of(i * bq, bq)
    grad = g_s[pl.ds(q_at, bq), :]
    q_heads = head_parts(x_ref[pl.ds(q_at, bq), 0:GW])
    g_heads = head_parts(grad)
    dots = (grad.astype(F32) * o_ref[pl.ds(q_at, bq), :].astype(F32)).T
    row_dot = [
        jnp.sum(dots[h * HD : (h + 1) * HD, :], axis=0, keepdims=True) for h in range(HG)
    ]
    lse = [lse_ref[h : h + 1, pl.ds(q_at, bq)] for h in range(HG)]

    def step(j, dq):
        k_at = pl.multiple_of(j * bk, bk)
        here = pl.ds(k_at, bk)
        keys = k_s[here, :]
        values = v_s[here, :]
        key_heads = head_parts(keys)
        mask = pair_mask(row_ref, col_ref, q_at, k_at, bk, bq)
        dk = dk_s[here, :]
        dv = dv_s[here, :]
        for h in range(HG):
            scores = nt_dot(keys, q_heads[h]) * (SCORE_SCALE * LOG2E)
            scores = jnp.where(mask, scores - lse[h], NEGATIVE)
            soft = jnp.exp2(scores)
            g_soft = nt_dot(values, g_heads[h])
            g_scores = (soft * (g_soft - row_dot[h])).astype(BF)
            dv = dv + dot(soft.astype(BF), g_heads[h])
            dk = dk + dot(g_scores, q_heads[h])
            dq = dq + tn_dot(g_scores, key_heads[h])
        dk_s[here, :] = dk
        dv_s[here, :] = dv
        return dq

    dq = lax.fori_loop(first_ref[i], i + 1, step, jnp.zeros((bq, GW), F32))
    dx_ref[pl.ds(q_at, bq), 0:GW] = (dq * SCORE_SCALE).astype(BF)

    @pl.when(i == pl.num_programs(0) - 1)
    def _():
        dx_ref[:, GW : 2 * GW] = (dk_s[...] * SCORE_SCALE).astype(BF)
        dx_ref[:, 2 * GW : 3 * GW] = dv_s[...].astype(BF)
        for s in range(sends):
            at = pl.ds(pl.multiple_of((me ^ s) * rows, rows), rows)
            out_pieces[s][...] = dx_ref[at, :]
        if stacked:
            half = rows // 2
            for b in range(count):
                at = b * rows
                stack_ref[b, :, 0 : 3 * GW] = dx_ref[at : at + half, :]
                stack_ref[b, :, 3 * GW : 6 * GW] = dx_ref[at + half : at + rows, :]


def attend(ids, meta, pieces, columns, bq, stacked=False):
    first, row_info, col_info = meta
    rows, width = pieces[0].shape
    count = len(pieces)
    sends = 0 if stacked else min(count, 2 * GROUPS)
    length = rows * count
    operands = [first, row_info] + ([] if col_info is None else [col_info])
    operands += list(pieces) + [columns]
    outs = [sds((rows, GW), BF)] * sends
    outs += [sds((count, rows // 2, 2 * GW), BF)] if stacked else []
    outs += [
        sds((length, GW), BF),
        sds((8, length), F32),
        sds((length, 3 * GW), BF),
    ]
    got = stage(
        partial(attend_kernel, bq, count, sends, stacked, col_info is not None),
        "attend",
        ids,
        operands,
        outs,
        [pltpu.VMEM((length, GW), BF)] * 2 + [pltpu.VMEM((GW, length), BF)],
        flops=length * length * GW * 2 + 6 * length * width * GW,
        grid=(length // bq,),
        specs={0: pl.BlockSpec(memory_space=pltpu.SMEM)},
    )
    return got[:-3], got[-3:]


def attend_back(ids, meta, kept, grads, bq, stacked=False):
    first, row_info, col_info = meta
    attended, lse, x = kept
    count = grads[0].shape[0] if stacked else len(grads)
    rows = attended.shape[0] // count
    sends = 0 if stacked else min(count, 2 * GROUPS)
    length = rows * count
    operands = [first, row_info] + ([] if col_info is None else [col_info])
    operands += [x] + list(grads) + [attended, lse]
    got = stage(
        partial(attend_back_kernel, bq, count, sends, stacked, col_info is not None),
        "attend_back",
        ids,
        operands,
        [sds((rows, 3 * GW), BF)] * sends
        + ([sds((count, rows // 2, 6 * GW), BF)] if stacked else [])
        + [sds(x.shape, BF)],
        [pltpu.VMEM((length, GW), BF)] * 3 + [pltpu.VMEM((length, GW), F32)] * 2,
        flops=length * length * GW * 5,
        grid=(length // bq,),
        specs={0: pl.BlockSpec(memory_space=pltpu.SMEM)},
    )
    return got[:-1], got[-1]


def project_grads_kernel(count, ids, dx_ref, *rest):
    pieces, (keep, send, total) = rest[:count], rest[count:]
    rows = pieces[0].shape[0]
    for s, piece in enumerate(pieces):
        at = pl.ds(pl.multiple_of((ids[0] ^ s) * rows, rows), rows)
        term = tn_dot(piece[...], dx_ref[at, :])
        total[...] = term if s == 0 else total[...] + term
    split_rows(ids[0], total, keep, send)


def project_grads(ids, wide_count, pieces, dx):
    rows, width = pieces[0].shape
    shape = (wide_count // 2, width // wide_count, 3 * GW)
    return stage(
        partial(project_grads_kernel, len(pieces)),
        "project_grads",
        ids,
        [dx] + list(pieces),
        [sds(shape, BF)] * 2,
        [pltpu.VMEM((width, 3 * GW), F32)],
        flops=6 * dx.size * width // 3,
    )


def group_columns_kernel(ids, project, out):
    group, _ = combo(ids[0])
    width = GROUPS * GW
    for c in range(GROUPS):

        @pl.when(group == c)
        def _():
            for t in range(3):
                at = t * width + c * GW
                out[:, t * GW : (t + 1) * GW] = project[:, at : at + GW]


def group_columns(ids, project):
    (out,) = stage(
        group_columns_kernel,
        "group_columns",
        ids,
        [project],
        [sds((project.shape[0], 3 * GW), BF)],
    )
    return out


def save_halves(me, normed, mine_ref, other_ref):
    rows = mine_ref.shape[0]
    core = lax.rem(me, 2)
    mine_ref[...] = normed[pl.ds(pl.multiple_of(core * rows, rows), rows), :]
    other_ref[...] = normed[pl.ds(pl.multiple_of((1 - core) * rows, rows), rows), :]


def routed_pre_kernel(count, ids, tok, sel, *rest):
    vectors, rest = rest[:count], rest[count:]
    mine_ref, other_ref, one_hot_ref, picked_ref, vecs, normed = rest
    rows = [vector[...].astype(F32).reshape(1, -1) for vector in vectors]
    rows.append(jnp.zeros((8 - count, tok.shape[1]), F32))
    vecs[...] = jnp.concatenate(rows, axis=0)
    span = one_hot_ref.shape[1]
    seqs = sel.shape[0]
    if sel.shape[1] != span:
        sel = sel[:, pl.ds(pl.multiple_of(ids[0] * span, span), span)]
    slots = span // 4
    upper = (
        lax.broadcasted_iota(jnp.int32, (span, span), 0)
        <= lax.broadcasted_iota(jnp.int32, (span, span), 1)
    ).astype(F32).astype(BF)
    slot = lax.broadcasted_iota(jnp.int32, (slots, span), 0).astype(F32)
    for q in range(seqs):
        chosen = jnp.broadcast_to(sel[q : q + 1, :].astype(F32), (8, span))
        rank = dot(chosen.astype(BF), upper)[0:1, :] * chosen[0:1, :] - 1.0
        one_hot = (slot == rank).astype(F32).astype(BF)
        one_hot_ref[q * slots : (q + 1) * slots, :] = one_hot
        picked_ref[q * slots : (q + 1) * slots, :] = dot(
            one_hot, tok[q * span : (q + 1) * span, :]
        ).astype(BF)
    picked = picked_ref[...].astype(F32)
    normed[...] = (picked * norm_scale(picked) * gain_of(vecs, 1)).astype(BF)
    save_halves(ids[0], normed, mine_ref, other_ref)


def gain_of(vecs, k):
    return vecs[k : k + 1, :]


def routed_pre(ids, tok, sel, span, vectors):
    rows, width = tok.shape[0] // 4, tok.shape[1]
    return stage(
        partial(routed_pre_kernel, len(vectors)),
        "routed_pre",
        ids,
        [tok, sel] + vectors,
        [
            sds((rows // 2, width), BF),
            sds((rows // 2, width), BF),
            sds((rows, span), BF),
            sds((rows, width), BF),
            sds((8, width), F32),
        ],
        [pltpu.VMEM((rows, width), BF)],
        flops=4 * rows * width * span,
    )


def routed_mid_kernel(count, ids, *rest):
    pieces = rest[:count]
    output, picked, vecs, branch_ref, low_ref, att_ref, parts = rest[count:]
    attended = load_pieces(ids[0], pieces, parts, 1)
    att_ref[...] = attended
    branch = dot(attended, output[...])
    branch_ref[...] = branch
    middle = picked[...].astype(F32) + branch
    low_ref[...] = (middle * norm_scale(middle) * gain_of(vecs, 2)).astype(BF)


def routed_mid(ids, pieces, output, picked, vecs):
    shape = picked.shape
    return stage(
        partial(routed_mid_kernel, len(pieces)),
        "routed_mid",
        ids,
        list(pieces) + [output, picked, vecs],
        [sds(shape, F32), sds(shape, BF), sds(shape, BF)],
        [pltpu.VMEM((GROUPS, shape[0], GW), BF)],
        flops=2 * shape[0] * shape[1] * shape[1],
    )


def hidden_forward_kernel(count, ids, *rest):
    pieces = rest[:count]
    expand, reduce_ref = rest[count : count + 2]
    outs = rest[count + 2 :]
    rows = pieces[0].shape[0]
    low = jnp.concatenate([piece[...] for piece in pieces], axis=0)
    hidden = gelu(dot(low, expand[...])).astype(BF)
    total = dot(hidden, reduce_ref[...]).astype(BF)
    for s, out in enumerate(outs):
        out[...] = total[s * rows : (s + 1) * rows, :]


def hidden_forward(ids, pieces, expand, reduce_part):
    return stage(
        partial(hidden_forward_kernel, len(pieces)),
        "hidden_forward",
        ids,
        list(pieces) + [expand, reduce_part],
        [sds(pieces[0].shape, BF)] * len(pieces),
        flops=4 * len(pieces) * pieces[0].size * expand.shape[1],
    )


def dense_pre_kernel(shares, ids, tok, one_hot, picked, vecs, branch, *rest):
    partials = rest[:shares]
    mine_ref, other_ref, mixed_ref, delta_ref, normed = rest[shares:]
    slots, span = one_hot.shape[0] // 2, one_hot.shape[1]
    delta = branch[...]
    for share in partials:
        delta = delta + share[...].astype(F32)
    delta_ref[...] = delta
    gate = jnp.sum(picked[...].astype(F32) * gain_of(vecs, 0), axis=-1, keepdims=True)
    lifted = gate * delta
    for q in range(2):
        at, spots = slice(q * span, (q + 1) * span), slice(q * slots, (q + 1) * slots)
        mixed = tok[at, :].astype(F32) + place(one_hot[spots, :], lifted[spots, :])
        mixed_ref[at, :] = mixed
        normed[at, :] = (mixed * norm_scale(mixed) * gain_of(vecs, 3)).astype(BF)
    save_halves(ids[0], normed, mine_ref, other_ref)


def dense_pre(ids, tok, one_hot, picked, vecs, branch, partials):
    rows, width = tok.shape
    return stage(
        partial(dense_pre_kernel, len(partials)),
        "dense_pre",
        ids,
        [tok, one_hot, picked, vecs, branch] + list(partials),
        [
            sds((rows // 2, width), BF),
            sds((rows // 2, width), BF),
            sds(tok.shape, F32),
            sds(picked.shape, F32),
        ],
        [pltpu.VMEM((rows, width), BF)],
        flops=6 * rows * width * one_hot.shape[0],
    )


def this_part(me, weights, scratch):
    if not scratch:
        return weights[0][0], weights[1][0]
    e_s, r_s = scratch
    core = lax.rem(me, 2)
    rows = weights[0].shape[-2]
    if len(weights) == 2:
        blocks = []
        for c in range(weights[0].shape[0]):
            blocks.append((weights[0], c, 2 * c + core))
            blocks.append((weights[1], c, 2 * c + 1 - core))
    else:
        blocks = [(weight, 0, me ^ s) for s, weight in enumerate(weights)]
    for weight, c, at in blocks:
        at = pl.ds(pl.multiple_of(at * rows, rows), rows)
        e_s[at, :] = weight[c, 0, 0]
        r_s[at, :] = weight[c, 0, 1]
    return e_s[...], r_s[...]


def part_specs(base, weights):
    if weights[0].ndim == 3:
        return {
            base + k: pl.BlockSpec((1,) + w.shape[1:], lambda n: (n, 0, 0))
            for k, w in enumerate(weights)
        }
    return {
        base + k: pl.BlockSpec(
            (w.shape[0], 1) + w.shape[2:], lambda n: (0, n, 0, 0, 0)
        )
        for k, w in enumerate(weights)
    }


def part_scratch(width, weights):
    if weights[0].ndim == 3:
        return []
    return [pltpu.VMEM((width, weights[0].shape[-1]), BF)] * 2


def dense_ffn_kernel(split, ids, stack, *rest):
    output, mixed, cot, vecs = rest[:4]
    gain = gain_of(vecs, 4)
    rest = rest[4:]
    weights, rest = rest[:split], rest[split:]
    act_ref, low_ref, back_ref, sum_ref, att_ref, gain_ref = rest[:6]
    g_stack, rest = rest[6], rest[7:]
    parts, branch_s, delta_s, grad_s = rest[:4]
    n = pl.program_id(0)
    me = ids[0]

    @pl.when(n == 0)
    def _():
        attended = load_stack(me, stack, parts, 1)
        att_ref[...] = attended
        branch = dot(attended, output[...])
        branch_s[...] = branch
        middle = mixed[...] + branch
        low_ref[...] = (middle * norm_scale(middle) * gain).astype(BF)
        delta_s[...] = jnp.zeros_like(delta_s)
        grad_s[...] = jnp.zeros_like(grad_s)

    expand, reduce_w = this_part(me, weights, rest[4:])
    value, slope = gelu_both(dot(low_ref[...], expand))
    delta_s[...] += dot(value.astype(BF), reduce_w)
    grad_pre = (nt_dot(cot[...], reduce_w) * slope).astype(BF)
    grad_s[...] += nt_dot(grad_pre, expand)

    @pl.when(n == pl.num_programs(0) - 1)
    def _():
        middle = mixed[...] + branch_s[...]
        act_ref[...] = (middle + delta_s[...]).astype(BF)
        grad_middle, gain_grad = norm_back(grad_s[...], middle, gain)
        gain_ref[...] = jnp.broadcast_to(gain_grad, gain_ref.shape)
        total = cot[...].astype(F32) + grad_middle
        sum_ref[...] = total
        back = total.astype(BF)
        back_ref[...] = back
        save_stack(nt_dot(back, output[...]).astype(BF), parts, g_stack)


def dense_ffn(ids, stack, output, mixed, cot, vecs, weights):
    rows, width = mixed.shape
    split = len(weights)
    parts_n = weights[0].shape[0 if weights[0].ndim == 3 else 1]
    hidden = weights[0].shape[-1]
    base = 5
    specs = part_specs(base, weights)
    scratch = [pltpu.VMEM((GROUPS, rows, GW), BF)] + [pltpu.VMEM((rows, width), F32)] * 3
    scratch += part_scratch(width, weights)
    outs = [
        sds((rows, width), BF),
        sds((rows, width), BF),
        sds((rows, width), BF),
        sds((rows, width), F32),
        sds((rows, width), BF),
        sds((8, width), F32),
        sds(stack.shape, BF),
    ]
    got = stage(
        partial(dense_ffn_kernel, split),
        "dense_ffn",
        ids,
        [stack, output, mixed, cot, vecs] + list(weights),
        outs,
        scratch,
        flops=8 * rows * width * hidden * parts_n + 4 * rows * width * width,
        grid=(parts_n,),
        specs=specs,
    )
    return got[:6], got[6]


def dense_post_kernel(ids, stack, *rest):
    project, vecs, mixed, total, one_hot, picked, delta = rest[:7]
    g_mixed_ref, g_delta_ref, g_low_ref, g_gate_ref, router_ref, parts = rest[7:]
    g_proj = load_stack(ids[0], stack, parts, 3)
    grad_rows, _ = norm_back(nt_dot(g_proj, project[...]), mixed[...], gain_of(vecs, 3))
    g_mixed_ref[...] = total[...] + grad_rows
    slots, span = one_hot.shape[0] // 2, one_hot.shape[1]
    rows = picked[...].astype(F32)
    gate = jnp.sum(rows * gain_of(vecs, 0), axis=-1, keepdims=True)
    router = jnp.zeros((1, rows.shape[1]), F32)
    for q in range(2):
        at, spots = slice(q * span, (q + 1) * span), slice(q * slots, (q + 1) * slots)
        lifted = pick(one_hot[spots, :], g_mixed_ref[at, :])
        g_delta = gate[spots, :] * lifted
        g_delta_ref[spots, :] = g_delta
        g_low_ref[spots, :] = g_delta.astype(BF)
        g_gate = jnp.sum(lifted * delta[spots, :], axis=-1, keepdims=True)
        g_gate_ref[spots, :] = jnp.broadcast_to(g_gate, (slots, g_gate_ref.shape[1]))
        router = router + jnp.sum(rows[spots, :] * g_gate, axis=0, keepdims=True)
    router_ref[...] = jnp.broadcast_to(router, router_ref.shape)


def dense_post(ids, stack, project, vecs, mixed, total, one_hot, picked, delta):
    rows, width = mixed.shape
    return stage(
        dense_post_kernel,
        "dense_post",
        ids,
        [stack, project, vecs, mixed, total, one_hot, picked, delta],
        [
            sds((rows, width), F32),
            sds(picked.shape, F32),
            sds(picked.shape, BF),
            sds((picked.shape[0], 128), F32),
            sds((8, width), F32),
        ],
        [pltpu.VMEM((GROUPS, rows, 3 * GW), BF)],
        flops=6 * rows * width * width,
    )


def routed_back_kernel(split, ids, low, g_low, branch, picked, vecs, g_delta, output, *rest):
    weights, rest = rest[:split], rest[split:]
    g_mid_ref, back_ref, gain_ref, stack, parts, grad_s = rest[:6]
    n = pl.program_id(0)

    @pl.when(n == 0)
    def _():
        grad_s[...] = jnp.zeros_like(grad_s)

    expand, reduce_w = this_part(ids[0], weights, rest[6:])
    _, slope = gelu_both(dot(low[...], expand))
    grad_pre = (nt_dot(g_low[...], reduce_w) * slope).astype(BF)
    grad_s[...] += nt_dot(grad_pre, expand)

    @pl.when(n == pl.num_programs(0) - 1)
    def _():
        middle = picked[...].astype(F32) + branch[...]
        g_middle, gain_grad = norm_back(grad_s[...], middle, gain_of(vecs, 2))
        gain_ref[...] = jnp.broadcast_to(gain_grad, gain_ref.shape)
        g_mid_ref[...] = g_middle
        back = (g_delta[...] + g_middle).astype(BF)
        back_ref[...] = back
        save_stack(nt_dot(back, output[...]).astype(BF), parts, stack)


def routed_back(ids, wide_count, low, g_low, branch, picked, vecs, g_delta, output, weights):
    rows, width = branch.shape
    parts_n = weights[0].shape[0 if weights[0].ndim == 3 else 1]
    return stage(
        partial(routed_back_kernel, len(weights)),
        "routed_back",
        ids,
        [low, g_low, branch, picked, vecs, g_delta, output] + list(weights),
        [
            sds((rows, width), F32),
            sds((rows, width), BF),
            sds((8, width), F32),
            sds((wide_count, rows // 4, 2 * GW), BF),
        ],
        [pltpu.VMEM((GROUPS, rows, GW), BF), pltpu.VMEM((rows, width), F32)]
        + part_scratch(width, weights),
        flops=6 * rows * width * parts_n * weights[0].shape[-1],
        grid=(parts_n,),
        specs=part_specs(7, weights),
    )


def routed_post_kernel(ids, stack, *rest):
    project, vecs, picked, g_mid, g_mixed, one_hot, g_gate = rest[:7]
    out_ref, parts = rest[7:]
    g_proj = load_stack(ids[0], stack, parts, 3)
    rows = picked[...].astype(F32)
    grad_rows, _ = norm_back(nt_dot(g_proj, project[...]), rows, gain_of(vecs, 1))
    spread = g_mid[...] + grad_rows + g_gate[:, 0:1] * gain_of(vecs, 0)
    slots, span = one_hot.shape[0] // 2, one_hot.shape[1]
    for q in range(2):
        at, spots = slice(q * span, (q + 1) * span), slice(q * slots, (q + 1) * slots)
        out_ref[at, :] = g_mixed[at, :] + place(one_hot[spots, :], spread[spots, :])


def routed_post(ids, stack, project, vecs, picked, g_mid, g_mixed, one_hot, g_gate):
    rows, width = picked.shape
    (out,) = stage(
        routed_post_kernel,
        "routed_post",
        ids,
        [stack, project, vecs, picked, g_mid, g_mixed, one_hot, g_gate],
        [sds(g_mixed.shape, F32)],
        [pltpu.VMEM((GROUPS, rows, 3 * GW), BF)],
        flops=6 * rows * width * width,
    )
    return out


def split_rows(me, total, keep, send):
    chips, rows = keep.shape[0], keep.shape[1]
    core = lax.rem(me, 2)
    for c in range(chips):
        mine = pl.multiple_of((2 * c + core) * rows, rows)
        other = pl.multiple_of((2 * c + 1 - core) * rows, rows)
        keep[c] = total[pl.ds(mine, rows), :].astype(BF)
        send[c] = total[pl.ds(other, rows), :].astype(BF)


def hidden_grads_kernel(ids, low, grad, expand, reduce_ref, out, total):
    i = pl.program_id(0)
    hidden = expand.shape[1]

    @pl.when(i == 0)
    def _():
        total[...] = jnp.zeros_like(total)

    value, slope = gelu_both(dot(low[...], expand[...]))
    grad_pre = (nt_dot(grad[...], reduce_ref[...]) * slope).astype(BF)
    total[:, 0:hidden] += tn_dot(low[...], grad_pre)
    total[:, hidden : 2 * hidden] += tn_dot(grad[...], value.astype(BF))

    @pl.when(i == pl.num_programs(0) - 1)
    def _():
        out[...] = total[...].astype(BF)


def hidden_grads(ids, low, grad, expand, reduce_part):
    width, hidden = expand.shape
    block = min(512, low.shape[0])
    row_spec = pl.BlockSpec((block, width), lambda i: (i, 0))
    (out,) = stage(
        hidden_grads_kernel,
        "hidden_grads",
        ids,
        [low, grad, expand, reduce_part],
        [sds((width, 2 * hidden), BF)],
        [pltpu.VMEM((width, 2 * hidden), F32)],
        flops=8 * low.size * hidden,
        grid=(low.shape[0] // block,),
        specs={0: row_spec, 1: row_spec},
    )
    return out


def output_grads_kernel(vectors, ids, att, back, *rest):
    rest = list(rest)
    vecs, rest = rest[:vectors], rest[vectors:]
    keep, send, total = rest
    width = att.shape[1]
    total[:, 0:width] = tn_dot(att[...], back[...])
    if vectors:
        rows = [vec[0:1, :] for vec in vecs]
        rows.append(jnp.zeros((128 - vectors, width), F32))
        total[:, width : width + 128] = jnp.concatenate(rows, axis=0).T
    split_rows(ids[0], total, keep, send)


def output_grads(ids, wide_count, att, back, vecs):
    rows, width = att.shape
    columns = width + (128 if vecs else 0)
    shape = (wide_count // 2, width // wide_count, columns)
    return stage(
        partial(output_grads_kernel, len(vecs)),
        "output_grads",
        ids,
        [att, back] + list(vecs),
        [sds(shape, BF), sds(shape, BF)],
        [pltpu.VMEM((width, columns), F32)],
        flops=3 * rows * width * width,
    )


def join_kernel(pairs, ids, *rest):
    keeps, cames, outs = rest[:pairs], rest[pairs : 2 * pairs], rest[2 * pairs :]
    chip = lax.div(ids[0], 2)
    for s, out in enumerate(outs):
        low = 0
        for keep, came in zip(keeps, cames):
            columns = keep.shape[2]
            total = keep[chip ^ s].astype(F32) + came[chip ^ s].astype(F32)
            out[:, low : low + columns] = total.astype(BF)
            low += columns


def join_chips(ids, keeps, cames):
    chips, rows = keeps[0].shape[:2]
    columns = sum(keep.shape[2] for keep in keeps)
    return stage(
        partial(join_kernel, len(keeps)),
        "join",
        ids,
        list(keeps) + list(cames),
        [sds((rows, columns), BF)] * chips,
    )


def chips_return(parts):
    return [parts[0]] + [chip_step(parts[s], s) for s in range(1, len(parts))]


def sum_terms(terms):
    total = terms[0].astype(F32)
    for term in terms[1:]:
        total = total + term.astype(F32)
    return total


def sum_split_kernel(count, ids, *rest):
    terms, outs, total = rest[:count], rest[count:-1], rest[-1]
    got = terms[0][...].astype(F32)
    for term in terms[1:]:
        got = got + term[...].astype(F32)
    total[...] = got
    rows = outs[0].shape[0]
    for s, out in enumerate(outs):
        at = pl.multiple_of((ids[1] ^ s) * rows, rows)
        out[...] = total[pl.ds(at, rows), :].astype(BF)


def sum_kernel(ids, *rest):
    got = rest[0][...].astype(F32)
    for term in rest[1:-1]:
        got = got + term[...].astype(F32)
    rest[-1][...] = got.astype(BF)


def gather_out_kernel(count, vectors, ids, *rest):
    pieces, outs = rest[:count], rest[count : -1 - vectors]
    vecs, wide_s = rest[-1 - vectors : -1], rest[-1]
    rows = pieces[0].shape[0]
    for s, piece in enumerate(pieces):
        at = pl.ds(pl.multiple_of((ids[1] ^ s) * rows, rows), rows)
        low = 0
        for out in outs:
            columns = out.shape[1]
            out[at, :] = piece[:, low : low + columns].astype(F32)
            low += columns
        wide_s[at, :] = piece[:, low:].astype(F32)
    turned = wide_s[...].T
    for k, vec in enumerate(vecs):
        vec[...] = turned[k : k + 1, :].reshape(vec.shape[0])


def narrow_terms(ids, terms):
    narrow_count = lax.axis_size("narrow")
    rows, columns = terms[0].shape
    if rows % (8 * narrow_count):
        return [sum_terms(terms).astype(BF)]
    return stage(
        partial(sum_split_kernel, len(terms)),
        "sum_split",
        ids,
        terms,
        [sds((rows // narrow_count, columns), BF)] * narrow_count,
        [pltpu.VMEM((rows, columns), F32)],
    )


def sum_narrow(ids, parts, first):
    if len(parts) == 1:
        return lax.psum(parts[0], "narrow")
    return sum_parts(ids, tie(narrow_return(parts), first))


def spread_narrow(ids, total, rows, widths, vectors, first):
    narrow_count = lax.axis_size("narrow")
    if total.shape[0] == rows:
        total = total.astype(F32)
        outs, low = [], 0
        for size in widths:
            outs.append(total[:, low : low + size])
            low += size
        return outs[:-1] + [outs[-1][:, k] for k in range(vectors)]
    return stage(
        partial(gather_out_kernel, narrow_count, vectors),
        "gather_out",
        ids,
        tie(narrow_gather(total), first),
        [sds((rows, size), F32) for size in widths[:-1]] + [sds((rows,), F32)] * vectors,
        [pltpu.VMEM((rows, widths[-1]), F32)],
    )


def join_narrow_kernel(turned, ids, keep, came, *outs):
    each = outs[0].shape[0]
    turn = lax.div(ids[0], 2) if turned else 0
    for t, out in enumerate(outs):
        for j in range(each):
            at = ((ids[1] ^ t) * each + j) ^ turn
            out[j] = (keep[at].astype(F32) + came[at].astype(F32)).astype(BF)


def route_kernel(count, ids, *rest):
    pieces, outs, blocks = rest[:count], rest[count:-1], rest[-1]
    each = pieces[0].shape[0]
    for t, piece in enumerate(pieces):
        for j in range(each):
            blocks[(ids[1] ^ t) * each + j] = piece[j]
    chip = lax.div(ids[0], 2)
    for s, out in enumerate(outs):
        out[...] = blocks[chip ^ s]


def unpack_kernel(turned, ids, *rest):
    pieces, (own, gain, out, gain_out, parts) = rest[:GROUPS], rest[GROUPS:]
    at = lax.div(ids[0], 2)
    if turned:
        at = at ^ ids[1]
    rows = out.shape[0]
    for s, piece in enumerate(pieces):
        parts[lax.rem(at ^ s, GROUPS)] = piece[...].astype(F32)
    total = jnp.zeros((rows, GW), F32)
    for t in range(3):
        for c in range(GROUPS):
            low = (t * GROUPS + c) * GW
            part = parts[c, :, t * GW : (t + 1) * GW]
            out[:, low : low + GW] = part
            total = total + part * own[:, low : low + GW].astype(F32)
    sums = jnp.broadcast_to(jnp.sum(total, axis=1, keepdims=True), (rows, 128)).T
    gain_out[...] = (sums[0:1, :] / gain[...]).reshape(rows)


def unpack(ids, pieces, own, gain):
    rows, columns = pieces[0].shape
    return stage(
        partial(unpack_kernel, direct_delivery()),
        "unpack",
        ids,
        list(pieces) + [own, gain],
        [sds((rows, GROUPS * columns), F32), sds((rows,), F32)],
        [pltpu.VMEM((GROUPS, rows, columns), F32)],
    )


def split_narrow(ids, keep, came):
    narrow_count = lax.axis_size("narrow")
    chips, rows, columns = keep.shape
    shape = (chips // narrow_count, rows, columns)
    return stage(
        partial(join_narrow_kernel, direct_delivery()),
        "join_narrow",
        ids,
        [keep, came],
        [sds(shape, BF)] * narrow_count,
    )


def join_all_kernel(turned, ids, keep, came, out):
    turn = lax.div(ids[0], 2) if turned else 0
    for n in range(out.shape[0]):
        out[n] = (keep[n ^ turn].astype(F32) + came[n ^ turn].astype(F32)).astype(BF)


def join_all(ids, keep, came):
    (total,) = stage(
        partial(join_all_kernel, direct_delivery()),
        "join_all",
        ids,
        [keep, came],
        [sds(keep.shape, BF)],
    )
    return total


def sum_parts(ids, terms):
    (total,) = stage(sum_kernel, "sum_terms", ids, terms, [sds(terms[0].shape, BF)])
    return total


def route_project(ids, gathered, chips):
    rows, columns = gathered[0].shape[1:]
    return stage(
        partial(route_kernel, len(gathered)),
        "route",
        ids,
        gathered,
        [sds((rows, columns), BF)] * GROUPS,
        [pltpu.VMEM((chips, rows, columns), BF)],
    )


def direct_delivery():
    return lax.axis_size("narrow") == GROUPS and lax.axis_size("wide") == 2 * GROUPS


def deliver(ids, total, chips):
    narrow_count = lax.axis_size("narrow")
    if not direct_delivery():
        return chips_return(route_project(ids, narrow_gather(total), chips))
    total = total[0]

    def moves(k):
        pairs = []
        for chip in range(chips):
            for core in range(2):
                for n in range(narrow_count):
                    to = (2 * (chip ^ n) + core) * narrow_count + (n ^ k)
                    pairs.append(((2 * chip + core) * narrow_count + n, to))
        return pairs

    return [lax.ppermute(total, ("wide", "narrow"), moves(k)) for k in range(narrow_count)]


def finish_hidden_kernel(ids, dense, routed, e_d, r_d, e_r, r_r):
    hidden = e_d.shape[1]
    for total, e_ref, r_ref in ((dense, e_d, r_d), (routed, e_r, r_r)):
        e_ref[...] = total[:, 0:hidden].astype(F32)
        r_ref[...] = total[:, hidden : 2 * hidden].astype(F32)


def finish_hidden(ids, dense, routed):
    rows, columns = dense.shape
    return stage(
        finish_hidden_kernel,
        "finish_hidden",
        ids,
        [dense, routed],
        [sds((rows, columns // 2), F32)] * 4,
    )


def tie(x, *first):
    return lax.optimization_barrier((x, first))[0]


def narrow_step(x, s):
    return lax.ppermute(x, "narrow", [(j, j ^ s) for j in range(lax.axis_size("narrow"))])


def narrow_gather(x):
    return [x] + [narrow_step(x, s) for s in range(1, lax.axis_size("narrow"))]


def narrow_return(parts):
    return [parts[0]] + [narrow_step(parts[s], s) for s in range(1, len(parts))]


def exchange(pieces):
    wide_count = lax.axis_size("wide")
    return [pieces[0]] + [
        lax.ppermute(pieces[s], "wide", [(j, j ^ s) for j in range(wide_count)])
        for s in range(1, len(pieces))
    ]


def exchange_rows(mine, other):
    wide_count = lax.axis_size("wide")
    if wide_count != 8:
        return exchange([mine, other] * (wide_count // 2))
    beside = core_step(other)
    from_x = [chip_step(mine, 1), chip_step(beside, 1)]
    from_y = [chip_step(mine, 2), chip_step(beside, 2)]
    corner = [chip_step(from_y[0], 1), chip_step(from_x[1], 2)]
    return [mine, beside] + from_x + from_y + corner


def hidden_share(expand, reduce_part):
    wide_count = lax.axis_size("wide")
    here = lax.axis_index("wide")
    width, hidden = expand.shape
    rows = width // wide_count
    if width != hidden or rows % 16:
        return None
    return jnp.stack(
        [
            lax.dynamic_slice_in_dim(expand, here * rows, rows, 0),
            lax.dynamic_slice_in_dim(reduce_part, here * rows, rows, 0),
        ]
    )


def all_chips(x):
    groups = [list(range(core, lax.axis_size("wide"), 2)) for core in range(2)]
    return lax.all_gather(x, "wide", axis=0, axis_index_groups=groups)


def chip_step(x, s):
    return lax.ppermute(
        x, "wide", [(j, j ^ (2 * s)) for j in range(lax.axis_size("wide"))]
    )


def core_step(x):
    return lax.ppermute(x, "wide", [(j, j ^ 1) for j in range(lax.axis_size("wide"))])


def on_device(
    tokens,
    cotangent,
    selected,
    segments,
    router_vector,
    project_routed,
    output_routed,
    prenorm_routed,
    midnorm_routed,
    expand_routed,
    reduce_routed,
    project_dense,
    output_dense,
    prenorm_dense,
    midnorm_dense,
    expand_dense,
    reduce_dense,
):
    seq_count, span_rows, width = tokens.shape
    row_length = selected.shape[1]
    hidden = expand_dense.shape[1]
    wide_count = lax.axis_size("wide")
    narrow_count = lax.axis_size("narrow")
    here = lax.axis_index("wide")
    slot_count = span_rows // 4
    bq_dense = min(256, row_length)
    bq_routed = min(256, slot_count * wide_count)
    ids = jnp.stack([here, lax.axis_index("narrow")]).astype(jnp.int32)
    tok = tokens.reshape(-1, width)
    cot = cotangent.reshape(-1, width)

    share_d = hidden_share(expand_dense, reduce_dense)
    staged = share_d is not None
    if staged:
        own_d = lax.all_gather(share_d, "narrow", axis=0)

    mine = here % seq_count
    seq_segments = lax.dynamic_slice_in_dim(segments, mine, 1, 0)[0]
    seq_selected = lax.dynamic_slice_in_dim(selected, mine, 1, 0)[0].reshape(wide_count, span_rows)
    upper = (
        lax.broadcasted_iota(jnp.int32, (span_rows, span_rows), 0)
        <= lax.broadcasted_iota(jnp.int32, (span_rows, span_rows), 1)
    ).astype(BF)
    slots = jnp.arange(slot_count, dtype=jnp.int32)
    seq_rank = jnp.dot(seq_selected.astype(BF), upper, preferred_element_type=F32)
    seq_rank = jnp.where(seq_selected > 0, seq_rank.astype(jnp.int32) - 1, -1)
    slot_segments = (
        jnp.sum(
            jnp.where(
                seq_rank[:, None, :] == slots[None, :, None],
                seq_segments.reshape(wide_count, 1, span_rows) + 1,
                0,
            ),
            axis=-1,
        )
        - 1
    ).reshape(-1)
    meta_routed = (
        jnp.zeros((slot_segments.shape[0] // bq_routed,), jnp.int32),
        jnp.broadcast_to(slot_segments[None], (8, slot_segments.shape[0])),
        slot_segments[:, None],
    )
    own_selected = selected
    if span_rows % 128:
        own_selected = lax.dynamic_slice_in_dim(selected, here * span_rows, span_rows, 1)
    mine_r, other_r, one_hot, picked, vecs = routed_pre(
        ids,
        tok,
        own_selected,
        span_rows,
        [router_vector, prenorm_routed, midnorm_routed, prenorm_dense, midnorm_dense],
    )
    columns_r = group_columns(ids, tie(project_routed, mine_r))
    rows_r = exchange([mine_r, other_r] * (wide_count // 2))
    rows_r, meta_routed = lax.optimization_barrier((rows_r, meta_routed))
    pieces, kept_r = attend(ids, meta_routed, rows_r, columns_r, bq_routed)
    pieces = exchange(pieces)
    if staged:
        pieces, own_d = lax.optimization_barrier((pieces, own_d))
        chips_d = all_chips(own_d)
    branch_r, low_r, att_r = routed_mid(ids, pieces, output_routed, picked, vecs)
    dense_segments = tie(seq_segments, low_r)
    starts = sum(
        jnp.where(dense_segments == value, jnp.sum((dense_segments < value).astype(jnp.int32)), 0)
        for value in range(1, 4)
    )
    meta_dense = (
        starts[::bq_dense] // bq_dense,
        jnp.broadcast_to(starts[None], (8, row_length)),
        None,
    )

    own_at = here * (width // wide_count)

    def own_slice(x):
        return lax.dynamic_slice_in_dim(tie(x, low_r), own_at, width // wide_count, 0)

    own_rows = (
        own_slice(project_routed),
        own_slice(project_dense),
        own_slice(prenorm_routed).astype(F32)[None],
        own_slice(prenorm_dense).astype(F32)[None],
    )
    columns_d = group_columns(ids, tie(project_dense, low_r))
    share_r = hidden_share(tie(expand_routed, low_r), reduce_routed)
    low_pieces, columns_d, meta_dense, own_rows, share_r = lax.optimization_barrier(
        (narrow_gather(low_r), columns_d, meta_dense, own_rows, share_r)
    )
    partials = narrow_return(hidden_forward(ids, low_pieces, expand_routed, reduce_routed))

    mine_d, other_d, mixed, delta_r = dense_pre(
        ids, tok, one_hot, picked, vecs, branch_r, partials
    )
    if staged:
        mine_d, other_d, chips_d = lax.optimization_barrier((mine_d, other_d, chips_d))
        own_r = lax.all_gather(tie(share_r, mine_d), "narrow", axis=0)[None]
        rows_d, own_r = lax.optimization_barrier((exchange_rows(mine_d, other_d), own_r))
        weights_d = [chips_d, core_step(chips_d)]
    else:
        rows_d = exchange_rows(mine_d, other_d)
        weights_d = [
            lax.all_gather(expand_dense, "narrow", axis=0),
            lax.all_gather(reduce_dense, "narrow", axis=0),
        ]
        weights_r = [
            lax.all_gather(expand_routed, "narrow", axis=0),
            lax.all_gather(reduce_routed, "narrow", axis=0),
        ]
    cot_all = lax.all_gather(tie(cot, rows_d), "narrow", axis=0, tiled=True)
    (stack,), kept_d = attend(ids, meta_dense, rows_d, columns_d, bq_dense, stacked=True)
    stack, weights_d = lax.optimization_barrier((stack, weights_d))
    stack = lax.all_to_all(stack, "wide", 0, 0)
    if staged:
        stack, own_r = lax.optimization_barrier((stack, own_r))
        corner_r = chip_step(own_r, 3)
    (activations, low_d, back_d, sum_d, att_d, mid_gain_d), stack = dense_ffn(
        ids, stack, output_dense, mixed, cot, vecs, weights_d
    )
    if staged:
        stack, low_d, cot_all, corner_r = lax.optimization_barrier(
            (stack, low_d, cot_all, corner_r)
        )
    low_all = lax.all_gather(low_d, "narrow", axis=0, tiled=True)
    keep_d, send_d = output_grads(ids, wide_count, att_d, back_d, [])
    stack, keep_d, send_d = lax.optimization_barrier(
        (lax.all_to_all(stack, "wide", 0, 0), keep_d, send_d)
    )
    came_d = core_step(send_d)
    if staged:
        stack, own_r = lax.optimization_barrier((stack, own_r))
        sides_r = [chip_step(own_r, 1), chip_step(own_r, 2)]
        corner_r = [corner_r, core_step(corner_r)]
        weights_r = [own_r, core_step(own_r)]
    (stack,), dx_d = attend_back(ids, meta_dense, kept_d, [stack], bq_dense, stacked=True)
    stack, dx_d, weights_r, came_d = lax.optimization_barrier(
        (stack, dx_d, weights_r, came_d)
    )
    if staged:
        stack, dx_d, sides_r = lax.optimization_barrier((stack, dx_d, sides_r))
        weights_r += [w for own in sides_r for w in (own, core_step(own))] + corner_r
    stack = lax.all_to_all(stack, "wide", 0, 0)
    keep, send = project_grads(ids, wide_count, rows_d, dx_d)
    project_d = join_all(ids, keep, core_step(send))
    low_all, project_d = lax.optimization_barrier((low_all, project_d))
    project_d = lax.psum_scatter(project_d, "narrow", scatter_dimension=0, tiled=True)
    hidden_d = hidden_grads(ids, low_all, cot_all, expand_dense, reduce_dense)
    stack, hidden_d, weights_r = lax.optimization_barrier((stack, hidden_d, weights_r))
    ffn_d = lax.psum_scatter(hidden_d, "wide", scatter_dimension=0, tiled=True)
    g_mixed, g_delta, g_low, g_gate, router_grad = dense_post(
        ids, stack, project_dense, vecs, mixed, sum_d, one_hot, picked, delta_r
    )

    g_pieces = narrow_gather(g_low)
    g_mid_r, back_r, mid_gain_r, stack = routed_back(
        ids,
        wide_count,
        low_r,
        g_low,
        branch_r,
        picked,
        vecs,
        g_delta,
        output_routed,
        weights_r,
    )
    back_r, g_pieces = lax.optimization_barrier((back_r, g_pieces))
    keep_r, send_r = output_grads(
        ids, wide_count, att_r, back_r, [mid_gain_r, mid_gain_d, router_grad]
    )
    came_r = core_step(send_r)
    hidden_r = hidden_grads(
        ids,
        jnp.concatenate(tie(low_pieces, keep_r), axis=0),
        jnp.concatenate(g_pieces, axis=0),
        expand_routed,
        reduce_routed,
    )
    stack, keep_r, send_r, hidden_r = lax.optimization_barrier(
        (lax.all_to_all(stack, "wide", 0, 0), keep_r, send_r, hidden_r)
    )
    delivered_d = deliver(ids, tie(project_d, back_r), wide_count // 2)
    (stack,), dx_r = attend_back(ids, meta_routed, kept_r, [stack], bq_routed, stacked=True)
    stack, dx_r, came_r, delivered_d = lax.optimization_barrier(
        (stack, dx_r, came_r, delivered_d)
    )
    ffn_r = lax.psum_scatter(tie(hidden_r, dx_r), "wide", scatter_dimension=0, tiled=True)
    keep, send = project_grads(ids, wide_count, rows_r, dx_r)
    came = core_step(send)
    output_parts = join_chips(ids, tie([keep_d, keep_r], send), [came_d, came_r])
    project_parts = split_narrow(ids, tie(keep, output_parts), came)
    returned = narrow_return(project_parts)
    project_d_grad, pre_gain_d = unpack(
        ids, tie(delivered_d, project_parts), own_rows[1], own_rows[3]
    )
    stack = lax.all_to_all(tie(stack, project_parts), "wide", 0, 0)
    project_r = sum_parts(ids, tie(returned, project_d_grad))
    output_parts = narrow_terms(ids, tie(chips_return(output_parts), project_r))
    tokens_gradient = routed_post(
        ids,
        tie(stack, output_parts),
        project_routed,
        vecs,
        picked,
        g_mid_r,
        g_mixed,
        one_hot,
        g_gate,
    )
    output_total = sum_narrow(ids, output_parts, tokens_gradient)
    project_r_grad, pre_gain_r = unpack(
        ids,
        tie(deliver(ids, project_r, keep.shape[0]), output_total),
        own_rows[0],
        own_rows[2],
    )
    output_d_grad, output_r_grad, mid_r_grad, mid_d_grad, router_grad = spread_narrow(
        ids, output_total, width // wide_count, [width, width, 128], 3, project_r_grad
    )
    expand_d_grad, reduce_d_grad, expand_r_grad, reduce_r_grad = finish_hidden(
        ids, ffn_d, ffn_r
    )
    return (
        activations.reshape(tokens.shape),
        tokens_gradient.reshape(tokens.shape),
        router_grad,
        project_r_grad,
        output_r_grad,
        pre_gain_r,
        mid_r_grad,
        expand_r_grad,
        reduce_r_grad.T,
        project_d_grad,
        output_d_grad,
        pre_gain_d,
        mid_d_grad,
        expand_d_grad,
        reduce_d_grad.T,
    )


def solution(mesh):
    return jax.shard_map(
        on_device,
        mesh=mesh,
        in_specs=(
            P("narrow", "wide", None),
            P("narrow", "wide", None),
            P("narrow", None),
            P("narrow", None),
            P(),
            P(),
            P(),
            P(),
            P(),
            P(None, "narrow"),
            P("narrow", None),
            P(),
            P(),
            P(),
            P(),
            P(None, "narrow"),
            P("narrow", None),
        ),
        out_specs=(
            P("narrow", "wide", None),
            P("narrow", "wide", None),
            P("wide"),
            P("wide", None),
            P("wide", None),
            P("wide"),
            P("wide"),
            P("wide", "narrow"),
            P("narrow", "wide"),
            P("wide", None),
            P("wide", None),
            P("wide"),
            P("wide"),
            P("wide", "narrow"),
            P("narrow", "wide"),
        ),
        check_vma=False,
    )
```

```python
from functools import partial

import jax
import jax.numpy as jnp
from jax import lax
from jax.experimental import pallas as pl
from jax.experimental.pallas import tpu as pltpu
from jax.sharding import PartitionSpec as P

H = 12
HD = 64
GROUPS = 4
HG = H // GROUPS
GW = HG * HD

EPSILON = 1e-06
NEGATIVE = -1e30
SCORE_SCALE = 0.125
LOG2E = 1.4426950408889634
GELU_A = 0.7978845608028654
GELU_B = 0.044715
BF = jnp.bfloat16
F32 = jnp.float32
VMEM = 56 << 20


def nt_dot(left, right):
    return lax.dot_general(left, right, (((1,), (1,)), ((), ())), preferred_element_type=F32)


def tn_dot(left, right):
    return lax.dot_general(left, right, (((0,), (0,)), ((), ())), preferred_element_type=F32)


def dot(left, right):
    return jnp.dot(left, right, preferred_element_type=F32)


def sds(shape, dtype):
    return jax.ShapeDtypeStruct(shape, dtype)


def norm_scale(rows):
    return lax.rsqrt(jnp.mean(rows * rows, axis=-1, keepdims=True) + EPSILON)


def norm_back(grad, rows, gain):
    scale = norm_scale(rows)
    inner = grad * gain
    mean = jnp.mean(inner * rows, axis=-1, keepdims=True)
    grad_rows = scale * inner - rows * (scale * scale * scale * mean)
    return grad_rows, jnp.sum(grad * rows * scale, axis=0, keepdims=True)


def gelu(a):
    return 0.5 * a * (1.0 + jnp.tanh(GELU_A * (a + GELU_B * (a * a * a))))


def gelu_both(a):
    square = a * a
    bend = jnp.tanh(GELU_A * (a + GELU_B * (square * a)))
    half = 0.5 * (1.0 + bend)
    slope = half + 0.5 * a * (1.0 - bend * bend) * (GELU_A * (1.0 + 3.0 * GELU_B * square))
    return a * half, slope


def three_parts(x):
    first = x.astype(BF)
    rest = x - first.astype(F32)
    second = rest.astype(BF)
    third = (rest - second.astype(F32)).astype(BF)
    return [first, second, third]


def place(one_hot, x):
    return tn_dot(
        jnp.concatenate([one_hot] * 3, axis=0), jnp.concatenate(three_parts(x), axis=0)
    )


def pick(one_hot, x):
    return dot(jnp.concatenate([one_hot] * 3, axis=1), jnp.concatenate(three_parts(x), axis=0))


def combo(index):
    return lax.rem(lax.div(index, 2), GROUPS), lax.rem(index, 2)


def save_pieces(me, full, parts, pieces):
    rows = full.shape[0] // 2
    thirds = full.shape[1] // (GROUPS * GW)
    for c in range(GROUPS):
        for t in range(thirds):
            at = t * GROUPS * GW + c * GW
            parts[c, :, t * GW : (t + 1) * GW] = full[:, at : at + GW]
    for s, piece in enumerate(pieces):
        c, r = combo(me ^ s)
        piece[...] = parts[c, pl.ds(pl.multiple_of(r * rows, rows), rows), :]


def load_pieces(me, pieces, parts, thirds):
    rows = pieces[0].shape[0]
    for s, piece in enumerate(pieces):
        c, r = combo(me ^ s)
        parts[c, pl.ds(pl.multiple_of(r * rows, rows), rows), :] = piece[...]
    return jnp.concatenate(
        [parts[c, :, t * GW : (t + 1) * GW] for t in range(thirds) for c in range(GROUPS)],
        axis=1,
    )


def save_stack(full, parts, stack):
    rows = full.shape[0] // 2
    thirds = full.shape[1] // (GROUPS * GW)
    half, columns = rows // 2, thirds * GW
    for c in range(GROUPS):
        for t in range(thirds):
            at = t * GROUPS * GW + c * GW
            parts[c, :, t * GW : (t + 1) * GW] = full[:, at : at + GW]
    for b in range(stack.shape[0]):
        c, at = (b // 2) % GROUPS, (b % 2) * rows
        stack[b, :, 0:columns] = parts[c, at : at + half, :]
        stack[b, :, columns : 2 * columns] = parts[c, at + half : at + rows, :]


def load_stack(me, stack, parts, thirds):
    half, columns = stack.shape[1], stack.shape[2] // 2
    first = lax.div(me, 2 * GROUPS) * (2 * GROUPS)
    for w in range(2 * GROUPS):
        c, at = w // 2, (w % 2) * 2 * half
        parts[c, at : at + half, :] = stack[first + w, :, 0:columns]
        parts[c, at + half : at + 2 * half, :] = stack[first + w, :, columns : 2 * columns]
    return jnp.concatenate(
        [parts[c, :, t * GW : (t + 1) * GW] for t in range(thirds) for c in range(GROUPS)],
        axis=1,
    )


def stage(body, name, ids, operands, outs, scratch=(), flops=0, grid=None, specs=None):
    kwargs = {}
    if grid is not None:
        kwargs["grid"] = grid
    in_specs = [pl.BlockSpec(memory_space=pltpu.SMEM)]
    for k, operand in enumerate(operands):
        spec = None if specs is None else specs.get(k)
        if spec is None:
            zeros = (0,) * operand.ndim
            spec = pl.BlockSpec(operand.shape, lambda *_, z=zeros: z)
        in_specs.append(spec)
    out_specs = tuple(
        pl.BlockSpec(out.shape, lambda *_, z=(0,) * len(out.shape): z) for out in outs
    )
    moved = sum(a.size * a.dtype.itemsize for a in operands)
    moved += sum(math_prod(a.shape) * a.dtype.itemsize for a in outs)
    return pl.pallas_call(
        body,
        out_shape=tuple(outs),
        in_specs=in_specs,
        out_specs=out_specs,
        scratch_shapes=list(scratch),
        compiler_params=pltpu.CompilerParams(vmem_limit_bytes=VMEM),
        cost_estimate=pl.CostEstimate(flops=flops, bytes_accessed=moved, transcendentals=0),
        name=name,
        **kwargs,
    )(ids, *operands)


def math_prod(shape):
    total = 1
    for size in shape:
        total *= size
    return total


def head_parts(rows):
    lane = lax.broadcasted_iota(jnp.int32, rows.shape, 1)
    zero = jnp.zeros_like(rows)
    return [
        jnp.where((lane >= h * HD) & (lane < (h + 1) * HD), rows, zero) for h in range(HG)
    ]


def pair_mask(row_ref, col_ref, q_at, k_at, bk, bq):
    k_iota = lax.broadcasted_iota(jnp.int32, (bk, bq), 0) + k_at
    q_iota = lax.broadcasted_iota(jnp.int32, (bk, bq), 1) + q_at
    info = row_ref[0:1, pl.ds(q_at, bq)]
    if col_ref is None:
        return (k_iota >= info) & (k_iota <= q_iota)
    return (col_ref[pl.ds(k_at, bk), :] == info) & (k_iota <= q_iota)


def attend_kernel(bq, count, sends, stacked, by_column, ids, first_ref, row_ref, *rest):
    rest = list(rest)
    col_ref = rest.pop(0) if by_column else None
    pieces, rest = rest[:count], rest[count:]
    columns = rest.pop(0)
    out_pieces, rest = rest[:sends], rest[sends:]
    stack_ref = rest.pop(0) if stacked else None
    o_ref, lse_ref, x_ref, k_s, v_s, vt_s = rest
    i = pl.program_id(0)
    me = ids[0]
    rows = pieces[0].shape[0]
    bk = bq

    @pl.when(i == 0)
    def _():
        for s in range(count):
            at = pl.ds(pl.multiple_of((me ^ s) * rows, rows), rows)
            x = dot(pieces[s][...], columns[...]).astype(BF)
            x_ref[at, :] = x
            k_s[at, :] = x[:, GW : 2 * GW]
            v_s[at, :] = x[:, 2 * GW : 3 * GW]
        vt_s[...] = v_s[...].T

    q_at = pl.multiple_of(i * bq, bq)
    q_heads = head_parts(x_ref[pl.ds(q_at, bq), 0:GW])

    def step(j, carry):
        k_at = pl.multiple_of(j * bk, bk)
        keys = k_s[pl.ds(k_at, bk), :]
        mask = pair_mask(row_ref, col_ref, q_at, k_at, bk, bq)
        out = []
        for h in range(HG):
            top, total, acc = carry[h]
            scores = nt_dot(keys, q_heads[h]) * (SCORE_SCALE * LOG2E)
            scores = jnp.where(mask, scores, NEGATIVE)
            top_new = jnp.maximum(top, jnp.max(scores, axis=0, keepdims=True))
            weight = jnp.exp2(scores - top_new)
            fade = jnp.exp2(top - top_new)
            total = total * fade + jnp.sum(weight, axis=0, keepdims=True)
            values_t = vt_s[h * HD : (h + 1) * HD, pl.ds(k_at, bk)]
            acc = acc * fade + dot(values_t, weight.astype(BF))
            out.append((top_new, total, acc))
        return tuple(out)

    start = tuple(
        (
            jnp.full((1, bq), NEGATIVE, F32),
            jnp.zeros((1, bq), F32),
            jnp.zeros((HD, bq), F32),
        )
        for _ in range(HG)
    )
    done = lax.fori_loop(first_ref[i], i + 1, step, start)
    outs = jnp.concatenate([acc / total for _, total, acc in done], axis=0)
    o_ref[pl.ds(q_at, bq), :] = outs.T.astype(BF)
    for h in range(HG):
        top, total, _ = done[h]
        lse_ref[h : h + 1, pl.ds(q_at, bq)] = top + jnp.log2(total)

    @pl.when(i == pl.num_programs(0) - 1)
    def _():
        for s in range(sends):
            at = pl.ds(pl.multiple_of((me ^ s) * rows, rows), rows)
            out_pieces[s][...] = o_ref[at, :]
        if stacked:
            half = rows // 2
            for b in range(count):
                at = b * rows
                stack_ref[b, :, 0:GW] = o_ref[at : at + half, :]
                stack_ref[b, :, GW : 2 * GW] = o_ref[at + half : at + rows, :]


def attend_back_kernel(bq, count, sends, stacked, by_column, ids, first_ref, row_ref, *rest):
    rest = list(rest)
    col_ref = rest.pop(0) if by_column else None
    x_ref = rest.pop(0)
    given = 1 if stacked else count
    grads, rest = rest[:given], rest[given:]
    o_ref, lse_ref = rest[:2]
    out_pieces, rest = rest[2 : 2 + sends], rest[2 + sends :]
    stack_ref = rest.pop(0) if stacked else None
    dx_ref, k_s, v_s, g_s, dk_s, dv_s = rest
    i = pl.program_id(0)
    me = ids[0]
    rows = g_s.shape[0] // count
    bk = bq

    @pl.when(i == 0)
    def _():
        k_s[...] = x_ref[:, GW : 2 * GW]
        v_s[...] = x_ref[:, 2 * GW : 3 * GW]
        for s in range(count):
            if stacked:
                half = rows // 2
                g_s[s * rows : s * rows + half, :] = grads[0][s, :, 0:GW]
                g_s[s * rows + half : (s + 1) * rows, :] = grads[0][s, :, GW : 2 * GW]
            else:
                at = pl.ds(pl.multiple_of((me ^ s) * rows, rows), rows)
                g_s[at, :] = grads[s][...]
        dk_s[...] = jnp.zeros_like(dk_s)
        dv_s[...] = jnp.zeros_like(dv_s)

    q_at = pl.multiple_of(i * bq, bq)
    grad = g_s[pl.ds(q_at, bq), :]
    q_heads = head_parts(x_ref[pl.ds(q_at, bq), 0:GW])
    g_heads = head_parts(grad)
    dots = (grad.astype(F32) * o_ref[pl.ds(q_at, bq), :].astype(F32)).T
    row_dot = [
        jnp.sum(dots[h * HD : (h + 1) * HD, :], axis=0, keepdims=True) for h in range(HG)
    ]
    lse = [lse_ref[h : h + 1, pl.ds(q_at, bq)] for h in range(HG)]

    def step(j, dq):
        k_at = pl.multiple_of(j * bk, bk)
        here = pl.ds(k_at, bk)
        keys = k_s[here, :]
        values = v_s[here, :]
        key_heads = head_parts(keys)
        mask = pair_mask(row_ref, col_ref, q_at, k_at, bk, bq)
        dk = dk_s[here, :]
        dv = dv_s[here, :]
        for h in range(HG):
            scores = nt_dot(keys, q_heads[h]) * (SCORE_SCALE * LOG2E)
            scores = jnp.where(mask, scores - lse[h], NEGATIVE)
            soft = jnp.exp2(scores)
            g_soft = nt_dot(values, g_heads[h])
            g_scores = (soft * (g_soft - row_dot[h])).astype(BF)
            dv = dv + dot(soft.astype(BF), g_heads[h])
            dk = dk + dot(g_scores, q_heads[h])
            dq = dq + tn_dot(g_scores, key_heads[h])
        dk_s[here, :] = dk
        dv_s[here, :] = dv
        return dq

    dq = lax.fori_loop(first_ref[i], i + 1, step, jnp.zeros((bq, GW), F32))
    dx_ref[pl.ds(q_at, bq), 0:GW] = (dq * SCORE_SCALE).astype(BF)

    @pl.when(i == pl.num_programs(0) - 1)
    def _():
        dx_ref[:, GW : 2 * GW] = (dk_s[...] * SCORE_SCALE).astype(BF)
        dx_ref[:, 2 * GW : 3 * GW] = dv_s[...].astype(BF)
        for s in range(sends):
            at = pl.ds(pl.multiple_of((me ^ s) * rows, rows), rows)
            out_pieces[s][...] = dx_ref[at, :]
        if stacked:
            half = rows // 2
            for b in range(count):
                at = b * rows
                stack_ref[b, :, 0 : 3 * GW] = dx_ref[at : at + half, :]
                stack_ref[b, :, 3 * GW : 6 * GW] = dx_ref[at + half : at + rows, :]


def attend(ids, meta, pieces, columns, bq, stacked=False):
    first, row_info, col_info = meta
    rows, width = pieces[0].shape
    count = len(pieces)
    sends = 0 if stacked else min(count, 2 * GROUPS)
    length = rows * count
    operands = [first, row_info] + ([] if col_info is None else [col_info])
    operands += list(pieces) + [columns]
    outs = [sds((rows, GW), BF)] * sends
    outs += [sds((count, rows // 2, 2 * GW), BF)] if stacked else []
    outs += [
        sds((length, GW), BF),
        sds((8, length), F32),
        sds((length, 3 * GW), BF),
    ]
    got = stage(
        partial(attend_kernel, bq, count, sends, stacked, col_info is not None),
        "attend",
        ids,
        operands,
        outs,
        [pltpu.VMEM((length, GW), BF)] * 2 + [pltpu.VMEM((GW, length), BF)],
        flops=length * length * GW * 2 + 6 * length * width * GW,
        grid=(length // bq,),
        specs={0: pl.BlockSpec(memory_space=pltpu.SMEM)},
    )
    return got[:-3], got[-3:]


def attend_back(ids, meta, kept, grads, bq, stacked=False):
    first, row_info, col_info = meta
    attended, lse, x = kept
    count = grads[0].shape[0] if stacked else len(grads)
    rows = attended.shape[0] // count
    sends = 0 if stacked else min(count, 2 * GROUPS)
    length = rows * count
    operands = [first, row_info] + ([] if col_info is None else [col_info])
    operands += [x] + list(grads) + [attended, lse]
    got = stage(
        partial(attend_back_kernel, bq, count, sends, stacked, col_info is not None),
        "attend_back",
        ids,
        operands,
        [sds((rows, 3 * GW), BF)] * sends
        + ([sds((count, rows // 2, 6 * GW), BF)] if stacked else [])
        + [sds(x.shape, BF)],
        [pltpu.VMEM((length, GW), BF)] * 3 + [pltpu.VMEM((length, GW), F32)] * 2,
        flops=length * length * GW * 5,
        grid=(length // bq,),
        specs={0: pl.BlockSpec(memory_space=pltpu.SMEM)},
    )
    return got[:-1], got[-1]


def project_grads_kernel(count, ids, dx_ref, *rest):
    pieces, (keep, send, total) = rest[:count], rest[count:]
    rows = pieces[0].shape[0]
    for s, piece in enumerate(pieces):
        at = pl.ds(pl.multiple_of((ids[0] ^ s) * rows, rows), rows)
        term = tn_dot(piece[...], dx_ref[at, :])
        total[...] = term if s == 0 else total[...] + term
    split_rows(ids[0], total, keep, send)


def project_grads(ids, wide_count, pieces, dx):
    rows, width = pieces[0].shape
    shape = (wide_count // 2, width // wide_count, 3 * GW)
    return stage(
        partial(project_grads_kernel, len(pieces)),
        "project_grads",
        ids,
        [dx] + list(pieces),
        [sds(shape, BF)] * 2,
        [pltpu.VMEM((width, 3 * GW), F32)],
        flops=6 * dx.size * width // 3,
    )


def group_columns_kernel(ids, project, out):
    group, _ = combo(ids[0])
    width = GROUPS * GW
    for c in range(GROUPS):

        @pl.when(group == c)
        def _():
            for t in range(3):
                at = t * width + c * GW
                out[:, t * GW : (t + 1) * GW] = project[:, at : at + GW]


def group_columns(ids, project):
    (out,) = stage(
        group_columns_kernel,
        "group_columns",
        ids,
        [project],
        [sds((project.shape[0], 3 * GW), BF)],
    )
    return out


def save_halves(me, normed, mine_ref, other_ref):
    rows = mine_ref.shape[0]
    core = lax.rem(me, 2)
    mine_ref[...] = normed[pl.ds(pl.multiple_of(core * rows, rows), rows), :]
    other_ref[...] = normed[pl.ds(pl.multiple_of((1 - core) * rows, rows), rows), :]


def routed_pre_kernel(count, ids, tok, sel, *rest):
    vectors, rest = rest[:count], rest[count:]
    mine_ref, other_ref, one_hot_ref, picked_ref, vecs, normed = rest
    rows = [vector[...].astype(F32).reshape(1, -1) for vector in vectors]
    rows.append(jnp.zeros((8 - count, tok.shape[1]), F32))
    vecs[...] = jnp.concatenate(rows, axis=0)
    span = one_hot_ref.shape[1]
    seqs = sel.shape[0]
    if sel.shape[1] != span:
        sel = sel[:, pl.ds(pl.multiple_of(ids[0] * span, span), span)]
    slots = span // 4
    upper = (
        lax.broadcasted_iota(jnp.int32, (span, span), 0)
        <= lax.broadcasted_iota(jnp.int32, (span, span), 1)
    ).astype(F32).astype(BF)
    slot = lax.broadcasted_iota(jnp.int32, (slots, span), 0).astype(F32)
    for q in range(seqs):
        chosen = jnp.broadcast_to(sel[q : q + 1, :].astype(F32), (8, span))
        rank = dot(chosen.astype(BF), upper)[0:1, :] * chosen[0:1, :] - 1.0
        one_hot = (slot == rank).astype(F32).astype(BF)
        one_hot_ref[q * slots : (q + 1) * slots, :] = one_hot
        picked_ref[q * slots : (q + 1) * slots, :] = dot(
            one_hot, tok[q * span : (q + 1) * span, :]
        ).astype(BF)
    picked = picked_ref[...].astype(F32)
    normed[...] = (picked * norm_scale(picked) * gain_of(vecs, 1)).astype(BF)
    save_halves(ids[0], normed, mine_ref, other_ref)


def gain_of(vecs, k):
    return vecs[k : k + 1, :]


def routed_pre(ids, tok, sel, span, vectors):
    rows, width = tok.shape[0] // 4, tok.shape[1]
    return stage(
        partial(routed_pre_kernel, len(vectors)),
        "routed_pre",
        ids,
        [tok, sel] + vectors,
        [
            sds((rows // 2, width), BF),
            sds((rows // 2, width), BF),
            sds((rows, span), BF),
            sds((rows, width), BF),
            sds((8, width), F32),
        ],
        [pltpu.VMEM((rows, width), BF)],
        flops=4 * rows * width * span,
    )


def routed_mid_kernel(count, ids, *rest):
    pieces = rest[:count]
    output, picked, vecs, branch_ref, low_ref, att_ref, parts = rest[count:]
    attended = load_pieces(ids[0], pieces, parts, 1)
    att_ref[...] = attended
    branch = dot(attended, output[...])
    branch_ref[...] = branch
    middle = picked[...].astype(F32) + branch
    low_ref[...] = (middle * norm_scale(middle) * gain_of(vecs, 2)).astype(BF)


def routed_mid(ids, pieces, output, picked, vecs):
    shape = picked.shape
    return stage(
        partial(routed_mid_kernel, len(pieces)),
        "routed_mid",
        ids,
        list(pieces) + [output, picked, vecs],
        [sds(shape, F32), sds(shape, BF), sds(shape, BF)],
        [pltpu.VMEM((GROUPS, shape[0], GW), BF)],
        flops=2 * shape[0] * shape[1] * shape[1],
    )


def hidden_forward_kernel(count, ids, *rest):
    pieces = rest[:count]
    expand, reduce_ref = rest[count : count + 2]
    outs = rest[count + 2 :]
    rows = pieces[0].shape[0]
    low = jnp.concatenate([piece[...] for piece in pieces], axis=0)
    hidden = gelu(dot(low, expand[...])).astype(BF)
    total = dot(hidden, reduce_ref[...]).astype(BF)
    for s, out in enumerate(outs):
        out[...] = total[s * rows : (s + 1) * rows, :]


def hidden_forward(ids, pieces, expand, reduce_part):
    return stage(
        partial(hidden_forward_kernel, len(pieces)),
        "hidden_forward",
        ids,
        list(pieces) + [expand, reduce_part],
        [sds(pieces[0].shape, BF)] * len(pieces),
        flops=4 * len(pieces) * pieces[0].size * expand.shape[1],
    )


def dense_pre_kernel(shares, ids, tok, one_hot, picked, vecs, branch, *rest):
    partials = rest[:shares]
    mine_ref, other_ref, mixed_ref, delta_ref, normed = rest[shares:]
    slots, span = one_hot.shape[0] // 2, one_hot.shape[1]
    delta = branch[...]
    for share in partials:
        delta = delta + share[...].astype(F32)
    delta_ref[...] = delta
    gate = jnp.sum(picked[...].astype(F32) * gain_of(vecs, 0), axis=-1, keepdims=True)
    lifted = gate * delta
    for q in range(2):
        at, spots = slice(q * span, (q + 1) * span), slice(q * slots, (q + 1) * slots)
        mixed = tok[at, :].astype(F32) + place(one_hot[spots, :], lifted[spots, :])
        mixed_ref[at, :] = mixed
        normed[at, :] = (mixed * norm_scale(mixed) * gain_of(vecs, 3)).astype(BF)
    save_halves(ids[0], normed, mine_ref, other_ref)


def dense_pre(ids, tok, one_hot, picked, vecs, branch, partials):
    rows, width = tok.shape
    return stage(
        partial(dense_pre_kernel, len(partials)),
        "dense_pre",
        ids,
        [tok, one_hot, picked, vecs, branch] + list(partials),
        [
            sds((rows // 2, width), BF),
            sds((rows // 2, width), BF),
            sds(tok.shape, F32),
            sds(picked.shape, F32),
        ],
        [pltpu.VMEM((rows, width), BF)],
        flops=6 * rows * width * one_hot.shape[0],
    )


def this_part(me, weights, scratch):
    if not scratch:
        return weights[0][0], weights[1][0]
    e_s, r_s = scratch
    core = lax.rem(me, 2)
    rows = weights[0].shape[-2]
    if len(weights) == 2:
        blocks = []
        for c in range(weights[0].shape[0]):
            blocks.append((weights[0], c, 2 * c + core))
            blocks.append((weights[1], c, 2 * c + 1 - core))
    else:
        blocks = [(weight, 0, me ^ s) for s, weight in enumerate(weights)]
    for weight, c, at in blocks:
        at = pl.ds(pl.multiple_of(at * rows, rows), rows)
        e_s[at, :] = weight[c, 0, 0]
        r_s[at, :] = weight[c, 0, 1]
    return e_s[...], r_s[...]


def part_specs(base, weights):
    if weights[0].ndim == 3:
        return {
            base + k: pl.BlockSpec((1,) + w.shape[1:], lambda n: (n, 0, 0))
            for k, w in enumerate(weights)
        }
    return {
        base + k: pl.BlockSpec(
            (w.shape[0], 1) + w.shape[2:], lambda n: (0, n, 0, 0, 0)
        )
        for k, w in enumerate(weights)
    }


def part_scratch(width, weights):
    if weights[0].ndim == 3:
        return []
    return [pltpu.VMEM((width, weights[0].shape[-1]), BF)] * 2


def dense_ffn_kernel(split, ids, stack, *rest):
    output, mixed, cot, vecs = rest[:4]
    gain = gain_of(vecs, 4)
    rest = rest[4:]
    weights, rest = rest[:split], rest[split:]
    act_ref, low_ref, back_ref, sum_ref, att_ref, gain_ref = rest[:6]
    g_stack, rest = rest[6], rest[7:]
    parts, branch_s, delta_s, grad_s = rest[:4]
    n = pl.program_id(0)
    me = ids[0]

    @pl.when(n == 0)
    def _():
        attended = load_stack(me, stack, parts, 1)
        att_ref[...] = attended
        branch = dot(attended, output[...])
        branch_s[...] = branch
        middle = mixed[...] + branch
        low_ref[...] = (middle * norm_scale(middle) * gain).astype(BF)
        delta_s[...] = jnp.zeros_like(delta_s)
        grad_s[...] = jnp.zeros_like(grad_s)

    expand, reduce_w = this_part(me, weights, rest[4:])
    value, slope = gelu_both(dot(low_ref[...], expand))
    delta_s[...] += dot(value.astype(BF), reduce_w)
    grad_pre = (nt_dot(cot[...], reduce_w) * slope).astype(BF)
    grad_s[...] += nt_dot(grad_pre, expand)

    @pl.when(n == pl.num_programs(0) - 1)
    def _():
        middle = mixed[...] + branch_s[...]
        act_ref[...] = (middle + delta_s[...]).astype(BF)
        grad_middle, gain_grad = norm_back(grad_s[...], middle, gain)
        gain_ref[...] = jnp.broadcast_to(gain_grad, gain_ref.shape)
        total = cot[...].astype(F32) + grad_middle
        sum_ref[...] = total
        back = total.astype(BF)
        back_ref[...] = back
        save_stack(nt_dot(back, output[...]).astype(BF), parts, g_stack)


def dense_ffn(ids, stack, output, mixed, cot, vecs, weights):
    rows, width = mixed.shape
    split = len(weights)
    parts_n = weights[0].shape[0 if weights[0].ndim == 3 else 1]
    hidden = weights[0].shape[-1]
    base = 5
    specs = part_specs(base, weights)
    scratch = [pltpu.VMEM((GROUPS, rows, GW), BF)] + [pltpu.VMEM((rows, width), F32)] * 3
    scratch += part_scratch(width, weights)
    outs = [
        sds((rows, width), BF),
        sds((rows, width), BF),
        sds((rows, width), BF),
        sds((rows, width), F32),
        sds((rows, width), BF),
        sds((8, width), F32),
        sds(stack.shape, BF),
    ]
    got = stage(
        partial(dense_ffn_kernel, split),
        "dense_ffn",
        ids,
        [stack, output, mixed, cot, vecs] + list(weights),
        outs,
        scratch,
        flops=8 * rows * width * hidden * parts_n + 4 * rows * width * width,
        grid=(parts_n,),
        specs=specs,
    )
    return got[:6], got[6]


def dense_post_kernel(ids, stack, *rest):
    project, vecs, mixed, total, one_hot, picked, delta = rest[:7]
    g_mixed_ref, g_delta_ref, g_low_ref, g_gate_ref, router_ref, parts = rest[7:]
    g_proj = load_stack(ids[0], stack, parts, 3)
    grad_rows, _ = norm_back(nt_dot(g_proj, project[...]), mixed[...], gain_of(vecs, 3))
    g_mixed_ref[...] = total[...] + grad_rows
    slots, span = one_hot.shape[0] // 2, one_hot.shape[1]
    rows = picked[...].astype(F32)
    gate = jnp.sum(rows * gain_of(vecs, 0), axis=-1, keepdims=True)
    router = jnp.zeros((1, rows.shape[1]), F32)
    for q in range(2):
        at, spots = slice(q * span, (q + 1) * span), slice(q * slots, (q + 1) * slots)
        lifted = pick(one_hot[spots, :], g_mixed_ref[at, :])
        g_delta = gate[spots, :] * lifted
        g_delta_ref[spots, :] = g_delta
        g_low_ref[spots, :] = g_delta.astype(BF)
        g_gate = jnp.sum(lifted * delta[spots, :], axis=-1, keepdims=True)
        g_gate_ref[spots, :] = jnp.broadcast_to(g_gate, (slots, g_gate_ref.shape[1]))
        router = router + jnp.sum(rows[spots, :] * g_gate, axis=0, keepdims=True)
    router_ref[...] = jnp.broadcast_to(router, router_ref.shape)


def dense_post(ids, stack, project, vecs, mixed, total, one_hot, picked, delta):
    rows, width = mixed.shape
    return stage(
        dense_post_kernel,
        "dense_post",
        ids,
        [stack, project, vecs, mixed, total, one_hot, picked, delta],
        [
            sds((rows, width), F32),
            sds(picked.shape, F32),
            sds(picked.shape, BF),
            sds((picked.shape[0], 128), F32),
            sds((8, width), F32),
        ],
        [pltpu.VMEM((GROUPS, rows, 3 * GW), BF)],
        flops=6 * rows * width * width,
    )


def routed_back_kernel(split, ids, low, g_low, branch, picked, vecs, g_delta, output, *rest):
    weights, rest = rest[:split], rest[split:]
    g_mid_ref, back_ref, gain_ref, stack, parts, grad_s = rest[:6]
    n = pl.program_id(0)

    @pl.when(n == 0)
    def _():
        grad_s[...] = jnp.zeros_like(grad_s)

    expand, reduce_w = this_part(ids[0], weights, rest[6:])
    _, slope = gelu_both(dot(low[...], expand))
    grad_pre = (nt_dot(g_low[...], reduce_w) * slope).astype(BF)
    grad_s[...] += nt_dot(grad_pre, expand)

    @pl.when(n == pl.num_programs(0) - 1)
    def _():
        middle = picked[...].astype(F32) + branch[...]
        g_middle, gain_grad = norm_back(grad_s[...], middle, gain_of(vecs, 2))
        gain_ref[...] = jnp.broadcast_to(gain_grad, gain_ref.shape)
        g_mid_ref[...] = g_middle
        back = (g_delta[...] + g_middle).astype(BF)
        back_ref[...] = back
        save_stack(nt_dot(back, output[...]).astype(BF), parts, stack)


def routed_back(ids, wide_count, low, g_low, branch, picked, vecs, g_delta, output, weights):
    rows, width = branch.shape
    parts_n = weights[0].shape[0 if weights[0].ndim == 3 else 1]
    return stage(
        partial(routed_back_kernel, len(weights)),
        "routed_back",
        ids,
        [low, g_low, branch, picked, vecs, g_delta, output] + list(weights),
        [
            sds((rows, width), F32),
            sds((rows, width), BF),
            sds((8, width), F32),
            sds((wide_count, rows // 4, 2 * GW), BF),
        ],
        [pltpu.VMEM((GROUPS, rows, GW), BF), pltpu.VMEM((rows, width), F32)]
        + part_scratch(width, weights),
        flops=6 * rows * width * parts_n * weights[0].shape[-1],
        grid=(parts_n,),
        specs=part_specs(7, weights),
    )


def routed_post_kernel(ids, stack, *rest):
    project, vecs, picked, g_mid, g_mixed, one_hot, g_gate = rest[:7]
    out_ref, parts = rest[7:]
    g_proj = load_stack(ids[0], stack, parts, 3)
    rows = picked[...].astype(F32)
    grad_rows, _ = norm_back(nt_dot(g_proj, project[...]), rows, gain_of(vecs, 1))
    spread = g_mid[...] + grad_rows + g_gate[:, 0:1] * gain_of(vecs, 0)
    slots, span = one_hot.shape[0] // 2, one_hot.shape[1]
    for q in range(2):
        at, spots = slice(q * span, (q + 1) * span), slice(q * slots, (q + 1) * slots)
        out_ref[at, :] = g_mixed[at, :] + place(one_hot[spots, :], spread[spots, :])


def routed_post(ids, stack, project, vecs, picked, g_mid, g_mixed, one_hot, g_gate):
    rows, width = picked.shape
    (out,) = stage(
        routed_post_kernel,
        "routed_post",
        ids,
        [stack, project, vecs, picked, g_mid, g_mixed, one_hot, g_gate],
        [sds(g_mixed.shape, F32)],
        [pltpu.VMEM((GROUPS, rows, 3 * GW), BF)],
        flops=6 * rows * width * width,
    )
    return out


def split_rows(me, total, keep, send):
    chips, rows = keep.shape[0], keep.shape[1]
    core = lax.rem(me, 2)
    for c in range(chips):
        mine = pl.multiple_of((2 * c + core) * rows, rows)
        other = pl.multiple_of((2 * c + 1 - core) * rows, rows)
        keep[c] = total[pl.ds(mine, rows), :].astype(BF)
        send[c] = total[pl.ds(other, rows), :].astype(BF)


def hidden_grads_kernel(ids, low, grad, expand, reduce_ref, out, total):
    i = pl.program_id(0)
    hidden = expand.shape[1]

    @pl.when(i == 0)
    def _():
        total[...] = jnp.zeros_like(total)

    value, slope = gelu_both(dot(low[...], expand[...]))
    grad_pre = (nt_dot(grad[...], reduce_ref[...]) * slope).astype(BF)
    total[:, 0:hidden] += tn_dot(low[...], grad_pre)
    total[:, hidden : 2 * hidden] += tn_dot(grad[...], value.astype(BF))

    @pl.when(i == pl.num_programs(0) - 1)
    def _():
        out[...] = total[...].astype(BF)


def hidden_grads(ids, low, grad, expand, reduce_part):
    width, hidden = expand.shape
    block = min(512, low.shape[0])
    row_spec = pl.BlockSpec((block, width), lambda i: (i, 0))
    (out,) = stage(
        hidden_grads_kernel,
        "hidden_grads",
        ids,
        [low, grad, expand, reduce_part],
        [sds((width, 2 * hidden), BF)],
        [pltpu.VMEM((width, 2 * hidden), F32)],
        flops=8 * low.size * hidden,
        grid=(low.shape[0] // block,),
        specs={0: row_spec, 1: row_spec},
    )
    return out


def output_grads_kernel(vectors, ids, att, back, *rest):
    rest = list(rest)
    vecs, rest = rest[:vectors], rest[vectors:]
    keep, send, total = rest
    width = att.shape[1]
    total[:, 0:width] = tn_dot(att[...], back[...])
    if vectors:
        rows = [vec[0:1, :] for vec in vecs]
        rows.append(jnp.zeros((128 - vectors, width), F32))
        total[:, width : width + 128] = jnp.concatenate(rows, axis=0).T
    split_rows(ids[0], total, keep, send)


def output_grads(ids, wide_count, att, back, vecs):
    rows, width = att.shape
    columns = width + (128 if vecs else 0)
    shape = (wide_count // 2, width // wide_count, columns)
    return stage(
        partial(output_grads_kernel, len(vecs)),
        "output_grads",
        ids,
        [att, back] + list(vecs),
        [sds(shape, BF), sds(shape, BF)],
        [pltpu.VMEM((width, columns), F32)],
        flops=3 * rows * width * width,
    )


def join_kernel(pairs, ids, *rest):
    keeps, cames, outs = rest[:pairs], rest[pairs : 2 * pairs], rest[2 * pairs :]
    chip = lax.div(ids[0], 2)
    for s, out in enumerate(outs):
        low = 0
        for keep, came in zip(keeps, cames):
            columns = keep.shape[2]
            total = keep[chip ^ s].astype(F32) + came[chip ^ s].astype(F32)
            out[:, low : low + columns] = total.astype(BF)
            low += columns


def join_chips(ids, keeps, cames):
    chips, rows = keeps[0].shape[:2]
    columns = sum(keep.shape[2] for keep in keeps)
    return stage(
        partial(join_kernel, len(keeps)),
        "join",
        ids,
        list(keeps) + list(cames),
        [sds((rows, columns), BF)] * chips,
    )


def chips_return(parts):
    return [parts[0]] + [chip_step(parts[s], s) for s in range(1, len(parts))]


def sum_terms(terms):
    total = terms[0].astype(F32)
    for term in terms[1:]:
        total = total + term.astype(F32)
    return total


def sum_split_kernel(count, ids, *rest):
    terms, outs, total = rest[:count], rest[count:-1], rest[-1]
    got = terms[0][...].astype(F32)
    for term in terms[1:]:
        got = got + term[...].astype(F32)
    total[...] = got
    rows = outs[0].shape[0]
    for s, out in enumerate(outs):
        at = pl.multiple_of((ids[1] ^ s) * rows, rows)
        out[...] = total[pl.ds(at, rows), :].astype(BF)


def sum_kernel(ids, *rest):
    got = rest[0][...].astype(F32)
    for term in rest[1:-1]:
        got = got + term[...].astype(F32)
    rest[-1][...] = got.astype(BF)


def gather_out_kernel(count, vectors, ids, *rest):
    pieces, outs = rest[:count], rest[count : -1 - vectors]
    vecs, wide_s = rest[-1 - vectors : -1], rest[-1]
    rows = pieces[0].shape[0]
    for s, piece in enumerate(pieces):
        at = pl.ds(pl.multiple_of((ids[1] ^ s) * rows, rows), rows)
        low = 0
        for out in outs:
            columns = out.shape[1]
            out[at, :] = piece[:, low : low + columns].astype(F32)
            low += columns
        wide_s[at, :] = piece[:, low:].astype(F32)
    turned = wide_s[...].T
    for k, vec in enumerate(vecs):
        vec[...] = turned[k : k + 1, :].reshape(vec.shape[0])


def narrow_terms(ids, terms):
    narrow_count = lax.axis_size("narrow")
    rows, columns = terms[0].shape
    if rows % (8 * narrow_count):
        return [sum_terms(terms).astype(BF)]
    return stage(
        partial(sum_split_kernel, len(terms)),
        "sum_split",
        ids,
        terms,
        [sds((rows // narrow_count, columns), BF)] * narrow_count,
        [pltpu.VMEM((rows, columns), F32)],
    )


def sum_narrow(ids, parts, first):
    if len(parts) == 1:
        return lax.psum(parts[0], "narrow")
    return sum_parts(ids, tie(narrow_return(parts), first))


def spread_narrow(ids, total, rows, widths, vectors, first):
    narrow_count = lax.axis_size("narrow")
    if total.shape[0] == rows:
        total = total.astype(F32)
        outs, low = [], 0
        for size in widths:
            outs.append(total[:, low : low + size])
            low += size
        return outs[:-1] + [outs[-1][:, k] for k in range(vectors)]
    return stage(
        partial(gather_out_kernel, narrow_count, vectors),
        "gather_out",
        ids,
        tie(narrow_gather(total), first),
        [sds((rows, size), F32) for size in widths[:-1]] + [sds((rows,), F32)] * vectors,
        [pltpu.VMEM((rows, widths[-1]), F32)],
    )


def join_narrow_kernel(turned, ids, keep, came, *outs):
    each = outs[0].shape[0]
    turn = lax.div(ids[0], 2) if turned else 0
    for t, out in enumerate(outs):
        for j in range(each):
            at = ((ids[1] ^ t) * each + j) ^ turn
            out[j] = (keep[at].astype(F32) + came[at].astype(F32)).astype(BF)


def route_kernel(count, ids, *rest):
    pieces, outs, blocks = rest[:count], rest[count:-1], rest[-1]
    each = pieces[0].shape[0]
    for t, piece in enumerate(pieces):
        for j in range(each):
            blocks[(ids[1] ^ t) * each + j] = piece[j]
    chip = lax.div(ids[0], 2)
    for s, out in enumerate(outs):
        out[...] = blocks[chip ^ s]


def unpack_kernel(turned, ids, *rest):
    pieces, (own, gain, out, gain_out, parts) = rest[:GROUPS], rest[GROUPS:]
    at = lax.div(ids[0], 2)
    if turned:
        at = at ^ ids[1]
    rows = out.shape[0]
    for s, piece in enumerate(pieces):
        parts[lax.rem(at ^ s, GROUPS)] = piece[...].astype(F32)
    total = jnp.zeros((rows, GW), F32)
    for t in range(3):
        for c in range(GROUPS):
            low = (t * GROUPS + c) * GW
            part = parts[c, :, t * GW : (t + 1) * GW]
            out[:, low : low + GW] = part
            total = total + part * own[:, low : low + GW].astype(F32)
    sums = jnp.broadcast_to(jnp.sum(total, axis=1, keepdims=True), (rows, 128)).T
    gain_out[...] = (sums[0:1, :] / gain[...]).reshape(rows)


def unpack(ids, pieces, own, gain):
    rows, columns = pieces[0].shape
    return stage(
        partial(unpack_kernel, direct_delivery()),
        "unpack",
        ids,
        list(pieces) + [own, gain],
        [sds((rows, GROUPS * columns), F32), sds((rows,), F32)],
        [pltpu.VMEM((GROUPS, rows, columns), F32)],
    )


def split_narrow(ids, keep, came):
    narrow_count = lax.axis_size("narrow")
    chips, rows, columns = keep.shape
    shape = (chips // narrow_count, rows, columns)
    return stage(
        partial(join_narrow_kernel, direct_delivery()),
        "join_narrow",
        ids,
        [keep, came],
        [sds(shape, BF)] * narrow_count,
    )


def join_all_kernel(turned, ids, keep, came, out):
    turn = lax.div(ids[0], 2) if turned else 0
    for n in range(out.shape[0]):
        out[n] = (keep[n ^ turn].astype(F32) + came[n ^ turn].astype(F32)).astype(BF)


def join_all(ids, keep, came):
    (total,) = stage(
        partial(join_all_kernel, direct_delivery()),
        "join_all",
        ids,
        [keep, came],
        [sds(keep.shape, BF)],
    )
    return total


def sum_parts(ids, terms):
    (total,) = stage(sum_kernel, "sum_terms", ids, terms, [sds(terms[0].shape, BF)])
    return total


def route_project(ids, gathered, chips):
    rows, columns = gathered[0].shape[1:]
    return stage(
        partial(route_kernel, len(gathered)),
        "route",
        ids,
        gathered,
        [sds((rows, columns), BF)] * GROUPS,
        [pltpu.VMEM((chips, rows, columns), BF)],
    )


def direct_delivery():
    return lax.axis_size("narrow") == GROUPS and lax.axis_size("wide") == 2 * GROUPS


def deliver(ids, total, chips):
    narrow_count = lax.axis_size("narrow")
    if not direct_delivery():
        return chips_return(route_project(ids, narrow_gather(total), chips))
    total = total[0]

    def moves(k):
        pairs = []
        for chip in range(chips):
            for core in range(2):
                for n in range(narrow_count):
                    to = (2 * (chip ^ n) + core) * narrow_count + (n ^ k)
                    pairs.append(((2 * chip + core) * narrow_count + n, to))
        return pairs

    return [lax.ppermute(total, ("wide", "narrow"), moves(k)) for k in range(narrow_count)]


def finish_hidden_kernel(ids, dense, routed, e_d, r_d, e_r, r_r):
    hidden = e_d.shape[1]
    for total, e_ref, r_ref in ((dense, e_d, r_d), (routed, e_r, r_r)):
        e_ref[...] = total[:, 0:hidden].astype(F32)
        r_ref[...] = total[:, hidden : 2 * hidden].astype(F32)


def finish_hidden(ids, dense, routed):
    rows, columns = dense.shape
    return stage(
        finish_hidden_kernel,
        "finish_hidden",
        ids,
        [dense, routed],
        [sds((rows, columns // 2), F32)] * 4,
    )


def tie(x, *first):
    return lax.optimization_barrier((x, first))[0]


def narrow_step(x, s):
    return lax.ppermute(x, "narrow", [(j, j ^ s) for j in range(lax.axis_size("narrow"))])


def narrow_gather(x):
    return [x] + [narrow_step(x, s) for s in range(1, lax.axis_size("narrow"))]


def narrow_return(parts):
    return [parts[0]] + [narrow_step(parts[s], s) for s in range(1, len(parts))]


def exchange(pieces):
    wide_count = lax.axis_size("wide")
    return [pieces[0]] + [
        lax.ppermute(pieces[s], "wide", [(j, j ^ s) for j in range(wide_count)])
        for s in range(1, len(pieces))
    ]


def exchange_rows(mine, other):
    wide_count = lax.axis_size("wide")
    if wide_count != 8:
        return exchange([mine, other] * (wide_count // 2))
    beside = core_step(other)
    from_x = [chip_step(mine, 1), chip_step(beside, 1)]
    from_y = [chip_step(mine, 2), chip_step(beside, 2)]
    corner = [chip_step(from_y[0], 1), chip_step(from_x[1], 2)]
    return [mine, beside] + from_x + from_y + corner


def hidden_share(expand, reduce_part):
    wide_count = lax.axis_size("wide")
    here = lax.axis_index("wide")
    width, hidden = expand.shape
    rows = width // wide_count
    if width != hidden or rows % 16:
        return None
    return jnp.stack(
        [
            lax.dynamic_slice_in_dim(expand, here * rows, rows, 0),
            lax.dynamic_slice_in_dim(reduce_part, here * rows, rows, 0),
        ]
    )


def all_chips(x):
    groups = [list(range(core, lax.axis_size("wide"), 2)) for core in range(2)]
    return lax.all_gather(x, "wide", axis=0, axis_index_groups=groups)


def chip_step(x, s):
    return lax.ppermute(
        x, "wide", [(j, j ^ (2 * s)) for j in range(lax.axis_size("wide"))]
    )


def core_step(x):
    return lax.ppermute(x, "wide", [(j, j ^ 1) for j in range(lax.axis_size("wide"))])


def on_device(
    tokens,
    cotangent,
    selected,
    segments,
    router_vector,
    project_routed,
    output_routed,
    prenorm_routed,
    midnorm_routed,
    expand_routed,
    reduce_routed,
    project_dense,
    output_dense,
    prenorm_dense,
    midnorm_dense,
    expand_dense,
    reduce_dense,
):
    seq_count, span_rows, width = tokens.shape
    row_length = selected.shape[1]
    hidden = expand_dense.shape[1]
    wide_count = lax.axis_size("wide")
    narrow_count = lax.axis_size("narrow")
    here = lax.axis_index("wide")
    slot_count = span_rows // 4
    bq_dense = min(512, row_length)
    bq_routed = min(512, slot_count * wide_count)
    ids = jnp.stack([here, lax.axis_index("narrow")]).astype(jnp.int32)
    tok = tokens.reshape(-1, width)
    cot = cotangent.reshape(-1, width)

    share_d = hidden_share(expand_dense, reduce_dense)
    staged = share_d is not None
    if staged:
        own_d = lax.all_gather(share_d, "narrow", axis=0)

    mine = here % seq_count
    seq_segments = lax.dynamic_slice_in_dim(segments, mine, 1, 0)[0]
    seq_selected = lax.dynamic_slice_in_dim(selected, mine, 1, 0)[0].reshape(wide_count, span_rows)
    upper = (
        lax.broadcasted_iota(jnp.int32, (span_rows, span_rows), 0)
        <= lax.broadcasted_iota(jnp.int32, (span_rows, span_rows), 1)
    ).astype(BF)
    slots = jnp.arange(slot_count, dtype=jnp.int32)
    seq_rank = jnp.dot(seq_selected.astype(BF), upper, preferred_element_type=F32)
    seq_rank = jnp.where(seq_selected > 0, seq_rank.astype(jnp.int32) - 1, -1)
    slot_segments = (
        jnp.sum(
            jnp.where(
                seq_rank[:, None, :] == slots[None, :, None],
                seq_segments.reshape(wide_count, 1, span_rows) + 1,
                0,
            ),
            axis=-1,
        )
        - 1
    ).reshape(-1)
    meta_routed = (
        jnp.zeros((slot_segments.shape[0] // bq_routed,), jnp.int32),
        jnp.broadcast_to(slot_segments[None], (8, slot_segments.shape[0])),
        slot_segments[:, None],
    )
    own_selected = selected
    if span_rows % 128:
        own_selected = lax.dynamic_slice_in_dim(selected, here * span_rows, span_rows, 1)
    mine_r, other_r, one_hot, picked, vecs = routed_pre(
        ids,
        tok,
        own_selected,
        span_rows,
        [router_vector, prenorm_routed, midnorm_routed, prenorm_dense, midnorm_dense],
    )
    columns_r = group_columns(ids, tie(project_routed, mine_r))
    rows_r = exchange([mine_r, other_r] * (wide_count // 2))
    rows_r, meta_routed = lax.optimization_barrier((rows_r, meta_routed))
    pieces, kept_r = attend(ids, meta_routed, rows_r, columns_r, bq_routed)
    pieces = exchange(pieces)
    if staged:
        pieces, own_d = lax.optimization_barrier((pieces, own_d))
        chips_d = all_chips(own_d)
    branch_r, low_r, att_r = routed_mid(ids, pieces, output_routed, picked, vecs)
    dense_segments = tie(seq_segments, low_r)
    starts = sum(
        jnp.where(dense_segments == value, jnp.sum((dense_segments < value).astype(jnp.int32)), 0)
        for value in range(1, 4)
    )
    meta_dense = (
        starts[::bq_dense] // bq_dense,
        jnp.broadcast_to(starts[None], (8, row_length)),
        None,
    )

    own_at = here * (width // wide_count)

    def own_slice(x):
        return lax.dynamic_slice_in_dim(tie(x, low_r), own_at, width // wide_count, 0)

    own_rows = (
        own_slice(project_routed),
        own_slice(project_dense),
        own_slice(prenorm_routed).astype(F32)[None],
        own_slice(prenorm_dense).astype(F32)[None],
    )
    columns_d = group_columns(ids, tie(project_dense, low_r))
    share_r = hidden_share(tie(expand_routed, low_r), reduce_routed)
    low_pieces, columns_d, meta_dense, own_rows, share_r = lax.optimization_barrier(
        (narrow_gather(low_r), columns_d, meta_dense, own_rows, share_r)
    )
    partials = narrow_return(hidden_forward(ids, low_pieces, expand_routed, reduce_routed))

    mine_d, other_d, mixed, delta_r = dense_pre(
        ids, tok, one_hot, picked, vecs, branch_r, partials
    )
    if staged:
        mine_d, other_d, chips_d = lax.optimization_barrier((mine_d, other_d, chips_d))
        own_r = lax.all_gather(tie(share_r, mine_d), "narrow", axis=0)[None]
        rows_d, own_r = lax.optimization_barrier((exchange_rows(mine_d, other_d), own_r))
        weights_d = [chips_d, core_step(chips_d)]
    else:
        rows_d = exchange_rows(mine_d, other_d)
        weights_d = [
            lax.all_gather(expand_dense, "narrow", axis=0),
            lax.all_gather(reduce_dense, "narrow", axis=0),
        ]
        weights_r = [
            lax.all_gather(expand_routed, "narrow", axis=0),
            lax.all_gather(reduce_routed, "narrow", axis=0),
        ]
    cot_all = lax.all_gather(tie(cot, rows_d), "narrow", axis=0, tiled=True)
    (stack,), kept_d = attend(ids, meta_dense, rows_d, columns_d, bq_dense, stacked=True)
    stack, weights_d = lax.optimization_barrier((stack, weights_d))
    stack = lax.all_to_all(stack, "wide", 0, 0)
    if staged:
        stack, own_r = lax.optimization_barrier((stack, own_r))
        corner_r = chip_step(own_r, 3)
    (activations, low_d, back_d, sum_d, att_d, mid_gain_d), stack = dense_ffn(
        ids, stack, output_dense, mixed, cot, vecs, weights_d
    )
    if staged:
        stack, low_d, cot_all, corner_r = lax.optimization_barrier(
            (stack, low_d, cot_all, corner_r)
        )
    low_all = lax.all_gather(low_d, "narrow", axis=0, tiled=True)
    keep_d, send_d = output_grads(ids, wide_count, att_d, back_d, [])
    stack, keep_d, send_d = lax.optimization_barrier(
        (lax.all_to_all(stack, "wide", 0, 0), keep_d, send_d)
    )
    came_d = core_step(send_d)
    if staged:
        stack, own_r = lax.optimization_barrier((stack, own_r))
        sides_r = [chip_step(own_r, 1), chip_step(own_r, 2)]
        corner_r = [corner_r, core_step(corner_r)]
        weights_r = [own_r, core_step(own_r)]
    (stack,), dx_d = attend_back(ids, meta_dense, kept_d, [stack], bq_dense, stacked=True)
    stack, dx_d, weights_r, came_d = lax.optimization_barrier(
        (stack, dx_d, weights_r, came_d)
    )
    if staged:
        stack, dx_d, sides_r = lax.optimization_barrier((stack, dx_d, sides_r))
        weights_r += [w for own in sides_r for w in (own, core_step(own))] + corner_r
    stack = lax.all_to_all(stack, "wide", 0, 0)
    keep, send = project_grads(ids, wide_count, rows_d, dx_d)
    project_d = join_all(ids, keep, core_step(send))
    low_all, project_d = lax.optimization_barrier((low_all, project_d))
    project_d = lax.psum_scatter(project_d, "narrow", scatter_dimension=0, tiled=True)
    hidden_d = hidden_grads(ids, low_all, cot_all, expand_dense, reduce_dense)
    stack, hidden_d, weights_r = lax.optimization_barrier((stack, hidden_d, weights_r))
    ffn_d = lax.psum_scatter(hidden_d, "wide", scatter_dimension=0, tiled=True)
    g_mixed, g_delta, g_low, g_gate, router_grad = dense_post(
        ids, stack, project_dense, vecs, mixed, sum_d, one_hot, picked, delta_r
    )

    g_pieces = narrow_gather(g_low)
    g_mid_r, back_r, mid_gain_r, stack = routed_back(
        ids,
        wide_count,
        low_r,
        g_low,
        branch_r,
        picked,
        vecs,
        g_delta,
        output_routed,
        weights_r,
    )
    back_r, g_pieces = lax.optimization_barrier((back_r, g_pieces))
    keep_r, send_r = output_grads(
        ids, wide_count, att_r, back_r, [mid_gain_r, mid_gain_d, router_grad]
    )
    came_r = core_step(send_r)
    hidden_r = hidden_grads(
        ids,
        jnp.concatenate(tie(low_pieces, keep_r), axis=0),
        jnp.concatenate(g_pieces, axis=0),
        expand_routed,
        reduce_routed,
    )
    stack, keep_r, send_r, hidden_r = lax.optimization_barrier(
        (lax.all_to_all(stack, "wide", 0, 0), keep_r, send_r, hidden_r)
    )
    delivered_d = deliver(ids, tie(project_d, back_r), wide_count // 2)
    (stack,), dx_r = attend_back(ids, meta_routed, kept_r, [stack], bq_routed, stacked=True)
    stack, dx_r, came_r, delivered_d = lax.optimization_barrier(
        (stack, dx_r, came_r, delivered_d)
    )
    ffn_r = lax.psum_scatter(tie(hidden_r, dx_r), "wide", scatter_dimension=0, tiled=True)
    keep, send = project_grads(ids, wide_count, rows_r, dx_r)
    came = core_step(send)
    output_parts = join_chips(ids, tie([keep_d, keep_r], send), [came_d, came_r])
    project_parts = split_narrow(ids, tie(keep, output_parts), came)
    returned = narrow_return(project_parts)
    stack = lax.all_to_all(tie(stack, project_parts), "wide", 0, 0)
    output_terms = chips_return(tie(output_parts, returned[1]))
    project_d_grad, pre_gain_d = unpack(
        ids, tie(delivered_d, project_parts), own_rows[1], own_rows[3]
    )
    project_r = sum_parts(ids, tie(returned, project_d_grad))
    tokens_gradient = routed_post(
        ids,
        tie(stack, project_r),
        project_routed,
        vecs,
        picked,
        g_mid_r,
        g_mixed,
        one_hot,
        g_gate,
    )
    output_parts = narrow_terms(ids, tie(output_terms, tokens_gradient))
    project_r_grad, pre_gain_r = unpack(
        ids,
        tie(deliver(ids, project_r, keep.shape[0]), output_parts),
        own_rows[0],
        own_rows[2],
    )
    output_total = sum_narrow(ids, output_parts, project_r_grad)
    output_d_grad, output_r_grad, mid_r_grad, mid_d_grad, router_grad = spread_narrow(
        ids, output_total, width // wide_count, [width, width, 128], 3, project_r_grad
    )
    expand_d_grad, reduce_d_grad, expand_r_grad, reduce_r_grad = finish_hidden(
        ids, ffn_d, ffn_r
    )
    return (
        activations.reshape(tokens.shape),
        tokens_gradient.reshape(tokens.shape),
        router_grad,
        project_r_grad,
        output_r_grad,
        pre_gain_r,
        mid_r_grad,
        expand_r_grad,
        reduce_r_grad.T,
        project_d_grad,
        output_d_grad,
        pre_gain_d,
        mid_d_grad,
        expand_d_grad,
        reduce_d_grad.T,
    )


def solution(mesh):
    return jax.shard_map(
        on_device,
        mesh=mesh,
        in_specs=(
            P("narrow", "wide", None),
            P("narrow", "wide", None),
            P("narrow", None),
            P("narrow", None),
            P(),
            P(),
            P(),
            P(),
            P(),
            P(None, "narrow"),
            P("narrow", None),
            P(),
            P(),
            P(),
            P(),
            P(None, "narrow"),
            P("narrow", None),
        ),
        out_specs=(
            P("narrow", "wide", None),
            P("narrow", "wide", None),
            P("wide"),
            P("wide", None),
            P("wide", None),
            P("wide"),
            P("wide"),
            P("wide", "narrow"),
            P("narrow", "wide"),
            P("wide", None),
            P("wide", None),
            P("wide"),
            P("wide"),
            P("wide", "narrow"),
            P("narrow", "wide"),
        ),
        check_vma=False,
    )
```

```python
from functools import partial

import jax
import jax.numpy as jnp
from jax import lax
from jax.experimental import pallas as pl
from jax.experimental.pallas import tpu as pltpu
from jax.sharding import PartitionSpec as P

H = 12
HD = 64
GROUPS = 4
HG = H // GROUPS
GW = HG * HD

EPSILON = 1e-06
NEGATIVE = -1e30
SCORE_SCALE = 0.125
LOG2E = 1.4426950408889634
GELU_A = 0.7978845608028654
GELU_B = 0.044715
BF = jnp.bfloat16
F32 = jnp.float32
VMEM = 56 << 20


def nt_dot(left, right):
    return lax.dot_general(left, right, (((1,), (1,)), ((), ())), preferred_element_type=F32)


def tn_dot(left, right):
    return lax.dot_general(left, right, (((0,), (0,)), ((), ())), preferred_element_type=F32)


def dot(left, right):
    return jnp.dot(left, right, preferred_element_type=F32)


def sds(shape, dtype):
    return jax.ShapeDtypeStruct(shape, dtype)


def norm_scale(rows):
    return lax.rsqrt(jnp.mean(rows * rows, axis=-1, keepdims=True) + EPSILON)


def norm_back(grad, rows, gain):
    scale = norm_scale(rows)
    inner = grad * gain
    mean = jnp.mean(inner * rows, axis=-1, keepdims=True)
    grad_rows = scale * inner - rows * (scale * scale * scale * mean)
    return grad_rows, jnp.sum(grad * rows * scale, axis=0, keepdims=True)


def gelu(a):
    return 0.5 * a * (1.0 + jnp.tanh(GELU_A * (a + GELU_B * (a * a * a))))


def gelu_both(a):
    square = a * a
    bend = jnp.tanh(GELU_A * (a + GELU_B * (square * a)))
    half = 0.5 * (1.0 + bend)
    slope = half + 0.5 * a * (1.0 - bend * bend) * (GELU_A * (1.0 + 3.0 * GELU_B * square))
    return a * half, slope


def three_parts(x):
    first = x.astype(BF)
    rest = x - first.astype(F32)
    second = rest.astype(BF)
    third = (rest - second.astype(F32)).astype(BF)
    return [first, second, third]


def place(one_hot, x):
    return tn_dot(
        jnp.concatenate([one_hot] * 3, axis=0), jnp.concatenate(three_parts(x), axis=0)
    )


def pick(one_hot, x):
    return dot(jnp.concatenate([one_hot] * 3, axis=1), jnp.concatenate(three_parts(x), axis=0))


def combo(index):
    return lax.rem(lax.div(index, 2), GROUPS), lax.rem(index, 2)


def save_pieces(me, full, parts, pieces):
    rows = full.shape[0] // 2
    thirds = full.shape[1] // (GROUPS * GW)
    for c in range(GROUPS):
        for t in range(thirds):
            at = t * GROUPS * GW + c * GW
            parts[c, :, t * GW : (t + 1) * GW] = full[:, at : at + GW]
    for s, piece in enumerate(pieces):
        c, r = combo(me ^ s)
        piece[...] = parts[c, pl.ds(pl.multiple_of(r * rows, rows), rows), :]


def load_pieces(me, pieces, parts, thirds):
    rows = pieces[0].shape[0]
    for s, piece in enumerate(pieces):
        c, r = combo(me ^ s)
        parts[c, pl.ds(pl.multiple_of(r * rows, rows), rows), :] = piece[...]
    return jnp.concatenate(
        [parts[c, :, t * GW : (t + 1) * GW] for t in range(thirds) for c in range(GROUPS)],
        axis=1,
    )


def save_stack(full, parts, stack):
    rows = full.shape[0] // 2
    thirds = full.shape[1] // (GROUPS * GW)
    half, columns = rows // 2, thirds * GW
    for c in range(GROUPS):
        for t in range(thirds):
            at = t * GROUPS * GW + c * GW
            parts[c, :, t * GW : (t + 1) * GW] = full[:, at : at + GW]
    for b in range(stack.shape[0]):
        c, at = (b // 2) % GROUPS, (b % 2) * rows
        stack[b, :, 0:columns] = parts[c, at : at + half, :]
        stack[b, :, columns : 2 * columns] = parts[c, at + half : at + rows, :]


def load_stack(me, stack, parts, thirds):
    half, columns = stack.shape[1], stack.shape[2] // 2
    first = lax.div(me, 2 * GROUPS) * (2 * GROUPS)
    for w in range(2 * GROUPS):
        c, at = w // 2, (w % 2) * 2 * half
        parts[c, at : at + half, :] = stack[first + w, :, 0:columns]
        parts[c, at + half : at + 2 * half, :] = stack[first + w, :, columns : 2 * columns]
    return jnp.concatenate(
        [parts[c, :, t * GW : (t + 1) * GW] for t in range(thirds) for c in range(GROUPS)],
        axis=1,
    )


def stage(body, name, ids, operands, outs, scratch=(), flops=0, grid=None, specs=None):
    kwargs = {}
    if grid is not None:
        kwargs["grid"] = grid
    in_specs = [pl.BlockSpec(memory_space=pltpu.SMEM)]
    for k, operand in enumerate(operands):
        spec = None if specs is None else specs.get(k)
        if spec is None:
            zeros = (0,) * operand.ndim
            spec = pl.BlockSpec(operand.shape, lambda *_, z=zeros: z)
        in_specs.append(spec)
    out_specs = tuple(
        pl.BlockSpec(out.shape, lambda *_, z=(0,) * len(out.shape): z) for out in outs
    )
    moved = sum(a.size * a.dtype.itemsize for a in operands)
    moved += sum(math_prod(a.shape) * a.dtype.itemsize for a in outs)
    return pl.pallas_call(
        body,
        out_shape=tuple(outs),
        in_specs=in_specs,
        out_specs=out_specs,
        scratch_shapes=list(scratch),
        compiler_params=pltpu.CompilerParams(vmem_limit_bytes=VMEM),
        cost_estimate=pl.CostEstimate(flops=flops, bytes_accessed=moved, transcendentals=0),
        name=name,
        **kwargs,
    )(ids, *operands)


def math_prod(shape):
    total = 1
    for size in shape:
        total *= size
    return total


def head_parts(rows):
    lane = lax.broadcasted_iota(jnp.int32, rows.shape, 1)
    zero = jnp.zeros_like(rows)
    return [
        jnp.where((lane >= h * HD) & (lane < (h + 1) * HD), rows, zero) for h in range(HG)
    ]


def pair_mask(row_ref, col_ref, q_at, k_at, bk, bq):
    k_iota = lax.broadcasted_iota(jnp.int32, (bk, bq), 0) + k_at
    q_iota = lax.broadcasted_iota(jnp.int32, (bk, bq), 1) + q_at
    info = row_ref[0:1, pl.ds(q_at, bq)]
    if col_ref is None:
        return (k_iota >= info) & (k_iota <= q_iota)
    info = info.astype(F32)
    return (col_ref[pl.ds(k_at, bk), 0:1] == info) & (k_iota <= q_iota)


def turn(row):
    return jnp.broadcast_to(row.astype(F32), (128, row.shape[1])).T


def attend_kernel(bq, count, sends, stacked, by_column, ids, first_ref, row_ref, *rest):
    rest = list(rest)
    pieces, rest = rest[:count], rest[count:]
    columns = rest.pop(0)
    out_pieces, rest = rest[:sends], rest[sends:]
    stack_ref = rest.pop(0) if stacked else None
    o_ref, lse_ref, x_ref, k_s, v_s, vt_s = rest[:6]
    col_ref = rest[6] if by_column else None
    i = pl.program_id(0)
    me = ids[0]
    rows = pieces[0].shape[0]
    bk = bq

    @pl.when(i == 0)
    def _():
        for s in range(count):
            at = pl.ds(pl.multiple_of((me ^ s) * rows, rows), rows)
            x = dot(pieces[s][...], columns[...]).astype(BF)
            x_ref[at, :] = x
            k_s[at, :] = x[:, GW : 2 * GW]
            v_s[at, :] = x[:, 2 * GW : 3 * GW]
        vt_s[...] = v_s[...].T
        if by_column:
            col_ref[...] = turn(row_ref[...])

    q_at = pl.multiple_of(i * bq, bq)
    q_heads = head_parts(x_ref[pl.ds(q_at, bq), 0:GW])

    def step(j, carry):
        k_at = pl.multiple_of(j * bk, bk)
        keys = k_s[pl.ds(k_at, bk), :]
        mask = pair_mask(row_ref, col_ref, q_at, k_at, bk, bq)
        out = []
        for h in range(HG):
            top, total, acc = carry[h]
            scores = nt_dot(keys, q_heads[h]) * (SCORE_SCALE * LOG2E)
            scores = jnp.where(mask, scores, NEGATIVE)
            top_new = jnp.maximum(top, jnp.max(scores, axis=0, keepdims=True))
            weight = jnp.exp2(scores - top_new)
            fade = jnp.exp2(top - top_new)
            total = total * fade + jnp.sum(weight, axis=0, keepdims=True)
            values_t = vt_s[h * HD : (h + 1) * HD, pl.ds(k_at, bk)]
            acc = acc * fade + dot(values_t, weight.astype(BF))
            out.append((top_new, total, acc))
        return tuple(out)

    start = tuple(
        (
            jnp.full((1, bq), NEGATIVE, F32),
            jnp.zeros((1, bq), F32),
            jnp.zeros((HD, bq), F32),
        )
        for _ in range(HG)
    )
    done = lax.fori_loop(0 if by_column else first_ref[i], i + 1, step, start)
    outs = jnp.concatenate([acc / total for _, total, acc in done], axis=0)
    o_ref[pl.ds(q_at, bq), :] = outs.T.astype(BF)
    for h in range(HG):
        top, total, _ = done[h]
        lse_ref[h : h + 1, pl.ds(q_at, bq)] = top + jnp.log2(total)

    @pl.when(i == pl.num_programs(0) - 1)
    def _():
        for s in range(sends):
            at = pl.ds(pl.multiple_of((me ^ s) * rows, rows), rows)
            out_pieces[s][...] = o_ref[at, :]
        if stacked:
            half = rows // 2
            for b in range(count):
                at = b * rows
                stack_ref[b, :, 0:GW] = o_ref[at : at + half, :]
                stack_ref[b, :, GW : 2 * GW] = o_ref[at + half : at + rows, :]


def attend_back_kernel(bq, count, sends, stacked, by_column, ids, first_ref, row_ref, *rest):
    rest = list(rest)
    x_ref = rest.pop(0)
    given = 1 if stacked else count
    grads, rest = rest[:given], rest[given:]
    o_ref, lse_ref = rest[:2]
    out_pieces, rest = rest[2 : 2 + sends], rest[2 + sends :]
    stack_ref = rest.pop(0) if stacked else None
    dx_ref, k_s, v_s, g_s, dk_s, dv_s = rest[:6]
    col_ref = rest[6] if by_column else None
    i = pl.program_id(0)
    me = ids[0]
    rows = g_s.shape[0] // count
    bk = bq

    @pl.when(i == 0)
    def _():
        k_s[...] = x_ref[:, GW : 2 * GW]
        v_s[...] = x_ref[:, 2 * GW : 3 * GW]
        for s in range(count):
            if stacked:
                half = rows // 2
                g_s[s * rows : s * rows + half, :] = grads[0][s, :, 0:GW]
                g_s[s * rows + half : (s + 1) * rows, :] = grads[0][s, :, GW : 2 * GW]
            else:
                at = pl.ds(pl.multiple_of((me ^ s) * rows, rows), rows)
                g_s[at, :] = grads[s][...]
        if by_column:
            col_ref[...] = turn(row_ref[...])
        dk_s[...] = jnp.zeros_like(dk_s)
        dv_s[...] = jnp.zeros_like(dv_s)

    q_at = pl.multiple_of(i * bq, bq)
    grad = g_s[pl.ds(q_at, bq), :]
    q_heads = head_parts(x_ref[pl.ds(q_at, bq), 0:GW])
    g_heads = head_parts(grad)
    dots = (grad.astype(F32) * o_ref[pl.ds(q_at, bq), :].astype(F32)).T
    row_dot = [
        jnp.sum(dots[h * HD : (h + 1) * HD, :], axis=0, keepdims=True) for h in range(HG)
    ]
    lse = [lse_ref[h : h + 1, pl.ds(q_at, bq)] for h in range(HG)]

    def step(j, dq):
        k_at = pl.multiple_of(j * bk, bk)
        here = pl.ds(k_at, bk)
        keys = k_s[here, :]
        values = v_s[here, :]
        key_heads = head_parts(keys)
        mask = pair_mask(row_ref, col_ref, q_at, k_at, bk, bq)
        dk = dk_s[here, :]
        dv = dv_s[here, :]
        for h in range(HG):
            scores = nt_dot(keys, q_heads[h]) * (SCORE_SCALE * LOG2E)
            scores = jnp.where(mask, scores - lse[h], NEGATIVE)
            soft = jnp.exp2(scores)
            g_soft = nt_dot(values, g_heads[h])
            g_scores = (soft * (g_soft - row_dot[h])).astype(BF)
            dv = dv + dot(soft.astype(BF), g_heads[h])
            dk = dk + dot(g_scores, q_heads[h])
            dq = dq + tn_dot(g_scores, key_heads[h])
        dk_s[here, :] = dk
        dv_s[here, :] = dv
        return dq

    dq = lax.fori_loop(0 if by_column else first_ref[i], i + 1, step, jnp.zeros((bq, GW), F32))
    dx_ref[pl.ds(q_at, bq), 0:GW] = (dq * SCORE_SCALE).astype(BF)

    @pl.when(i == pl.num_programs(0) - 1)
    def _():
        dx_ref[:, GW : 2 * GW] = (dk_s[...] * SCORE_SCALE).astype(BF)
        dx_ref[:, 2 * GW : 3 * GW] = dv_s[...].astype(BF)
        for s in range(sends):
            at = pl.ds(pl.multiple_of((me ^ s) * rows, rows), rows)
            out_pieces[s][...] = dx_ref[at, :]
        if stacked:
            half = rows // 2
            for b in range(count):
                at = b * rows
                stack_ref[b, :, 0 : 3 * GW] = dx_ref[at : at + half, :]
                stack_ref[b, :, 3 * GW : 6 * GW] = dx_ref[at + half : at + rows, :]


def attend(ids, meta, pieces, columns, bq, stacked=False):
    first, row_info = meta
    by_column = first is None
    if by_column:
        first = ids
    rows, width = pieces[0].shape
    count = len(pieces)
    sends = 0 if stacked else min(count, 2 * GROUPS)
    length = rows * count
    operands = [first, row_info]
    operands += list(pieces) + [columns]
    outs = [sds((rows, GW), BF)] * sends
    outs += [sds((count, rows // 2, 2 * GW), BF)] if stacked else []
    outs += [
        sds((length, GW), BF),
        sds((8, length), F32),
        sds((length, 3 * GW), BF),
    ]
    got = stage(
        partial(attend_kernel, bq, count, sends, stacked, by_column),
        "attend",
        ids,
        operands,
        outs,
        [pltpu.VMEM((length, GW), BF)] * 2
        + [pltpu.VMEM((GW, length), BF)]
        + ([pltpu.VMEM((length, 128), F32)] if by_column else []),
        flops=length * length * GW * 2 + 6 * length * width * GW,
        grid=(length // bq,),
        specs={0: pl.BlockSpec(memory_space=pltpu.SMEM)},
    )
    return got[:-3], got[-3:]


def attend_back(ids, meta, kept, grads, bq, stacked=False):
    first, row_info = meta
    by_column = first is None
    if by_column:
        first = ids
    attended, lse, x = kept
    count = grads[0].shape[0] if stacked else len(grads)
    rows = attended.shape[0] // count
    sends = 0 if stacked else min(count, 2 * GROUPS)
    length = rows * count
    operands = [first, row_info]
    operands += [x] + list(grads) + [attended, lse]
    got = stage(
        partial(attend_back_kernel, bq, count, sends, stacked, by_column),
        "attend_back",
        ids,
        operands,
        [sds((rows, 3 * GW), BF)] * sends
        + ([sds((count, rows // 2, 6 * GW), BF)] if stacked else [])
        + [sds(x.shape, BF)],
        [pltpu.VMEM((length, GW), BF)] * 3
        + [pltpu.VMEM((length, GW), F32)] * 2
        + ([pltpu.VMEM((length, 128), F32)] if by_column else []),
        flops=length * length * GW * 5,
        grid=(length // bq,),
        specs={0: pl.BlockSpec(memory_space=pltpu.SMEM)},
    )
    return got[:-1], got[-1]


def project_grads_kernel(count, ids, dx_ref, *rest):
    pieces, (keep, send, rows_s, total) = rest[:count], rest[count:]
    rows = pieces[0].shape[0]
    for s, piece in enumerate(pieces):
        rows_s[pl.ds(pl.multiple_of((ids[0] ^ s) * rows, rows), rows), :] = piece[...]
    total[...] = tn_dot(rows_s[...], dx_ref[...])
    split_rows(ids[0], total, keep, send)


def project_grads(ids, wide_count, pieces, dx):
    rows, width = pieces[0].shape
    shape = (wide_count // 2, width // wide_count, 3 * GW)
    return stage(
        partial(project_grads_kernel, len(pieces)),
        "project_grads",
        ids,
        [dx] + list(pieces),
        [sds(shape, BF)] * 2,
        [pltpu.VMEM((dx.shape[0], width), BF), pltpu.VMEM((width, 3 * GW), F32)],
        flops=6 * dx.size * width // 3,
    )


def group_columns_kernel(ids, project, out):
    group, _ = combo(ids[0])
    width = GROUPS * GW
    for c in range(GROUPS):

        @pl.when(group == c)
        def _():
            for t in range(3):
                at = t * width + c * GW
                out[:, t * GW : (t + 1) * GW] = project[:, at : at + GW]


def group_columns(ids, project):
    (out,) = stage(
        group_columns_kernel,
        "group_columns",
        ids,
        [project],
        [sds((project.shape[0], 3 * GW), BF)],
    )
    return out


def save_halves(me, normed, mine_ref, other_ref):
    rows = mine_ref.shape[0]
    core = lax.rem(me, 2)
    mine_ref[...] = normed[pl.ds(pl.multiple_of(core * rows, rows), rows), :]
    other_ref[...] = normed[pl.ds(pl.multiple_of((1 - core) * rows, rows), rows), :]


def routed_pre_kernel(count, ids, tok, sel, *rest):
    vectors, rest = rest[:count], rest[count:]
    mine_ref, other_ref, one_hot_ref, picked_ref, vecs, normed = rest
    rows = [vector[...].astype(F32).reshape(1, -1) for vector in vectors]
    rows.append(jnp.zeros((8 - count, tok.shape[1]), F32))
    vecs[...] = jnp.concatenate(rows, axis=0)
    span = one_hot_ref.shape[1]
    seqs = sel.shape[0]
    if sel.shape[1] != span:
        sel = sel[:, pl.ds(pl.multiple_of(ids[0] * span, span), span)]
    slots = span // 4
    upper = (
        lax.broadcasted_iota(jnp.int32, (span, span), 0)
        <= lax.broadcasted_iota(jnp.int32, (span, span), 1)
    ).astype(F32).astype(BF)
    slot = lax.broadcasted_iota(jnp.int32, (slots, span), 0).astype(F32)
    for q in range(seqs):
        chosen = jnp.broadcast_to(sel[q : q + 1, :].astype(F32), (8, span))
        rank = dot(chosen.astype(BF), upper)[0:1, :] * chosen[0:1, :] - 1.0
        one_hot = (slot == rank).astype(F32).astype(BF)
        one_hot_ref[q * slots : (q + 1) * slots, :] = one_hot
        picked_ref[q * slots : (q + 1) * slots, :] = dot(
            one_hot, tok[q * span : (q + 1) * span, :]
        ).astype(BF)
    picked = picked_ref[...].astype(F32)
    normed[...] = (picked * norm_scale(picked) * gain_of(vecs, 1)).astype(BF)
    save_halves(ids[0], normed, mine_ref, other_ref)


def gain_of(vecs, k):
    return vecs[k : k + 1, :]


def routed_pre(ids, tok, sel, span, vectors):
    rows, width = tok.shape[0] // 4, tok.shape[1]
    return stage(
        partial(routed_pre_kernel, len(vectors)),
        "routed_pre",
        ids,
        [tok, sel] + vectors,
        [
            sds((rows // 2, width), BF),
            sds((rows // 2, width), BF),
            sds((rows, span), BF),
            sds((rows, width), BF),
            sds((8, width), F32),
        ],
        [pltpu.VMEM((rows, width), BF)],
        flops=4 * rows * width * span,
    )


def routed_mid_kernel(count, ids, *rest):
    pieces = rest[:count]
    output, picked, vecs, branch_ref, low_ref, att_ref, parts = rest[count:]
    attended = load_pieces(ids[0], pieces, parts, 1)
    att_ref[...] = attended
    branch = dot(attended, output[...])
    branch_ref[...] = branch
    middle = picked[...].astype(F32) + branch
    low_ref[...] = (middle * norm_scale(middle) * gain_of(vecs, 2)).astype(BF)


def routed_mid(ids, pieces, output, picked, vecs):
    shape = picked.shape
    return stage(
        partial(routed_mid_kernel, len(pieces)),
        "routed_mid",
        ids,
        list(pieces) + [output, picked, vecs],
        [sds(shape, F32), sds(shape, BF), sds(shape, BF)],
        [pltpu.VMEM((GROUPS, shape[0], GW), BF)],
        flops=2 * shape[0] * shape[1] * shape[1],
    )


def hidden_forward_kernel(count, ids, *rest):
    pieces = rest[:count]
    expand, reduce_ref = rest[count : count + 2]
    outs = rest[count + 2 :]
    rows = pieces[0].shape[0]
    low = jnp.concatenate([piece[...] for piece in pieces], axis=0)
    hidden = gelu(dot(low, expand[...])).astype(BF)
    total = dot(hidden, reduce_ref[...]).astype(BF)
    for s, out in enumerate(outs):
        out[...] = total[s * rows : (s + 1) * rows, :]


def hidden_forward(ids, pieces, expand, reduce_part):
    return stage(
        partial(hidden_forward_kernel, len(pieces)),
        "hidden_forward",
        ids,
        list(pieces) + [expand, reduce_part],
        [sds(pieces[0].shape, BF)] * len(pieces),
        flops=4 * len(pieces) * pieces[0].size * expand.shape[1],
    )


def dense_pre_kernel(shares, ids, tok, one_hot, picked, vecs, branch, *rest):
    partials = rest[:shares]
    mine_ref, other_ref, mixed_ref, delta_ref, normed = rest[shares:]
    slots, span = one_hot.shape[0] // 2, one_hot.shape[1]
    delta = branch[...]
    for share in partials:
        delta = delta + share[...].astype(F32)
    delta_ref[...] = delta
    gate = jnp.sum(picked[...].astype(F32) * gain_of(vecs, 0), axis=-1, keepdims=True)
    lifted = gate * delta
    for q in range(2):
        at, spots = slice(q * span, (q + 1) * span), slice(q * slots, (q + 1) * slots)
        mixed = tok[at, :].astype(F32) + place(one_hot[spots, :], lifted[spots, :])
        mixed_ref[at, :] = mixed
        normed[at, :] = (mixed * norm_scale(mixed) * gain_of(vecs, 3)).astype(BF)
    save_halves(ids[0], normed, mine_ref, other_ref)


def dense_pre(ids, tok, one_hot, picked, vecs, branch, partials):
    rows, width = tok.shape
    return stage(
        partial(dense_pre_kernel, len(partials)),
        "dense_pre",
        ids,
        [tok, one_hot, picked, vecs, branch] + list(partials),
        [
            sds((rows // 2, width), BF),
            sds((rows // 2, width), BF),
            sds(tok.shape, F32),
            sds(picked.shape, F32),
        ],
        [pltpu.VMEM((rows, width), BF)],
        flops=6 * rows * width * one_hot.shape[0],
    )


def this_part(me, weights, scratch):
    if not scratch:
        return weights[0][0], weights[1][0]
    e_s, r_s = scratch
    core = lax.rem(me, 2)
    rows = weights[0].shape[-2]
    if len(weights) == 2:
        blocks = []
        for c in range(weights[0].shape[0]):
            blocks.append((weights[0], c, 2 * c + core))
            blocks.append((weights[1], c, 2 * c + 1 - core))
    else:
        blocks = [(weight, 0, me ^ s) for s, weight in enumerate(weights)]
    for weight, c, at in blocks:
        at = pl.ds(pl.multiple_of(at * rows, rows), rows)
        e_s[at, :] = weight[c, 0, 0]
        r_s[at, :] = weight[c, 0, 1]
    return e_s[...], r_s[...]


def part_specs(base, weights):
    if weights[0].ndim == 3:
        return {
            base + k: pl.BlockSpec((1,) + w.shape[1:], lambda n: (n, 0, 0))
            for k, w in enumerate(weights)
        }
    return {
        base + k: pl.BlockSpec(
            (w.shape[0], 1) + w.shape[2:], lambda n: (0, n, 0, 0, 0)
        )
        for k, w in enumerate(weights)
    }


def part_scratch(width, weights):
    if weights[0].ndim == 3:
        return []
    return [pltpu.VMEM((width, weights[0].shape[-1]), BF)] * 2


def dense_ffn_kernel(split, ids, stack, *rest):
    output, mixed, cot, vecs = rest[:4]
    gain = gain_of(vecs, 4)
    rest = rest[4:]
    weights, rest = rest[:split], rest[split:]
    act_ref, low_ref, back_ref, sum_ref, att_ref, gain_ref = rest[:6]
    g_stack, rest = rest[6], rest[7:]
    parts, branch_s, delta_s, grad_s = rest[:4]
    n = pl.program_id(0)
    me = ids[0]

    @pl.when(n == 0)
    def _():
        attended = load_stack(me, stack, parts, 1)
        att_ref[...] = attended
        branch = dot(attended, output[...])
        branch_s[...] = branch
        middle = mixed[...] + branch
        low_ref[...] = (middle * norm_scale(middle) * gain).astype(BF)
        delta_s[...] = jnp.zeros_like(delta_s)
        grad_s[...] = jnp.zeros_like(grad_s)

    expand, reduce_w = this_part(me, weights, rest[4:])
    value, slope = gelu_both(dot(low_ref[...], expand))
    delta_s[...] += dot(value.astype(BF), reduce_w)
    grad_pre = (nt_dot(cot[...], reduce_w) * slope).astype(BF)
    grad_s[...] += nt_dot(grad_pre, expand)

    @pl.when(n == pl.num_programs(0) - 1)
    def _():
        middle = mixed[...] + branch_s[...]
        act_ref[...] = (middle + delta_s[...]).astype(BF)
        grad_middle, gain_grad = norm_back(grad_s[...], middle, gain)
        gain_ref[...] = jnp.broadcast_to(gain_grad, gain_ref.shape)
        total = cot[...].astype(F32) + grad_middle
        sum_ref[...] = total
        back = total.astype(BF)
        back_ref[...] = back
        save_stack(nt_dot(back, output[...]).astype(BF), parts, g_stack)


def dense_ffn(ids, stack, output, mixed, cot, vecs, weights):
    rows, width = mixed.shape
    split = len(weights)
    parts_n = weights[0].shape[0 if weights[0].ndim == 3 else 1]
    hidden = weights[0].shape[-1]
    base = 5
    specs = part_specs(base, weights)
    scratch = [pltpu.VMEM((GROUPS, rows, GW), BF)] + [pltpu.VMEM((rows, width), F32)] * 3
    scratch += part_scratch(width, weights)
    outs = [
        sds((rows, width), BF),
        sds((rows, width), BF),
        sds((rows, width), BF),
        sds((rows, width), F32),
        sds((rows, width), BF),
        sds((8, width), F32),
        sds(stack.shape, BF),
    ]
    got = stage(
        partial(dense_ffn_kernel, split),
        "dense_ffn",
        ids,
        [stack, output, mixed, cot, vecs] + list(weights),
        outs,
        scratch,
        flops=8 * rows * width * hidden * parts_n + 4 * rows * width * width,
        grid=(parts_n,),
        specs=specs,
    )
    return got[:6], got[6]


def dense_post_kernel(ids, stack, *rest):
    project, vecs, mixed, total, one_hot, picked, delta = rest[:7]
    g_mixed_ref, g_delta_ref, g_low_ref, g_gate_ref, router_ref, parts = rest[7:]
    g_proj = load_stack(ids[0], stack, parts, 3)
    grad_rows, _ = norm_back(nt_dot(g_proj, project[...]), mixed[...], gain_of(vecs, 3))
    g_mixed_ref[...] = total[...] + grad_rows
    slots, span = one_hot.shape[0] // 2, one_hot.shape[1]
    rows = picked[...].astype(F32)
    gate = jnp.sum(rows * gain_of(vecs, 0), axis=-1, keepdims=True)
    router = jnp.zeros((1, rows.shape[1]), F32)
    for q in range(2):
        at, spots = slice(q * span, (q + 1) * span), slice(q * slots, (q + 1) * slots)
        lifted = pick(one_hot[spots, :], g_mixed_ref[at, :])
        g_delta = gate[spots, :] * lifted
        g_delta_ref[spots, :] = g_delta
        g_low_ref[spots, :] = g_delta.astype(BF)
        g_gate = jnp.sum(lifted * delta[spots, :], axis=-1, keepdims=True)
        g_gate_ref[spots, :] = jnp.broadcast_to(g_gate, (slots, g_gate_ref.shape[1]))
        router = router + jnp.sum(rows[spots, :] * g_gate, axis=0, keepdims=True)
    router_ref[...] = jnp.broadcast_to(router, router_ref.shape)


def dense_post(ids, stack, project, vecs, mixed, total, one_hot, picked, delta):
    rows, width = mixed.shape
    return stage(
        dense_post_kernel,
        "dense_post",
        ids,
        [stack, project, vecs, mixed, total, one_hot, picked, delta],
        [
            sds((rows, width), F32),
            sds(picked.shape, F32),
            sds(picked.shape, BF),
            sds((picked.shape[0], 128), F32),
            sds((8, width), F32),
        ],
        [pltpu.VMEM((GROUPS, rows, 3 * GW), BF)],
        flops=6 * rows * width * width,
    )


def routed_back_kernel(split, ids, low, g_low, branch, picked, vecs, g_delta, output, *rest):
    weights, rest = rest[:split], rest[split:]
    g_mid_ref, back_ref, gain_ref, stack, parts, grad_s = rest[:6]
    n = pl.program_id(0)

    @pl.when(n == 0)
    def _():
        grad_s[...] = jnp.zeros_like(grad_s)

    expand, reduce_w = this_part(ids[0], weights, rest[6:])
    _, slope = gelu_both(dot(low[...], expand))
    grad_pre = (nt_dot(g_low[...], reduce_w) * slope).astype(BF)
    grad_s[...] += nt_dot(grad_pre, expand)

    @pl.when(n == pl.num_programs(0) - 1)
    def _():
        middle = picked[...].astype(F32) + branch[...]
        g_middle, gain_grad = norm_back(grad_s[...], middle, gain_of(vecs, 2))
        gain_ref[...] = jnp.broadcast_to(gain_grad, gain_ref.shape)
        g_mid_ref[...] = g_middle
        back = (g_delta[...] + g_middle).astype(BF)
        back_ref[...] = back
        save_stack(nt_dot(back, output[...]).astype(BF), parts, stack)


def routed_back(ids, wide_count, low, g_low, branch, picked, vecs, g_delta, output, weights):
    rows, width = branch.shape
    parts_n = weights[0].shape[0 if weights[0].ndim == 3 else 1]
    return stage(
        partial(routed_back_kernel, len(weights)),
        "routed_back",
        ids,
        [low, g_low, branch, picked, vecs, g_delta, output] + list(weights),
        [
            sds((rows, width), F32),
            sds((rows, width), BF),
            sds((8, width), F32),
            sds((wide_count, rows // 4, 2 * GW), BF),
        ],
        [pltpu.VMEM((GROUPS, rows, GW), BF), pltpu.VMEM((rows, width), F32)]
        + part_scratch(width, weights),
        flops=6 * rows * width * parts_n * weights[0].shape[-1],
        grid=(parts_n,),
        specs=part_specs(7, weights),
    )


def routed_post_kernel(ids, stack, *rest):
    project, vecs, picked, g_mid, g_mixed, one_hot, g_gate = rest[:7]
    out_ref, parts = rest[7:]
    g_proj = load_stack(ids[0], stack, parts, 3)
    rows = picked[...].astype(F32)
    grad_rows, _ = norm_back(nt_dot(g_proj, project[...]), rows, gain_of(vecs, 1))
    spread = g_mid[...] + grad_rows + g_gate[:, 0:1] * gain_of(vecs, 0)
    slots, span = one_hot.shape[0] // 2, one_hot.shape[1]
    for q in range(2):
        at, spots = slice(q * span, (q + 1) * span), slice(q * slots, (q + 1) * slots)
        out_ref[at, :] = g_mixed[at, :] + place(one_hot[spots, :], spread[spots, :])


def routed_post(ids, stack, project, vecs, picked, g_mid, g_mixed, one_hot, g_gate):
    rows, width = picked.shape
    (out,) = stage(
        routed_post_kernel,
        "routed_post",
        ids,
        [stack, project, vecs, picked, g_mid, g_mixed, one_hot, g_gate],
        [sds(g_mixed.shape, F32)],
        [pltpu.VMEM((GROUPS, rows, 3 * GW), BF)],
        flops=6 * rows * width * width,
    )
    return out


def split_rows(me, total, keep, send):
    chips, rows = keep.shape[0], keep.shape[1]
    core = lax.rem(me, 2)
    for c in range(chips):
        mine = pl.multiple_of((2 * c + core) * rows, rows)
        other = pl.multiple_of((2 * c + 1 - core) * rows, rows)
        keep[c] = total[pl.ds(mine, rows), :].astype(BF)
        send[c] = total[pl.ds(other, rows), :].astype(BF)


def hidden_grads_kernel(ids, low, grad, expand, reduce_ref, out, total):
    i = pl.program_id(0)
    hidden = expand.shape[1]

    @pl.when(i == 0)
    def _():
        total[...] = jnp.zeros_like(total)

    value, slope = gelu_both(dot(low[...], expand[...]))
    grad_pre = (nt_dot(grad[...], reduce_ref[...]) * slope).astype(BF)
    total[:, 0:hidden] += tn_dot(low[...], grad_pre)
    total[:, hidden : 2 * hidden] += tn_dot(grad[...], value.astype(BF))

    @pl.when(i == pl.num_programs(0) - 1)
    def _():
        out[...] = total[...].astype(BF)


def hidden_grads_pieces_kernel(count, ids, *rest):
    lows, grads = rest[:count], rest[count : 2 * count]
    expand, reduce_ref, out = rest[2 * count :]
    hidden = expand.shape[1]
    low = jnp.concatenate([piece[...] for piece in lows], axis=0)
    grad = jnp.concatenate([piece[...] for piece in grads], axis=0)
    value, slope = gelu_both(dot(low, expand[...]))
    grad_pre = (nt_dot(grad, reduce_ref[...]) * slope).astype(BF)
    out[:, 0:hidden] = tn_dot(low, grad_pre).astype(BF)
    out[:, hidden : 2 * hidden] = tn_dot(grad, value.astype(BF)).astype(BF)


def hidden_grads(ids, low, grad, expand, reduce_part):
    width, hidden = expand.shape
    if isinstance(grad, (list, tuple)):
        (out,) = stage(
            partial(hidden_grads_pieces_kernel, len(grad)),
            "hidden_grads",
            ids,
            list(low) + list(grad) + [expand, reduce_part],
            [sds((width, 2 * hidden), BF)],
            flops=8 * len(grad) * grad[0].size * hidden,
        )
        return out
    block = min(512, low.shape[0])
    row_spec = pl.BlockSpec((block, width), lambda i: (i, 0))
    (out,) = stage(
        hidden_grads_kernel,
        "hidden_grads",
        ids,
        [low, grad, expand, reduce_part],
        [sds((width, 2 * hidden), BF)],
        [pltpu.VMEM((width, 2 * hidden), F32)],
        flops=8 * low.size * hidden,
        grid=(low.shape[0] // block,),
        specs={0: row_spec, 1: row_spec},
    )
    return out


def output_grads_kernel(vectors, ids, att, back, *rest):
    rest = list(rest)
    vecs, rest = rest[:vectors], rest[vectors:]
    keep, send, total = rest
    width = att.shape[1]
    total[:, 0:width] = tn_dot(att[...], back[...])
    if vectors:
        rows = [vec[0:1, :] for vec in vecs]
        rows.append(jnp.zeros((128 - vectors, width), F32))
        total[:, width : width + 128] = jnp.concatenate(rows, axis=0).T
    split_rows(ids[0], total, keep, send)


def output_grads(ids, wide_count, att, back, vecs):
    rows, width = att.shape
    columns = width + (128 if vecs else 0)
    shape = (wide_count // 2, width // wide_count, columns)
    return stage(
        partial(output_grads_kernel, len(vecs)),
        "output_grads",
        ids,
        [att, back] + list(vecs),
        [sds(shape, BF), sds(shape, BF)],
        [pltpu.VMEM((width, columns), F32)],
        flops=3 * rows * width * width,
    )


def join_kernel(pairs, ids, *rest):
    keeps, cames, outs = rest[:pairs], rest[pairs : 2 * pairs], rest[2 * pairs :]
    chip = lax.div(ids[0], 2)
    for s, out in enumerate(outs):
        low = 0
        for keep, came in zip(keeps, cames):
            columns = keep.shape[2]
            total = keep[chip ^ s].astype(F32) + came[chip ^ s].astype(F32)
            out[:, low : low + columns] = total.astype(BF)
            low += columns


def join_chips(ids, keeps, cames):
    chips, rows = keeps[0].shape[:2]
    columns = sum(keep.shape[2] for keep in keeps)
    return stage(
        partial(join_kernel, len(keeps)),
        "join",
        ids,
        list(keeps) + list(cames),
        [sds((rows, columns), BF)] * chips,
    )


def chips_return(parts):
    return [parts[0]] + [chip_step(parts[s], s) for s in range(1, len(parts))]


def sum_terms(terms):
    total = terms[0].astype(F32)
    for term in terms[1:]:
        total = total + term.astype(F32)
    return total


def sum_split_kernel(count, ids, *rest):
    terms, outs, total = rest[:count], rest[count:-1], rest[-1]
    got = terms[0][...].astype(F32)
    for term in terms[1:]:
        got = got + term[...].astype(F32)
    total[...] = got
    rows = outs[0].shape[0]
    for s, out in enumerate(outs):
        at = pl.multiple_of((ids[1] ^ s) * rows, rows)
        out[...] = total[pl.ds(at, rows), :].astype(BF)


def sum_kernel(ids, *rest):
    got = rest[0][...].astype(F32)
    for term in rest[1:-1]:
        got = got + term[...].astype(F32)
    rest[-1][...] = got.astype(BF)


def gather_out_kernel(count, vectors, ids, *rest):
    pieces, outs = rest[:count], rest[count : -1 - vectors]
    vecs, wide_s = rest[-1 - vectors : -1], rest[-1]
    rows = pieces[0].shape[0]
    for s, piece in enumerate(pieces):
        at = pl.ds(pl.multiple_of((ids[1] ^ s) * rows, rows), rows)
        low = 0
        for out in outs:
            columns = out.shape[1]
            out[at, :] = piece[:, low : low + columns].astype(F32)
            low += columns
        wide_s[at, :] = piece[:, low:].astype(F32)
    turned = wide_s[...].T
    for k, vec in enumerate(vecs):
        vec[...] = turned[k : k + 1, :].reshape(vec.shape[0])


def narrow_terms(ids, terms):
    narrow_count = lax.axis_size("narrow")
    rows, columns = terms[0].shape
    if rows % (8 * narrow_count):
        return [sum_terms(terms).astype(BF)]
    return stage(
        partial(sum_split_kernel, len(terms)),
        "sum_split",
        ids,
        terms,
        [sds((rows // narrow_count, columns), BF)] * narrow_count,
        [pltpu.VMEM((rows, columns), F32)],
    )


def spread_parts(parts):
    if len(parts) == 1:
        return [lax.psum(parts[0], "narrow")]
    return narrow_return(parts)


def sum_narrow(ids, terms, first):
    if len(terms) == 1:
        return terms[0]
    return sum_parts(ids, tie(terms, first))


def spread_narrow(ids, total, rows, widths, vectors, first):
    narrow_count = lax.axis_size("narrow")
    if total.shape[0] == rows:
        total = total.astype(F32)
        outs, low = [], 0
        for size in widths:
            outs.append(total[:, low : low + size])
            low += size
        return outs[:-1] + [outs[-1][:, k] for k in range(vectors)]
    return stage(
        partial(gather_out_kernel, narrow_count, vectors),
        "gather_out",
        ids,
        tie(narrow_gather(total), first),
        [sds((rows, size), F32) for size in widths[:-1]] + [sds((rows,), F32)] * vectors,
        [pltpu.VMEM((rows, widths[-1]), F32)],
    )


def join_narrow_kernel(turned, ids, keep, came, *outs):
    each = outs[0].shape[0]
    turn = lax.div(ids[0], 2) if turned else 0
    for t, out in enumerate(outs):
        for j in range(each):
            at = ((ids[1] ^ t) * each + j) ^ turn
            out[j] = (keep[at].astype(F32) + came[at].astype(F32)).astype(BF)


def route_kernel(count, ids, *rest):
    pieces, outs, blocks = rest[:count], rest[count:-1], rest[-1]
    each = pieces[0].shape[0]
    for t, piece in enumerate(pieces):
        for j in range(each):
            blocks[(ids[1] ^ t) * each + j] = piece[j]
    chip = lax.div(ids[0], 2)
    for s, out in enumerate(outs):
        out[...] = blocks[chip ^ s]


def unpack_kernel(turned, ids, *rest):
    pieces, rest = rest[:GROUPS], rest[GROUPS:]
    owns, gains, outs, gain_outs, parts = rest[0:2], rest[2:4], rest[4:8:2], rest[5:8:2], rest[8]
    at = lax.div(ids[0], 2)
    if turned:
        at = at ^ ids[1]
    rows = outs[0].shape[0]
    for block in range(2):
        for s, piece in enumerate(pieces):
            parts[lax.rem(at ^ s, GROUPS)] = piece[block].astype(F32)
        total = jnp.zeros((rows, GW), F32)
        for t in range(3):
            for c in range(GROUPS):
                low = (t * GROUPS + c) * GW
                part = parts[c, :, t * GW : (t + 1) * GW]
                outs[block][:, low : low + GW] = part
                total = total + part * owns[block][:, low : low + GW].astype(F32)
        sums = jnp.broadcast_to(jnp.sum(total, axis=1, keepdims=True), (rows, 128)).T
        gain_outs[block][...] = (sums[0:1, :] / gains[block][...]).reshape(rows)


def unpack(ids, pieces, own_rows):
    rows, columns = pieces[0].shape[1:]
    own_r, own_d, gain_r, gain_d = own_rows
    return stage(
        partial(unpack_kernel, direct_delivery()),
        "unpack",
        ids,
        list(pieces) + [own_d, own_r, gain_d, gain_r],
        [sds((rows, GROUPS * columns), F32), sds((rows,), F32)] * 2,
        [pltpu.VMEM((GROUPS, rows, columns), F32)],
    )


def split_narrow(ids, keep, came):
    narrow_count = lax.axis_size("narrow")
    chips, rows, columns = keep.shape
    shape = (chips // narrow_count, rows, columns)
    return stage(
        partial(join_narrow_kernel, direct_delivery()),
        "join_narrow",
        ids,
        [keep, came],
        [sds(shape, BF)] * narrow_count,
    )


def join_all_kernel(turned, ids, keep, came, out):
    turn = lax.div(ids[0], 2) if turned else 0
    for n in range(out.shape[0]):
        out[n] = (keep[n ^ turn].astype(F32) + came[n ^ turn].astype(F32)).astype(BF)


def join_all(ids, keep, came):
    (total,) = stage(
        partial(join_all_kernel, direct_delivery()),
        "join_all",
        ids,
        [keep, came],
        [sds(keep.shape, BF)],
    )
    return total


def sum_parts(ids, terms):
    (total,) = stage(sum_kernel, "sum_terms", ids, terms, [sds(terms[0].shape, BF)])
    return total


def sum_beside_kernel(ids, beside, *rest):
    terms, out = rest[:-1], rest[-1]
    total = terms[0][...].astype(F32)
    for term in terms[1:]:
        total = total + term[...].astype(F32)
    out[0] = beside[...]
    out[1] = total.astype(BF)


def sum_beside(ids, beside, terms):
    (out,) = stage(
        sum_beside_kernel,
        "sum_beside",
        ids,
        [beside] + list(terms),
        [sds((2,) + beside.shape, BF)],
    )
    return out


def route_project(ids, gathered, chips):
    rows, columns = gathered[0].shape[1:]
    return stage(
        partial(route_kernel, len(gathered)),
        "route",
        ids,
        gathered,
        [sds((rows, columns), BF)] * GROUPS,
        [pltpu.VMEM((chips, rows, columns), BF)],
    )


def direct_delivery():
    return lax.axis_size("narrow") == GROUPS and lax.axis_size("wide") == 2 * GROUPS


def deliver(ids, totals, chips):
    narrow_count = lax.axis_size("narrow")
    if not direct_delivery():
        both = [
            chips_return(route_project(ids, narrow_gather(total), chips)) for total in totals
        ]
        return [jnp.stack(pair) for pair in zip(*both)]
    totals = totals.reshape((2,) + totals.shape[2:])

    def moves(k):
        pairs = []
        for chip in range(chips):
            for core in range(2):
                for n in range(narrow_count):
                    to = (2 * (chip ^ n) + core) * narrow_count + (n ^ k)
                    pairs.append(((2 * chip + core) * narrow_count + n, to))
        return pairs

    return [lax.ppermute(totals, ("wide", "narrow"), moves(k)) for k in range(narrow_count)]


def finish_hidden_kernel(ids, dense, routed, e_d, r_d, e_r, r_r):
    hidden = e_d.shape[1]
    for total, e_ref, r_ref in ((dense, e_d, r_d), (routed, e_r, r_r)):
        e_ref[...] = total[:, 0:hidden].astype(F32)
        r_ref[...] = total[:, hidden : 2 * hidden].astype(F32)


def finish_hidden(ids, dense, routed):
    rows, columns = dense.shape
    return stage(
        finish_hidden_kernel,
        "finish_hidden",
        ids,
        [dense, routed],
        [sds((rows, columns // 2), F32)] * 4,
    )


def tie(x, *first):
    return lax.optimization_barrier((x, first))[0]


def narrow_step(x, s):
    return lax.ppermute(x, "narrow", [(j, j ^ s) for j in range(lax.axis_size("narrow"))])


def narrow_gather(x):
    return [x] + [narrow_step(x, s) for s in range(1, lax.axis_size("narrow"))]


def narrow_return(parts):
    return [parts[0]] + [narrow_step(parts[s], s) for s in range(1, len(parts))]


def exchange(pieces):
    wide_count = lax.axis_size("wide")
    return [pieces[0]] + [
        lax.ppermute(pieces[s], "wide", [(j, j ^ s) for j in range(wide_count)])
        for s in range(1, len(pieces))
    ]


def exchange_rows(mine, other):
    wide_count = lax.axis_size("wide")
    if wide_count != 8:
        return exchange([mine, other] * (wide_count // 2))
    beside = core_step(other)
    from_x = [chip_step(mine, 1), chip_step(beside, 1)]
    from_y = [chip_step(mine, 2), chip_step(beside, 2)]
    corner = [chip_step(from_y[0], 1), chip_step(from_x[1], 2)]
    return [mine, beside] + from_x + from_y + corner


def hidden_share(expand, reduce_part):
    wide_count = lax.axis_size("wide")
    here = lax.axis_index("wide")
    width, hidden = expand.shape
    rows = width // wide_count
    if width != hidden or rows % 16:
        return None
    return jnp.stack(
        [
            lax.dynamic_slice_in_dim(expand, here * rows, rows, 0),
            lax.dynamic_slice_in_dim(reduce_part, here * rows, rows, 0),
        ]
    )


def all_chips(x):
    groups = [list(range(core, lax.axis_size("wide"), 2)) for core in range(2)]
    return lax.all_gather(x, "wide", axis=0, axis_index_groups=groups)


def chip_step(x, s):
    return lax.ppermute(
        x, "wide", [(j, j ^ (2 * s)) for j in range(lax.axis_size("wide"))]
    )


def core_step(x):
    return lax.ppermute(x, "wide", [(j, j ^ 1) for j in range(lax.axis_size("wide"))])


def on_device(
    tokens,
    cotangent,
    selected,
    segments,
    router_vector,
    project_routed,
    output_routed,
    prenorm_routed,
    midnorm_routed,
    expand_routed,
    reduce_routed,
    project_dense,
    output_dense,
    prenorm_dense,
    midnorm_dense,
    expand_dense,
    reduce_dense,
):
    seq_count, span_rows, width = tokens.shape
    row_length = selected.shape[1]
    hidden = expand_dense.shape[1]
    wide_count = lax.axis_size("wide")
    narrow_count = lax.axis_size("narrow")
    here = lax.axis_index("wide")
    slot_count = span_rows // 4
    bq_dense = min(512, row_length)
    bq_routed = min(512, slot_count * wide_count)
    ids = jnp.stack([here, lax.axis_index("narrow")]).astype(jnp.int32)
    tok = tokens.reshape(-1, width)
    cot = cotangent.reshape(-1, width)

    share_d = hidden_share(expand_dense, reduce_dense)
    staged = share_d is not None
    if staged:
        own_d = lax.all_gather(share_d, "narrow", axis=0)

    mine = here % seq_count
    seq_segments = lax.dynamic_slice_in_dim(segments, mine, 1, 0)[0]
    seq_selected = lax.dynamic_slice_in_dim(selected, mine, 1, 0)[0].reshape(wide_count, span_rows)
    upper = (
        lax.broadcasted_iota(jnp.int32, (span_rows, span_rows), 0)
        <= lax.broadcasted_iota(jnp.int32, (span_rows, span_rows), 1)
    ).astype(BF)
    slots = jnp.arange(slot_count, dtype=jnp.int32)
    seq_rank = jnp.dot(seq_selected.astype(BF), upper, preferred_element_type=F32)
    seq_rank = jnp.where(seq_selected > 0, seq_rank.astype(jnp.int32) - 1, -1)
    slot_segments = (
        jnp.sum(
            jnp.where(
                seq_rank[:, None, :] == slots[None, :, None],
                seq_segments.reshape(wide_count, 1, span_rows) + 1,
                0,
            ),
            axis=-1,
        )
        - 1
    ).reshape(-1)
    meta_routed = (None, slot_segments[None])
    own_selected = selected
    if span_rows % 128:
        own_selected = lax.dynamic_slice_in_dim(selected, here * span_rows, span_rows, 1)
    mine_r, other_r, one_hot, picked, vecs = routed_pre(
        ids,
        tok,
        own_selected,
        span_rows,
        [router_vector, prenorm_routed, midnorm_routed, prenorm_dense, midnorm_dense],
    )
    columns_r = group_columns(ids, tie(project_routed, mine_r))
    rows_r = exchange([mine_r, other_r] * (wide_count // 2))
    rows_r, slot_segments = lax.optimization_barrier((rows_r, meta_routed[1]))
    meta_routed = (None, slot_segments)
    pieces, kept_r = attend(ids, meta_routed, rows_r, columns_r, bq_routed)
    pieces = exchange(pieces)
    if staged:
        pieces, own_d = lax.optimization_barrier((pieces, own_d))
        chips_d = all_chips(own_d)
    branch_r, low_r, att_r = routed_mid(ids, pieces, output_routed, picked, vecs)
    dense_segments = tie(seq_segments, low_r)
    starts = sum(
        jnp.where(dense_segments == value, jnp.sum((dense_segments < value).astype(jnp.int32)), 0)
        for value in range(1, 4)
    )
    meta_dense = (starts[::bq_dense] // bq_dense, starts[None])

    own_at = here * (width // wide_count)

    def own_slice(x):
        return lax.dynamic_slice_in_dim(tie(x, low_r), own_at, width // wide_count, 0)

    own_rows = (
        own_slice(project_routed),
        own_slice(project_dense),
        own_slice(prenorm_routed).astype(F32)[None],
        own_slice(prenorm_dense).astype(F32)[None],
    )
    columns_d = group_columns(ids, tie(project_dense, low_r))
    share_r = hidden_share(tie(expand_routed, low_r), reduce_routed)
    low_pieces, columns_d, meta_dense, own_rows, share_r = lax.optimization_barrier(
        (narrow_gather(low_r), columns_d, meta_dense, own_rows, share_r)
    )
    partials = narrow_return(hidden_forward(ids, low_pieces, expand_routed, reduce_routed))

    mine_d, other_d, mixed, delta_r = dense_pre(
        ids, tok, one_hot, picked, vecs, branch_r, partials
    )
    if staged:
        rows_d = exchange_rows(mine_d, other_d)
        own_r = lax.all_gather(tie(share_r, rows_d[1], chips_d), "narrow", axis=0)[None]
        rows_d, own_r = lax.optimization_barrier((rows_d, own_r))
        weights_d = [chips_d, core_step(chips_d)]
    else:
        rows_d = exchange_rows(mine_d, other_d)
        weights_d = [
            lax.all_gather(expand_dense, "narrow", axis=0),
            lax.all_gather(reduce_dense, "narrow", axis=0),
        ]
        weights_r = [
            lax.all_gather(expand_routed, "narrow", axis=0),
            lax.all_gather(reduce_routed, "narrow", axis=0),
        ]
    cot_all = lax.all_gather(tie(cot, rows_d), "narrow", axis=0, tiled=True)
    (stack,), kept_d = attend(ids, meta_dense, rows_d, columns_d, bq_dense, stacked=True)
    stack, weights_d = lax.optimization_barrier((stack, weights_d))
    stack = lax.all_to_all(stack, "wide", 0, 0)
    if staged:
        stack, own_r = lax.optimization_barrier((stack, own_r))
        corner_r = chip_step(own_r, 3)
    (activations, low_d, back_d, sum_d, att_d, mid_gain_d), stack = dense_ffn(
        ids, stack, output_dense, mixed, cot, vecs, weights_d
    )
    if staged:
        stack, low_d, cot_all, corner_r = lax.optimization_barrier(
            (stack, low_d, cot_all, corner_r)
        )
    low_all = lax.all_gather(low_d, "narrow", axis=0, tiled=True)
    keep_d, send_d = output_grads(ids, wide_count, att_d, back_d, [])
    stack, keep_d, send_d = lax.optimization_barrier(
        (lax.all_to_all(stack, "wide", 0, 0), keep_d, send_d)
    )
    came_d = core_step(send_d)
    if staged:
        stack, own_r = lax.optimization_barrier((stack, own_r))
        sides_r = [chip_step(own_r, 1), chip_step(own_r, 2)]
        corner_r = [corner_r, core_step(corner_r)]
        weights_r = [own_r, core_step(own_r)]
    (stack,), dx_d = attend_back(ids, meta_dense, kept_d, [stack], bq_dense, stacked=True)
    stack, dx_d, weights_r, came_d = lax.optimization_barrier(
        (stack, dx_d, weights_r, came_d)
    )
    if staged:
        stack, dx_d, sides_r = lax.optimization_barrier((stack, dx_d, sides_r))
        weights_r += [w for own in sides_r for w in (own, core_step(own))] + corner_r
    stack = lax.all_to_all(stack, "wide", 0, 0)
    keep, send = project_grads(ids, wide_count, rows_d, dx_d)
    project_d = join_all(ids, keep, core_step(send))
    low_all, project_d = lax.optimization_barrier((low_all, project_d))
    project_d = lax.psum_scatter(project_d, "narrow", scatter_dimension=0, tiled=True)
    hidden_d = hidden_grads(ids, low_all, cot_all, expand_dense, reduce_dense)
    stack, hidden_d, weights_r = lax.optimization_barrier((stack, hidden_d, weights_r))
    ffn_d = lax.psum_scatter(hidden_d, "wide", scatter_dimension=0, tiled=True)
    g_mixed, g_delta, g_low, g_gate, router_grad = dense_post(
        ids, stack, project_dense, vecs, mixed, sum_d, one_hot, picked, delta_r
    )

    g_pieces = narrow_gather(g_low)
    g_mid_r, back_r, mid_gain_r, stack = routed_back(
        ids,
        wide_count,
        low_r,
        g_low,
        branch_r,
        picked,
        vecs,
        g_delta,
        output_routed,
        weights_r,
    )
    back_r, g_pieces = lax.optimization_barrier((back_r, g_pieces))
    keep_r, send_r = output_grads(
        ids, wide_count, att_r, back_r, [mid_gain_r, mid_gain_d, router_grad]
    )
    came_r = core_step(send_r)
    hidden_r = hidden_grads(
        ids,
        tie(low_pieces, keep_r),
        g_pieces,
        expand_routed,
        reduce_routed,
    )
    stack, keep_r, send_r, hidden_r = lax.optimization_barrier(
        (lax.all_to_all(stack, "wide", 0, 0), keep_r, send_r, hidden_r)
    )
    output_parts = join_chips(ids, tie([keep_d, keep_r], hidden_r), [came_d, came_r])
    stack, output_parts = lax.optimization_barrier((stack, output_parts))
    output_terms = chips_return(output_parts)
    (stack,), dx_r = attend_back(ids, meta_routed, kept_r, [stack], bq_routed, stacked=True)
    stack, dx_r, output_terms[1], project_d = lax.optimization_barrier(
        (stack, dx_r, output_terms[1], project_d)
    )
    keep, send = project_grads(ids, wide_count, rows_r, dx_r)
    came = core_step(send)
    output_parts = narrow_terms(ids, tie(output_terms, send))
    ffn_r = lax.psum_scatter(
        tie(hidden_r, output_parts), "wide", scatter_dimension=0, tiled=True
    )
    project_parts = split_narrow(ids, tie(keep, output_parts), came)
    returned = narrow_return(project_parts)
    stack = lax.all_to_all(tie(stack, send), "wide", 0, 0)
    returned, output_parts = lax.optimization_barrier(
        (returned, spread_parts(output_parts))
    )
    projects = sum_beside(ids, project_d, returned)
    output_total = sum_narrow(ids, output_parts, projects)
    tokens_gradient = routed_post(
        ids,
        tie(stack, output_total),
        project_routed,
        vecs,
        picked,
        g_mid_r,
        g_mixed,
        one_hot,
        g_gate,
    )
    delivered = deliver(ids, projects, keep.shape[0])
    project_d_grad, pre_gain_d, project_r_grad, pre_gain_r = unpack(
        ids, tie(delivered, tokens_gradient), own_rows
    )
    output_d_grad, output_r_grad, mid_r_grad, mid_d_grad, router_grad = spread_narrow(
        ids, output_total, width // wide_count, [width, width, 128], 3, project_r_grad
    )
    expand_d_grad, reduce_d_grad, expand_r_grad, reduce_r_grad = finish_hidden(
        ids, ffn_d, ffn_r
    )
    return (
        activations.reshape(tokens.shape),
        tokens_gradient.reshape(tokens.shape),
        router_grad,
        project_r_grad,
        output_r_grad,
        pre_gain_r,
        mid_r_grad,
        expand_r_grad,
        reduce_r_grad.T,
        project_d_grad,
        output_d_grad,
        pre_gain_d,
        mid_d_grad,
        expand_d_grad,
        reduce_d_grad.T,
    )


def solution(mesh):
    return jax.shard_map(
        on_device,
        mesh=mesh,
        in_specs=(
            P("narrow", "wide", None),
            P("narrow", "wide", None),
            P("narrow", None),
            P("narrow", None),
            P(),
            P(),
            P(),
            P(),
            P(),
            P(None, "narrow"),
            P("narrow", None),
            P(),
            P(),
            P(),
            P(),
            P(None, "narrow"),
            P("narrow", None),
        ),
        out_specs=(
            P("narrow", "wide", None),
            P("narrow", "wide", None),
            P("wide"),
            P("wide", None),
            P("wide", None),
            P("wide"),
            P("wide"),
            P("wide", "narrow"),
            P("narrow", "wide"),
            P("wide", None),
            P("wide", None),
            P("wide"),
            P("wide"),
            P("wide", "narrow"),
            P("narrow", "wide"),
        ),
        check_vma=False,
    )
```

```python
from functools import partial

import jax
import jax.numpy as jnp
from jax import lax
from jax.experimental import pallas as pl
from jax.experimental.pallas import tpu as pltpu
from jax.sharding import PartitionSpec as P

H = 12
HD = 64
GROUPS = 4
HG = H // GROUPS
GW = HG * HD

EPSILON = 1e-06
NEGATIVE = -1e30
SCORE_SCALE = 0.125
LOG2E = 1.4426950408889634
GELU_A = 0.7978845608028654
GELU_B = 0.044715
BF = jnp.bfloat16
F32 = jnp.float32
VMEM = 56 << 20


def nt_dot(left, right):
    return lax.dot_general(left, right, (((1,), (1,)), ((), ())), preferred_element_type=F32)


def tn_dot(left, right):
    return lax.dot_general(left, right, (((0,), (0,)), ((), ())), preferred_element_type=F32)


def dot(left, right):
    return jnp.dot(left, right, preferred_element_type=F32)


def sds(shape, dtype):
    return jax.ShapeDtypeStruct(shape, dtype)


def norm_scale(rows):
    return lax.rsqrt(jnp.mean(rows * rows, axis=-1, keepdims=True) + EPSILON)


def norm_back(grad, rows, gain):
    scale = norm_scale(rows)
    inner = grad * gain
    mean = jnp.mean(inner * rows, axis=-1, keepdims=True)
    grad_rows = scale * inner - rows * (scale * scale * scale * mean)
    return grad_rows, jnp.sum(grad * rows * scale, axis=0, keepdims=True)


def gelu(a):
    return 0.5 * a * (1.0 + jnp.tanh(GELU_A * (a + GELU_B * (a * a * a))))


def gelu_both(a):
    square = a * a
    bend = jnp.tanh(GELU_A * (a + GELU_B * (square * a)))
    half = 0.5 * (1.0 + bend)
    slope = half + 0.5 * a * (1.0 - bend * bend) * (GELU_A * (1.0 + 3.0 * GELU_B * square))
    return a * half, slope


def three_parts(x):
    first = x.astype(BF)
    rest = x - first.astype(F32)
    second = rest.astype(BF)
    third = (rest - second.astype(F32)).astype(BF)
    return [first, second, third]


def place(one_hot, x):
    return tn_dot(
        jnp.concatenate([one_hot] * 3, axis=0), jnp.concatenate(three_parts(x), axis=0)
    )


def pick(one_hot, x):
    return dot(jnp.concatenate([one_hot] * 3, axis=1), jnp.concatenate(three_parts(x), axis=0))


def combo(index):
    return lax.rem(lax.div(index, 2), GROUPS), lax.rem(index, 2)


def save_pieces(me, full, parts, pieces):
    rows = full.shape[0] // 2
    thirds = full.shape[1] // (GROUPS * GW)
    for c in range(GROUPS):
        for t in range(thirds):
            at = t * GROUPS * GW + c * GW
            parts[c, :, t * GW : (t + 1) * GW] = full[:, at : at + GW]
    for s, piece in enumerate(pieces):
        c, r = combo(me ^ s)
        piece[...] = parts[c, pl.ds(pl.multiple_of(r * rows, rows), rows), :]


def load_pieces(me, pieces, parts, thirds):
    rows = pieces[0].shape[0]
    for s, piece in enumerate(pieces):
        c, r = combo(me ^ s)
        parts[c, pl.ds(pl.multiple_of(r * rows, rows), rows), :] = piece[...]
    return jnp.concatenate(
        [parts[c, :, t * GW : (t + 1) * GW] for t in range(thirds) for c in range(GROUPS)],
        axis=1,
    )


def save_stack(full, parts, stack):
    rows = full.shape[0] // 2
    thirds = full.shape[1] // (GROUPS * GW)
    half, columns = rows // 2, thirds * GW
    for c in range(GROUPS):
        for t in range(thirds):
            at = t * GROUPS * GW + c * GW
            parts[c, :, t * GW : (t + 1) * GW] = full[:, at : at + GW]
    for b in range(stack.shape[0]):
        c, at = (b // 2) % GROUPS, (b % 2) * rows
        stack[b, :, 0:columns] = parts[c, at : at + half, :]
        stack[b, :, columns : 2 * columns] = parts[c, at + half : at + rows, :]


def load_stack(me, stack, parts, thirds):
    half, columns = stack.shape[1], stack.shape[2] // 2
    first = lax.div(me, 2 * GROUPS) * (2 * GROUPS)
    for w in range(2 * GROUPS):
        c, at = w // 2, (w % 2) * 2 * half
        parts[c, at : at + half, :] = stack[first + w, :, 0:columns]
        parts[c, at + half : at + 2 * half, :] = stack[first + w, :, columns : 2 * columns]
    return jnp.concatenate(
        [parts[c, :, t * GW : (t + 1) * GW] for t in range(thirds) for c in range(GROUPS)],
        axis=1,
    )


def stage(body, name, ids, operands, outs, scratch=(), flops=0, grid=None, specs=None):
    kwargs = {}
    if grid is not None:
        kwargs["grid"] = grid
    in_specs = [pl.BlockSpec(memory_space=pltpu.SMEM)]
    for k, operand in enumerate(operands):
        spec = None if specs is None else specs.get(k)
        if spec is None:
            zeros = (0,) * operand.ndim
            spec = pl.BlockSpec(operand.shape, lambda *_, z=zeros: z)
        in_specs.append(spec)
    out_specs = tuple(
        pl.BlockSpec(out.shape, lambda *_, z=(0,) * len(out.shape): z) for out in outs
    )
    moved = sum(a.size * a.dtype.itemsize for a in operands)
    moved += sum(math_prod(a.shape) * a.dtype.itemsize for a in outs)
    return pl.pallas_call(
        body,
        out_shape=tuple(outs),
        in_specs=in_specs,
        out_specs=out_specs,
        scratch_shapes=list(scratch),
        compiler_params=pltpu.CompilerParams(vmem_limit_bytes=VMEM),
        cost_estimate=pl.CostEstimate(flops=flops, bytes_accessed=moved, transcendentals=0),
        name=name,
        **kwargs,
    )(ids, *operands)


def math_prod(shape):
    total = 1
    for size in shape:
        total *= size
    return total


def head_parts(rows):
    lane = lax.broadcasted_iota(jnp.int32, rows.shape, 1)
    zero = jnp.zeros_like(rows)
    return [
        jnp.where((lane >= h * HD) & (lane < (h + 1) * HD), rows, zero) for h in range(HG)
    ]


def pair_mask(row_ref, col_ref, q_at, k_at, bk, bq):
    k_iota = lax.broadcasted_iota(jnp.int32, (bk, bq), 0) + k_at
    q_iota = lax.broadcasted_iota(jnp.int32, (bk, bq), 1) + q_at
    info = row_ref[0:1, pl.ds(q_at, bq)]
    if col_ref is None:
        return (k_iota >= info) & (k_iota <= q_iota)
    info = info.astype(F32)
    return (col_ref[pl.ds(k_at, bk), 0:1] == info) & (k_iota <= q_iota)


def turn(row):
    return jnp.broadcast_to(row.astype(F32), (128, row.shape[1])).T


def attend_kernel(bq, count, sends, stacked, by_column, ids, first_ref, row_ref, *rest):
    rest = list(rest)
    pieces, rest = rest[:count], rest[count:]
    columns = rest.pop(0)
    out_pieces, rest = rest[:sends], rest[sends:]
    stack_ref = rest.pop(0) if stacked else None
    o_ref, lse_ref, x_ref, k_s, v_s, vt_s = rest[:6]
    col_ref = rest[6] if by_column else None
    i = pl.program_id(0)
    me = ids[0]
    rows = pieces[0].shape[0]
    bk = bq

    @pl.when(i == 0)
    def _():
        for s in range(count):
            at = pl.ds(pl.multiple_of((me ^ s) * rows, rows), rows)
            x = dot(pieces[s][...], columns[...]).astype(BF)
            x_ref[at, :] = x
            k_s[at, :] = x[:, GW : 2 * GW]
            v_s[at, :] = x[:, 2 * GW : 3 * GW]
        vt_s[...] = v_s[...].T
        if by_column:
            col_ref[...] = turn(row_ref[...])

    q_at = pl.multiple_of(i * bq, bq)
    q_heads = head_parts(x_ref[pl.ds(q_at, bq), 0:GW])

    def step(j, carry):
        k_at = pl.multiple_of(j * bk, bk)
        keys = k_s[pl.ds(k_at, bk), :]
        mask = pair_mask(row_ref, col_ref, q_at, k_at, bk, bq)
        out = []
        for h in range(HG):
            top, total, acc = carry[h]
            scores = nt_dot(keys, q_heads[h]) * (SCORE_SCALE * LOG2E)
            scores = jnp.where(mask, scores, NEGATIVE)
            top_new = jnp.maximum(top, jnp.max(scores, axis=0, keepdims=True))
            weight = jnp.exp2(scores - top_new)
            fade = jnp.exp2(top - top_new)
            total = total * fade + jnp.sum(weight, axis=0, keepdims=True)
            values_t = vt_s[h * HD : (h + 1) * HD, pl.ds(k_at, bk)]
            acc = acc * fade + dot(values_t, weight.astype(BF))
            out.append((top_new, total, acc))
        return tuple(out)

    start = tuple(
        (
            jnp.full((1, bq), NEGATIVE, F32),
            jnp.zeros((1, bq), F32),
            jnp.zeros((HD, bq), F32),
        )
        for _ in range(HG)
    )
    done = lax.fori_loop(0 if by_column else first_ref[i], i + 1, step, start)
    outs = jnp.concatenate([acc / total for _, total, acc in done], axis=0)
    o_ref[pl.ds(q_at, bq), :] = outs.T.astype(BF)
    for h in range(HG):
        top, total, _ = done[h]
        lse_ref[h : h + 1, pl.ds(q_at, bq)] = top + jnp.log2(total)

    @pl.when(i == pl.num_programs(0) - 1)
    def _():
        for s in range(sends):
            at = pl.ds(pl.multiple_of((me ^ s) * rows, rows), rows)
            out_pieces[s][...] = o_ref[at, :]
        if stacked:
            half = rows // 2
            for b in range(count):
                at = b * rows
                stack_ref[b, :, 0:GW] = o_ref[at : at + half, :]
                stack_ref[b, :, GW : 2 * GW] = o_ref[at + half : at + rows, :]


def attend_back_kernel(bq, count, sends, stacked, by_column, ids, first_ref, row_ref, *rest):
    rest = list(rest)
    x_ref = rest.pop(0)
    given = 1 if stacked else count
    grads, rest = rest[:given], rest[given:]
    o_ref, lse_ref = rest[:2]
    out_pieces, rest = rest[2 : 2 + sends], rest[2 + sends :]
    stack_ref = rest.pop(0) if stacked else None
    dx_ref, k_s, v_s, g_s, dk_s, dv_s = rest[:6]
    col_ref = rest[6] if by_column else None
    i = pl.program_id(0)
    me = ids[0]
    rows = g_s.shape[0] // count
    bk = bq

    @pl.when(i == 0)
    def _():
        k_s[...] = x_ref[:, GW : 2 * GW]
        v_s[...] = x_ref[:, 2 * GW : 3 * GW]
        for s in range(count):
            if stacked:
                half = rows // 2
                g_s[s * rows : s * rows + half, :] = grads[0][s, :, 0:GW]
                g_s[s * rows + half : (s + 1) * rows, :] = grads[0][s, :, GW : 2 * GW]
            else:
                at = pl.ds(pl.multiple_of((me ^ s) * rows, rows), rows)
                g_s[at, :] = grads[s][...]
        if by_column:
            col_ref[...] = turn(row_ref[...])
        dk_s[...] = jnp.zeros_like(dk_s)
        dv_s[...] = jnp.zeros_like(dv_s)

    q_at = pl.multiple_of(i * bq, bq)
    grad = g_s[pl.ds(q_at, bq), :]
    q_heads = head_parts(x_ref[pl.ds(q_at, bq), 0:GW])
    g_heads = head_parts(grad)
    dots = (grad.astype(F32) * o_ref[pl.ds(q_at, bq), :].astype(F32)).T
    row_dot = [
        jnp.sum(dots[h * HD : (h + 1) * HD, :], axis=0, keepdims=True) for h in range(HG)
    ]
    lse = [lse_ref[h : h + 1, pl.ds(q_at, bq)] for h in range(HG)]

    def step(j, dq):
        k_at = pl.multiple_of(j * bk, bk)
        here = pl.ds(k_at, bk)
        keys = k_s[here, :]
        values = v_s[here, :]
        key_heads = head_parts(keys)
        mask = pair_mask(row_ref, col_ref, q_at, k_at, bk, bq)
        dk = dk_s[here, :]
        dv = dv_s[here, :]
        for h in range(HG):
            scores = nt_dot(keys, q_heads[h]) * (SCORE_SCALE * LOG2E)
            scores = jnp.where(mask, scores - lse[h], NEGATIVE)
            soft = jnp.exp2(scores)
            g_soft = nt_dot(values, g_heads[h])
            g_scores = (soft * (g_soft - row_dot[h])).astype(BF)
            dv = dv + dot(soft.astype(BF), g_heads[h])
            dk = dk + dot(g_scores, q_heads[h])
            dq = dq + tn_dot(g_scores, key_heads[h])
        dk_s[here, :] = dk
        dv_s[here, :] = dv
        return dq

    dq = lax.fori_loop(0 if by_column else first_ref[i], i + 1, step, jnp.zeros((bq, GW), F32))
    dx_ref[pl.ds(q_at, bq), 0:GW] = (dq * SCORE_SCALE).astype(BF)

    @pl.when(i == pl.num_programs(0) - 1)
    def _():
        dx_ref[:, GW : 2 * GW] = (dk_s[...] * SCORE_SCALE).astype(BF)
        dx_ref[:, 2 * GW : 3 * GW] = dv_s[...].astype(BF)
        for s in range(sends):
            at = pl.ds(pl.multiple_of((me ^ s) * rows, rows), rows)
            out_pieces[s][...] = dx_ref[at, :]
        if stacked:
            half = rows // 2
            for b in range(count):
                at = b * rows
                stack_ref[b, :, 0 : 3 * GW] = dx_ref[at : at + half, :]
                stack_ref[b, :, 3 * GW : 6 * GW] = dx_ref[at + half : at + rows, :]


def attend(ids, meta, pieces, columns, bq, stacked=False):
    first, row_info = meta
    by_column = first is None
    if by_column:
        first = ids
    rows, width = pieces[0].shape
    count = len(pieces)
    sends = 0 if stacked else min(count, 2 * GROUPS)
    length = rows * count
    operands = [first, row_info]
    operands += list(pieces) + [columns]
    outs = [sds((rows, GW), BF)] * sends
    outs += [sds((count, rows // 2, 2 * GW), BF)] if stacked else []
    outs += [
        sds((length, GW), BF),
        sds((8, length), F32),
        sds((length, 3 * GW), BF),
    ]
    got = stage(
        partial(attend_kernel, bq, count, sends, stacked, by_column),
        "attend",
        ids,
        operands,
        outs,
        [pltpu.VMEM((length, GW), BF)] * 2
        + [pltpu.VMEM((GW, length), BF)]
        + ([pltpu.VMEM((length, 128), F32)] if by_column else []),
        flops=length * length * GW * 2 + 6 * length * width * GW,
        grid=(length // bq,),
        specs={0: pl.BlockSpec(memory_space=pltpu.SMEM)},
    )
    return got[:-3], got[-3:]


def attend_back(ids, meta, kept, grads, bq, stacked=False):
    first, row_info = meta
    by_column = first is None
    if by_column:
        first = ids
    attended, lse, x = kept
    count = grads[0].shape[0] if stacked else len(grads)
    rows = attended.shape[0] // count
    sends = 0 if stacked else min(count, 2 * GROUPS)
    length = rows * count
    operands = [first, row_info]
    operands += [x] + list(grads) + [attended, lse]
    got = stage(
        partial(attend_back_kernel, bq, count, sends, stacked, by_column),
        "attend_back",
        ids,
        operands,
        [sds((rows, 3 * GW), BF)] * sends
        + ([sds((count, rows // 2, 6 * GW), BF)] if stacked else [])
        + [sds(x.shape, BF)],
        [pltpu.VMEM((length, GW), BF)] * 3
        + [pltpu.VMEM((length, GW), F32)] * 2
        + ([pltpu.VMEM((length, 128), F32)] if by_column else []),
        flops=length * length * GW * 5,
        grid=(length // bq,),
        specs={0: pl.BlockSpec(memory_space=pltpu.SMEM)},
    )
    return got[:-1], got[-1]


def project_grads_kernel(count, ids, dx_ref, *rest):
    pieces, (keep, send, rows_s, total) = rest[:count], rest[count:]
    rows = pieces[0].shape[0]
    for s, piece in enumerate(pieces):
        rows_s[pl.ds(pl.multiple_of((ids[0] ^ s) * rows, rows), rows), :] = piece[...]
    total[...] = tn_dot(rows_s[...], dx_ref[...])
    split_rows(ids[0], total, keep, send)


def project_grads(ids, wide_count, pieces, dx):
    rows, width = pieces[0].shape
    shape = (wide_count // 2, width // wide_count, 3 * GW)
    return stage(
        partial(project_grads_kernel, len(pieces)),
        "project_grads",
        ids,
        [dx] + list(pieces),
        [sds(shape, BF)] * 2,
        [pltpu.VMEM((dx.shape[0], width), BF), pltpu.VMEM((width, 3 * GW), F32)],
        flops=6 * dx.size * width // 3,
    )


def group_columns_kernel(ids, project, out):
    group, _ = combo(ids[0])
    width = GROUPS * GW
    for c in range(GROUPS):

        @pl.when(group == c)
        def _():
            for t in range(3):
                at = t * width + c * GW
                out[:, t * GW : (t + 1) * GW] = project[:, at : at + GW]


def group_columns(ids, project):
    (out,) = stage(
        group_columns_kernel,
        "group_columns",
        ids,
        [project],
        [sds((project.shape[0], 3 * GW), BF)],
    )
    return out


def save_halves(me, normed, mine_ref, other_ref):
    rows = mine_ref.shape[0]
    core = lax.rem(me, 2)
    mine_ref[...] = normed[pl.ds(pl.multiple_of(core * rows, rows), rows), :]
    other_ref[...] = normed[pl.ds(pl.multiple_of((1 - core) * rows, rows), rows), :]


def routed_pre_kernel(count, ids, tok, sel, *rest):
    vectors, rest = rest[:count], rest[count:]
    mine_ref, other_ref, one_hot_ref, picked_ref, vecs, normed = rest
    rows = [vector[...].astype(F32).reshape(1, -1) for vector in vectors]
    rows.append(jnp.zeros((8 - count, tok.shape[1]), F32))
    vecs[...] = jnp.concatenate(rows, axis=0)
    span = one_hot_ref.shape[1]
    seqs = sel.shape[0]
    if sel.shape[1] != span:
        sel = sel[:, pl.ds(pl.multiple_of(ids[0] * span, span), span)]
    slots = span // 4
    upper = (
        lax.broadcasted_iota(jnp.int32, (span, span), 0)
        <= lax.broadcasted_iota(jnp.int32, (span, span), 1)
    ).astype(F32).astype(BF)
    slot = lax.broadcasted_iota(jnp.int32, (slots, span), 0).astype(F32)
    for q in range(seqs):
        chosen = jnp.broadcast_to(sel[q : q + 1, :].astype(F32), (8, span))
        rank = dot(chosen.astype(BF), upper)[0:1, :] * chosen[0:1, :] - 1.0
        one_hot = (slot == rank).astype(F32).astype(BF)
        one_hot_ref[q * slots : (q + 1) * slots, :] = one_hot
        picked_ref[q * slots : (q + 1) * slots, :] = dot(
            one_hot, tok[q * span : (q + 1) * span, :]
        ).astype(BF)
    picked = picked_ref[...].astype(F32)
    normed[...] = (picked * norm_scale(picked) * gain_of(vecs, 1)).astype(BF)
    save_halves(ids[0], normed, mine_ref, other_ref)


def gain_of(vecs, k):
    return vecs[k : k + 1, :]


def routed_pre(ids, tok, sel, span, vectors):
    rows, width = tok.shape[0] // 4, tok.shape[1]
    return stage(
        partial(routed_pre_kernel, len(vectors)),
        "routed_pre",
        ids,
        [tok, sel] + vectors,
        [
            sds((rows // 2, width), BF),
            sds((rows // 2, width), BF),
            sds((rows, span), BF),
            sds((rows, width), BF),
            sds((8, width), F32),
        ],
        [pltpu.VMEM((rows, width), BF)],
        flops=4 * rows * width * span,
    )


def routed_mid_kernel(count, ids, *rest):
    pieces = rest[:count]
    output, picked, vecs, branch_ref, low_ref, att_ref, parts = rest[count:]
    attended = load_pieces(ids[0], pieces, parts, 1)
    att_ref[...] = attended
    branch = dot(attended, output[...])
    branch_ref[...] = branch
    middle = picked[...].astype(F32) + branch
    low_ref[...] = (middle * norm_scale(middle) * gain_of(vecs, 2)).astype(BF)


def routed_mid(ids, pieces, output, picked, vecs):
    shape = picked.shape
    return stage(
        partial(routed_mid_kernel, len(pieces)),
        "routed_mid",
        ids,
        list(pieces) + [output, picked, vecs],
        [sds(shape, F32), sds(shape, BF), sds(shape, BF)],
        [pltpu.VMEM((GROUPS, shape[0], GW), BF)],
        flops=2 * shape[0] * shape[1] * shape[1],
    )


def hidden_forward_kernel(count, ids, *rest):
    pieces = rest[:count]
    expand, reduce_ref = rest[count : count + 2]
    outs = rest[count + 2 :]
    rows = pieces[0].shape[0]
    low = jnp.concatenate([piece[...] for piece in pieces], axis=0)
    hidden = gelu(dot(low, expand[...])).astype(BF)
    total = dot(hidden, reduce_ref[...]).astype(BF)
    for s, out in enumerate(outs):
        out[...] = total[s * rows : (s + 1) * rows, :]


def hidden_forward(ids, pieces, expand, reduce_part):
    return stage(
        partial(hidden_forward_kernel, len(pieces)),
        "hidden_forward",
        ids,
        list(pieces) + [expand, reduce_part],
        [sds(pieces[0].shape, BF)] * len(pieces),
        flops=4 * len(pieces) * pieces[0].size * expand.shape[1],
    )


def dense_pre_kernel(shares, ids, tok, one_hot, picked, vecs, branch, *rest):
    partials = rest[:shares]
    mine_ref, other_ref, mixed_ref, delta_ref, normed = rest[shares:]
    slots, span = one_hot.shape[0] // 2, one_hot.shape[1]
    delta = branch[...]
    for share in partials:
        delta = delta + share[...].astype(F32)
    delta_ref[...] = delta
    gate = jnp.sum(picked[...].astype(F32) * gain_of(vecs, 0), axis=-1, keepdims=True)
    lifted = gate * delta
    for q in range(2):
        at, spots = slice(q * span, (q + 1) * span), slice(q * slots, (q + 1) * slots)
        mixed = tok[at, :].astype(F32) + place(one_hot[spots, :], lifted[spots, :])
        mixed_ref[at, :] = mixed
        normed[at, :] = (mixed * norm_scale(mixed) * gain_of(vecs, 3)).astype(BF)
    save_halves(ids[0], normed, mine_ref, other_ref)


def dense_pre(ids, tok, one_hot, picked, vecs, branch, partials):
    rows, width = tok.shape
    return stage(
        partial(dense_pre_kernel, len(partials)),
        "dense_pre",
        ids,
        [tok, one_hot, picked, vecs, branch] + list(partials),
        [
            sds((rows // 2, width), BF),
            sds((rows // 2, width), BF),
            sds(tok.shape, F32),
            sds(picked.shape, F32),
        ],
        [pltpu.VMEM((rows, width), BF)],
        flops=6 * rows * width * one_hot.shape[0],
    )


def this_part(me, weights, scratch):
    if not scratch:
        return weights[0][0], weights[1][0]
    e_s, r_s = scratch
    core = lax.rem(me, 2)
    rows = weights[0].shape[-2]
    if len(weights) == 2:
        blocks = []
        for c in range(weights[0].shape[0]):
            blocks.append((weights[0], c, 2 * c + core))
            blocks.append((weights[1], c, 2 * c + 1 - core))
    else:
        blocks = [(weight, 0, me ^ s) for s, weight in enumerate(weights)]
    for weight, c, at in blocks:
        at = pl.ds(pl.multiple_of(at * rows, rows), rows)
        e_s[at, :] = weight[c, 0, 0]
        r_s[at, :] = weight[c, 0, 1]
    return e_s[...], r_s[...]


def part_specs(base, weights):
    if weights[0].ndim == 3:
        return {
            base + k: pl.BlockSpec((1,) + w.shape[1:], lambda n: (n, 0, 0))
            for k, w in enumerate(weights)
        }
    return {
        base + k: pl.BlockSpec(
            (w.shape[0], 1) + w.shape[2:], lambda n: (0, n, 0, 0, 0)
        )
        for k, w in enumerate(weights)
    }


def part_scratch(width, weights):
    if weights[0].ndim == 3:
        return []
    return [pltpu.VMEM((width, weights[0].shape[-1]), BF)] * 2


def dense_ffn_kernel(split, ids, stack, *rest):
    output, mixed, cot, vecs = rest[:4]
    gain = gain_of(vecs, 4)
    rest = rest[4:]
    weights, rest = rest[:split], rest[split:]
    act_ref, low_ref, back_ref, sum_ref, att_ref, gain_ref = rest[:6]
    g_stack, rest = rest[6], rest[7:]
    parts, branch_s, delta_s, grad_s = rest[:4]
    n = pl.program_id(0)
    me = ids[0]

    @pl.when(n == 0)
    def _():
        attended = load_stack(me, stack, parts, 1)
        att_ref[...] = attended
        branch = dot(attended, output[...])
        branch_s[...] = branch
        middle = mixed[...] + branch
        low_ref[...] = (middle * norm_scale(middle) * gain).astype(BF)
        delta_s[...] = jnp.zeros_like(delta_s)
        grad_s[...] = jnp.zeros_like(grad_s)

    expand, reduce_w = this_part(me, weights, rest[4:])
    value, slope = gelu_both(dot(low_ref[...], expand))
    delta_s[...] += dot(value.astype(BF), reduce_w)
    grad_pre = (nt_dot(cot[...], reduce_w) * slope).astype(BF)
    grad_s[...] += nt_dot(grad_pre, expand)

    @pl.when(n == pl.num_programs(0) - 1)
    def _():
        middle = mixed[...] + branch_s[...]
        act_ref[...] = (middle + delta_s[...]).astype(BF)
        grad_middle, gain_grad = norm_back(grad_s[...], middle, gain)
        gain_ref[...] = jnp.broadcast_to(gain_grad, gain_ref.shape)
        total = cot[...].astype(F32) + grad_middle
        sum_ref[...] = total
        back = total.astype(BF)
        back_ref[...] = back
        save_stack(nt_dot(back, output[...]).astype(BF), parts, g_stack)


def dense_ffn(ids, stack, output, mixed, cot, vecs, weights):
    rows, width = mixed.shape
    split = len(weights)
    parts_n = weights[0].shape[0 if weights[0].ndim == 3 else 1]
    hidden = weights[0].shape[-1]
    base = 5
    specs = part_specs(base, weights)
    scratch = [pltpu.VMEM((GROUPS, rows, GW), BF)] + [pltpu.VMEM((rows, width), F32)] * 3
    scratch += part_scratch(width, weights)
    outs = [
        sds((rows, width), BF),
        sds((rows, width), BF),
        sds((rows, width), BF),
        sds((rows, width), F32),
        sds((rows, width), BF),
        sds((8, width), F32),
        sds(stack.shape, BF),
    ]
    got = stage(
        partial(dense_ffn_kernel, split),
        "dense_ffn",
        ids,
        [stack, output, mixed, cot, vecs] + list(weights),
        outs,
        scratch,
        flops=8 * rows * width * hidden * parts_n + 4 * rows * width * width,
        grid=(parts_n,),
        specs=specs,
    )
    return got[:6], got[6]


def dense_post_kernel(ids, stack, *rest):
    project, vecs, mixed, total, one_hot, picked, delta = rest[:7]
    g_mixed_ref, g_delta_ref, g_low_ref, g_gate_ref, router_ref, parts = rest[7:]
    g_proj = load_stack(ids[0], stack, parts, 3)
    grad_rows, _ = norm_back(nt_dot(g_proj, project[...]), mixed[...], gain_of(vecs, 3))
    g_mixed_ref[...] = total[...] + grad_rows
    slots, span = one_hot.shape[0] // 2, one_hot.shape[1]
    rows = picked[...].astype(F32)
    gate = jnp.sum(rows * gain_of(vecs, 0), axis=-1, keepdims=True)
    router = jnp.zeros((1, rows.shape[1]), F32)
    for q in range(2):
        at, spots = slice(q * span, (q + 1) * span), slice(q * slots, (q + 1) * slots)
        lifted = pick(one_hot[spots, :], g_mixed_ref[at, :])
        g_delta = gate[spots, :] * lifted
        g_delta_ref[spots, :] = g_delta
        g_low_ref[spots, :] = g_delta.astype(BF)
        g_gate = jnp.sum(lifted * delta[spots, :], axis=-1, keepdims=True)
        g_gate_ref[spots, :] = jnp.broadcast_to(g_gate, (slots, g_gate_ref.shape[1]))
        router = router + jnp.sum(rows[spots, :] * g_gate, axis=0, keepdims=True)
    router_ref[...] = jnp.broadcast_to(router, router_ref.shape)


def dense_post(ids, stack, project, vecs, mixed, total, one_hot, picked, delta):
    rows, width = mixed.shape
    return stage(
        dense_post_kernel,
        "dense_post",
        ids,
        [stack, project, vecs, mixed, total, one_hot, picked, delta],
        [
            sds((rows, width), F32),
            sds(picked.shape, F32),
            sds(picked.shape, BF),
            sds((picked.shape[0], 128), F32),
            sds((8, width), F32),
        ],
        [pltpu.VMEM((GROUPS, rows, 3 * GW), BF)],
        flops=6 * rows * width * width,
    )


def routed_back_kernel(split, ids, low, g_low, branch, picked, vecs, g_delta, output, *rest):
    weights, rest = rest[:split], rest[split:]
    g_mid_ref, back_ref, gain_ref, stack, parts, grad_s = rest[:6]
    n = pl.program_id(0)

    @pl.when(n == 0)
    def _():
        grad_s[...] = jnp.zeros_like(grad_s)

    expand, reduce_w = this_part(ids[0], weights, rest[6:])
    _, slope = gelu_both(dot(low[...], expand))
    grad_pre = (nt_dot(g_low[...], reduce_w) * slope).astype(BF)
    grad_s[...] += nt_dot(grad_pre, expand)

    @pl.when(n == pl.num_programs(0) - 1)
    def _():
        middle = picked[...].astype(F32) + branch[...]
        g_middle, gain_grad = norm_back(grad_s[...], middle, gain_of(vecs, 2))
        gain_ref[...] = jnp.broadcast_to(gain_grad, gain_ref.shape)
        g_mid_ref[...] = g_middle
        back = (g_delta[...] + g_middle).astype(BF)
        back_ref[...] = back
        save_stack(nt_dot(back, output[...]).astype(BF), parts, stack)


def routed_back(ids, wide_count, low, g_low, branch, picked, vecs, g_delta, output, weights):
    rows, width = branch.shape
    parts_n = weights[0].shape[0 if weights[0].ndim == 3 else 1]
    return stage(
        partial(routed_back_kernel, len(weights)),
        "routed_back",
        ids,
        [low, g_low, branch, picked, vecs, g_delta, output] + list(weights),
        [
            sds((rows, width), F32),
            sds((rows, width), BF),
            sds((8, width), F32),
            sds((wide_count, rows // 4, 2 * GW), BF),
        ],
        [pltpu.VMEM((GROUPS, rows, GW), BF), pltpu.VMEM((rows, width), F32)]
        + part_scratch(width, weights),
        flops=6 * rows * width * parts_n * weights[0].shape[-1],
        grid=(parts_n,),
        specs=part_specs(7, weights),
    )


def routed_post_kernel(ids, stack, *rest):
    project, vecs, picked, g_mid, g_mixed, one_hot, g_gate = rest[:7]
    out_ref, parts = rest[7:]
    g_proj = load_stack(ids[0], stack, parts, 3)
    rows = picked[...].astype(F32)
    grad_rows, _ = norm_back(nt_dot(g_proj, project[...]), rows, gain_of(vecs, 1))
    spread = g_mid[...] + grad_rows + g_gate[:, 0:1] * gain_of(vecs, 0)
    slots, span = one_hot.shape[0] // 2, one_hot.shape[1]
    for q in range(2):
        at, spots = slice(q * span, (q + 1) * span), slice(q * slots, (q + 1) * slots)
        out_ref[at, :] = g_mixed[at, :] + place(one_hot[spots, :], spread[spots, :])


def routed_post(ids, stack, project, vecs, picked, g_mid, g_mixed, one_hot, g_gate):
    rows, width = picked.shape
    (out,) = stage(
        routed_post_kernel,
        "routed_post",
        ids,
        [stack, project, vecs, picked, g_mid, g_mixed, one_hot, g_gate],
        [sds(g_mixed.shape, F32)],
        [pltpu.VMEM((GROUPS, rows, 3 * GW), BF)],
        flops=6 * rows * width * width,
    )
    return out


def split_rows(me, total, keep, send):
    chips, rows = keep.shape[0], keep.shape[1]
    core = lax.rem(me, 2)
    for c in range(chips):
        mine = pl.multiple_of((2 * c + core) * rows, rows)
        other = pl.multiple_of((2 * c + 1 - core) * rows, rows)
        keep[c] = total[pl.ds(mine, rows), :].astype(BF)
        send[c] = total[pl.ds(other, rows), :].astype(BF)


def hidden_grads_kernel(ids, low, grad, expand, reduce_ref, out, total):
    i = pl.program_id(0)
    hidden = expand.shape[1]

    @pl.when(i == 0)
    def _():
        total[...] = jnp.zeros_like(total)

    value, slope = gelu_both(dot(low[...], expand[...]))
    grad_pre = (nt_dot(grad[...], reduce_ref[...]) * slope).astype(BF)
    total[:, 0:hidden] += tn_dot(low[...], grad_pre)
    total[:, hidden : 2 * hidden] += tn_dot(grad[...], value.astype(BF))

    @pl.when(i == pl.num_programs(0) - 1)
    def _():
        out[...] = total[...].astype(BF)


def hidden_grads_pieces_kernel(count, ids, *rest):
    lows, grads = rest[:count], rest[count : 2 * count]
    expand, reduce_ref, out = rest[2 * count :]
    hidden = expand.shape[1]
    low = jnp.concatenate([piece[...] for piece in lows], axis=0)
    grad = jnp.concatenate([piece[...] for piece in grads], axis=0)
    value, slope = gelu_both(dot(low, expand[...]))
    grad_pre = (nt_dot(grad, reduce_ref[...]) * slope).astype(BF)
    out[:, 0:hidden] = tn_dot(low, grad_pre).astype(BF)
    out[:, hidden : 2 * hidden] = tn_dot(grad, value.astype(BF)).astype(BF)


def hidden_grads(ids, low, grad, expand, reduce_part):
    width, hidden = expand.shape
    if isinstance(grad, (list, tuple)):
        (out,) = stage(
            partial(hidden_grads_pieces_kernel, len(grad)),
            "hidden_grads",
            ids,
            list(low) + list(grad) + [expand, reduce_part],
            [sds((width, 2 * hidden), BF)],
            flops=8 * len(grad) * grad[0].size * hidden,
        )
        return out
    block = min(512, low.shape[0])
    row_spec = pl.BlockSpec((block, width), lambda i: (i, 0))
    (out,) = stage(
        hidden_grads_kernel,
        "hidden_grads",
        ids,
        [low, grad, expand, reduce_part],
        [sds((width, 2 * hidden), BF)],
        [pltpu.VMEM((width, 2 * hidden), F32)],
        flops=8 * low.size * hidden,
        grid=(low.shape[0] // block,),
        specs={0: row_spec, 1: row_spec},
    )
    return out


def output_grads_kernel(vectors, ids, att, back, *rest):
    rest = list(rest)
    vecs, rest = rest[:vectors], rest[vectors:]
    keep, send, total = rest
    width = att.shape[1]
    total[:, 0:width] = tn_dot(att[...], back[...])
    if vectors:
        rows = [vec[0:1, :] for vec in vecs]
        rows.append(jnp.zeros((128 - vectors, width), F32))
        total[:, width : width + 128] = jnp.concatenate(rows, axis=0).T
    split_rows(ids[0], total, keep, send)


def output_grads(ids, wide_count, att, back, vecs):
    rows, width = att.shape
    columns = width + (128 if vecs else 0)
    shape = (wide_count // 2, width // wide_count, columns)
    return stage(
        partial(output_grads_kernel, len(vecs)),
        "output_grads",
        ids,
        [att, back] + list(vecs),
        [sds(shape, BF), sds(shape, BF)],
        [pltpu.VMEM((width, columns), F32)],
        flops=3 * rows * width * width,
    )


def join_kernel(pairs, ids, *rest):
    keeps, cames, outs = rest[:pairs], rest[pairs : 2 * pairs], rest[2 * pairs :]
    chip = lax.div(ids[0], 2)
    for s, out in enumerate(outs):
        low = 0
        for keep, came in zip(keeps, cames):
            columns = keep.shape[2]
            total = keep[chip ^ s].astype(F32) + came[chip ^ s].astype(F32)
            out[:, low : low + columns] = total.astype(BF)
            low += columns


def join_chips(ids, keeps, cames):
    chips, rows = keeps[0].shape[:2]
    columns = sum(keep.shape[2] for keep in keeps)
    return stage(
        partial(join_kernel, len(keeps)),
        "join",
        ids,
        list(keeps) + list(cames),
        [sds((rows, columns), BF)] * chips,
    )


def chips_return(parts):
    return [parts[0]] + [chip_step(parts[s], s) for s in range(1, len(parts))]


def sum_terms(terms):
    total = terms[0].astype(F32)
    for term in terms[1:]:
        total = total + term.astype(F32)
    return total


def sum_split_kernel(count, ids, *rest):
    terms, outs, total = rest[:count], rest[count:-1], rest[-1]
    got = terms[0][...].astype(F32)
    for term in terms[1:]:
        got = got + term[...].astype(F32)
    total[...] = got
    rows = outs[0].shape[0]
    for s, out in enumerate(outs):
        at = pl.multiple_of((ids[1] ^ s) * rows, rows)
        out[...] = total[pl.ds(at, rows), :].astype(BF)


def sum_kernel(ids, *rest):
    got = rest[0][...].astype(F32)
    for term in rest[1:-1]:
        got = got + term[...].astype(F32)
    rest[-1][...] = got.astype(BF)


def gather_out_kernel(count, vectors, ids, *rest):
    pieces, outs = rest[:count], rest[count : -1 - vectors]
    vecs, wide_s = rest[-1 - vectors : -1], rest[-1]
    rows = pieces[0].shape[0]
    for s, piece in enumerate(pieces):
        at = pl.ds(pl.multiple_of((ids[1] ^ s) * rows, rows), rows)
        low = 0
        for out in outs:
            columns = out.shape[1]
            out[at, :] = piece[:, low : low + columns].astype(F32)
            low += columns
        wide_s[at, :] = piece[:, low:].astype(F32)
    turned = wide_s[...].T
    for k, vec in enumerate(vecs):
        vec[...] = turned[k : k + 1, :].reshape(vec.shape[0])


def narrow_terms(ids, terms):
    narrow_count = lax.axis_size("narrow")
    rows, columns = terms[0].shape
    if rows % (8 * narrow_count):
        return [sum_terms(terms).astype(BF)]
    return stage(
        partial(sum_split_kernel, len(terms)),
        "sum_split",
        ids,
        terms,
        [sds((rows // narrow_count, columns), BF)] * narrow_count,
        [pltpu.VMEM((rows, columns), F32)],
    )


def spread_parts(parts):
    if len(parts) == 1:
        return [lax.psum(parts[0], "narrow")]
    return narrow_return(parts)


def sum_narrow(ids, terms, first):
    if len(terms) == 1:
        return terms[0]
    return sum_parts(ids, tie(terms, first))


def spread_narrow(ids, total, rows, widths, vectors, first):
    narrow_count = lax.axis_size("narrow")
    if total.shape[0] == rows:
        total = total.astype(F32)
        outs, low = [], 0
        for size in widths:
            outs.append(total[:, low : low + size])
            low += size
        return outs[:-1] + [outs[-1][:, k] for k in range(vectors)]
    return stage(
        partial(gather_out_kernel, narrow_count, vectors),
        "gather_out",
        ids,
        tie(narrow_gather(total), first),
        [sds((rows, size), F32) for size in widths[:-1]] + [sds((rows,), F32)] * vectors,
        [pltpu.VMEM((rows, widths[-1]), F32)],
    )


def join_narrow_kernel(turned, ids, keep, came, *outs):
    each = outs[0].shape[0]
    turn = lax.div(ids[0], 2) if turned else 0
    for t, out in enumerate(outs):
        for j in range(each):
            at = ((ids[1] ^ t) * each + j) ^ turn
            out[j] = (keep[at].astype(F32) + came[at].astype(F32)).astype(BF)


def route_kernel(count, ids, *rest):
    pieces, outs, blocks = rest[:count], rest[count:-1], rest[-1]
    each = pieces[0].shape[0]
    for t, piece in enumerate(pieces):
        for j in range(each):
            blocks[(ids[1] ^ t) * each + j] = piece[j]
    chip = lax.div(ids[0], 2)
    for s, out in enumerate(outs):
        out[...] = blocks[chip ^ s]


def unpack_kernel(turned, ids, *rest):
    pieces, rest = rest[:GROUPS], rest[GROUPS:]
    owns, gains, outs, gain_outs, parts = rest[0:2], rest[2:4], rest[4:8:2], rest[5:8:2], rest[8]
    at = lax.div(ids[0], 2)
    if turned:
        at = at ^ ids[1]
    rows = outs[0].shape[0]
    for block in range(2):
        for s, piece in enumerate(pieces):
            parts[lax.rem(at ^ s, GROUPS)] = piece[block].astype(F32)
        total = jnp.zeros((rows, GW), F32)
        for t in range(3):
            for c in range(GROUPS):
                low = (t * GROUPS + c) * GW
                part = parts[c, :, t * GW : (t + 1) * GW]
                outs[block][:, low : low + GW] = part
                total = total + part * owns[block][:, low : low + GW].astype(F32)
        sums = jnp.broadcast_to(jnp.sum(total, axis=1, keepdims=True), (rows, 128)).T
        gain_outs[block][...] = (sums[0:1, :] / gains[block][...]).reshape(rows)


def unpack(ids, pieces, own_rows):
    rows, columns = pieces[0].shape[1:]
    own_r, own_d, gain_r, gain_d = own_rows
    return stage(
        partial(unpack_kernel, direct_delivery()),
        "unpack",
        ids,
        list(pieces) + [own_d, own_r, gain_d, gain_r],
        [sds((rows, GROUPS * columns), F32), sds((rows,), F32)] * 2,
        [pltpu.VMEM((GROUPS, rows, columns), F32)],
    )


def split_narrow(ids, keep, came):
    narrow_count = lax.axis_size("narrow")
    chips, rows, columns = keep.shape
    shape = (chips // narrow_count, rows, columns)
    return stage(
        partial(join_narrow_kernel, direct_delivery()),
        "join_narrow",
        ids,
        [keep, came],
        [sds(shape, BF)] * narrow_count,
    )


def join_all_kernel(turned, ids, keep, came, out):
    turn = lax.div(ids[0], 2) if turned else 0
    for n in range(out.shape[0]):
        out[n] = (keep[n ^ turn].astype(F32) + came[n ^ turn].astype(F32)).astype(BF)


def join_all(ids, keep, came):
    (total,) = stage(
        partial(join_all_kernel, direct_delivery()),
        "join_all",
        ids,
        [keep, came],
        [sds(keep.shape, BF)],
    )
    return total


def sum_parts(ids, terms):
    (total,) = stage(sum_kernel, "sum_terms", ids, terms, [sds(terms[0].shape, BF)])
    return total


def sum_beside_kernel(ids, beside, *rest):
    terms, out = rest[:-1], rest[-1]
    total = terms[0][...].astype(F32)
    for term in terms[1:]:
        total = total + term[...].astype(F32)
    out[0] = beside[...]
    out[1] = total.astype(BF)


def sum_beside(ids, beside, terms):
    (out,) = stage(
        sum_beside_kernel,
        "sum_beside",
        ids,
        [beside] + list(terms),
        [sds((2,) + beside.shape, BF)],
    )
    return out


def route_project(ids, gathered, chips):
    rows, columns = gathered[0].shape[1:]
    return stage(
        partial(route_kernel, len(gathered)),
        "route",
        ids,
        gathered,
        [sds((rows, columns), BF)] * GROUPS,
        [pltpu.VMEM((chips, rows, columns), BF)],
    )


def direct_delivery():
    return lax.axis_size("narrow") == GROUPS and lax.axis_size("wide") == 2 * GROUPS


def deliver(ids, totals, chips):
    narrow_count = lax.axis_size("narrow")
    if not direct_delivery():
        both = [
            chips_return(route_project(ids, narrow_gather(total), chips)) for total in totals
        ]
        return [jnp.stack(pair) for pair in zip(*both)]
    totals = totals.reshape((2,) + totals.shape[2:])

    def moves(k):
        pairs = []
        for chip in range(chips):
            for core in range(2):
                for n in range(narrow_count):
                    to = (2 * (chip ^ n) + core) * narrow_count + (n ^ k)
                    pairs.append(((2 * chip + core) * narrow_count + n, to))
        return pairs

    return [lax.ppermute(totals, ("wide", "narrow"), moves(k)) for k in range(narrow_count)]


def finish_hidden_kernel(ids, dense, routed, e_d, r_d, e_r, r_r):
    hidden = e_d.shape[1]
    for total, e_ref, r_ref in ((dense, e_d, r_d), (routed, e_r, r_r)):
        e_ref[...] = total[:, 0:hidden].astype(F32)
        r_ref[...] = total[:, hidden : 2 * hidden].astype(F32)


def finish_hidden(ids, dense, routed):
    rows, columns = dense.shape
    return stage(
        finish_hidden_kernel,
        "finish_hidden",
        ids,
        [dense, routed],
        [sds((rows, columns // 2), F32)] * 4,
    )


def tie(x, *first):
    return lax.optimization_barrier((x, first))[0]


def narrow_step(x, s):
    return lax.ppermute(x, "narrow", [(j, j ^ s) for j in range(lax.axis_size("narrow"))])


def narrow_gather(x):
    return [x] + [narrow_step(x, s) for s in range(1, lax.axis_size("narrow"))]


def narrow_return(parts):
    return [parts[0]] + [narrow_step(parts[s], s) for s in range(1, len(parts))]


def exchange(pieces):
    wide_count = lax.axis_size("wide")
    return [pieces[0]] + [
        lax.ppermute(pieces[s], "wide", [(j, j ^ s) for j in range(wide_count)])
        for s in range(1, len(pieces))
    ]


def exchange_rows(mine, other):
    wide_count = lax.axis_size("wide")
    if wide_count != 8:
        return exchange([mine, other] * (wide_count // 2))
    beside = core_step(other)
    from_x = [chip_step(mine, 1), chip_step(beside, 1)]
    from_y = [chip_step(mine, 2), chip_step(beside, 2)]
    corner = [chip_step(from_y[0], 1), chip_step(from_x[1], 2)]
    return [mine, beside] + from_x + from_y + corner


def hidden_share(expand, reduce_part):
    wide_count = lax.axis_size("wide")
    here = lax.axis_index("wide")
    width, hidden = expand.shape
    rows = width // wide_count
    if width != hidden or rows % 16:
        return None
    return jnp.stack(
        [
            lax.dynamic_slice_in_dim(expand, here * rows, rows, 0),
            lax.dynamic_slice_in_dim(reduce_part, here * rows, rows, 0),
        ]
    )


def all_chips(x):
    groups = [list(range(core, lax.axis_size("wide"), 2)) for core in range(2)]
    return lax.all_gather(x, "wide", axis=0, axis_index_groups=groups)


def chip_step(x, s):
    return lax.ppermute(
        x, "wide", [(j, j ^ (2 * s)) for j in range(lax.axis_size("wide"))]
    )


def core_step(x):
    return lax.ppermute(x, "wide", [(j, j ^ 1) for j in range(lax.axis_size("wide"))])


def on_device(
    tokens,
    cotangent,
    selected,
    segments,
    router_vector,
    project_routed,
    output_routed,
    prenorm_routed,
    midnorm_routed,
    expand_routed,
    reduce_routed,
    project_dense,
    output_dense,
    prenorm_dense,
    midnorm_dense,
    expand_dense,
    reduce_dense,
):
    seq_count, span_rows, width = tokens.shape
    row_length = selected.shape[1]
    hidden = expand_dense.shape[1]
    wide_count = lax.axis_size("wide")
    narrow_count = lax.axis_size("narrow")
    here = lax.axis_index("wide")
    slot_count = span_rows // 4
    bq_dense = min(512, row_length)
    bq_routed = min(512, slot_count * wide_count)
    ids = jnp.stack([here, lax.axis_index("narrow")]).astype(jnp.int32)
    tok = tokens.reshape(-1, width)
    cot = cotangent.reshape(-1, width)

    share_d = hidden_share(expand_dense, reduce_dense)
    staged = share_d is not None
    if staged:
        own_d = lax.all_gather(share_d, "narrow", axis=0)

    mine = here % seq_count
    seq_segments = lax.dynamic_slice_in_dim(segments, mine, 1, 0)[0]
    seq_selected = lax.dynamic_slice_in_dim(selected, mine, 1, 0)[0].reshape(wide_count, span_rows)
    upper = (
        lax.broadcasted_iota(jnp.int32, (span_rows, span_rows), 0)
        <= lax.broadcasted_iota(jnp.int32, (span_rows, span_rows), 1)
    ).astype(BF)
    slots = jnp.arange(slot_count, dtype=jnp.int32)
    seq_rank = jnp.dot(seq_selected.astype(BF), upper, preferred_element_type=F32)
    seq_rank = jnp.where(seq_selected > 0, seq_rank.astype(jnp.int32) - 1, -1)
    slot_segments = (
        jnp.sum(
            jnp.where(
                seq_rank[:, None, :] == slots[None, :, None],
                seq_segments.reshape(wide_count, 1, span_rows) + 1,
                0,
            ),
            axis=-1,
        )
        - 1
    ).reshape(-1)
    meta_routed = (None, slot_segments[None])
    own_selected = selected
    if span_rows % 128:
        own_selected = lax.dynamic_slice_in_dim(selected, here * span_rows, span_rows, 1)
    mine_r, other_r, one_hot, picked, vecs = routed_pre(
        ids,
        tok,
        own_selected,
        span_rows,
        [router_vector, prenorm_routed, midnorm_routed, prenorm_dense, midnorm_dense],
    )
    columns_r = group_columns(ids, tie(project_routed, mine_r))
    rows_r = exchange([mine_r, other_r] * (wide_count // 2))
    rows_r, slot_segments = lax.optimization_barrier((rows_r, meta_routed[1]))
    meta_routed = (None, slot_segments)
    pieces, kept_r = attend(ids, meta_routed, rows_r, columns_r, bq_routed)
    pieces = exchange(pieces)
    if staged:
        pieces, own_d = lax.optimization_barrier((pieces, own_d))
        chips_d = all_chips(own_d)
    branch_r, low_r, att_r = routed_mid(ids, pieces, output_routed, picked, vecs)
    dense_segments = tie(seq_segments, low_r)
    starts = sum(
        jnp.where(dense_segments == value, jnp.sum((dense_segments < value).astype(jnp.int32)), 0)
        for value in range(1, 4)
    )
    meta_dense = (starts[::bq_dense] // bq_dense, starts[None])

    own_at = here * (width // wide_count)

    def own_slice(x):
        return lax.dynamic_slice_in_dim(tie(x, low_r), own_at, width // wide_count, 0)

    own_rows = (
        own_slice(project_routed),
        own_slice(project_dense),
        own_slice(prenorm_routed).astype(F32)[None],
        own_slice(prenorm_dense).astype(F32)[None],
    )
    columns_d = group_columns(ids, tie(project_dense, low_r))
    share_r = hidden_share(tie(expand_routed, low_r), reduce_routed)
    low_pieces, columns_d, meta_dense, own_rows, share_r = lax.optimization_barrier(
        (narrow_gather(low_r), columns_d, meta_dense, own_rows, share_r)
    )
    partials = narrow_return(hidden_forward(ids, low_pieces, expand_routed, reduce_routed))

    mine_d, other_d, mixed, delta_r = dense_pre(
        ids, tok, one_hot, picked, vecs, branch_r, partials
    )
    if staged:
        rows_d = exchange_rows(mine_d, other_d)
        own_r = lax.all_gather(tie(share_r, rows_d[1], chips_d), "narrow", axis=0)[None]
        rows_d, own_r = lax.optimization_barrier((rows_d, own_r))
        weights_d = [chips_d, core_step(chips_d)]
    else:
        rows_d = exchange_rows(mine_d, other_d)
        weights_d = [
            lax.all_gather(expand_dense, "narrow", axis=0),
            lax.all_gather(reduce_dense, "narrow", axis=0),
        ]
        weights_r = [
            lax.all_gather(expand_routed, "narrow", axis=0),
            lax.all_gather(reduce_routed, "narrow", axis=0),
        ]
    cot_all = lax.all_gather(tie(cot, rows_d), "narrow", axis=0, tiled=True)
    (stack,), kept_d = attend(ids, meta_dense, rows_d, columns_d, bq_dense, stacked=True)
    stack, weights_d = lax.optimization_barrier((stack, weights_d))
    stack = lax.all_to_all(stack, "wide", 0, 0)
    if staged:
        stack, own_r = lax.optimization_barrier((stack, own_r))
        corner_r = chip_step(own_r, 3)
    (activations, low_d, back_d, sum_d, att_d, mid_gain_d), stack = dense_ffn(
        ids, stack, output_dense, mixed, cot, vecs, weights_d
    )
    if staged:
        stack, low_d, cot_all, corner_r = lax.optimization_barrier(
            (stack, low_d, cot_all, corner_r)
        )
    low_all = lax.all_gather(low_d, "narrow", axis=0, tiled=True)
    keep_d, send_d = output_grads(ids, wide_count, att_d, back_d, [])
    stack, keep_d, send_d = lax.optimization_barrier(
        (lax.all_to_all(stack, "wide", 0, 0), keep_d, send_d)
    )
    came_d = core_step(send_d)
    if staged:
        stack, own_r = lax.optimization_barrier((stack, own_r))
        sides_r = [chip_step(own_r, 1), chip_step(own_r, 2)]
        corner_r = [corner_r, core_step(corner_r)]
        weights_r = [own_r, core_step(own_r)]
    (stack,), dx_d = attend_back(ids, meta_dense, kept_d, [stack], bq_dense, stacked=True)
    stack, dx_d, weights_r, came_d = lax.optimization_barrier(
        (stack, dx_d, weights_r, came_d)
    )
    if staged:
        dx_d, sides_r = lax.optimization_barrier((dx_d, sides_r))
        weights_r += [w for own in sides_r for w in (own, core_step(own))] + corner_r
    stack = lax.all_to_all(stack, "wide", 0, 0)
    keep, send = project_grads(ids, wide_count, rows_d, dx_d)
    project_d = join_all(ids, keep, core_step(send))
    low_all, project_d = lax.optimization_barrier((low_all, project_d))
    project_d = lax.psum_scatter(project_d, "narrow", scatter_dimension=0, tiled=True)
    hidden_d = hidden_grads(ids, low_all, cot_all, expand_dense, reduce_dense)
    stack, hidden_d, weights_r = lax.optimization_barrier((stack, hidden_d, weights_r))
    ffn_d = lax.psum_scatter(hidden_d, "wide", scatter_dimension=0, tiled=True)
    g_mixed, g_delta, g_low, g_gate, router_grad = dense_post(
        ids, stack, project_dense, vecs, mixed, sum_d, one_hot, picked, delta_r
    )

    g_pieces = narrow_gather(g_low)
    g_mid_r, back_r, mid_gain_r, stack = routed_back(
        ids,
        wide_count,
        low_r,
        g_low,
        branch_r,
        picked,
        vecs,
        g_delta,
        output_routed,
        weights_r,
    )
    back_r, g_pieces = lax.optimization_barrier((back_r, g_pieces))
    keep_r, send_r = output_grads(
        ids, wide_count, att_r, back_r, [mid_gain_r, mid_gain_d, router_grad]
    )
    came_r = core_step(send_r)
    hidden_r = hidden_grads(
        ids,
        tie(low_pieces, keep_r),
        g_pieces,
        expand_routed,
        reduce_routed,
    )
    stack, keep_r, send_r, hidden_r = lax.optimization_barrier(
        (lax.all_to_all(stack, "wide", 0, 0), keep_r, send_r, hidden_r)
    )
    output_parts = join_chips(ids, tie([keep_d, keep_r], hidden_r), [came_d, came_r])
    stack, output_parts = lax.optimization_barrier((stack, output_parts))
    output_terms = chips_return(output_parts)
    (stack,), dx_r = attend_back(ids, meta_routed, kept_r, [stack], bq_routed, stacked=True)
    stack, dx_r, output_terms[1], project_d = lax.optimization_barrier(
        (stack, dx_r, output_terms[1], project_d)
    )
    keep, send = project_grads(ids, wide_count, rows_r, dx_r)
    came = core_step(send)
    output_parts = narrow_terms(ids, tie(output_terms, send))
    ffn_r = lax.psum_scatter(
        tie(hidden_r, output_parts), "wide", scatter_dimension=0, tiled=True
    )
    project_parts = split_narrow(ids, tie(keep, output_parts), came)
    returned = narrow_return(project_parts)
    stack = lax.all_to_all(tie(stack, send), "wide", 0, 0)
    returned, output_parts = lax.optimization_barrier(
        (returned, spread_parts(output_parts))
    )
    projects = sum_beside(ids, project_d, returned)
    output_total = sum_narrow(ids, output_parts, projects)
    tokens_gradient = routed_post(
        ids,
        tie(stack, output_total),
        project_routed,
        vecs,
        picked,
        g_mid_r,
        g_mixed,
        one_hot,
        g_gate,
    )
    delivered = deliver(ids, projects, keep.shape[0])
    project_d_grad, pre_gain_d, project_r_grad, pre_gain_r = unpack(
        ids, tie(delivered, tokens_gradient), own_rows
    )
    output_d_grad, output_r_grad, mid_r_grad, mid_d_grad, router_grad = spread_narrow(
        ids, output_total, width // wide_count, [width, width, 128], 3, project_r_grad
    )
    expand_d_grad, reduce_d_grad, expand_r_grad, reduce_r_grad = finish_hidden(
        ids, ffn_d, ffn_r
    )
    return (
        activations.reshape(tokens.shape),
        tokens_gradient.reshape(tokens.shape),
        router_grad,
        project_r_grad,
        output_r_grad,
        pre_gain_r,
        mid_r_grad,
        expand_r_grad,
        reduce_r_grad.T,
        project_d_grad,
        output_d_grad,
        pre_gain_d,
        mid_d_grad,
        expand_d_grad,
        reduce_d_grad.T,
    )


def solution(mesh):
    return jax.shard_map(
        on_device,
        mesh=mesh,
        in_specs=(
            P("narrow", "wide", None),
            P("narrow", "wide", None),
            P("narrow", None),
            P("narrow", None),
            P(),
            P(),
            P(),
            P(),
            P(),
            P(None, "narrow"),
            P("narrow", None),
            P(),
            P(),
            P(),
            P(),
            P(None, "narrow"),
            P("narrow", None),
        ),
        out_specs=(
            P("narrow", "wide", None),
            P("narrow", "wide", None),
            P("wide"),
            P("wide", None),
            P("wide", None),
            P("wide"),
            P("wide"),
            P("wide", "narrow"),
            P("narrow", "wide"),
            P("wide", None),
            P("wide", None),
            P("wide"),
            P("wide"),
            P("wide", "narrow"),
            P("narrow", "wide"),
        ),
        check_vma=False,
    )
```
